32 devices in a mesh: dp: 4 (over y, core), fsdp: 8 (over z, x).
Axes of the slice: x: 2, y: 2, z: 4, core: 2. Of those that a mesh axis runs over, the one named last changes fastest.
Arguments:
- tokens: bfloat16 [64, 512, 768], P(('dp', 'fsdp')), may hold values from -6 to 6
- counts: int32 [64], P(('dp', 'fsdp')), may hold values from 30 to 512, as said below
- cotangent: bfloat16 [64, 512, 768], P(('dp', 'fsdp')), may hold values from -6 to 6
- query_weight: bfloat16 [768, 768], P('fsdp'), may hold values from -0.21875 to 0.21875
- key_weight: bfloat16 [768, 768], P('fsdp'), may hold values from -0.21875 to 0.21875
- value_weight: bfloat16 [768, 768], P('fsdp'), may hold values from -0.21875 to 0.21875
- out_weight: bfloat16 [768, 768], P('fsdp'), may hold values from -2.5 to 2.5
- query_bias: bfloat16 [768], P('fsdp'), may hold values from -1 to 1
- value_bias: bfloat16 [768], P('fsdp'), may hold values from -1 to 1
- out_bias: bfloat16 [768], P('fsdp'), may hold values from -1 to 1
- attention_gain: bfloat16 [768], P('fsdp'), may hold values from 0.5 to 1.5
- attention_shift: bfloat16 [768], P('fsdp'), may hold values from -1 to 1
- up_weight: bfloat16 [768, 3072], P('fsdp'), may hold values from -0.21875 to 0.21875
- up_bias: bfloat16 [3072], P('fsdp'), may hold values from -1 to 1
- down_weight: bfloat16 [3072, 768], P('fsdp'), may hold values from -0.109375 to 0.109375
- down_bias: bfloat16 [768], P('fsdp'), may hold values from -1 to 1
- feed_gain: bfloat16 [768], P('fsdp'), may hold values from 0.5 to 1.5
- feed_shift: bfloat16 [768], P('fsdp'), may hold values from -1 to 1
Outputs:
- layer_out: bfloat16 [64, 512, 768], P(('dp', 'fsdp'))
- input_grad: float32 [64, 512, 768], P(('dp', 'fsdp'))
- grad_query_weight: float32 [768, 768], P('fsdp')
- grad_key_weight: float32 [768, 768], P('fsdp')
- grad_value_weight: float32 [768, 768], P('fsdp')
- grad_out_weight: float32 [768, 768], P('fsdp')
- grad_query_bias: float32 [768], P('fsdp')
- grad_value_bias: float32 [768], P('fsdp')
- grad_out_bias: float32 [768], P('fsdp')
- grad_attention_gain: float32 [768], P('fsdp')
- grad_attention_shift: float32 [768], P('fsdp')
- grad_up_weight: float32 [768, 3072], P('fsdp')
- grad_up_bias: float32 [3072], P('fsdp')
- grad_down_weight: float32 [3072, 768], P('fsdp')
- grad_down_bias: float32 [768], P('fsdp')
- grad_feed_gain: float32 [768], P('fsdp')
- grad_feed_shift: float32 [768], P('fsdp')
The draws below stay inside these ranges and needn't reach their ends.
Inputs may be any that keep to these rules, and one draw needn't show every extreme that they name: `counts`: true tokens of each slot; some slot holds 512.
All inputs are finite; a program needn't handle non-finite values.
Results may differ from the reference program's by a relative error of at most 0.018.
Values may be sent and summed in bfloat16 or wider, within the bound.
A program may use at most 192 MiB of HBM per device.

```python
import math
import jax
import jax.numpy as jnp
from jax import lax

D = 768
HEADS = 12
HEAD_DIM = 64
FF = 3072
SEQ = 512
MIN_LEN = 30
DOCS = 64


def draw_counts(key, part):
    drawn = jax.random.randint(key, (DOCS,), MIN_LEN, SEQ + 1)
    return drawn.at[0].set(SEQ).astype(jnp.int32)


def block_scale(own_key, shape, pieces, low, top_value):
    loudness = 1.0
    for position, shards_of in pieces:
        steps = jax.random.uniform(jax.random.fold_in(jax.random.fold_in(own_key, 6), position), (shards_of,), jnp.float32, low / len(pieces), top_value / len(pieces))
        loudness = loudness * jnp.repeat(jnp.exp(steps), shape[position] // shards_of).reshape((-1,) + (1,) * (len(shape) - 1 - position))
    return loudness


def gaussian(key, shape, scale, limit, shards=(), kind=jnp.bfloat16):
    level = block_scale(key, shape, shards, -0.22, 0.18) if shards else 1.0
    values = jax.random.normal(key, shape, jnp.float32) * scale * level
    return jnp.minimum(jnp.maximum(values, -limit), limit).astype(kind)


def setup_inputs(seed: int = 0) -> dict:
    key_of = jax.random.split(jax.random.key(seed), 19)
    tokens = gaussian(key_of[0], (DOCS, SEQ, D), 1.0, 6.0, ((0, 32),))
    counts = draw_counts(jax.random.fold_in(key_of[18], 71), 0)
    cotangent = gaussian(key_of[2], (DOCS, SEQ, D), 1.0, 6.0, ((0, 32),))
    query_weight = gaussian(key_of[3], (D, D), D ** -0.5, 0.21875, ((0, 8),))
    key_weight = gaussian(key_of[4], (D, D), D ** -0.5, 0.21875, ((0, 8),))
    value_weight = gaussian(key_of[5], (D, D), D ** -0.5, 0.21875, ((0, 8),))
    out_weight = gaussian(key_of[6], (D, D), (max(1, D * 4 // SEQ)) ** -0.5, 2.5, ((0, 8),))
    query_bias = gaussian(key_of[7], (D,), 0.2, 1.0, ((0, 8),))
    value_bias = gaussian(key_of[8], (D,), 0.2, 1.0, ((0, 8),))
    out_bias = gaussian(key_of[9], (D,), 0.2, 1.0, ((0, 8),))
    attention_gain = jnp.clip(1.0 + 0.1 * jax.random.normal(key_of[10], (D,), jnp.float32), 0.5, 1.5).astype(jnp.bfloat16)
    attention_shift = gaussian(key_of[11], (D,), 0.2, 1.0, ((0, 8),))
    up_weight = gaussian(key_of[12], (D, FF), D ** -0.5, 0.21875, ((0, 8),))
    up_bias = gaussian(key_of[13], (FF,), 0.2, 1.0, ((0, 8),))
    down_weight = gaussian(key_of[14], (FF, D), FF ** -0.5, 0.109375, ((0, 8),))
    down_bias = gaussian(key_of[15], (D,), 0.2, 1.0, ((0, 8),))
    feed_gain = jnp.clip(1.0 + 0.1 * jax.random.normal(key_of[16], (D,), jnp.float32), 0.5, 1.5).astype(jnp.bfloat16)
    feed_shift = gaussian(key_of[17], (D,), 0.2, 1.0, ((0, 8),))
    return {"tokens": tokens, "counts": counts, "cotangent": cotangent, "query_weight": query_weight, "key_weight": key_weight, "value_weight": value_weight, "out_weight": out_weight, "query_bias": query_bias, "value_bias": value_bias, "out_bias": out_bias, "attention_gain": attention_gain, "attention_shift": attention_shift, "up_weight": up_weight, "up_bias": up_bias, "down_weight": down_weight, "down_bias": down_bias, "feed_gain": feed_gain, "feed_shift": feed_shift}


@jax.custom_vjp
def low(v):
    return lax.optimization_barrier(v.astype(jnp.bfloat16)).astype(jnp.float32)

@jax.custom_vjp
def low_back(v):
    return v

def low_keep(v):
    return (low(v), None)

def low_pass(kept, grad):
    return (grad,)

def back_keep(v):
    return (v, None)

def back_low(kept, grad):
    return (low(grad),)
low.defvjp(low_keep, low_pass)
low_back.defvjp(back_keep, back_low)
epsilon = 1e-05
precise = lax.Precision.HIGHEST

def product(left, right):
    return jnp.dot(left, right, precision=precise)

def normed(resid, gain, shift):
    average = lax.optimization_barrier(jnp.mean(resid, axis=-1, keepdims=True))
    centred = resid - average
    spread = lax.optimization_barrier(jnp.mean(centred * centred, axis=-1, keepdims=True))
    return centred * lax.rsqrt(spread + epsilon) * gain + shift

def attend(block):
    query, keys, values, count = block
    raw = low_back(jnp.einsum('qhd,khd->hqk', query, keys, precision=precise))
    live = jnp.arange(SEQ, dtype=jnp.int32) < count
    scores = jnp.where(live[None, None, :], raw * HEAD_DIM ** (-0.5), -1000000000.0)
    probs = low(jax.nn.softmax(scores, axis=-1))
    context = jnp.einsum('hqk,khd->qhd', probs, values, precision=precise)
    return context.reshape(SEQ, D)

def split_heads(value):
    return value.reshape(-1, SEQ, HEADS, HEAD_DIM)

def layer(params, inputs, counts):
    query_weight, key_weight, value_weight, out_weight, query_bias, value_bias, out_bias, attention_gain, attention_shift, up_weight, up_bias, down_weight, down_bias, feed_gain, feed_shift = params
    rows = inputs.reshape(-1, D)
    query = low(low_back(product(rows, query_weight) + query_bias))
    keys = low(low_back(product(rows, key_weight)))
    values = low(low_back(product(rows, value_weight) + value_bias))
    context = lax.map(jax.checkpoint(attend), (split_heads(query), split_heads(keys), split_heads(values), counts))
    context = low(low_back(context.reshape(-1, D)))
    branch = low_back(product(context, out_weight) + out_bias)
    first = normed(rows + branch, attention_gain, attention_shift)
    hidden = low_back(product(low(first), up_weight) + up_bias)
    second = low_back(product(low(jax.nn.gelu(hidden, approximate=False)), down_weight) + down_bias)
    output = normed(first + second, feed_gain, feed_shift)
    live = (jnp.arange(SEQ, dtype=jnp.int32)[None, :] < counts[:, None]).reshape(-1, 1)
    return jnp.where(live, output, 0.0).reshape(inputs.shape)

def reference(tokens, counts, cotangent, query_weight, key_weight, value_weight, out_weight, query_bias, value_bias, out_bias, attention_gain, attention_shift, up_weight, up_bias, down_weight, down_bias, feed_gain, feed_shift):
    params = tuple((p.astype(jnp.float32) for p in (query_weight, key_weight, value_weight, out_weight, query_bias, value_bias, out_bias, attention_gain, attention_shift, up_weight, up_bias, down_weight, down_bias, feed_gain, feed_shift)))
    group = math.gcd(DOCS, max(1, 4096 // SEQ))
    rounds = DOCS // group

    def run(totals, block):
        inputs, count, upstream = block

        def forward(weights, values):
            return layer(weights, values, count)
        output, pull = jax.vjp(forward, params, inputs.astype(jnp.float32))
        grad_params, grad_inputs = pull(upstream.astype(jnp.float32))
        totals = jax.tree.map(jnp.add, totals, grad_params)
        return (totals, (output.astype(jnp.bfloat16), grad_inputs))
    zeros = tuple((jnp.zeros_like(p) for p in params))
    totals, (outputs, grads) = lax.scan(run, zeros, (tokens.reshape(rounds, group, SEQ, D), counts.reshape(rounds, group), cotangent.reshape(rounds, group, SEQ, D)))
    return (outputs.reshape(DOCS, SEQ, D), grads.reshape(DOCS, SEQ, D), totals[0], totals[1], totals[2], totals[3], totals[4], totals[5], totals[6], totals[7], totals[8], totals[9], totals[10], totals[11], totals[12], totals[13], totals[14])
```

```python
import functools

import jax
import jax.numpy as jnp
from jax import lax
from jax.experimental import pallas as pl
from jax.experimental.pallas import tpu as pltpu
from jax.sharding import PartitionSpec as P

HEAD_DIM = 64
epsilon = 1e-05
F32 = jnp.float32
BF16 = jnp.bfloat16
MESH = pl.DeviceIdType.MESH
VMEM_LIMIT = 63 * 2**20
Shape = jax.ShapeDtypeStruct


def dot(left, right):
    return lax.dot_general(
        left, right, (((1,), (0,)), ((), ())), preferred_element_type=F32
    )


def dot_t(left, right):
    return lax.dot_general(
        left, right, (((1,), (1,)), ((), ())), preferred_element_type=F32
    )


def params(**extra):
    return pltpu.CompilerParams(vmem_limit_bytes=VMEM_LIMIT, **extra)


def whole(shape):
    return pl.BlockSpec(shape, lambda *_: (0,) * len(shape), pipeline_mode=pl.Buffered(1))


NX, NZ, ROWS = 2, 4, 96


def place():
    member = lax.axis_index("dp")
    shard = lax.axis_index("fsdp")
    return shard % NX, member // 2, shard // NX, member % 2


def at(x, y, z, core):
    return {"dp": y * 2 + core, "fsdp": z * NX + x}


def greet(peers):
    barrier = pltpu.get_barrier_semaphore()
    for peer in peers:
        pl.semaphore_signal(barrier, inc=1, device_id=peer, device_id_type=MESH)
    pl.semaphore_wait(barrier, len(peers))


def all_peers():
    x, y, z, core = place()
    near = [at(x, 1 - y, z, core), at(x, y, z, 1 - core)]
    for step in range(1, NX * NZ):
        near.append({"dp": y * 2 + core, "fsdp": (z * NX + x + step) % (NX * NZ)})
    return near


class Wire:
    def __init__(self, send, recv):
        self.send, self.recv, self.used = send, recv, 0

    def copy(self, source, target, peer):
        slot = self.used
        self.used += 1
        return pltpu.make_async_remote_copy(
            src_ref=source,
            dst_ref=target,
            send_sem=self.send.at[slot],
            recv_sem=self.recv.at[slot],
            device_id=peer,
            device_id_type=MESH,
        )


def gather_kernel(wq, wk, wv, wo, wu, wd, vec, g4, gu, gd, gv, local, send, recv):
    x, y, z, core = place()
    shard = z * NX + x
    member, other = y * 2 + core, (1 - y) * 2 + core

    def part(group, who, zs, xs):
        if group == 0:
            return g4.at[who, zs, xs]
        if group == 1:
            return gu.at[zs, xs, :, pl.ds(pl.multiple_of(who * 768, 768), 768)]
        return gd.at[zs, xs, who]

    own = [
        (wq, part(0, member, z, x)),
        (wu.at[:, pl.ds(pl.multiple_of(member * 768, 768), 768)], part(1, member, z, x)),
        (wd.at[member], part(2, member, z, x)),
        (vec, gv.at[shard]),
    ]
    own = [pltpu.make_async_copy(a, b, local.at[i]) for i, (a, b) in enumerate(own)]
    for i, w in enumerate((wq, wk, wv, wo)):

        @pl.when(member == i)
        def _():
            pltpu.make_async_copy(w, part(0, i, z, x), local.at[0]).start()

    for c in own[1:]:
        c.start()
    greet(all_peers())
    for c in own:
        c.wait()
    wire = Wire(send, recv)
    x_peer, y_peer, c_peer = at(1 - x, y, z, core), at(x, 1 - y, z, core), at(x, y, z, 1 - core)
    every = slice(None)
    sent = []

    def start(source, peer):
        c = wire.copy(source, source, peer)
        c.start()
        sent.append(c)
        return c

    vecs = [
        start(gv.at[shard], {"dp": member, "fsdp": (shard + k) % (NX * NZ)})
        for k in range(1, NX * NZ)
    ]
    along_z = [
        [start(part(g, member, z, x), at(x, y, (z + k) % NZ, core)) for k in range(1, NZ)]
        for g in range(3)
    ]
    first, second, last = [], [], []

    def plane(g):
        for c in along_z[g]:
            c.wait_recv()
        mine = part(g, member, every, x)
        first.append((start(mine, x_peer), start(mine, y_peer)))
        last.append(start(mine, c_peer))

    def corner(g):
        from_x, from_y = first[g]
        from_y.wait_recv()
        a = start(part(g, other, pl.ds(0, 2), x), x_peer)
        last.append(start(part(g, other, every, x), c_peer))
        from_x.wait_recv()
        b = start(part(g, member, pl.ds(2, 2), 1 - x), y_peer)
        last.append(start(part(g, member, every, 1 - x), c_peer))
        second.append((a, b))

    def rest(g):
        for c in second[g]:
            c.wait_recv()
        last.append(start(part(g, other, every, 1 - x), c_peer))

    plane(0)
    plane(1)
    corner(0)
    plane(2)
    corner(1)
    rest(0)
    corner(2)
    rest(1)
    rest(2)
    for c in vecs + last:
        c.wait_recv()
    for c in sent:
        c.wait_send()


def gather_all(wq, wk, wv, wo, wu, wd, vec):
    rows, width = wq.shape
    columns = wu.shape[1]
    copies = 7 + 3 * (3 + 2 + 2 + 4)
    hbm = pl.BlockSpec(memory_space=pl.ANY)
    return pl.pallas_call(
        gather_kernel,
        name="gather_all",
        in_specs=[pl.BlockSpec(memory_space=pltpu.VMEM)] * 7,
        out_specs=[hbm] * 4,
        out_shape=[
            Shape((4, NZ, NX, rows, width), BF16),
            Shape((NZ, NX, rows, columns), BF16),
            Shape((NZ, NX, 4, rows, width), BF16),
            Shape((NX * NZ,) + vec.shape, BF16),
        ],
        scratch_shapes=[
            pltpu.SemaphoreType.DMA((7,)),
            pltpu.SemaphoreType.DMA((copies,)),
            pltpu.SemaphoreType.DMA((copies,)),
        ],
        compiler_params=params(collective_id=0, has_side_effects=True),
    )(wq, wk, wv, wo, wu, wd.reshape(4, rows, width), vec)


def reduce_kernel(p4, pu, pd, pv, o4, ou, od, ov, *scratch):
    bufs, (va, vb), (send, recv) = scratch[:21], scratch[21:23], scratch[23:]
    x, y, z, core = place()
    shard = z * NX + x
    member, other = y * 2 + core, (1 - y) * 2 + core
    wire = Wire(send, recv)
    x_peer, y_peer, c_peer = at(1 - x, y, z, core), at(x, 1 - y, z, core), at(x, y, z, 1 - core)
    sent = []

    def start(source, target, peer):
        c = wire.copy(source, target, peer)
        c.start()
        sent.append(c)
        return c

    greet(all_peers())
    groups = [(p,) + tuple(bufs[7 * i : 7 * i + 7]) for i, p in enumerate((p4, pu, pd))]
    over_core, over_x, over_y, then_x, then_y, over_z = [], [], [], [], [], []

    vec_a = []
    for k in range(1, NX * NZ):
        to = (shard + k) % (NX * NZ)
        vec_a.append(start(pv.at[to], va.at[k - 1], {"dp": member, "fsdp": to}))
    for p, rc, *_ in groups:
        over_core.append([start(p.at[yy * 2 + 1 - core], rc.at[yy], c_peer) for yy in range(2)])

    def chip(g):
        p, rc, bx, by, cx, cy, bz, fin = groups[g]
        for yy in range(2):
            over_core[g][yy].wait_recv()

            @pl.loop(0, NZ)
            def _(zz):
                for xx in range(NX):
                    rc[yy, zz, xx] = rc[yy, zz, xx] + p[yy * 2 + core, zz, xx]

        over_x.append(start(rc.at[:, pl.ds(0, 2), 1 - x], bx, x_peer))
        over_y.append(start(rc.at[1 - y, pl.ds(2, 2)], by, y_peer))

    def plane(g):
        p, rc, bx, by, cx, cy, bz, fin = groups[g]
        over_x[g].wait_recv()

        @pl.loop(0, 2)
        def _(zz):
            for yy in range(2):
                rc[yy, zz, x] = rc[yy, zz, x] + bx[yy, zz]

        then_y.append(start(rc.at[1 - y, pl.ds(0, 2), x], cy, y_peer))
        over_y[g].wait_recv()

        @pl.loop(0, 2)
        def _(zz):
            for xx in range(NX):
                rc[y, 2 + zz, xx] = rc[y, 2 + zz, xx] + by[zz, xx]

        then_x.append(start(rc.at[y, pl.ds(2, 2), 1 - x], cx, x_peer))

    def depth(g):
        p, rc, bx, by, cx, cy, bz, fin = groups[g]
        then_y[g].wait_recv()
        then_x[g].wait_recv()

        @pl.loop(0, 2)
        def _(zz):
            rc[y, zz, x] = rc[y, zz, x] + cy[zz]
            rc[y, 2 + zz, x] = rc[y, 2 + zz, x] + cx[zz]

        over_z.append(
            [
                start(rc.at[y, (z + k) % NZ, x], bz.at[k - 1], at(x, y, (z + k) % NZ, core))
                for k in range(1, NZ)
            ]
        )

    to_y, to_c, relay = [], [], []

    def total(g):
        p, rc, bx, by, cx, cy, bz, fin = groups[g]
        for c in over_z[g]:
            c.wait_recv()
        summed = rc[y, z, x].astype(F32)
        for k in range(NZ - 1):
            summed = summed + bz[k].astype(F32)
        fin[member] = summed.astype(BF16)
        to_y.append(start(fin.at[member], fin.at[member], y_peer))
        to_c.append(start(fin.at[member], fin.at[member], c_peer))

    def spread(g):
        fin = groups[g][7]
        to_y[g].wait_recv()
        relay.append(start(fin.at[other], fin.at[other], c_peer))

    for step in (chip, plane, depth, total, spread):
        if step is chip:
            for g in range(3):
                chip(g)
            for c in vec_a:
                c.wait_recv()
            part = pv[shard]
            for k in range(NX * NZ - 1):
                part = part + va[k]
            vb[member] = part
            vec_b = [
                start(vb.at[member], vb.at[member], at(x, (y + dy) % 2, z, (core + dc) % 2))
                for dy, dc in ((0, 1), (1, 0), (1, 1))
            ]
        else:
            for g in range(3):
                step(g)
    for c in vec_b:
        c.wait_recv()
    ov[...] = (vb[0] + vb[1]) + (vb[2] + vb[3])
    for g in range(3):
        to_c[g].wait_recv()
        relay[g].wait_recv()
    width = o4.shape[2]
    for i in range(4):
        o4[i] = groups[0][7][i].astype(F32)
        ou[:, i * width : (i + 1) * width] = groups[1][7][i].astype(F32)
        rows = groups[2][7].shape[1]
        od[:, i * rows : (i + 1) * rows] = groups[2][7][i].astype(F32).T
    for c in sent:
        c.wait_send()


def reduce_all(p4, pu, pd, pv):
    rows, width = p4.shape[3:]
    copies = 7 + 3 + 3 * (2 + 2 + 2 + 3 + 3)
    scratch = []
    for p in (p4, pu, pd):
        a, b = p.shape[3:]
        scratch += [
            pltpu.VMEM((2, NZ, NX, a, b), BF16),
            pltpu.VMEM((2, 2, a, b), BF16),
            pltpu.VMEM((2, NX, a, b), BF16),
            pltpu.VMEM((2, a, b), BF16),
            pltpu.VMEM((2, a, b), BF16),
            pltpu.VMEM((NZ - 1, a, b), BF16),
            pltpu.VMEM((4, a, b), BF16),
        ]
    scratch += [pltpu.VMEM((NX * NZ - 1,) + pv.shape[1:], F32), pltpu.VMEM((4,) + pv.shape[1:], F32)]
    vmem = pl.BlockSpec(memory_space=pltpu.VMEM)
    return pl.pallas_call(
        reduce_kernel,
        name="reduce_all",
        in_specs=[vmem] * 4,
        out_specs=[vmem] * 4,
        out_shape=[
            Shape((4, rows, width), F32),
            Shape((rows, 4 * width), F32),
            Shape((pd.shape[4], 4 * pd.shape[3]), F32),
            Shape(pv.shape[1:], F32),
        ],
        scratch_shapes=scratch
        + [pltpu.SemaphoreType.DMA((copies,)), pltpu.SemaphoreType.DMA((copies,))],
        compiler_params=params(collective_id=1, has_side_effects=True),
    )(p4, pu, pd, pv)


GROUP = 4 * HEAD_DIM


def half(index, shape):
    lanes = lax.broadcasted_iota(jnp.int32, shape, 1)
    return lanes < HEAD_DIM if index == 0 else lanes >= HEAD_DIM


def keep_half(index, value):
    return jnp.where(half(index, value.shape), value, jnp.zeros_like(value))


def attend_kernel(counts, tokens, w4, bias, query, keys, values, powers, context_t, inverse):
    slot = pl.program_id(1)
    x = tokens[...]
    q = (dot(x, w4[0]) + bias[0:1].astype(F32)).astype(BF16)
    k = dot(x, w4[1]).astype(BF16)
    v = (dot(x, w4[2]) + bias[1:2].astype(F32)).astype(BF16)
    query[...], keys[...], values[...] = q, k, v
    length = x.shape[0]
    rows = lax.broadcasted_iota(jnp.int32, (length, 1), 0)
    hidden_keys = jnp.where(rows < counts[slot], 0.0, -1000000000.0)
    for pair in range(2):
        cols = slice(pair * 128, pair * 128 + 128)
        q2 = q[:, cols] * jnp.asarray(HEAD_DIM**-0.5, BF16)
        k2, v_t = k[:, cols], v[:, cols].T
        for h in range(2):
            scores = dot_t(keep_half(h, k2), q2) + hidden_keys
            highest = jnp.max(scores, 0, keepdims=True)
            power = jnp.exp(scores - highest)
            inv = 1.0 / jnp.sum(power, 0, keepdims=True)
            low = power.astype(BF16)
            powers[pair * 2 + h] = low
            inverse[pair * 2 + h : pair * 2 + h + 1] = inv
            out = dot(v_t[h * HEAD_DIM : (h + 1) * HEAD_DIM], low) * inv
            context_t[pair * 128 + h * HEAD_DIM : pair * 128 + (h + 1) * HEAD_DIM] = out.astype(
                BF16
            )


def attend(counts, rows, w4, bias, length):
    total, width = rows.shape
    slots, groups = total // length, width // GROUP
    block = pl.BlockSpec((length, GROUP), lambda g, s: (s, g))
    return pl.pallas_call(
        attend_kernel,
        name="attention_forward",
        grid=(groups, slots),
        in_specs=[
            pl.BlockSpec(memory_space=pltpu.SMEM),
            pl.BlockSpec((length, width), lambda g, s: (s, 0)),
            pl.BlockSpec((4, width, GROUP), lambda g, s: (0, 0, g)),
            pl.BlockSpec((8, GROUP), lambda g, s: (0, g)),
        ],
        out_specs=[
            block,
            block,
            block,
            pl.BlockSpec((None, 4, length, length), lambda g, s: (s, g, 0, 0)),
            pl.BlockSpec((GROUP, length), lambda g, s: (g, s)),
            pl.BlockSpec((None, None, 4, length), lambda g, s: (s, g, 0, 0)),
        ],
        out_shape=[Shape((total, width), BF16)] * 3
        + [
            Shape((slots, groups * 4, length, length), BF16),
            Shape((width, total), BF16),
            Shape((slots, groups, 4, length), F32),
        ],
        compiler_params=params(),
    )(counts, rows, w4, bias)


SQRT_HALF = 0.7071067811865476
PDF_SCALE = 0.3989422804014327


def normal_parts(value):
    z = jnp.abs(value) * SQRT_HALF
    t = 1.0 / (1.0 + 0.3275911 * z)
    bell = jnp.exp(-(z * z))
    poly = 1.061405429 * t - 1.453152027
    poly = poly * t + 1.421413741
    poly = poly * t - 0.284496736
    poly = poly * t + 0.254829592
    tail = (0.5 * poly * t) * bell
    return jnp.where(value >= 0, 1.0 - tail, tail), bell * PDF_SCALE


def middle_kernel(
    counts, tokens, context_t, cotangent, w4, wu, wd, vec, up_bias,
    layer_out, resid_one, grad_context, first_t, err_two_t, err_one, act, grad_hidden, sums, sums_up,
    pull, first_low, err_two,
):
    slot = pl.program_id(0)
    length, width = tokens.shape
    columns = wu.shape[1]
    chunk = 1024
    v = vec[...].astype(F32)
    out_bias, gain_one, shift_one, down_bias, gain_two, shift_two = [v[i : i + 1] for i in range(2, 8)]

    @pl.when(slot == 0)
    def _():
        sums[...] = jnp.zeros_like(sums)
        sums_up[...] = jnp.zeros_like(sums_up)

    def centre(resid):
        centred = resid - jnp.mean(resid, 1, keepdims=True)
        inv = lax.rsqrt(jnp.mean(centred * centred, 1, keepdims=True) + epsilon)
        return centred * inv, inv

    def pull_back(scaled, normal, inv):
        return inv * (
            scaled
            - jnp.mean(scaled, 1, keepdims=True)
            - normal * jnp.mean(scaled * normal, 1, keepdims=True)
        )

    def note(row, value):
        sums[row : row + 1] += jnp.sum(value, 0, keepdims=True)

    r1 = tokens[...].astype(F32) + dot(context_t[...].T, w4[3]) + out_bias
    normal_one, inverse_one = centre(r1)
    first = normal_one * gain_one + shift_one
    first_low[...] = first.astype(BF16)
    first_t[...] = first_low[...].T

    def up(j, acc):
        cols = pl.ds(pl.multiple_of(j * chunk, chunk), chunk)
        hidden = dot(first_low[...], wu[:, cols]) + up_bias[:, cols].astype(F32)
        cdf, density = normal_parts(hidden)
        low = (hidden * cdf).astype(BF16)
        act[:, cols] = low
        pull[:, cols] = (cdf + hidden * density).astype(BF16)
        return acc + dot(low, wd[cols, :])

    second = lax.fori_loop(0, columns // chunk, up, jnp.zeros((length, width), F32))
    normal_two, inverse_two = centre(first + second + down_bias)
    live = lax.broadcasted_iota(jnp.int32, (length, 1), 0) < counts[slot]
    layer_out[...] = jnp.where(live, normal_two * gain_two + shift_two, 0.0).astype(BF16)
    grad_y = jnp.where(live, cotangent[...].astype(F32), 0.0)
    resid_two = pull_back(grad_y * gain_two, normal_two, inverse_two)
    err_two[...] = resid_two.astype(BF16)
    err_two_t[...] = err_two[...].T
    note(6, grad_y * normal_two)
    note(7, grad_y)
    note(5, err_two[...].astype(F32))

    def down(j, acc):
        cols = pl.ds(pl.multiple_of(j * chunk, chunk), chunk)
        low = (dot_t(err_two[...], wd[cols, :]) * pull[:, cols].astype(F32)).astype(BF16)
        grad_hidden[:, cols] = low
        sums_up[:, cols] += jnp.sum(low.astype(F32), 0, keepdims=True)
        return acc + dot_t(low, wu[:, cols])

    grad_first = resid_two + lax.fori_loop(
        0, columns // chunk, down, jnp.zeros((length, width), F32)
    )
    note(3, grad_first * normal_one)
    note(4, grad_first)
    resid = pull_back(grad_first * gain_one, normal_one, inverse_one)
    resid_one[...] = resid
    low = resid.astype(BF16)
    err_one[...] = low
    note(2, low.astype(F32))
    grad_context[...] = dot_t(low, w4[3]).astype(BF16)


def middle(counts, rows, context_t, cotangent, w4, wu, wd, vec, up_bias, length):
    total, width = rows.shape
    columns = wu.shape[1]

    def by_row(n):
        return pl.BlockSpec((length, n), lambda s: (s, 0))

    by_lane = pl.BlockSpec((width, length), lambda s: (0, s))
    return pl.pallas_call(
        middle_kernel,
        name="middle",
        grid=(total // length,),
        in_specs=[
            pl.BlockSpec(memory_space=pltpu.SMEM),
            by_row(width),
            by_lane,
            by_row(width),
            whole(w4.shape),
            whole(wu.shape),
            whole(wd.shape),
            whole(vec.shape),
            whole(up_bias.shape),
        ],
        out_specs=[
            by_row(width),
            by_row(width),
            by_row(width),
            by_lane,
            by_lane,
            by_row(width),
            by_row(columns),
            by_row(columns),
            pl.BlockSpec((8, width), lambda s: (0, 0)),
            pl.BlockSpec((1, columns), lambda s: (0, 0)),
        ],
        out_shape=[
            Shape((total, width), BF16),
            Shape((total, width), F32),
            Shape((total, width), BF16),
            Shape((width, total), BF16),
            Shape((width, total), BF16),
            Shape((total, width), BF16),
            Shape((total, columns), BF16),
            Shape((total, columns), BF16),
            Shape((8, width), F32),
            Shape((1, columns), F32),
        ],
        scratch_shapes=[
            pltpu.VMEM((length, columns), BF16),
            pltpu.VMEM((length, width), BF16),
            pltpu.VMEM((length, width), BF16),
        ],
        compiler_params=params(),
    )(counts, rows, context_t, cotangent, w4, wu, wd, vec, up_bias)


def outer_kernel(left, right, out):
    out[...] = dot(left[...], right[...]).astype(BF16).reshape(out.shape)


def outer_up(first_t, grad_hidden):
    width, total = first_t.shape
    return pl.pallas_call(
        outer_kernel,
        name="grad_up",
        grid=(4,),
        in_specs=[whole(first_t.shape), pl.BlockSpec((total, width), lambda i: (0, i))],
        out_specs=pl.BlockSpec((None, NZ, NX, ROWS, width), lambda i: (i, 0, 0, 0, 0)),
        out_shape=Shape((4, NZ, NX, ROWS, width), BF16),
        compiler_params=params(),
    )(first_t, grad_hidden)


def outer_down(err_two_t, act):
    width, total = err_two_t.shape
    part = act.shape[1] // (NX * NZ)
    return pl.pallas_call(
        outer_kernel,
        name="grad_down",
        grid=(NX * NZ,),
        in_specs=[whole(err_two_t.shape), pl.BlockSpec((total, part), lambda i: (0, i))],
        out_specs=pl.BlockSpec(
            (4, None, None, width // 4, part), lambda i: (0, i // NX, i % NX, 0, 0)
        ),
        out_shape=Shape((4, NZ, NX, width // 4, part), BF16),
        compiler_params=params(),
    )(err_two_t, act)


def attend_back_kernel(query, keys, values, powers, inverse, context_t, grad, dq_o, dk_o, dv_o):
    scale = HEAD_DIM**-0.5
    for pair in range(2):
        cols = slice(pair * 128, pair * 128 + 128)
        q2 = query[:, cols] * jnp.asarray(scale, BF16)
        k2, v2 = keys[:, cols], values[:, cols]
        grad_t = grad[:, cols].astype(F32).T
        product = grad_t * context_t[cols, :].astype(F32)
        k_t = k2.T
        inv = [inverse[pair * 2 + h : pair * 2 + h + 1] for h in range(2)]
        scaled_t = jnp.concatenate(
            [grad_t[:HEAD_DIM] * inv[0], grad_t[HEAD_DIM:] * inv[1]], 0
        ).astype(BF16)
        scaled = scaled_t.T
        dq, dk, dv = [], 0.0, 0.0
        for h in range(2):
            rows = slice(h * HEAD_DIM, (h + 1) * HEAD_DIM)
            inner = jnp.sum(product[rows], 0, keepdims=True) * inv[h]
            power = powers[pair * 2 + h]
            grad_probs = dot(keep_half(h, v2), scaled_t)
            grad_scores = (power.astype(F32) * (grad_probs - inner)).astype(BF16)
            dv = dv + dot(power, keep_half(h, scaled))
            dk = dk + dot(grad_scores, keep_half(h, q2))
            dq.append(dot(k_t[rows], grad_scores))
        dv_o[:, cols] = dv.astype(BF16)
        dk_o[:, cols] = dk.astype(BF16)
        dq_o[:, cols] = (jnp.concatenate(dq, 0) * scale).astype(BF16).T


def attend_back(query, keys, values, powers, inverse, context_t, grad, length):
    total, width = query.shape
    slots, groups = total // length, width // GROUP
    block = pl.BlockSpec((length, GROUP), lambda g, s: (s, g))
    return pl.pallas_call(
        attend_back_kernel,
        name="attention_backward",
        grid=(groups, slots),
        in_specs=[
            block,
            block,
            block,
            pl.BlockSpec((None, 4, length, length), lambda g, s: (s, g, 0, 0)),
            pl.BlockSpec((None, None, 4, length), lambda g, s: (s, g, 0, 0)),
            pl.BlockSpec((GROUP, length), lambda g, s: (g, s)),
            block,
        ],
        out_specs=[block] * 3,
        out_shape=[Shape((total, width), BF16)] * 3,
        compiler_params=params(),
    )(query, keys, values, powers, inverse, context_t, grad)


def inputs_kernel(tokens, context_t, err_one, dq, dk, dv, w4, resid_one, p4, grad_in, sums, tokens_t):
    tokens_t[...] = tokens[...].T
    step = 256
    width = tokens.shape[1]

    def emit(index, left, right):
        for i in range(width // step):
            cols = slice(i * step, (i + 1) * step)
            p4[index, :, :, :, cols] = (
                dot(left[...], right[:, cols]).astype(BF16).reshape(NZ, NX, ROWS, step)
            )

    emit(0, tokens_t, dq)
    emit(1, tokens_t, dk)
    emit(2, tokens_t, dv)
    emit(3, context_t, err_one)
    sums[0:1] = jnp.sum(dq[...].astype(F32), 0, keepdims=True)
    sums[1:2] = jnp.sum(dv[...].astype(F32), 0, keepdims=True)
    for i in range(width // step):
        cols = slice(i * step, (i + 1) * step)
        grad_in[:, cols] = (
            resid_one[:, cols]
            + dot_t(dq[...], w4[0, cols])
            + dot_t(dk[...], w4[1, cols])
            + dot_t(dv[...], w4[2, cols])
        )


def inputs_back(rows, context_t, err_one, dq, dk, dv, w4, resid_one):
    total, width = rows.shape
    vmem = pl.BlockSpec(memory_space=pltpu.VMEM)
    return pl.pallas_call(
        inputs_kernel,
        name="inputs_backward",
        in_specs=[vmem] * 8,
        out_specs=[vmem] * 3,
        out_shape=[
            Shape((4, NZ, NX, ROWS, width), BF16),
            Shape((total, width), F32),
            Shape((2, width), F32),
        ],
        scratch_shapes=[pltpu.VMEM((width, total), BF16)],
        compiler_params=params(),
    )(rows, context_t, err_one, dq, dk, dv, w4, resid_one)


def fused_layer(
    tokens, counts, cotangent, query_weight, key_weight, value_weight, out_weight, query_bias,
    value_bias, out_bias, attention_gain, attention_shift, up_weight, up_bias, down_weight,
    down_bias, feed_gain, feed_shift,
):
    slots, length, width = tokens.shape
    shards = NX * NZ
    columns = up_weight.shape[1]
    rows = tokens.reshape(-1, width)
    vec = jnp.stack(
        [query_bias, value_bias, out_bias, attention_gain, attention_shift, down_bias, feed_gain, feed_shift]
    )
    vec = jnp.concatenate([vec, up_bias.reshape(4, ROWS)], 0)
    vec = jnp.pad(vec, ((0, 4), (0, 128 - ROWS)))
    g4, gu, gd, gv = gather_all(
        query_weight, key_weight, value_weight, out_weight, up_weight, down_weight, vec
    )
    w4 = g4.reshape(4, width, width)
    wu = gu.reshape(width, columns)
    wd = gd.reshape(columns, width)
    vec8 = gv[:, :8, :ROWS].transpose(1, 0, 2).reshape(8, width)
    up_row = gv[:, 8:12, :ROWS].reshape(1, columns)
    query, keys, values, powers, context_t, inverse = attend(counts, rows, w4, vec8, length)
    (
        layer_out, resid_one, grad_context, first_t, err_two_t, err_one, act, grad_hidden, sums, sums_up,
    ) = middle(
        counts, rows, context_t, cotangent.reshape(-1, width), w4, wu, wd, vec8, up_row, length
    )
    pu = outer_up(first_t, grad_hidden)
    pd = outer_down(err_two_t, act)
    dq, dk, dv = attend_back(query, keys, values, powers, inverse, context_t, grad_context, length)
    p4, input_grad, sums_qv = inputs_back(rows, context_t, err_one, dq, dk, dv, w4, resid_one)
    total8 = jnp.concatenate([sums_qv, sums[2:8]], 0)
    pv = total8.reshape(8, shards, ROWS).transpose(1, 0, 2)
    pv = jnp.concatenate([pv, sums_up.reshape(shards, 4, ROWS)], 1)
    pv = jnp.pad(pv, ((0, 0), (0, 4), (0, 128 - ROWS)))
    o4, ou, od, ov = reduce_all(p4, pu, pd, pv)
    v = [ov[i, :ROWS] for i in range(8)]
    return (
        layer_out.reshape(tokens.shape),
        input_grad.reshape(tokens.shape),
        o4[0], o4[1], o4[2], o4[3],
        v[0], v[1], v[2], v[3], v[4],
        ou, ov[8:12, :ROWS].reshape(-1), od, v[5], v[6], v[7],
    )


def exact_gelu(value):
    return jax.nn.gelu(value, approximate=False)


def norm_forward(resid, gain, shift):
    average = jnp.mean(resid, axis=-1, keepdims=True)
    centred = resid - average
    spread = jnp.mean(centred * centred, axis=-1, keepdims=True)
    inverse = lax.rsqrt(spread + epsilon)
    normal = centred * inverse
    return (normal * gain + shift, normal, inverse)


def norm_backward(grad_out, normal, inverse, gain):
    scaled = grad_out * gain
    first_mean = jnp.mean(scaled, axis=-1, keepdims=True)
    second_mean = jnp.mean(scaled * normal, axis=-1, keepdims=True)
    grad_resid = inverse * (scaled - first_mean - normal * second_mean)
    return (grad_resid, jnp.sum(grad_out * normal, 0), jnp.sum(grad_out, 0))


def linear(rows, weight):
    return jnp.dot(rows, weight, preferred_element_type=jnp.float32)


def linear_back(grads, weight):
    return lax.dot_general(
        grads, weight, (((1,), (1,)), ((), ())), preferred_element_type=jnp.float32
    )


def outer_sum(rows, grads):
    return lax.dot_general(
        rows, grads, (((0,), (0,)), ((), ())), preferred_element_type=jnp.float32
    )


def column_sum(grads):
    return jnp.sum(grads.astype(jnp.float32), 0)


def on_device(
    tokens,
    counts,
    cotangent,
    query_weight,
    key_weight,
    value_weight,
    out_weight,
    query_bias,
    value_bias,
    out_bias,
    attention_gain,
    attention_shift,
    up_weight,
    up_bias,
    down_weight,
    down_bias,
    feed_gain,
    feed_shift,
):
    slots, length, width = tokens.shape
    heads = width // HEAD_DIM
    factor = HEAD_DIM ** (-0.5)
    positions = jnp.arange(length, dtype=jnp.int32)

    def split_heads(value):
        return value.reshape(slots, length, heads, HEAD_DIM)

    def masked_scores(query, keys, count):
        raw = jnp.einsum("qhd,khd->hqk", query, keys, preferred_element_type=jnp.float32)
        live = positions < count
        return jnp.where(live[None, None, :], raw * factor, -1000000000.0)

    def attend_forward(block):
        query, keys, values, count = block
        scores = masked_scores(query, keys, count)
        highest = jnp.max(scores, axis=-1, keepdims=True)
        powers = jnp.exp(scores - highest)
        totals = jnp.sum(powers, axis=-1, keepdims=True)
        probs = (powers / totals).astype(jnp.bfloat16)
        context = jnp.einsum("hqk,khd->qhd", probs, values, preferred_element_type=jnp.float32)
        return (context.reshape(length, width), highest + jnp.log(totals))

    def attend_backward(block):
        query, keys, values, count, logsum, grad_context = block
        scores = masked_scores(query, keys, count)
        probs = jnp.exp(scores - logsum)
        probs_low = probs.astype(jnp.bfloat16)
        grad_probs = jnp.einsum(
            "qhd,khd->hqk", grad_context, values, preferred_element_type=jnp.float32
        )
        inner = jnp.sum(probs * grad_probs, axis=-1, keepdims=True)
        grad_scores = (probs * (grad_probs - inner) * factor).astype(jnp.bfloat16)
        grad_query = jnp.einsum(
            "hqk,khd->qhd", grad_scores, keys, preferred_element_type=jnp.float32
        )
        grad_keys = jnp.einsum(
            "hqk,qhd->khd", grad_scores, query, preferred_element_type=jnp.float32
        )
        grad_values = jnp.einsum(
            "hqk,qhd->khd", probs_low, grad_context, preferred_element_type=jnp.float32
        )
        return (
            grad_query.reshape(length, width).astype(jnp.bfloat16),
            grad_keys.reshape(length, width).astype(jnp.bfloat16),
            grad_values.reshape(length, width).astype(jnp.bfloat16),
        )

    attention_set = (
        lax.all_gather(query_weight, "fsdp", axis=0, tiled=True),
        lax.all_gather(key_weight, "fsdp", axis=0, tiled=True),
        lax.all_gather(value_weight, "fsdp", axis=0, tiled=True),
        lax.all_gather(out_weight, "fsdp", axis=0, tiled=True),
        lax.all_gather(query_bias, "fsdp", axis=0, tiled=True),
        lax.all_gather(value_bias, "fsdp", axis=0, tiled=True),
        lax.all_gather(out_bias, "fsdp", axis=0, tiled=True),
        lax.all_gather(attention_gain, "fsdp", axis=0, tiled=True),
        lax.all_gather(attention_shift, "fsdp", axis=0, tiled=True),
    )
    feed_set = (
        lax.all_gather(up_weight, "fsdp", axis=0, tiled=True),
        lax.all_gather(up_bias, "fsdp", axis=0, tiled=True),
        lax.all_gather(down_weight, "fsdp", axis=0, tiled=True),
        lax.all_gather(down_bias, "fsdp", axis=0, tiled=True),
        lax.all_gather(feed_gain, "fsdp", axis=0, tiled=True),
        lax.all_gather(feed_shift, "fsdp", axis=0, tiled=True),
    )
    whole_query, whole_key, whole_value, whole_out = (
        attention_set[0],
        attention_set[1],
        attention_set[2],
        attention_set[3],
    )
    whole_up, whole_down = (feed_set[0], feed_set[2])
    rows = tokens.reshape(-1, width)
    query = (linear(rows, whole_query) + attention_set[4].astype(jnp.float32)).astype(jnp.bfloat16)
    keys = linear(rows, whole_key).astype(jnp.bfloat16)
    values = (linear(rows, whole_value) + attention_set[5].astype(jnp.float32)).astype(jnp.bfloat16)
    context_rows, logsum = lax.map(
        attend_forward, (split_heads(query), split_heads(keys), split_heads(values), counts)
    )
    context = context_rows.reshape(-1, width).astype(jnp.bfloat16)
    branch = linear(context, whole_out) + attention_set[6].astype(jnp.float32)
    gain_one = attention_set[7].astype(jnp.float32)
    first, normal_one, inverse_one = norm_forward(
        rows.astype(jnp.float32) + branch, gain_one, attention_set[8].astype(jnp.float32)
    )
    first_low = first.astype(jnp.bfloat16)
    hidden = linear(first_low, whole_up) + feed_set[1].astype(jnp.float32)
    activated, gelu_pull = jax.vjp(exact_gelu, hidden)
    act_low = activated.astype(jnp.bfloat16)
    second = linear(act_low, whole_down) + feed_set[3].astype(jnp.float32)
    gain_two = feed_set[4].astype(jnp.float32)
    output, normal_two, inverse_two = norm_forward(
        first + second, gain_two, feed_set[5].astype(jnp.float32)
    )
    live = (positions[None, :] < counts[:, None]).reshape(-1, 1)
    layer_out = jnp.where(live, output, 0.0).astype(jnp.bfloat16).reshape(tokens.shape)
    back_feed = (
        lax.all_gather(up_weight, "fsdp", axis=0, tiled=True),
        lax.all_gather(down_weight, "fsdp", axis=0, tiled=True),
    )
    back_up, back_down = (back_feed[0], back_feed[1])
    grad_y = jnp.where(live, cotangent.reshape(-1, width).astype(jnp.float32), 0.0)
    resid_two, grad_feed_gain, grad_feed_shift = norm_backward(
        grad_y, normal_two, inverse_two, gain_two
    )
    err_two = resid_two.astype(jnp.bfloat16)
    grad_down_weight = outer_sum(act_low, err_two)
    grad_down_bias = column_sum(err_two)
    grad_act = linear_back(err_two, back_down)
    grad_hidden = gelu_pull(grad_act)[0].astype(jnp.bfloat16)
    grad_up_weight = outer_sum(first_low, grad_hidden)
    grad_up_bias = column_sum(grad_hidden)
    grad_first = resid_two + linear_back(grad_hidden, back_up)
    feed_shards = (
        lax.psum_scatter(
            grad_up_weight.astype(jnp.bfloat16), "fsdp", scatter_dimension=0, tiled=True
        ).astype(jnp.float32),
        lax.psum_scatter(
            grad_up_bias.astype(jnp.bfloat16), "fsdp", scatter_dimension=0, tiled=True
        ).astype(jnp.float32),
        lax.psum_scatter(
            grad_down_weight.astype(jnp.bfloat16), "fsdp", scatter_dimension=0, tiled=True
        ).astype(jnp.float32),
        lax.psum_scatter(
            grad_down_bias.astype(jnp.bfloat16), "fsdp", scatter_dimension=0, tiled=True
        ).astype(jnp.float32),
        lax.psum_scatter(
            grad_feed_gain.astype(jnp.bfloat16), "fsdp", scatter_dimension=0, tiled=True
        ).astype(jnp.float32),
        lax.psum_scatter(
            grad_feed_shift.astype(jnp.bfloat16), "fsdp", scatter_dimension=0, tiled=True
        ).astype(jnp.float32),
    )
    back_attention = (
        lax.all_gather(query_weight, "fsdp", axis=0, tiled=True),
        lax.all_gather(key_weight, "fsdp", axis=0, tiled=True),
        lax.all_gather(value_weight, "fsdp", axis=0, tiled=True),
        lax.all_gather(out_weight, "fsdp", axis=0, tiled=True),
    )
    back_query, back_key, back_value, back_out = (
        back_attention[0],
        back_attention[1],
        back_attention[2],
        back_attention[3],
    )
    resid_one, grad_attention_gain, grad_attention_shift = norm_backward(
        grad_first, normal_one, inverse_one, gain_one
    )
    err_one = resid_one.astype(jnp.bfloat16)
    grad_out_weight = outer_sum(context, err_one)
    grad_out_bias = column_sum(err_one)
    grad_context = linear_back(err_one, back_out).astype(jnp.bfloat16)
    grad_query, grad_keys, grad_values = lax.map(
        attend_backward,
        (
            split_heads(query),
            split_heads(keys),
            split_heads(values),
            counts,
            logsum,
            split_heads(grad_context),
        ),
    )
    grad_query = grad_query.reshape(-1, width)
    grad_keys = grad_keys.reshape(-1, width)
    grad_values = grad_values.reshape(-1, width)
    grad_query_weight = outer_sum(rows, grad_query)
    grad_key_weight = outer_sum(rows, grad_keys)
    grad_value_weight = outer_sum(rows, grad_values)
    grad_query_bias = column_sum(grad_query)
    grad_value_bias = column_sum(grad_values)
    input_grad = (
        resid_one
        + linear_back(grad_query, back_query)
        + linear_back(grad_keys, back_key)
        + linear_back(grad_values, back_value)
    )
    attention_shards = (
        lax.psum_scatter(
            grad_query_weight.astype(jnp.bfloat16), "fsdp", scatter_dimension=0, tiled=True
        ).astype(jnp.float32),
        lax.psum_scatter(
            grad_key_weight.astype(jnp.bfloat16), "fsdp", scatter_dimension=0, tiled=True
        ).astype(jnp.float32),
        lax.psum_scatter(
            grad_value_weight.astype(jnp.bfloat16), "fsdp", scatter_dimension=0, tiled=True
        ).astype(jnp.float32),
        lax.psum_scatter(
            grad_out_weight.astype(jnp.bfloat16), "fsdp", scatter_dimension=0, tiled=True
        ).astype(jnp.float32),
        lax.psum_scatter(
            grad_query_bias.astype(jnp.bfloat16), "fsdp", scatter_dimension=0, tiled=True
        ).astype(jnp.float32),
        lax.psum_scatter(
            grad_value_bias.astype(jnp.bfloat16), "fsdp", scatter_dimension=0, tiled=True
        ).astype(jnp.float32),
        lax.psum_scatter(
            grad_out_bias.astype(jnp.bfloat16), "fsdp", scatter_dimension=0, tiled=True
        ).astype(jnp.float32),
        lax.psum_scatter(
            grad_attention_gain.astype(jnp.bfloat16), "fsdp", scatter_dimension=0, tiled=True
        ).astype(jnp.float32),
        lax.psum_scatter(
            grad_attention_shift.astype(jnp.bfloat16), "fsdp", scatter_dimension=0, tiled=True
        ).astype(jnp.float32),
    )
    summed = lax.psum(
        (
            attention_shards[0],
            attention_shards[1],
            attention_shards[2],
            attention_shards[3],
            attention_shards[4],
            attention_shards[5],
            attention_shards[6],
            attention_shards[7],
            attention_shards[8],
            feed_shards[0],
            feed_shards[1],
            feed_shards[2],
            feed_shards[3],
            feed_shards[4],
            feed_shards[5],
        ),
        "dp",
    )
    return (
        layer_out,
        input_grad.reshape(tokens.shape),
        summed[0],
        summed[1],
        summed[2],
        summed[3],
        summed[4],
        summed[5],
        summed[6],
        summed[7],
        summed[8],
        summed[9],
        summed[10],
        summed[11],
        summed[12],
        summed[13],
        summed[14],
    )


def solution(mesh):
    small = mesh.shape["dp"] == 4 and mesh.shape["fsdp"] == NX * NZ
    return jax.shard_map(
        fused_layer if small else on_device,
        mesh=mesh,
        in_specs=(
            P(("dp", "fsdp"), None, None),
            P(("dp", "fsdp")),
            P(("dp", "fsdp"), None, None),
            P("fsdp", None),
            P("fsdp", None),
            P("fsdp", None),
            P("fsdp", None),
            P("fsdp"),
            P("fsdp"),
            P("fsdp"),
            P("fsdp"),
            P("fsdp"),
            P("fsdp", None),
            P("fsdp"),
            P("fsdp", None),
            P("fsdp"),
            P("fsdp"),
            P("fsdp"),
        ),
        out_specs=(
            P(("dp", "fsdp"), None, None),
            P(("dp", "fsdp"), None, None),
            P("fsdp", None),
            P("fsdp", None),
            P("fsdp", None),
            P("fsdp", None),
            P("fsdp"),
            P("fsdp"),
            P("fsdp"),
            P("fsdp"),
            P("fsdp"),
            P("fsdp", None),
            P("fsdp"),
            P("fsdp", None),
            P("fsdp"),
            P("fsdp"),
            P("fsdp"),
        ),
        check_vma=False,
    )
```

```python
import functools

import jax
import jax.numpy as jnp
from jax import lax
from jax.experimental import pallas as pl
from jax.experimental.pallas import tpu as pltpu
from jax.sharding import PartitionSpec as P

HEAD_DIM = 64
epsilon = 1e-05
F32 = jnp.float32
BF16 = jnp.bfloat16
MESH = pl.DeviceIdType.MESH
VMEM_LIMIT = 63 * 2**20
Shape = jax.ShapeDtypeStruct


def dot(left, right):
    return lax.dot_general(
        left, right, (((1,), (0,)), ((), ())), preferred_element_type=F32
    )


def dot_t(left, right):
    return lax.dot_general(
        left, right, (((1,), (1,)), ((), ())), preferred_element_type=F32
    )


def params(**extra):
    return pltpu.CompilerParams(vmem_limit_bytes=VMEM_LIMIT, **extra)


def whole(shape):
    return pl.BlockSpec(shape, lambda *_: (0,) * len(shape), pipeline_mode=pl.Buffered(1))


NX, NZ, ROWS = 2, 4, 96


def place():
    member = lax.axis_index("dp")
    shard = lax.axis_index("fsdp")
    return shard % NX, member // 2, shard // NX, member % 2


def at(x, y, z, core):
    return {"dp": y * 2 + core, "fsdp": z * NX + x}


def greet(peers):
    barrier = pltpu.get_barrier_semaphore()
    for peer in peers:
        pl.semaphore_signal(barrier, inc=1, device_id=peer, device_id_type=MESH)
    pl.semaphore_wait(barrier, len(peers))


def all_peers():
    x, y, z, core = place()
    near = [at(x, 1 - y, z, core), at(x, y, z, 1 - core)]
    for step in range(1, NX * NZ):
        near.append({"dp": y * 2 + core, "fsdp": (z * NX + x + step) % (NX * NZ)})
    return near


class Wire:
    def __init__(self, send, recv):
        self.send, self.recv, self.slots = send, recv, {}

    def copy(self, key, source, target, peer):
        slot = self.slots.setdefault(key, len(self.slots))
        return pltpu.make_async_remote_copy(
            src_ref=source,
            dst_ref=target,
            send_sem=self.send.at[slot],
            recv_sem=self.recv.at[slot],
            device_id=peer,
            device_id_type=MESH,
        )


def gather_kernel(wq, wk, wv, wo, wu, wd, vec, g4, gu, gd, gv, local, send, recv):
    x, y, z, core = place()
    shard = z * NX + x
    member, other = y * 2 + core, (1 - y) * 2 + core

    def part(group, who, zs, xs):
        if group == 0:
            return g4.at[who, zs, xs]
        if group == 1:
            return gu.at[zs, xs, :, pl.ds(pl.multiple_of(who * 768, 768), 768)]
        return gd.at[zs, xs, who]

    own = [
        (wq, part(0, member, z, x)),
        (wu.at[:, pl.ds(pl.multiple_of(member * 768, 768), 768)], part(1, member, z, x)),
        (wd.at[member], part(2, member, z, x)),
        (vec, gv.at[shard]),
    ]
    own = [pltpu.make_async_copy(a, b, local.at[i]) for i, (a, b) in enumerate(own)]
    for i, w in enumerate((wq, wk, wv, wo)):

        @pl.when(member == i)
        def _():
            pltpu.make_async_copy(w, part(0, i, z, x), local.at[0]).start()

    for c in own[1:]:
        c.start()
    greet(all_peers())
    for c in own:
        c.wait()
    wire = Wire(send, recv)
    x_peer, y_peer, c_peer = at(1 - x, y, z, core), at(x, 1 - y, z, core), at(x, y, z, 1 - core)
    every = slice(None)
    sent = []

    def start(source, peer):
        c = wire.copy(len(sent), source, source, peer)
        c.start()
        sent.append(c)
        return c

    vecs = [
        start(gv.at[shard], {"dp": member, "fsdp": (shard + k) % (NX * NZ)})
        for k in range(1, NX * NZ)
    ]
    along_z = [
        [start(part(g, member, z, x), at(x, y, (z + k) % NZ, core)) for k in range(1, NZ)]
        for g in range(3)
    ]
    first, second, last = [], [], []

    def plane(g):
        for c in along_z[g]:
            c.wait_recv()
        mine = part(g, member, every, x)
        first.append((start(mine, x_peer), start(mine, y_peer)))
        last.append(start(mine, c_peer))

    def corner(g):
        from_x, from_y = first[g]
        from_y.wait_recv()
        a = start(part(g, other, pl.ds(0, 2), x), x_peer)
        last.append(start(part(g, other, every, x), c_peer))
        from_x.wait_recv()
        b = start(part(g, member, pl.ds(2, 2), 1 - x), y_peer)
        last.append(start(part(g, member, every, 1 - x), c_peer))
        second.append((a, b))

    def rest(g):
        for c in second[g]:
            c.wait_recv()
        last.append(start(part(g, other, every, 1 - x), c_peer))

    plane(0)
    plane(1)
    corner(0)
    plane(2)
    corner(1)
    rest(0)
    corner(2)
    rest(1)
    rest(2)
    for c in vecs + last:
        c.wait_recv()
    for c in sent:
        c.wait_send()


def gather_all(wq, wk, wv, wo, wu, wd, vec):
    rows, width = wq.shape
    columns = wu.shape[1]
    copies = 7 + 3 * (3 + 2 + 2 + 4)
    hbm = pl.BlockSpec(memory_space=pl.ANY)
    return pl.pallas_call(
        gather_kernel,
        name="gather_all",
        in_specs=[pl.BlockSpec(memory_space=pltpu.VMEM)] * 7,
        out_specs=[hbm] * 4,
        out_shape=[
            Shape((4, NZ, NX, rows, width), BF16),
            Shape((NZ, NX, rows, columns), BF16),
            Shape((NZ, NX, 4, rows, width), BF16),
            Shape((NX * NZ,) + vec.shape, BF16),
        ],
        scratch_shapes=[
            pltpu.SemaphoreType.DMA((7,)),
            pltpu.SemaphoreType.DMA((copies,)),
            pltpu.SemaphoreType.DMA((copies,)),
        ],
        compiler_params=params(collective_id=0, has_side_effects=True),
    )(wq, wk, wv, wo, wu, wd.reshape(4, rows, width), vec)


GROUP = 4 * HEAD_DIM


def half(index, shape):
    lanes = lax.broadcasted_iota(jnp.int32, shape, 1)
    return lanes < HEAD_DIM if index == 0 else lanes >= HEAD_DIM


def keep_half(index, value):
    return jnp.where(half(index, value.shape), value, jnp.zeros_like(value))


def attend_kernel(counts, tokens, w4, bias, query, keys, values, powers, context_t, inverse):
    slot = pl.program_id(1)
    x = tokens[...]
    q = (dot(x, w4[0]) + bias[0:1].astype(F32)).astype(BF16)
    k = dot(x, w4[1]).astype(BF16)
    v = (dot(x, w4[2]) + bias[1:2].astype(F32)).astype(BF16)
    query[...], keys[...], values[...] = q, k, v
    length = x.shape[0]
    rows = lax.broadcasted_iota(jnp.int32, (length, 1), 0)
    hidden_keys = jnp.where(rows < counts[slot], 0.0, -1000000000.0)
    for pair in range(2):
        cols = slice(pair * 128, pair * 128 + 128)
        q2 = q[:, cols] * jnp.asarray(HEAD_DIM**-0.5, BF16)
        k2, v_t = k[:, cols], v[:, cols].T
        for h in range(2):
            scores = dot_t(keep_half(h, k2), q2) + hidden_keys
            highest = jnp.max(scores, 0, keepdims=True)
            power = jnp.exp(scores - highest)
            inv = 1.0 / jnp.sum(power, 0, keepdims=True)
            low = power.astype(BF16)
            powers[pair * 2 + h] = low
            inverse[pair * 2 + h : pair * 2 + h + 1] = inv
            out = dot(v_t[h * HEAD_DIM : (h + 1) * HEAD_DIM], low) * inv
            context_t[pair * 128 + h * HEAD_DIM : pair * 128 + (h + 1) * HEAD_DIM] = out.astype(
                BF16
            )


def attend(counts, rows, w4, bias, length):
    total, width = rows.shape
    slots, groups = total // length, width // GROUP
    block = pl.BlockSpec((length, GROUP), lambda g, s: (s, g))
    return pl.pallas_call(
        attend_kernel,
        name="attention_forward",
        grid=(groups, slots),
        in_specs=[
            pl.BlockSpec(memory_space=pltpu.SMEM),
            pl.BlockSpec((length, width), lambda g, s: (s, 0)),
            pl.BlockSpec((4, width, GROUP), lambda g, s: (0, 0, g)),
            pl.BlockSpec((8, GROUP), lambda g, s: (0, g)),
        ],
        out_specs=[
            block,
            block,
            block,
            pl.BlockSpec((None, 4, length, length), lambda g, s: (s, g, 0, 0)),
            pl.BlockSpec((GROUP, length), lambda g, s: (g, s)),
            pl.BlockSpec((None, None, 4, length), lambda g, s: (s, g, 0, 0)),
        ],
        out_shape=[Shape((total, width), BF16)] * 3
        + [
            Shape((slots, groups * 4, length, length), BF16),
            Shape((width, total), BF16),
            Shape((slots, groups, 4, length), F32),
        ],
        compiler_params=params(),
    )(counts, rows, w4, bias)


SQRT_HALF = 0.7071067811865476
PDF_SCALE = 0.3989422804014327


def normal_parts(value):
    z = jnp.abs(value) * SQRT_HALF
    t = 1.0 / (1.0 + 0.3275911 * z)
    bell = jnp.exp(-(z * z))
    poly = 1.061405429 * t - 1.453152027
    poly = poly * t + 1.421413741
    poly = poly * t - 0.284496736
    poly = poly * t + 0.254829592
    tail = (0.5 * poly * t) * bell
    return jnp.where(value >= 0, 1.0 - tail, tail), bell * PDF_SCALE


def centre(resid):
    centred = resid - jnp.mean(resid, 1, keepdims=True)
    inv = lax.rsqrt(jnp.mean(centred * centred, 1, keepdims=True) + epsilon)
    return centred * inv, inv


def pull_back(scaled, normal, inv):
    return inv * (
        scaled
        - jnp.mean(scaled, 1, keepdims=True)
        - normal * jnp.mean(scaled * normal, 1, keepdims=True)
    )


def note(sums, row, value):
    sums[row : row + 1] += jnp.sum(value, 0, keepdims=True)


CHUNK = 1024


def middle_kernel(
    counts, tokens, context_t, cotangent, w4, wu, wd, vec, up_bias,
    layer_out, resid_two_o, normal_one_o, inverse_one_o, first_t, err_two, err_two_t, act, pull, sums,
    first_low,
):
    slot = pl.program_id(0)
    length, width = tokens.shape
    columns = wu.shape[1]
    v = vec[...].astype(F32)
    out_bias, gain_one, shift_one, down_bias, gain_two, shift_two = [v[i : i + 1] for i in range(2, 8)]

    @pl.when(slot == 0)
    def _():
        sums[...] = jnp.zeros_like(sums)

    r1 = tokens[...].astype(F32) + dot(context_t[...].T, w4[3]) + out_bias
    normal_one, inverse_one = centre(r1)
    normal_one_o[...] = normal_one
    inverse_one_o[...] = inverse_one
    first = normal_one * gain_one + shift_one
    first_low[...] = first.astype(BF16)
    first_t[...] = first_low[...].T

    def up(j, acc):
        cols = pl.ds(pl.multiple_of(j * CHUNK, CHUNK), CHUNK)
        hidden = dot(first_low[...], wu[:, cols]) + up_bias[:, cols].astype(F32)
        cdf, density = normal_parts(hidden)
        low = (hidden * cdf).astype(BF16)
        act[:, cols] = low
        pull[:, cols] = (cdf + hidden * density).astype(BF16)
        return acc + dot(low, wd[cols, :])

    second = lax.fori_loop(0, columns // CHUNK, up, jnp.zeros((length, width), F32))
    normal_two, inverse_two = centre(first + second + down_bias)
    live = lax.broadcasted_iota(jnp.int32, (length, 1), 0) < counts[slot]
    layer_out[...] = jnp.where(live, normal_two * gain_two + shift_two, 0.0).astype(BF16)
    grad_y = jnp.where(live, cotangent[...].astype(F32), 0.0)
    resid_two = pull_back(grad_y * gain_two, normal_two, inverse_two)
    resid_two_o[...] = resid_two
    err_two[...] = resid_two.astype(BF16)
    err_two_t[...] = err_two[...].T
    note(sums, 6, grad_y * normal_two)
    note(sums, 7, grad_y)
    note(sums, 5, err_two[...].astype(F32))


def middle(counts, rows, context_t, cotangent, w4, wu, wd, vec, up_bias, length):
    total, width = rows.shape
    columns = wu.shape[1]

    def by_row(n):
        return pl.BlockSpec((length, n), lambda s: (s, 0))

    by_lane = pl.BlockSpec((width, length), lambda s: (0, s))
    return pl.pallas_call(
        middle_kernel,
        name="middle",
        grid=(total // length,),
        in_specs=[
            pl.BlockSpec(memory_space=pltpu.SMEM),
            by_row(width),
            by_lane,
            by_row(width),
            whole(w4.shape),
            whole(wu.shape),
            whole(wd.shape),
            whole(vec.shape),
            whole(up_bias.shape),
        ],
        out_specs=[
            by_row(width),
            by_row(width),
            by_row(width),
            by_row(1),
            by_lane,
            by_row(width),
            by_lane,
            by_row(columns),
            by_row(columns),
            pl.BlockSpec((8, width), lambda s: (0, 0)),
        ],
        out_shape=[
            Shape((total, width), BF16),
            Shape((total, width), F32),
            Shape((total, width), F32),
            Shape((total, 1), F32),
            Shape((width, total), BF16),
            Shape((total, width), BF16),
            Shape((width, total), BF16),
            Shape((total, columns), BF16),
            Shape((total, columns), BF16),
            Shape((8, width), F32),
        ],
        scratch_shapes=[pltpu.VMEM((length, width), BF16)],
        compiler_params=params(),
    )(counts, rows, context_t, cotangent, w4, wu, wd, vec, up_bias)


def outer_kernel(left, right, out):
    out[...] = dot(left[...], right[...]).astype(BF16).reshape(out.shape)


def outer_down(err_two_t, act):
    width, total = err_two_t.shape
    part = act.shape[1] // (NX * NZ)
    return pl.pallas_call(
        outer_kernel,
        name="grad_down",
        grid=(NX * NZ,),
        in_specs=[whole(err_two_t.shape), pl.BlockSpec((total, part), lambda i: (0, i))],
        out_specs=pl.BlockSpec(
            (4, None, None, width // 4, part), lambda i: (0, i // NX, i % NX, 0, 0)
        ),
        out_shape=Shape((4, NZ, NX, width // 4, part), BF16),
        compiler_params=params(),
    )(err_two_t, act)


class Chunk:
    def __init__(self, name, wire, where, part, mine, scratch):
        self.name, self.wire, self.where = name, wire, where
        self.part, self.mine = part, mine
        self.rc, self.bx, self.by, self.cx, self.cy, self.bz, self.fin = scratch

    @staticmethod
    def scratch(a, b):
        return [
            pltpu.VMEM((2, NZ, NX, a, b), BF16),
            pltpu.VMEM((2, 2, a, b), BF16),
            pltpu.VMEM((2, NX, a, b), BF16),
            pltpu.VMEM((2, a, b), BF16),
            pltpu.VMEM((2, a, b), BF16),
            pltpu.VMEM((NZ - 1, a, b), BF16),
            pltpu.VMEM((4, a, b), BF16),
        ]

    def copies(self, stage):
        x, y, z, core = self.where
        member, other = y * 2 + core, (1 - y) * 2 + core
        x_peer, y_peer = at(1 - x, y, z, core), at(x, 1 - y, z, core)
        c_peer = at(x, y, z, 1 - core)
        rc, fin = self.rc, self.fin
        if stage == "core":
            plan = [(self.part.at[yy * 2 + 1 - core], rc.at[yy], c_peer) for yy in range(2)]
        elif stage == "plane":
            plan = [
                (rc.at[:, pl.ds(0, 2), 1 - x], self.bx, x_peer),
                (rc.at[1 - y, pl.ds(2, 2)], self.by, y_peer),
            ]
        elif stage == "turn":
            plan = [
                (rc.at[1 - y, pl.ds(0, 2), x], self.cy, y_peer),
                (rc.at[y, pl.ds(2, 2), 1 - x], self.cx, x_peer),
            ]
        elif stage == "depth":
            plan = [
                (rc.at[y, (z + k) % NZ, x], self.bz.at[k - 1], at(x, y, (z + k) % NZ, core))
                for k in range(1, NZ)
            ]
        elif stage == "spread":
            plan = [(fin.at[member], fin.at[member], peer) for peer in (y_peer, c_peer)]
        else:
            plan = [(fin.at[other], fin.at[other], c_peer)]
        return [
            self.wire.copy((self.name, stage, i), source, target, peer)
            for i, (source, target, peer) in enumerate(plan)
        ]

    def start(self, stage):
        for c in self.copies(stage):
            c.start()

    def arrive(self, stage):
        for c in self.copies(stage):
            c.wait_recv()

    def chip(self):
        core = self.where[3]
        self.arrive("core")
        rc, mine = self.rc, self.mine
        for yy in range(2):

            @pl.loop(0, NZ)
            def _(zz):
                for xx in range(NX):
                    rc[yy, zz, xx] = rc[yy, zz, xx] + mine(yy, core, zz, xx)

        self.start("plane")

    def turn(self):
        x, y, z, core = self.where
        rc, bx, by = self.rc, self.bx, self.by
        self.arrive("plane")

        @pl.loop(0, 2)
        def _(zz):
            for i in range(2):
                rc[i, zz, x] = rc[i, zz, x] + bx[i, zz]
                rc[y, 2 + zz, i] = rc[y, 2 + zz, i] + by[zz, i]

        self.start("turn")

    def depth(self):
        x, y, z, core = self.where
        rc, cx, cy = self.rc, self.cx, self.cy
        self.arrive("turn")

        @pl.loop(0, 2)
        def _(zz):
            rc[y, zz, x] = rc[y, zz, x] + cy[zz]
            rc[y, 2 + zz, x] = rc[y, 2 + zz, x] + cx[zz]

        self.start("depth")

    def total(self):
        x, y, z, core = self.where
        self.arrive("depth")
        summed = self.rc[y, z, x].astype(F32)
        for k in range(NZ - 1):
            summed = summed + self.bz[k].astype(F32)
        self.fin[y * 2 + core] = summed.astype(BF16)
        self.start("spread")

    def relay(self):
        self.copies("spread")[0].wait_recv()
        self.start("relay")

    def done(self):
        self.copies("spread")[1].wait_recv()
        self.arrive("relay")

    def drain(self):
        for stage in ("core", "plane", "turn", "depth", "spread", "relay"):
            for c in self.copies(stage):
                c.wait_send()


SCALE = HEAD_DIM**-0.5


def attend_back_step(query, keys, values, powers, inverse, context_t, grad, write):
    for pair in range(2):
        cols = slice(pair * 128, pair * 128 + 128)
        q2 = query[:, cols] * jnp.asarray(SCALE, BF16)
        k2, v2 = keys[:, cols], values[:, cols]
        grad_t = grad[:, cols].astype(F32).T
        product = grad_t * context_t[cols, :].astype(F32)
        k_t = k2.T
        inv = [inverse[pair * 2 + h : pair * 2 + h + 1] for h in range(2)]
        scaled_t = jnp.concatenate(
            [grad_t[:HEAD_DIM] * inv[0], grad_t[HEAD_DIM:] * inv[1]], 0
        ).astype(BF16)
        scaled = scaled_t.T
        dq, dk, dv = [], 0.0, 0.0
        for h in range(2):
            rows = slice(h * HEAD_DIM, (h + 1) * HEAD_DIM)
            inner = jnp.sum(product[rows], 0, keepdims=True) * inv[h]
            power = powers[pair * 2 + h]
            grad_probs = dot(keep_half(h, v2), scaled_t)
            grad_scores = (power.astype(F32) * (grad_probs - inner)).astype(BF16)
            dv = dv + dot(power, keep_half(h, scaled))
            dk = dk + dot(grad_scores, keep_half(h, q2))
            dq.append(dot(k_t[rows], grad_scores))
        write(0, cols, (jnp.concatenate(dq, 0) * SCALE).astype(BF16).T)
        write(1, cols, dk.astype(BF16))
        write(2, cols, dv.astype(BF16))


def backward_kernel(
    part_d, err_two_h, pull_h, wd_h, wu_h, resid_two_h, normal_one_h, inverse_one, first_t_h,
    query_h, keys_h, values_h, powers_h, inverse, context_t_h, tokens_h, w4_h, vec, sums_in,
    o4, ou, od, ov, input_grad,
    part_u, own_d, err_one, grad_context, grad_in, tokens_t, context_t, sums, sums_up,
    pv, va, vb, *rest,
):
    scratch, (send, recv, load) = rest[:35], rest[35:]
    where = x, y, z, core = place()
    shard, member = z * NX + x, y * 2 + core
    total, width = grad_in.shape
    length = total // 2
    columns = sums_up.shape[1]
    loops = columns // CHUNK
    wire = Wire(send, recv)

    def own_part(part):
        return lambda yy, core, zz, xx: part[yy * 2 + core, zz, xx]

    d = Chunk("d", wire, where, part_d, lambda yy, core, zz, xx: own_d[yy, zz, xx], scratch[:7])
    u = Chunk("u", wire, where, part_u, own_part(part_u), scratch[7:14])

    def block(j):
        return pl.ds(pl.multiple_of(j * CHUNK, CHUNK), CHUNK)

    own_loads = [
        pltpu.make_async_copy(part_d.at[yy * 2 + core], own_d.at[yy], load.at[0, yy])
        for yy in range(2)
    ]
    gain_one = vec[3:4].astype(F32)
    sums[...] = sums_in[...]
    sums_up[...] = jnp.zeros_like(sums_up)

    def feed_back(wd, wu, pull, err_two, normal_one, first_t, wo):
        first_loads = [
            pltpu.make_async_copy(err_two_h, err_two, load.at[1, 0]),
            pltpu.make_async_copy(resid_two_h, grad_in, load.at[1, 1]),
            pltpu.make_async_copy(normal_one_h, normal_one, load.at[1, 2]),
            pltpu.make_async_copy(w4_h.at[3], wo, load.at[1, 3]),
        ]
        late_loads = [
            pltpu.make_async_copy(first_t_h, first_t, load.at[2, 0]),
            pltpu.make_async_copy(context_t_h, context_t, load.at[2, 2]),
        ]

        def loads(j):
            return [
                pltpu.make_async_copy(wd_h.at[block(j)], wd.at[block(j)], load.at[3, j]),
                pltpu.make_async_copy(pull_h.at[:, block(j)], pull.at[:, block(j)], load.at[4, j]),
                pltpu.make_async_copy(wu_h.at[:, block(j)], wu.at[:, block(j)], load.at[5, j]),
            ]

        first_loads[0].start()
        for c in loads(0):
            c.start()
        for c in own_loads + first_loads[1:]:
            c.start()
        for j in range(1, loops):
            for c in loads(j):
                c.start()
        for c in late_loads:
            c.start()
        greet(all_peers())
        d.start("core")
        first_loads[0].wait()
        for s in range(2):
            rows = slice(s * length, (s + 1) * length)

            def down(j, acc):
                if s == 0:
                    for c in loads(j):
                        c.wait()

                    @pl.when(j == 1)
                    def _():
                        for c in own_loads:
                            c.wait()
                        d.chip()

                grads = dot_t(err_two[rows, :], wd[block(j), :])
                low = (grads * pull[rows, block(j)].astype(F32)).astype(BF16)
                pull[rows, block(j)] = low
                sums_up[:, block(j)] += jnp.sum(low.astype(F32), 0, keepdims=True)
                return acc + dot_t(low, wu[:, block(j)])

            grad_first = lax.fori_loop(0, loops, down, jnp.zeros((length, width), F32))
            if s == 0:
                for c in first_loads[1:]:
                    c.wait()
            grad_first = grad_first + grad_in[rows, :]
            normal = normal_one[rows, :]
            note(sums, 3, grad_first * normal)
            note(sums, 4, grad_first)
            resid = pull_back(grad_first * gain_one, normal, inverse_one[rows, :])
            grad_in[rows, :] = resid
            low = resid.astype(BF16)
            err_one[rows, :] = low
            note(sums, 2, low.astype(F32))
            grad_context[rows, :] = dot_t(low, wo[...]).astype(BF16)
        d.turn()
        for c in late_loads:
            c.wait()

        @pl.loop(0, 4)
        def _(m):
            cols = pl.ds(pl.multiple_of(m * width, width), width)
            part_u[m] = dot(first_t[...], pull[:, cols]).astype(BF16).reshape(part_u.shape[1:])

            @pl.when(m == 2)
            def _():
                d.depth()

        u.start("core")

    pl.run_scoped(
        feed_back,
        pltpu.VMEM((columns, width), BF16),
        pltpu.VMEM((width, columns), BF16),
        pltpu.VMEM((total, columns), BF16),
        pltpu.VMEM((total, width), BF16),
        pltpu.VMEM((total, width), F32),
        pltpu.VMEM((width, total), BF16),
        pltpu.VMEM((width, width), BF16),
    )

    def attend_and_inputs(qkv, powers, grads, weights, part_q, tokens):
        q = [
            Chunk(("q", g), wire, where, part_q.at[g], own_part(part_q.at[g]), scratch[14 + 7 * g : 21 + 7 * g])
            for g in range(3)
        ]
        def loads(g, s):
            rows, cols = pl.ds(pl.multiple_of(s * length, length), length), pl.ds(g * GROUP, GROUP)
            return [
                pltpu.make_async_copy(a.at[rows, cols], qkv.at[s, i], load.at[6 + i, s])
                for i, a in enumerate((query_h, keys_h, values_h))
            ] + [
                pltpu.make_async_copy(powers_h.at[s, pl.ds(g * 4, 4)], powers.at[s], load.at[9, s])
            ]

        weight_loads = [
            pltpu.make_async_copy(
                w4_h.at[i, :, pl.ds(g * GROUP, GROUP)],
                weights.at[g, :, pl.ds(i * GROUP, GROUP)],
                load.at[10 + g, i],
            )
            for g in range(3)
            for i in range(3)
        ]
        tokens_load = pltpu.make_async_copy(tokens_h, tokens, load.at[2, 1])
        for c in loads(0, 0) + [tokens_load] + weight_loads:
            c.start()
        for g in range(3):
            cols = slice(g * GROUP, (g + 1) * GROUP)

            @pl.loop(0, 2)
            def _(s):
                @pl.when(s == 0)
                def _():
                    for c in loads(g, 1):
                        c.start()

                if g < 2:

                    @pl.when(s == 1)
                    def _():
                        for c in loads(g + 1, 0):
                            c.start()

                for c in loads(g, s):
                    c.wait()
                rows = pl.ds(pl.multiple_of(s * length, length), length)

                def write(kind, pair, value):
                    lanes = slice(kind * GROUP + pair.start, kind * GROUP + pair.stop)
                    grads[g, rows, lanes] = value

                attend_back_step(
                    qkv.at[s, 0], qkv.at[s, 1], qkv.at[s, 2], powers.at[s],
                    inverse.at[s, g], context_t.at[cols, rows], grad_context.at[rows, cols], write,
                )

                @pl.when(s == 0)
                def _():
                    if g == 0:
                        u.chip()
                    elif g == 1:
                        d.total()
                        q[0].chip()
                    else:
                        q[1].chip()
                        q[0].turn()

            if g == 1:
                d.relay()
            if g == 0:
                tokens_load.wait()
                tokens_t[...] = tokens[...].T
            for i in range(3):
                lanes = slice(i * GROUP, (i + 1) * GROUP)
                part_q[g, i] = (
                    dot(tokens_t[...], grads[g, :, lanes])
                    .astype(BF16)
                    .reshape(NZ, NX, ROWS, GROUP)
                )
            part_q[g, 3] = (
                dot(context_t[...], err_one[:, cols]).astype(BF16).reshape(NZ, NX, ROWS, GROUP)
            )
            q[g].start("core")
            sums[0:1, cols] = jnp.sum(grads[g, :, :GROUP].astype(F32), 0, keepdims=True)
            sums[1:2, cols] = jnp.sum(grads[g, :, 2 * GROUP :].astype(F32), 0, keepdims=True)
            if g == 1:
                u.turn()
        u.depth()

        pv[...] = jnp.zeros_like(pv)
        lanes = lax.broadcasted_iota(jnp.int32, (width, NX * NZ * 128), 1)
        rows = lax.broadcasted_iota(jnp.int32, (width, NX * NZ * 128), 0)
        pick = (rows == (lanes // 128) * ROWS + lanes % 128) & (lanes % 128 < ROWS)
        spread8 = lax.dot_general(
            sums[...], pick.astype(F32), (((1,), (0,)), ((), ())),
            precision=lax.Precision.HIGHEST, preferred_element_type=F32,
        )
        per = columns // (NX * NZ)
        for f in range(NX * NZ):
            pv[f, 8:16, 0:128] = spread8[:, f * 128 : (f + 1) * 128]
            pv[f, 0:1, :] = sums_up[:, f * per : (f + 1) * per]

        def to_owner(k):
            to = (shard + k) % (NX * NZ)
            return wire.copy(("v", k), pv.at[to], va.at[k - 1], {"dp": member, "fsdp": to})

        for k in range(1, NX * NZ):
            to_owner(k).start()
        for c in weight_loads:
            c.wait()
        out = []
        for i in range(3):
            lanes = slice(i * GROUP, (i + 1) * GROUP)
            summed = grad_in[:, lanes]
            for g in range(3):
                summed = summed + dot_t(grads[g], weights[g, lanes, :])
            grad_in[:, lanes] = summed
            c = pltpu.make_async_copy(
                grad_in.at[:, lanes], input_grad.at[:, lanes], load.at[13, i]
            )
            c.start()
            out.append(c)
            if i == 0:
                q[2].chip()
            elif i == 1:
                q[1].turn()
                q[0].depth()

        for k in range(1, NX * NZ):
            to_owner(k).wait_recv()
        partial = pv[shard]
        for k in range(NX * NZ - 1):
            partial = partial + va[k]
        vb[member] = partial

        def to_member(i):
            dy, dc = ((0, 1), (1, 0), (1, 1))[i]
            peer = at(x, (y + dy) % 2, z, (core + dc) % 2)
            return wire.copy(("w", i), vb.at[member], vb.at[member], peer)

        for i in range(3):
            to_member(i).start()
        q[2].turn()
        q[1].depth()
        u.total()
        q[2].depth()
        q[0].total()
        u.relay()
        for i in range(3):
            to_member(i).wait_recv()
        ov[...] = (vb[0] + vb[1]) + (vb[2] + vb[3])
        d.done()
        per_d = d.fin.shape[1]
        for i in range(4):
            od[:, i * per_d : (i + 1) * per_d] = d.fin[i].astype(F32).T
        q[1].total()
        q[0].relay()
        u.done()
        for i in range(4):
            ou[:, i * width : (i + 1) * width] = u.fin[i].astype(F32)
        q[2].total()
        q[1].relay()
        q[0].done()
        q[2].relay()
        q[1].done()
        q[2].done()
        for g in range(3):
            for i in range(4):
                o4[i, :, g * GROUP : (g + 1) * GROUP] = q[g].fin[i].astype(F32)
        for c in out:
            c.wait()
        for c in [d, u] + q:
            c.drain()
        for k in range(1, NX * NZ):
            to_owner(k).wait_send()
        for i in range(3):
            to_member(i).wait_send()

    pl.run_scoped(
        attend_and_inputs,
        pltpu.VMEM((2, 3, length, GROUP), BF16),
        pltpu.VMEM((2, 4, length, length), BF16),
        pltpu.VMEM((3, total, width), BF16),
        pltpu.VMEM((3, width, width), BF16),
        pltpu.VMEM((3, 4, NZ, NX, ROWS, GROUP), BF16),
        pltpu.VMEM((total, width), BF16),
    )


def backward(
    part_d, err_two, pull, wd, wu, resid_two, normal_one, inverse_one, first_t,
    query, keys, values, powers, inverse, context_t, rows, w4, vec, sums_in,
):
    total, width = rows.shape
    columns = wu.shape[1]
    per = columns // (NX * NZ)
    hbm, vmem = pl.BlockSpec(memory_space=pl.ANY), pl.BlockSpec(memory_space=pltpu.VMEM)
    d_block, copies = part_d.shape[3:], 7 + 3 + 5 * (2 + 2 + 2 + 3 + 2 + 1)
    scratch = [
        pltpu.VMEM((4, NZ, NX, ROWS, width), BF16),
        pltpu.VMEM((2, NZ, NX) + d_block, BF16),
        pltpu.VMEM((total, width), BF16),
        pltpu.VMEM((total, width), BF16),
        pltpu.VMEM((total, width), F32),
        pltpu.VMEM((width, total), BF16),
        pltpu.VMEM((width, total), BF16),
        pltpu.VMEM((8, width), F32),
        pltpu.VMEM((1, columns), F32),
        pltpu.VMEM((NX * NZ, 16, per), F32),
        pltpu.VMEM((NX * NZ - 1, 16, per), F32),
        pltpu.VMEM((4, 16, per), F32),
    ]
    scratch += Chunk.scratch(*d_block) + Chunk.scratch(ROWS, width)
    scratch += Chunk.scratch(ROWS, GROUP) * 3
    scratch += [pltpu.SemaphoreType.DMA((copies,))] * 2 + [pltpu.SemaphoreType.DMA((14, 4))]
    return pl.pallas_call(
        backward_kernel,
        name="backward",
        in_specs=[hbm] * 7 + [vmem] + [hbm] * 5 + [vmem] + [hbm] * 3 + [vmem] * 2,
        out_specs=[vmem] * 4 + [hbm],
        out_shape=[
            Shape((4, ROWS, width), F32),
            Shape((ROWS, columns), F32),
            Shape((per, width), F32),
            Shape((16, per), F32),
            Shape((total, width), F32),
        ],
        scratch_shapes=scratch,
        compiler_params=params(collective_id=1, has_side_effects=True),
    )(
        part_d, err_two, pull, wd, wu, resid_two, normal_one, inverse_one, first_t,
        query, keys, values, powers, inverse, context_t, rows, w4, vec, sums_in,
    )


def fused_layer(
    tokens, counts, cotangent, query_weight, key_weight, value_weight, out_weight, query_bias,
    value_bias, out_bias, attention_gain, attention_shift, up_weight, up_bias, down_weight,
    down_bias, feed_gain, feed_shift,
):
    slots, length, width = tokens.shape
    shards = NX * NZ
    columns = up_weight.shape[1]
    rows = tokens.reshape(-1, width)
    vec = jnp.stack(
        [query_bias, value_bias, out_bias, attention_gain, attention_shift, down_bias, feed_gain, feed_shift]
    )
    vec = jnp.concatenate([vec, up_bias.reshape(4, ROWS)], 0)
    vec = jnp.pad(vec, ((0, 4), (0, 128 - ROWS)))
    g4, gu, gd, gv = gather_all(
        query_weight, key_weight, value_weight, out_weight, up_weight, down_weight, vec
    )
    w4 = g4.reshape(4, width, width)
    wu = gu.reshape(width, columns)
    wd = gd.reshape(columns, width)
    vec8 = gv[:, :8, :ROWS].transpose(1, 0, 2).reshape(8, width)
    up_row = gv[:, 8:12, :ROWS].reshape(1, columns)
    query, keys, values, powers, context_t, inverse = attend(counts, rows, w4, vec8, length)
    (
        layer_out, resid_two, normal_one, inverse_one, first_t, err_two, err_two_t, act, pull, sums,
    ) = middle(
        counts, rows, context_t, cotangent.reshape(-1, width), w4, wu, wd, vec8, up_row, length
    )
    part_d = outer_down(err_two_t, act)
    o4, ou, od, ov, input_grad = backward(
        part_d, err_two, pull, wd, wu, resid_two, normal_one, inverse_one, first_t,
        query, keys, values, powers, inverse, context_t, rows, w4, vec8, sums,
    )
    v = [ov[8 + i, :ROWS] for i in range(8)]
    return (
        layer_out.reshape(tokens.shape),
        input_grad.reshape(tokens.shape),
        o4[0], o4[1], o4[2], o4[3],
        v[0], v[1], v[2], v[3], v[4],
        ou, ov[0], od, v[5], v[6], v[7],
    )


def exact_gelu(value):
    return jax.nn.gelu(value, approximate=False)


def norm_forward(resid, gain, shift):
    average = jnp.mean(resid, axis=-1, keepdims=True)
    centred = resid - average
    spread = jnp.mean(centred * centred, axis=-1, keepdims=True)
    inverse = lax.rsqrt(spread + epsilon)
    normal = centred * inverse
    return (normal * gain + shift, normal, inverse)


def norm_backward(grad_out, normal, inverse, gain):
    scaled = grad_out * gain
    first_mean = jnp.mean(scaled, axis=-1, keepdims=True)
    second_mean = jnp.mean(scaled * normal, axis=-1, keepdims=True)
    grad_resid = inverse * (scaled - first_mean - normal * second_mean)
    return (grad_resid, jnp.sum(grad_out * normal, 0), jnp.sum(grad_out, 0))


def linear(rows, weight):
    return jnp.dot(rows, weight, preferred_element_type=jnp.float32)


def linear_back(grads, weight):
    return lax.dot_general(
        grads, weight, (((1,), (1,)), ((), ())), preferred_element_type=jnp.float32
    )


def outer_sum(rows, grads):
    return lax.dot_general(
        rows, grads, (((0,), (0,)), ((), ())), preferred_element_type=jnp.float32
    )


def column_sum(grads):
    return jnp.sum(grads.astype(jnp.float32), 0)


def on_device(
    tokens,
    counts,
    cotangent,
    query_weight,
    key_weight,
    value_weight,
    out_weight,
    query_bias,
    value_bias,
    out_bias,
    attention_gain,
    attention_shift,
    up_weight,
    up_bias,
    down_weight,
    down_bias,
    feed_gain,
    feed_shift,
):
    slots, length, width = tokens.shape
    heads = width // HEAD_DIM
    factor = HEAD_DIM ** (-0.5)
    positions = jnp.arange(length, dtype=jnp.int32)

    def split_heads(value):
        return value.reshape(slots, length, heads, HEAD_DIM)

    def masked_scores(query, keys, count):
        raw = jnp.einsum("qhd,khd->hqk", query, keys, preferred_element_type=jnp.float32)
        live = positions < count
        return jnp.where(live[None, None, :], raw * factor, -1000000000.0)

    def attend_forward(block):
        query, keys, values, count = block
        scores = masked_scores(query, keys, count)
        highest = jnp.max(scores, axis=-1, keepdims=True)
        powers = jnp.exp(scores - highest)
        totals = jnp.sum(powers, axis=-1, keepdims=True)
        probs = (powers / totals).astype(jnp.bfloat16)
        context = jnp.einsum("hqk,khd->qhd", probs, values, preferred_element_type=jnp.float32)
        return (context.reshape(length, width), highest + jnp.log(totals))

    def attend_backward(block):
        query, keys, values, count, logsum, grad_context = block
        scores = masked_scores(query, keys, count)
        probs = jnp.exp(scores - logsum)
        probs_low = probs.astype(jnp.bfloat16)
        grad_probs = jnp.einsum(
            "qhd,khd->hqk", grad_context, values, preferred_element_type=jnp.float32
        )
        inner = jnp.sum(probs * grad_probs, axis=-1, keepdims=True)
        grad_scores = (probs * (grad_probs - inner) * factor).astype(jnp.bfloat16)
        grad_query = jnp.einsum(
            "hqk,khd->qhd", grad_scores, keys, preferred_element_type=jnp.float32
        )
        grad_keys = jnp.einsum(
            "hqk,qhd->khd", grad_scores, query, preferred_element_type=jnp.float32
        )
        grad_values = jnp.einsum(
            "hqk,qhd->khd", probs_low, grad_context, preferred_element_type=jnp.float32
        )
        return (
            grad_query.reshape(length, width).astype(jnp.bfloat16),
            grad_keys.reshape(length, width).astype(jnp.bfloat16),
            grad_values.reshape(length, width).astype(jnp.bfloat16),
        )

    attention_set = (
        lax.all_gather(query_weight, "fsdp", axis=0, tiled=True),
        lax.all_gather(key_weight, "fsdp", axis=0, tiled=True),
        lax.all_gather(value_weight, "fsdp", axis=0, tiled=True),
        lax.all_gather(out_weight, "fsdp", axis=0, tiled=True),
        lax.all_gather(query_bias, "fsdp", axis=0, tiled=True),
        lax.all_gather(value_bias, "fsdp", axis=0, tiled=True),
        lax.all_gather(out_bias, "fsdp", axis=0, tiled=True),
        lax.all_gather(attention_gain, "fsdp", axis=0, tiled=True),
        lax.all_gather(attention_shift, "fsdp", axis=0, tiled=True),
    )
    feed_set = (
        lax.all_gather(up_weight, "fsdp", axis=0, tiled=True),
        lax.all_gather(up_bias, "fsdp", axis=0, tiled=True),
        lax.all_gather(down_weight, "fsdp", axis=0, tiled=True),
        lax.all_gather(down_bias, "fsdp", axis=0, tiled=True),
        lax.all_gather(feed_gain, "fsdp", axis=0, tiled=True),
        lax.all_gather(feed_shift, "fsdp", axis=0, tiled=True),
    )
    whole_query, whole_key, whole_value, whole_out = (
        attention_set[0],
        attention_set[1],
        attention_set[2],
        attention_set[3],
    )
    whole_up, whole_down = (feed_set[0], feed_set[2])
    rows = tokens.reshape(-1, width)
    query = (linear(rows, whole_query) + attention_set[4].astype(jnp.float32)).astype(jnp.bfloat16)
    keys = linear(rows, whole_key).astype(jnp.bfloat16)
    values = (linear(rows, whole_value) + attention_set[5].astype(jnp.float32)).astype(jnp.bfloat16)
    context_rows, logsum = lax.map(
        attend_forward, (split_heads(query), split_heads(keys), split_heads(values), counts)
    )
    context = context_rows.reshape(-1, width).astype(jnp.bfloat16)
    branch = linear(context, whole_out) + attention_set[6].astype(jnp.float32)
    gain_one = attention_set[7].astype(jnp.float32)
    first, normal_one, inverse_one = norm_forward(
        rows.astype(jnp.float32) + branch, gain_one, attention_set[8].astype(jnp.float32)
    )
    first_low = first.astype(jnp.bfloat16)
    hidden = linear(first_low, whole_up) + feed_set[1].astype(jnp.float32)
    activated, gelu_pull = jax.vjp(exact_gelu, hidden)
    act_low = activated.astype(jnp.bfloat16)
    second = linear(act_low, whole_down) + feed_set[3].astype(jnp.float32)
    gain_two = feed_set[4].astype(jnp.float32)
    output, normal_two, inverse_two = norm_forward(
        first + second, gain_two, feed_set[5].astype(jnp.float32)
    )
    live = (positions[None, :] < counts[:, None]).reshape(-1, 1)
    layer_out = jnp.where(live, output, 0.0).astype(jnp.bfloat16).reshape(tokens.shape)
    back_feed = (
        lax.all_gather(up_weight, "fsdp", axis=0, tiled=True),
        lax.all_gather(down_weight, "fsdp", axis=0, tiled=True),
    )
    back_up, back_down = (back_feed[0], back_feed[1])
    grad_y = jnp.where(live, cotangent.reshape(-1, width).astype(jnp.float32), 0.0)
    resid_two, grad_feed_gain, grad_feed_shift = norm_backward(
        grad_y, normal_two, inverse_two, gain_two
    )
    err_two = resid_two.astype(jnp.bfloat16)
    grad_down_weight = outer_sum(act_low, err_two)
    grad_down_bias = column_sum(err_two)
    grad_act = linear_back(err_two, back_down)
    grad_hidden = gelu_pull(grad_act)[0].astype(jnp.bfloat16)
    grad_up_weight = outer_sum(first_low, grad_hidden)
    grad_up_bias = column_sum(grad_hidden)
    grad_first = resid_two + linear_back(grad_hidden, back_up)
    feed_shards = (
        lax.psum_scatter(
            grad_up_weight.astype(jnp.bfloat16), "fsdp", scatter_dimension=0, tiled=True
        ).astype(jnp.float32),
        lax.psum_scatter(
            grad_up_bias.astype(jnp.bfloat16), "fsdp", scatter_dimension=0, tiled=True
        ).astype(jnp.float32),
        lax.psum_scatter(
            grad_down_weight.astype(jnp.bfloat16), "fsdp", scatter_dimension=0, tiled=True
        ).astype(jnp.float32),
        lax.psum_scatter(
            grad_down_bias.astype(jnp.bfloat16), "fsdp", scatter_dimension=0, tiled=True
        ).astype(jnp.float32),
        lax.psum_scatter(
            grad_feed_gain.astype(jnp.bfloat16), "fsdp", scatter_dimension=0, tiled=True
        ).astype(jnp.float32),
        lax.psum_scatter(
            grad_feed_shift.astype(jnp.bfloat16), "fsdp", scatter_dimension=0, tiled=True
        ).astype(jnp.float32),
    )
    back_attention = (
        lax.all_gather(query_weight, "fsdp", axis=0, tiled=True),
        lax.all_gather(key_weight, "fsdp", axis=0, tiled=True),
        lax.all_gather(value_weight, "fsdp", axis=0, tiled=True),
        lax.all_gather(out_weight, "fsdp", axis=0, tiled=True),
    )
    back_query, back_key, back_value, back_out = (
        back_attention[0],
        back_attention[1],
        back_attention[2],
        back_attention[3],
    )
    resid_one, grad_attention_gain, grad_attention_shift = norm_backward(
        grad_first, normal_one, inverse_one, gain_one
    )
    err_one = resid_one.astype(jnp.bfloat16)
    grad_out_weight = outer_sum(context, err_one)
    grad_out_bias = column_sum(err_one)
    grad_context = linear_back(err_one, back_out).astype(jnp.bfloat16)
    grad_query, grad_keys, grad_values = lax.map(
        attend_backward,
        (
            split_heads(query),
            split_heads(keys),
            split_heads(values),
            counts,
            logsum,
            split_heads(grad_context),
        ),
    )
    grad_query = grad_query.reshape(-1, width)
    grad_keys = grad_keys.reshape(-1, width)
    grad_values = grad_values.reshape(-1, width)
    grad_query_weight = outer_sum(rows, grad_query)
    grad_key_weight = outer_sum(rows, grad_keys)
    grad_value_weight = outer_sum(rows, grad_values)
    grad_query_bias = column_sum(grad_query)
    grad_value_bias = column_sum(grad_values)
    input_grad = (
        resid_one
        + linear_back(grad_query, back_query)
        + linear_back(grad_keys, back_key)
        + linear_back(grad_values, back_value)
    )
    attention_shards = (
        lax.psum_scatter(
            grad_query_weight.astype(jnp.bfloat16), "fsdp", scatter_dimension=0, tiled=True
        ).astype(jnp.float32),
        lax.psum_scatter(
            grad_key_weight.astype(jnp.bfloat16), "fsdp", scatter_dimension=0, tiled=True
        ).astype(jnp.float32),
        lax.psum_scatter(
            grad_value_weight.astype(jnp.bfloat16), "fsdp", scatter_dimension=0, tiled=True
        ).astype(jnp.float32),
        lax.psum_scatter(
            grad_out_weight.astype(jnp.bfloat16), "fsdp", scatter_dimension=0, tiled=True
        ).astype(jnp.float32),
        lax.psum_scatter(
            grad_query_bias.astype(jnp.bfloat16), "fsdp", scatter_dimension=0, tiled=True
        ).astype(jnp.float32),
        lax.psum_scatter(
            grad_value_bias.astype(jnp.bfloat16), "fsdp", scatter_dimension=0, tiled=True
        ).astype(jnp.float32),
        lax.psum_scatter(
            grad_out_bias.astype(jnp.bfloat16), "fsdp", scatter_dimension=0, tiled=True
        ).astype(jnp.float32),
        lax.psum_scatter(
            grad_attention_gain.astype(jnp.bfloat16), "fsdp", scatter_dimension=0, tiled=True
        ).astype(jnp.float32),
        lax.psum_scatter(
            grad_attention_shift.astype(jnp.bfloat16), "fsdp", scatter_dimension=0, tiled=True
        ).astype(jnp.float32),
    )
    summed = lax.psum(
        (
            attention_shards[0],
            attention_shards[1],
            attention_shards[2],
            attention_shards[3],
            attention_shards[4],
            attention_shards[5],
            attention_shards[6],
            attention_shards[7],
            attention_shards[8],
            feed_shards[0],
            feed_shards[1],
            feed_shards[2],
            feed_shards[3],
            feed_shards[4],
            feed_shards[5],
        ),
        "dp",
    )
    return (
        layer_out,
        input_grad.reshape(tokens.shape),
        summed[0],
        summed[1],
        summed[2],
        summed[3],
        summed[4],
        summed[5],
        summed[6],
        summed[7],
        summed[8],
        summed[9],
        summed[10],
        summed[11],
        summed[12],
        summed[13],
        summed[14],
    )


def solution(mesh):
    small = mesh.shape["dp"] == 4 and mesh.shape["fsdp"] == NX * NZ
    return jax.shard_map(
        fused_layer if small else on_device,
        mesh=mesh,
        in_specs=(
            P(("dp", "fsdp"), None, None),
            P(("dp", "fsdp")),
            P(("dp", "fsdp"), None, None),
            P("fsdp", None),
            P("fsdp", None),
            P("fsdp", None),
            P("fsdp", None),
            P("fsdp"),
            P("fsdp"),
            P("fsdp"),
            P("fsdp"),
            P("fsdp"),
            P("fsdp", None),
            P("fsdp"),
            P("fsdp", None),
            P("fsdp"),
            P("fsdp"),
            P("fsdp"),
        ),
        out_specs=(
            P(("dp", "fsdp"), None, None),
            P(("dp", "fsdp"), None, None),
            P("fsdp", None),
            P("fsdp", None),
            P("fsdp", None),
            P("fsdp", None),
            P("fsdp"),
            P("fsdp"),
            P("fsdp"),
            P("fsdp"),
            P("fsdp"),
            P("fsdp", None),
            P("fsdp"),
            P("fsdp", None),
            P("fsdp"),
            P("fsdp"),
            P("fsdp"),
        ),
        check_vma=False,
    )
```

```python
import functools

import jax
import jax.numpy as jnp
from jax import lax
from jax.experimental import pallas as pl
from jax.experimental.pallas import tpu as pltpu
from jax.sharding import PartitionSpec as P

HEAD_DIM = 64
epsilon = 1e-05
F32 = jnp.float32
BF16 = jnp.bfloat16
MESH = pl.DeviceIdType.MESH
VMEM_LIMIT = 63 * 2**20
Shape = jax.ShapeDtypeStruct


def dot(left, right):
    return lax.dot_general(
        left, right, (((1,), (0,)), ((), ())), preferred_element_type=F32
    )


def dot_t(left, right):
    return lax.dot_general(
        left, right, (((1,), (1,)), ((), ())), preferred_element_type=F32
    )


def params(**extra):
    return pltpu.CompilerParams(vmem_limit_bytes=VMEM_LIMIT, **extra)


def whole(shape):
    return pl.BlockSpec(shape, lambda *_: (0,) * len(shape), pipeline_mode=pl.Buffered(1))


NX, NZ, ROWS = 2, 4, 96


def place():
    member = lax.axis_index("dp")
    shard = lax.axis_index("fsdp")
    return shard % NX, member // 2, shard // NX, member % 2


def at(x, y, z, core):
    return {"dp": y * 2 + core, "fsdp": z * NX + x}


def greet(peers):
    barrier = pltpu.get_barrier_semaphore()
    for peer in peers:
        pl.semaphore_signal(barrier, inc=1, device_id=peer, device_id_type=MESH)
    pl.semaphore_wait(barrier, len(peers))


def all_peers():
    x, y, z, core = place()
    near = [at(x, 1 - y, z, core), at(x, y, z, 1 - core)]
    for step in range(1, NX * NZ):
        near.append({"dp": y * 2 + core, "fsdp": (z * NX + x + step) % (NX * NZ)})
    return near


class Wire:
    def __init__(self, send, recv):
        self.send, self.recv, self.slots = send, recv, {}

    def copy(self, key, source, target, peer):
        slot = self.slots.setdefault(key, len(self.slots))
        return pltpu.make_async_remote_copy(
            src_ref=source,
            dst_ref=target,
            send_sem=self.send.at[slot],
            recv_sem=self.recv.at[slot],
            device_id=peer,
            device_id_type=MESH,
        )


GROUP = 4 * HEAD_DIM
SCALE = HEAD_DIM**-0.5
CHUNK = 1024


class Piece:
    def __init__(self, name, wire, where, block):
        self.name, self.wire, self.where, self.block = name, wire, where, block

    def copy(self, key, source, peer):
        return self.wire.copy((self.name, key), source, source, peer)

    def copies(self, stage):
        x, y, z, core = self.where
        member, other = y * 2 + core, (1 - y) * 2 + core
        x_peer, y_peer = at(1 - x, y, z, core), at(x, 1 - y, z, core)
        c_peer = at(x, y, z, 1 - core)
        every, block = slice(None), self.block
        if stage == "depth":
            mine = block(member, z, x)
            plan = [(mine, at(x, y, (z + k) % NZ, core)) for k in range(1, NZ)]
        elif stage == "plane":
            mine = block(member, every, x)
            plan = [(mine, x_peer), (mine, y_peer)]
        elif stage == "turn":
            plan = [
                (block(other, pl.ds(0, 2), x), x_peer),
                (block(member, pl.ds(2, 2), 1 - x), y_peer),
            ]
        else:
            plan = [
                (block(member, every, x), c_peer),
                (block(other, every, x), c_peer),
                (block(member, every, 1 - x), c_peer),
                (block(other, every, 1 - x), c_peer),
            ]
        return [self.copy((stage, i), source, peer) for i, (source, peer) in enumerate(plan)]

    def send(self):
        for c in self.copies("depth"):
            c.start()

    def plane(self):
        for c in self.copies("depth"):
            c.wait_recv()
        for c in self.copies("plane"):
            c.start()
        self.copies("core")[0].start()

    def turn(self):
        from_x, from_y = self.copies("plane")
        from_y.wait_recv()
        self.copies("turn")[0].start()
        self.copies("core")[1].start()
        from_x.wait_recv()
        self.copies("turn")[1].start()
        self.copies("core")[2].start()

    def rest(self):
        for c in self.copies("turn"):
            c.wait_recv()
        self.copies("core")[3].start()

    def ready(self):
        for c in self.copies("core"):
            c.wait_recv()

    def drain(self):
        for stage in ("depth", "plane", "turn", "core"):
            for c in self.copies(stage):
                c.wait_send()


def half(index, shape):
    lanes = lax.broadcasted_iota(jnp.int32, shape, 1)
    return lanes < HEAD_DIM if index == 0 else lanes >= HEAD_DIM


def keep_half(index, value):
    return jnp.where(half(index, value.shape), value, jnp.zeros_like(value))


def attend_step(hidden_keys, q, k, v, powers, inverse, context_t):
    for pair in range(2):
        cols = slice(pair * 128, pair * 128 + 128)
        q2 = q[:, cols] * jnp.asarray(SCALE, BF16)
        k2, v_t = k[:, cols], v[:, cols].T
        for h in range(2):
            scores = dot_t(keep_half(h, k2), q2) + hidden_keys
            highest = jnp.max(scores, 0, keepdims=True)
            power = jnp.exp(scores - highest)
            inv = 1.0 / jnp.sum(power, 0, keepdims=True)
            low = power.astype(BF16)
            powers[pair * 2 + h] = low
            inverse[pair * 2 + h : pair * 2 + h + 1] = inv
            out = dot(v_t[h * HEAD_DIM : (h + 1) * HEAD_DIM], low) * inv
            context_t[pair * 128 + h * HEAD_DIM : pair * 128 + (h + 1) * HEAD_DIM] = out.astype(
                BF16
            )


SQRT_HALF = 0.7071067811865476
PDF_SCALE = 0.3989422804014327


def normal_parts(value):
    z = jnp.abs(value) * SQRT_HALF
    t = 1.0 / (1.0 + 0.3275911 * z)
    bell = jnp.exp(-(z * z))
    poly = 1.061405429 * t - 1.453152027
    poly = poly * t + 1.421413741
    poly = poly * t - 0.284496736
    poly = poly * t + 0.254829592
    tail = (0.5 * poly * t) * bell
    return jnp.where(value >= 0, 1.0 - tail, tail), bell * PDF_SCALE


def centre(resid):
    centred = resid - jnp.mean(resid, 1, keepdims=True)
    inv = lax.rsqrt(jnp.mean(centred * centred, 1, keepdims=True) + epsilon)
    return centred * inv, inv


def pull_back(scaled, normal, inv):
    return inv * (
        scaled
        - jnp.mean(scaled, 1, keepdims=True)
        - normal * jnp.mean(scaled * normal, 1, keepdims=True)
    )


def note(sums, row, value):
    sums[row : row + 1] += jnp.sum(value, 0, keepdims=True)


def forward_kernel(
    counts, tokens, vec, cotangent_h, wq, wk, wv, wo, wu_i, wd_i,
    w4_h, wu_h, wd_h, layer_out_h, query_h, keys_h, values_h, powers_h, context_t_h, first_t_h,
    err_two_h, resid_two_h, normal_one_h, pull_h, part_d_h, vec8, inverse, inverse_one, sums,
    w4, wu, wd, gv, up_row, context_t, send, recv, local,
):
    where = x, y, z, core = place()
    shard, member = z * NX + x, y * 2 + core
    total, width = tokens.shape
    length = total // 2
    columns = up_row.shape[1]
    wire = Wire(send, recv)

    def columns_of(g):
        return lambda who, zs, xs: w4.at[who, zs, xs, :, pl.ds(g * GROUP, GROUP)]

    def up_part(i):
        part = width // 2
        return lambda who, zs, xs: wu.at[
            zs, xs, :, pl.ds(pl.multiple_of(who * width + i * part, part), part)
        ]

    def down_part(i):
        part = ROWS // 2
        return lambda who, zs, xs: wd.at[zs, xs, who, pl.ds(i * part, part)]

    q = [Piece(("q", g), wire, where, columns_of(g)) for g in range(3)]
    u = [Piece(("u", i), wire, where, up_part(i)) for i in range(2)]
    d = [Piece(("d", i), wire, where, down_part(i)) for i in range(2)]
    pieces = q + u + d

    own = [
        pltpu.make_async_copy(wq, w4.at[member, z, x], local.at[0, 0]),
        pltpu.make_async_copy(
            wu_i.at[:, pl.ds(pl.multiple_of(member * width, width), width)],
            wu.at[z, x, :, pl.ds(pl.multiple_of(member * width, width), width)],
            local.at[0, 1],
        ),
        pltpu.make_async_copy(wd_i.at[member], wd.at[z, x, member], local.at[0, 2]),
        pltpu.make_async_copy(vec, gv.at[shard], local.at[0, 3]),
    ]
    for i, w in enumerate((wq, wk, wv, wo)):

        @pl.when(member == i)
        def _():
            pltpu.make_async_copy(w, w4.at[i, z, x], local.at[0, 0]).start()

    for c in own[1:]:
        c.start()
    greet(all_peers())
    for c in own:
        c.wait()

    def vec_copy(k):
        peer = {"dp": member, "fsdp": (shard + k) % (NX * NZ)}
        return wire.copy(("v", k), gv.at[shard], gv.at[shard], peer)

    for k in range(1, NX * NZ):
        vec_copy(k).start()
    for p in pieces:
        p.send()
    sums[...] = jnp.zeros_like(sums)
    q[0].plane()
    for k in range(1, NX * NZ):
        vec_copy(k).wait_recv()
    lanes = lax.broadcasted_iota(jnp.int32, (128, width), 0)
    features = lax.broadcasted_iota(jnp.int32, (128, width), 1)
    per = columns // (NX * NZ)
    joined = jnp.zeros((8, width), F32)
    for f in range(NX * NZ):
        pick = (features == f * ROWS + lanes) & (lanes < ROWS)
        joined = joined + dot(gv[f, 8:16, 0:128].astype(BF16), pick.astype(F32).astype(BF16))
        up_row[:, f * per : (f + 1) * per] = gv[f, 0:1, :]
    vec8[...] = joined
    q[1].plane()
    q[0].turn()
    q[2].plane()
    q[0].rest()
    q[0].ready()

    def attention(qkv, powers):
        def outs(g, s, slot):
            rows = pl.ds(pl.multiple_of(s * length, length), length)
            cols = pl.ds(pl.multiple_of(g * GROUP, GROUP), GROUP)
            heads = pl.ds(g * 4, 4)
            return [
                pltpu.make_async_copy(qkv.at[slot, i], a.at[rows, cols], local.at[1 + i, slot])
                for i, a in enumerate((query_h, keys_h, values_h))
            ] + [pltpu.make_async_copy(powers.at[slot], powers_h.at[s, heads], local.at[4, slot])]

        @pl.loop(0, 6)
        def _(t):
            g, s = t // 2, t % 2
            rows = pl.ds(pl.multiple_of(s * length, length), length)
            cols = pl.ds(pl.multiple_of(g * GROUP, GROUP), GROUP)

            @pl.when(t >= 2)
            def _():
                for c in outs(g, s, s):
                    c.wait()

            xs = tokens[rows, :]

            def weight(i):
                return w4[i, :, :, :, cols].reshape(width, GROUP)

            qkv[s, 0] = (dot(xs, weight(0)) + vec8[0:1, cols]).astype(BF16)
            qkv[s, 1] = dot(xs, weight(1)).astype(BF16)
            qkv[s, 2] = (dot(xs, weight(2)) + vec8[1:2, cols]).astype(BF16)
            key_rows = lax.broadcasted_iota(jnp.int32, (length, 1), 0)
            hidden_keys = jnp.where(key_rows < counts[s], 0.0, -1000000000.0)
            attend_step(
                hidden_keys, qkv.at[s, 0], qkv.at[s, 1], qkv.at[s, 2], powers.at[s],
                inverse.at[s, g], context_t.at[cols, rows],
            )
            for c in outs(g, s, s):
                c.start()

            @pl.when(t == 0)
            def _():
                q[1].turn()
                u[0].plane()

            @pl.when(t == 1)
            def _():
                q[1].rest()
                q[2].turn()
                q[1].ready()

            @pl.when(t == 2)
            def _():
                u[1].plane()

            @pl.when(t == 3)
            def _():
                q[2].rest()
                u[0].turn()
                q[2].ready()

            @pl.when(t == 4)
            def _():
                d[0].plane()

            @pl.when(t == 5)
            def _():
                u[0].rest()
                u[1].turn()

        for s in range(2):
            for c in outs(2, s, s):
                c.wait()

    pl.run_scoped(
        attention,
        pltpu.VMEM((2, 3, length, GROUP), BF16),
        pltpu.VMEM((2, 4, length, length), BF16),
    )

    def feed(act, pull, first_low, first_t, err_two, err_two_t, normal_one, resid_two, low_out, cotangent, part_d):
        v = [vec8[i : i + 1] for i in range(8)]
        out_bias, gain_one, shift_one, down_bias, gain_two, shift_two = v[2:]
        loads = [pltpu.make_async_copy(cotangent_h, cotangent, local.at[5, 0])]
        outs = [
            pltpu.make_async_copy(w4, w4_h, local.at[5, 1]),
            pltpu.make_async_copy(context_t, context_t_h, local.at[5, 2]),
        ]
        for c in loads + outs:
            c.start()

        def keep(source, target, slot):
            c = pltpu.make_async_copy(source, target, local.at[6 + slot // 4, slot % 4])
            c.start()
            outs.append(c)

        for s in range(2):
            rows = slice(s * length, (s + 1) * length)
            r1 = (
                tokens[rows, :].astype(F32)
                + dot(context_t[:, rows].T, w4[3].reshape(width, width))
                + out_bias
            )
            normal, inv = centre(r1)
            normal_one[rows, :] = normal
            inverse_one[rows, :] = inv
            low = (normal * gain_one + shift_one).astype(BF16)
            first_low[rows, :] = low
            first_t[:, rows] = low.T
            if s == 0:
                u[1].rest()
                d[1].plane()
                d[0].turn()
        keep(normal_one, normal_one_h, 0)
        keep(first_t, first_t_h, 1)
        u[0].ready()
        u[1].ready()
        keep(wu, wu_h, 2)
        for s in range(2):
            rows = slice(s * length, (s + 1) * length)

            @pl.loop(0, columns // CHUNK)
            def _(j):
                cols = pl.ds(pl.multiple_of(j * CHUNK, CHUNK), CHUNK)
                weight = wu[:, :, :, cols].reshape(width, CHUNK)
                hidden = dot(first_low[rows, :], weight) + up_row[:, cols]
                cdf, density = normal_parts(hidden)
                act[rows, cols] = (hidden * cdf).astype(BF16)
                pull[rows, cols] = (cdf + hidden * density).astype(BF16)

            if s == 0:
                d[0].rest()
                d[1].turn()
        keep(pull, pull_h, 3)
        d[1].rest()
        d[0].ready()
        d[1].ready()
        keep(wd, wd_h, 4)
        for c in loads:
            c.wait()
        for s in range(2):
            rows = slice(s * length, (s + 1) * length)
            first = normal_one[rows, :] * gain_one + shift_one
            second = dot(act[rows, :], wd[...].reshape(columns, width))
            normal, inv = centre(first + second + down_bias)
            live = lax.broadcasted_iota(jnp.int32, (length, 1), 0) < counts[s]
            low_out[rows, :] = jnp.where(live, normal * gain_two + shift_two, 0.0).astype(BF16)
            grad_y = jnp.where(live, cotangent[rows, :].astype(F32), 0.0)
            resid = pull_back(grad_y * gain_two, normal, inv)
            resid_two[rows, :] = resid
            low = resid.astype(BF16)
            err_two[rows, :] = low
            err_two_t[:, rows] = low.T
            note(sums, 6, grad_y * normal)
            note(sums, 7, grad_y)
            note(sums, 5, low.astype(F32))
        keep(low_out, layer_out_h, 5)
        keep(err_two, err_two_h, 6)
        keep(resid_two, resid_two_h, 7)

        @pl.loop(0, NX * NZ)
        def _(f):
            cols = pl.ds(pl.multiple_of(f * per, per), per)
            part_d[:, f // NX, f % NX] = (
                dot(err_two_t[...], act[:, cols]).astype(BF16).reshape(4, width // 4, per)
            )

        keep(part_d, part_d_h, 8)
        for c in outs:
            c.wait()
        for p in pieces:
            p.drain()
        for k in range(1, NX * NZ):
            vec_copy(k).wait_send()

    pl.run_scoped(
        feed,
        pltpu.VMEM((total, columns), BF16),
        pltpu.VMEM((total, columns), BF16),
        pltpu.VMEM((total, width), BF16),
        pltpu.VMEM((width, total), BF16),
        pltpu.VMEM((total, width), BF16),
        pltpu.VMEM((width, total), BF16),
        pltpu.VMEM((total, width), F32),
        pltpu.VMEM((total, width), F32),
        pltpu.VMEM((total, width), BF16),
        pltpu.VMEM((total, width), BF16),
        pltpu.VMEM((4, NZ, NX, width // 4, per), BF16),
    )


def forward(counts, rows, vec, cotangent, wq, wk, wv, wo, wu, wd):
    total, width = rows.shape
    columns = wu.shape[1]
    slots, length = 2, total // 2
    heads = width // HEAD_DIM
    per = columns // (NX * NZ)
    copies = 7 + 7 * (3 + 2 + 2 + 4)
    hbm, vmem = pl.BlockSpec(memory_space=pl.ANY), pl.BlockSpec(memory_space=pltpu.VMEM)
    w4_shape = (4, NZ, NX, ROWS, width)
    wu_shape = (NZ, NX, ROWS, columns)
    wd_shape = (NZ, NX, 4, ROWS, width)
    return pl.pallas_call(
        forward_kernel,
        name="forward",
        in_specs=[pl.BlockSpec(memory_space=pltpu.SMEM), vmem, vmem] + [hbm] * 7,
        out_specs=[hbm] * 15 + [vmem] * 4,
        out_shape=[
            Shape(w4_shape, BF16),
            Shape(wu_shape, BF16),
            Shape(wd_shape, BF16),
            Shape((total, width), BF16),
            Shape((total, width), BF16),
            Shape((total, width), BF16),
            Shape((total, width), BF16),
            Shape((slots, heads, length, length), BF16),
            Shape((width, total), BF16),
            Shape((width, total), BF16),
            Shape((total, width), BF16),
            Shape((total, width), F32),
            Shape((total, width), F32),
            Shape((total, columns), BF16),
            Shape((4, NZ, NX, width // 4, per), BF16),
            Shape((8, width), F32),
            Shape((slots, heads // 4, 4, length), F32),
            Shape((total, 1), F32),
            Shape((8, width), F32),
        ],
        scratch_shapes=[
            pltpu.VMEM(w4_shape, BF16),
            pltpu.VMEM(wu_shape, BF16),
            pltpu.VMEM(wd_shape, BF16),
            pltpu.VMEM((NX * NZ,) + vec.shape, F32),
            pltpu.VMEM((1, columns), F32),
            pltpu.VMEM((width, total), BF16),
            pltpu.SemaphoreType.DMA((copies,)),
            pltpu.SemaphoreType.DMA((copies,)),
            pltpu.SemaphoreType.DMA((9, 4)),
        ],
        compiler_params=params(collective_id=0, has_side_effects=True),
    )(counts, rows, vec, cotangent, wq, wk, wv, wo, wu, wd.reshape(4, ROWS, width))


class Chunk:
    def __init__(self, name, wire, where, part, mine, scratch):
        self.name, self.wire, self.where = name, wire, where
        self.part, self.mine = part, mine
        self.rc, self.bx, self.by, self.cx, self.cy, self.bz, self.fin = scratch

    @staticmethod
    def scratch(a, b):
        return [
            pltpu.VMEM((2, NZ, NX, a, b), BF16),
            pltpu.VMEM((2, 2, a, b), BF16),
            pltpu.VMEM((2, NX, a, b), BF16),
            pltpu.VMEM((2, a, b), BF16),
            pltpu.VMEM((2, a, b), BF16),
            pltpu.VMEM((NZ - 1, a, b), BF16),
            pltpu.VMEM((4, a, b), BF16),
        ]

    def copies(self, stage):
        x, y, z, core = self.where
        member, other = y * 2 + core, (1 - y) * 2 + core
        x_peer, y_peer = at(1 - x, y, z, core), at(x, 1 - y, z, core)
        c_peer = at(x, y, z, 1 - core)
        rc, fin = self.rc, self.fin
        if stage == "core":
            plan = [(self.part.at[yy * 2 + 1 - core], rc.at[yy], c_peer) for yy in range(2)]
        elif stage == "plane":
            plan = [
                (rc.at[:, pl.ds(0, 2), 1 - x], self.bx, x_peer),
                (rc.at[1 - y, pl.ds(2, 2)], self.by, y_peer),
            ]
        elif stage == "turn":
            plan = [
                (rc.at[1 - y, pl.ds(0, 2), x], self.cy, y_peer),
                (rc.at[y, pl.ds(2, 2), 1 - x], self.cx, x_peer),
            ]
        elif stage == "depth":
            plan = [
                (rc.at[y, (z + k) % NZ, x], self.bz.at[k - 1], at(x, y, (z + k) % NZ, core))
                for k in range(1, NZ)
            ]
        elif stage == "spread":
            plan = [(fin.at[member], fin.at[member], peer) for peer in (y_peer, c_peer)]
        else:
            plan = [(fin.at[other], fin.at[other], c_peer)]
        return [
            self.wire.copy((self.name, stage, i), source, target, peer)
            for i, (source, target, peer) in enumerate(plan)
        ]

    def start(self, stage):
        for c in self.copies(stage):
            c.start()

    def arrive(self, stage):
        for c in self.copies(stage):
            c.wait_recv()

    def chip(self):
        core = self.where[3]
        self.arrive("core")
        rc, mine = self.rc, self.mine
        for yy in range(2):

            @pl.loop(0, NZ)
            def _(zz):
                for xx in range(NX):
                    rc[yy, zz, xx] = rc[yy, zz, xx] + mine(yy, core, zz, xx)

        self.start("plane")

    def turn(self):
        x, y, z, core = self.where
        rc, bx, by = self.rc, self.bx, self.by
        self.arrive("plane")

        @pl.loop(0, 2)
        def _(zz):
            for i in range(2):
                rc[i, zz, x] = rc[i, zz, x] + bx[i, zz]
                rc[y, 2 + zz, i] = rc[y, 2 + zz, i] + by[zz, i]

        self.start("turn")

    def depth(self):
        x, y, z, core = self.where
        rc, cx, cy = self.rc, self.cx, self.cy
        self.arrive("turn")

        @pl.loop(0, 2)
        def _(zz):
            rc[y, zz, x] = rc[y, zz, x] + cy[zz]
            rc[y, 2 + zz, x] = rc[y, 2 + zz, x] + cx[zz]

        self.start("depth")

    def total(self):
        x, y, z, core = self.where
        self.arrive("depth")
        summed = self.rc[y, z, x].astype(F32)
        for k in range(NZ - 1):
            summed = summed + self.bz[k].astype(F32)
        self.fin[y * 2 + core] = summed.astype(BF16)
        self.start("spread")

    def relay(self):
        self.copies("spread")[0].wait_recv()
        self.start("relay")

    def done(self):
        self.copies("spread")[1].wait_recv()
        self.arrive("relay")

    def drain(self):
        for stage in ("core", "plane", "turn", "depth", "spread", "relay"):
            for c in self.copies(stage):
                c.wait_send()


def attend_back_step(query, keys, values, powers, inverse, context_t, grad, write):
    for pair in range(2):
        cols = slice(pair * 128, pair * 128 + 128)
        q2 = query[:, cols] * jnp.asarray(SCALE, BF16)
        k2, v2 = keys[:, cols], values[:, cols]
        grad_t = grad[:, cols].astype(F32).T
        product = grad_t * context_t[cols, :].astype(F32)
        k_t = k2.T
        inv = [inverse[pair * 2 + h : pair * 2 + h + 1] for h in range(2)]
        scaled_t = jnp.concatenate(
            [grad_t[:HEAD_DIM] * inv[0], grad_t[HEAD_DIM:] * inv[1]], 0
        ).astype(BF16)
        scaled = scaled_t.T
        dq, dk, dv = [], 0.0, 0.0
        for h in range(2):
            rows = slice(h * HEAD_DIM, (h + 1) * HEAD_DIM)
            inner = jnp.sum(product[rows], 0, keepdims=True) * inv[h]
            power = powers[pair * 2 + h]
            grad_probs = dot(keep_half(h, v2), scaled_t)
            grad_scores = (power.astype(F32) * (grad_probs - inner)).astype(BF16)
            dv = dv + dot(power, keep_half(h, scaled))
            dk = dk + dot(grad_scores, keep_half(h, q2))
            dq.append(dot(k_t[rows], grad_scores))
        write(0, cols, (jnp.concatenate(dq, 0) * SCALE).astype(BF16).T)
        write(1, cols, dk.astype(BF16))
        write(2, cols, dv.astype(BF16))


def backward_kernel(
    part_d, err_two_h, pull_h, wd_h, wu_h, resid_two_h, normal_one_h, inverse_one, first_t_h,
    query_h, keys_h, values_h, powers_h, inverse, context_t_h, tokens_h, w4_h, vec, sums_in,
    o4, ou, od, ov, input_grad,
    part_u, own_d, err_one, grad_context, grad_in, tokens_t, context_t, sums, sums_up,
    pv, va, vb, *rest,
):
    scratch, (send, recv, load) = rest[:35], rest[35:]
    where = x, y, z, core = place()
    shard, member = z * NX + x, y * 2 + core
    total, width = grad_in.shape
    length = total // 2
    columns = sums_up.shape[1]
    loops = columns // CHUNK
    wire = Wire(send, recv)

    def own_part(part):
        return lambda yy, core, zz, xx: part[yy * 2 + core, zz, xx]

    d = Chunk("d", wire, where, part_d, lambda yy, core, zz, xx: own_d[yy, zz, xx], scratch[:7])
    u = Chunk("u", wire, where, part_u, own_part(part_u), scratch[7:14])

    def block(j):
        return pl.ds(pl.multiple_of(j * CHUNK, CHUNK), CHUNK)

    own_loads = [
        pltpu.make_async_copy(part_d.at[yy * 2 + core], own_d.at[yy], load.at[0, yy])
        for yy in range(2)
    ]
    gain_one = vec[3:4].astype(F32)
    sums[...] = sums_in[...]
    sums_up[...] = jnp.zeros_like(sums_up)

    def feed_back(wd, wu, pull, err_two, normal_one, first_t, wo):
        first_loads = [
            pltpu.make_async_copy(err_two_h, err_two, load.at[1, 0]),
            pltpu.make_async_copy(resid_two_h, grad_in, load.at[1, 1]),
            pltpu.make_async_copy(normal_one_h, normal_one, load.at[1, 2]),
            pltpu.make_async_copy(w4_h.at[3], wo, load.at[1, 3]),
        ]
        late_loads = [
            pltpu.make_async_copy(first_t_h, first_t, load.at[2, 0]),
            pltpu.make_async_copy(context_t_h, context_t, load.at[2, 2]),
        ]

        def loads(j):
            return [
                pltpu.make_async_copy(wd_h.at[block(j)], wd.at[block(j)], load.at[3, j]),
                pltpu.make_async_copy(pull_h.at[:, block(j)], pull.at[:, block(j)], load.at[4, j]),
                pltpu.make_async_copy(wu_h.at[:, block(j)], wu.at[:, block(j)], load.at[5, j]),
            ]

        first_loads[0].start()
        for c in loads(0):
            c.start()
        for c in own_loads + first_loads[1:]:
            c.start()
        for j in range(1, loops):
            for c in loads(j):
                c.start()
        for c in late_loads:
            c.start()
        greet(all_peers())
        d.start("core")
        first_loads[0].wait()
        for s in range(2):
            rows = slice(s * length, (s + 1) * length)

            def down(j, acc):
                if s == 0:
                    for c in loads(j):
                        c.wait()

                    @pl.when(j == 1)
                    def _():
                        for c in own_loads:
                            c.wait()
                        d.chip()

                grads = dot_t(err_two[rows, :], wd[block(j), :])
                low = (grads * pull[rows, block(j)].astype(F32)).astype(BF16)
                pull[rows, block(j)] = low
                sums_up[:, block(j)] += jnp.sum(low.astype(F32), 0, keepdims=True)
                return acc + dot_t(low, wu[:, block(j)])

            grad_first = lax.fori_loop(0, loops, down, jnp.zeros((length, width), F32))
            if s == 0:
                for c in first_loads[1:]:
                    c.wait()
            grad_first = grad_first + grad_in[rows, :]
            normal = normal_one[rows, :]
            note(sums, 3, grad_first * normal)
            note(sums, 4, grad_first)
            resid = pull_back(grad_first * gain_one, normal, inverse_one[rows, :])
            grad_in[rows, :] = resid
            low = resid.astype(BF16)
            err_one[rows, :] = low
            note(sums, 2, low.astype(F32))
            grad_context[rows, :] = dot_t(low, wo[...]).astype(BF16)
        d.turn()
        for c in late_loads:
            c.wait()

        @pl.loop(0, 4)
        def _(m):
            cols = pl.ds(pl.multiple_of(m * width, width), width)
            part_u[m] = dot(first_t[...], pull[:, cols]).astype(BF16).reshape(part_u.shape[1:])

            @pl.when(m == 2)
            def _():
                d.depth()

        u.start("core")

    pl.run_scoped(
        feed_back,
        pltpu.VMEM((columns, width), BF16),
        pltpu.VMEM((width, columns), BF16),
        pltpu.VMEM((total, columns), BF16),
        pltpu.VMEM((total, width), BF16),
        pltpu.VMEM((total, width), F32),
        pltpu.VMEM((width, total), BF16),
        pltpu.VMEM((width, width), BF16),
    )

    def attend_and_inputs(qkv, powers, grads, weights, part_q, tokens):
        q = [
            Chunk(("q", g), wire, where, part_q.at[g], own_part(part_q.at[g]), scratch[14 + 7 * g : 21 + 7 * g])
            for g in range(3)
        ]
        def loads(g, s):
            rows, cols = pl.ds(pl.multiple_of(s * length, length), length), pl.ds(g * GROUP, GROUP)
            return [
                pltpu.make_async_copy(a.at[rows, cols], qkv.at[s, i], load.at[6 + i, s])
                for i, a in enumerate((query_h, keys_h, values_h))
            ] + [
                pltpu.make_async_copy(powers_h.at[s, pl.ds(g * 4, 4)], powers.at[s], load.at[9, s])
            ]

        weight_loads = [
            pltpu.make_async_copy(
                w4_h.at[i, :, pl.ds(g * GROUP, GROUP)],
                weights.at[g, :, pl.ds(i * GROUP, GROUP)],
                load.at[10 + g, i],
            )
            for g in range(3)
            for i in range(3)
        ]
        tokens_load = pltpu.make_async_copy(tokens_h, tokens, load.at[2, 1])
        for c in loads(0, 0) + [tokens_load] + weight_loads:
            c.start()
        for g in range(3):
            cols = slice(g * GROUP, (g + 1) * GROUP)

            @pl.loop(0, 2)
            def _(s):
                @pl.when(s == 0)
                def _():
                    for c in loads(g, 1):
                        c.start()

                if g < 2:

                    @pl.when(s == 1)
                    def _():
                        for c in loads(g + 1, 0):
                            c.start()

                for c in loads(g, s):
                    c.wait()
                rows = pl.ds(pl.multiple_of(s * length, length), length)

                def write(kind, pair, value):
                    lanes = slice(kind * GROUP + pair.start, kind * GROUP + pair.stop)
                    grads[g, rows, lanes] = value

                attend_back_step(
                    qkv.at[s, 0], qkv.at[s, 1], qkv.at[s, 2], powers.at[s],
                    inverse.at[s, g], context_t.at[cols, rows], grad_context.at[rows, cols], write,
                )

                @pl.when(s == 0)
                def _():
                    if g == 0:
                        u.chip()
                    elif g == 1:
                        d.total()
                        q[0].chip()
                    else:
                        q[1].chip()
                        q[0].turn()

            if g == 1:
                d.relay()
            if g == 0:
                tokens_load.wait()
                tokens_t[...] = tokens[...].T
            for i in range(3):
                lanes = slice(i * GROUP, (i + 1) * GROUP)
                part_q[g, i] = (
                    dot(tokens_t[...], grads[g, :, lanes])
                    .astype(BF16)
                    .reshape(NZ, NX, ROWS, GROUP)
                )
            part_q[g, 3] = (
                dot(context_t[...], err_one[:, cols]).astype(BF16).reshape(NZ, NX, ROWS, GROUP)
            )
            q[g].start("core")
            sums[0:1, cols] = jnp.sum(grads[g, :, :GROUP].astype(F32), 0, keepdims=True)
            sums[1:2, cols] = jnp.sum(grads[g, :, 2 * GROUP :].astype(F32), 0, keepdims=True)
            if g == 1:
                u.turn()
        u.depth()

        pv[...] = jnp.zeros_like(pv)
        lanes = lax.broadcasted_iota(jnp.int32, (width, NX * NZ * 128), 1)
        rows = lax.broadcasted_iota(jnp.int32, (width, NX * NZ * 128), 0)
        pick = (rows == (lanes // 128) * ROWS + lanes % 128) & (lanes % 128 < ROWS)
        spread8 = lax.dot_general(
            sums[...], pick.astype(F32), (((1,), (0,)), ((), ())),
            precision=lax.Precision.HIGHEST, preferred_element_type=F32,
        )
        per = columns // (NX * NZ)
        for f in range(NX * NZ):
            pv[f, 8:16, 0:128] = spread8[:, f * 128 : (f + 1) * 128]
            pv[f, 0:1, :] = sums_up[:, f * per : (f + 1) * per]

        def to_owner(k):
            to = (shard + k) % (NX * NZ)
            return wire.copy(("v", k), pv.at[to], va.at[k - 1], {"dp": member, "fsdp": to})

        for k in range(1, NX * NZ):
            to_owner(k).start()
        for c in weight_loads:
            c.wait()
        out = []
        for i in range(3):
            lanes = slice(i * GROUP, (i + 1) * GROUP)
            summed = grad_in[:, lanes]
            for g in range(3):
                summed = summed + dot_t(grads[g], weights[g, lanes, :])
            grad_in[:, lanes] = summed
            c = pltpu.make_async_copy(
                grad_in.at[:, lanes], input_grad.at[:, lanes], load.at[13, i]
            )
            c.start()
            out.append(c)
            if i == 0:
                q[2].chip()
            elif i == 1:
                q[1].turn()
                q[0].depth()

        for k in range(1, NX * NZ):
            to_owner(k).wait_recv()
        partial = pv[shard]
        for k in range(NX * NZ - 1):
            partial = partial + va[k]
        vb[member] = partial

        def to_member(i):
            dy, dc = ((0, 1), (1, 0), (1, 1))[i]
            peer = at(x, (y + dy) % 2, z, (core + dc) % 2)
            return wire.copy(("w", i), vb.at[member], vb.at[member], peer)

        for i in range(3):
            to_member(i).start()
        q[2].turn()
        q[1].depth()
        u.total()
        q[2].depth()
        q[0].total()
        u.relay()
        for i in range(3):
            to_member(i).wait_recv()
        ov[...] = (vb[0] + vb[1]) + (vb[2] + vb[3])
        d.done()
        per_d = d.fin.shape[1]
        for i in range(4):
            od[:, i * per_d : (i + 1) * per_d] = d.fin[i].astype(F32).T
        q[1].total()
        q[0].relay()
        u.done()
        for i in range(4):
            ou[:, i * width : (i + 1) * width] = u.fin[i].astype(F32)
        q[2].total()
        q[1].relay()
        q[0].done()
        q[2].relay()
        q[1].done()
        q[2].done()
        for g in range(3):
            for i in range(4):
                o4[i, :, g * GROUP : (g + 1) * GROUP] = q[g].fin[i].astype(F32)
        for c in out:
            c.wait()
        for c in [d, u] + q:
            c.drain()
        for k in range(1, NX * NZ):
            to_owner(k).wait_send()
        for i in range(3):
            to_member(i).wait_send()

    pl.run_scoped(
        attend_and_inputs,
        pltpu.VMEM((2, 3, length, GROUP), BF16),
        pltpu.VMEM((2, 4, length, length), BF16),
        pltpu.VMEM((3, total, width), BF16),
        pltpu.VMEM((3, width, width), BF16),
        pltpu.VMEM((3, 4, NZ, NX, ROWS, GROUP), BF16),
        pltpu.VMEM((total, width), BF16),
    )


def backward(
    part_d, err_two, pull, wd, wu, resid_two, normal_one, inverse_one, first_t,
    query, keys, values, powers, inverse, context_t, rows, w4, vec, sums_in,
):
    total, width = rows.shape
    columns = wu.shape[1]
    per = columns // (NX * NZ)
    hbm, vmem = pl.BlockSpec(memory_space=pl.ANY), pl.BlockSpec(memory_space=pltpu.VMEM)
    d_block, copies = part_d.shape[3:], 7 + 3 + 5 * (2 + 2 + 2 + 3 + 2 + 1)
    scratch = [
        pltpu.VMEM((4, NZ, NX, ROWS, width), BF16),
        pltpu.VMEM((2, NZ, NX) + d_block, BF16),
        pltpu.VMEM((total, width), BF16),
        pltpu.VMEM((total, width), BF16),
        pltpu.VMEM((total, width), F32),
        pltpu.VMEM((width, total), BF16),
        pltpu.VMEM((width, total), BF16),
        pltpu.VMEM((8, width), F32),
        pltpu.VMEM((1, columns), F32),
        pltpu.VMEM((NX * NZ, 16, per), F32),
        pltpu.VMEM((NX * NZ - 1, 16, per), F32),
        pltpu.VMEM((4, 16, per), F32),
    ]
    scratch += Chunk.scratch(*d_block) + Chunk.scratch(ROWS, width)
    scratch += Chunk.scratch(ROWS, GROUP) * 3
    scratch += [pltpu.SemaphoreType.DMA((copies,))] * 2 + [pltpu.SemaphoreType.DMA((14, 4))]
    return pl.pallas_call(
        backward_kernel,
        name="backward",
        in_specs=[hbm] * 7 + [vmem] + [hbm] * 5 + [vmem] + [hbm] * 3 + [vmem] * 2,
        out_specs=[vmem] * 4 + [hbm],
        out_shape=[
            Shape((4, ROWS, width), F32),
            Shape((ROWS, columns), F32),
            Shape((per, width), F32),
            Shape((16, per), F32),
            Shape((total, width), F32),
        ],
        scratch_shapes=scratch,
        compiler_params=params(collective_id=1, has_side_effects=True),
    )(
        part_d, err_two, pull, wd, wu, resid_two, normal_one, inverse_one, first_t,
        query, keys, values, powers, inverse, context_t, rows, w4, vec, sums_in,
    )


def fused_layer(
    tokens, counts, cotangent, query_weight, key_weight, value_weight, out_weight, query_bias,
    value_bias, out_bias, attention_gain, attention_shift, up_weight, up_bias, down_weight,
    down_bias, feed_gain, feed_shift,
):
    width = tokens.shape[2]
    shards = NX * NZ
    columns = up_weight.shape[1]
    rows = tokens.reshape(-1, width)
    per = columns // shards
    vec = jnp.stack(
        [query_bias, value_bias, out_bias, attention_gain, attention_shift, down_bias, feed_gain, feed_shift]
    )
    vec = jnp.concatenate(
        [jnp.pad(up_bias[None], ((0, 7), (0, 0))), jnp.pad(vec, ((0, 0), (0, per - ROWS)))], 0
    ).astype(F32)
    (
        w4, wu, wd, layer_out, query, keys, values, powers, context_t, first_t, err_two, resid_two,
        normal_one, pull, part_d, vec8, inverse, inverse_one, sums,
    ) = forward(
        counts, rows, vec, cotangent.reshape(-1, width), query_weight, key_weight, value_weight,
        out_weight, up_weight, down_weight,
    )
    o4, ou, od, ov, input_grad = backward(
        part_d, err_two, pull, wd.reshape(columns, width), wu.reshape(width, columns), resid_two,
        normal_one, inverse_one, first_t, query, keys, values, powers, inverse, context_t, rows,
        w4.reshape(4, width, width), vec8, sums,
    )
    v = [ov[8 + i, :ROWS] for i in range(8)]
    return (
        layer_out.reshape(tokens.shape),
        input_grad.reshape(tokens.shape),
        o4[0], o4[1], o4[2], o4[3],
        v[0], v[1], v[2], v[3], v[4],
        ou, ov[0], od, v[5], v[6], v[7],
    )


def exact_gelu(value):
    return jax.nn.gelu(value, approximate=False)


def norm_forward(resid, gain, shift):
    average = jnp.mean(resid, axis=-1, keepdims=True)
    centred = resid - average
    spread = jnp.mean(centred * centred, axis=-1, keepdims=True)
    inverse = lax.rsqrt(spread + epsilon)
    normal = centred * inverse
    return (normal * gain + shift, normal, inverse)


def norm_backward(grad_out, normal, inverse, gain):
    scaled = grad_out * gain
    first_mean = jnp.mean(scaled, axis=-1, keepdims=True)
    second_mean = jnp.mean(scaled * normal, axis=-1, keepdims=True)
    grad_resid = inverse * (scaled - first_mean - normal * second_mean)
    return (grad_resid, jnp.sum(grad_out * normal, 0), jnp.sum(grad_out, 0))


def linear(rows, weight):
    return jnp.dot(rows, weight, preferred_element_type=jnp.float32)


def linear_back(grads, weight):
    return lax.dot_general(
        grads, weight, (((1,), (1,)), ((), ())), preferred_element_type=jnp.float32
    )


def outer_sum(rows, grads):
    return lax.dot_general(
        rows, grads, (((0,), (0,)), ((), ())), preferred_element_type=jnp.float32
    )


def column_sum(grads):
    return jnp.sum(grads.astype(jnp.float32), 0)


def on_device(
    tokens,
    counts,
    cotangent,
    query_weight,
    key_weight,
    value_weight,
    out_weight,
    query_bias,
    value_bias,
    out_bias,
    attention_gain,
    attention_shift,
    up_weight,
    up_bias,
    down_weight,
    down_bias,
    feed_gain,
    feed_shift,
):
    slots, length, width = tokens.shape
    heads = width // HEAD_DIM
    factor = HEAD_DIM ** (-0.5)
    positions = jnp.arange(length, dtype=jnp.int32)

    def split_heads(value):
        return value.reshape(slots, length, heads, HEAD_DIM)

    def masked_scores(query, keys, count):
        raw = jnp.einsum("qhd,khd->hqk", query, keys, preferred_element_type=jnp.float32)
        live = positions < count
        return jnp.where(live[None, None, :], raw * factor, -1000000000.0)

    def attend_forward(block):
        query, keys, values, count = block
        scores = masked_scores(query, keys, count)
        highest = jnp.max(scores, axis=-1, keepdims=True)
        powers = jnp.exp(scores - highest)
        totals = jnp.sum(powers, axis=-1, keepdims=True)
        probs = (powers / totals).astype(jnp.bfloat16)
        context = jnp.einsum("hqk,khd->qhd", probs, values, preferred_element_type=jnp.float32)
        return (context.reshape(length, width), highest + jnp.log(totals))

    def attend_backward(block):
        query, keys, values, count, logsum, grad_context = block
        scores = masked_scores(query, keys, count)
        probs = jnp.exp(scores - logsum)
        probs_low = probs.astype(jnp.bfloat16)
        grad_probs = jnp.einsum(
            "qhd,khd->hqk", grad_context, values, preferred_element_type=jnp.float32
        )
        inner = jnp.sum(probs * grad_probs, axis=-1, keepdims=True)
        grad_scores = (probs * (grad_probs - inner) * factor).astype(jnp.bfloat16)
        grad_query = jnp.einsum(
            "hqk,khd->qhd", grad_scores, keys, preferred_element_type=jnp.float32
        )
        grad_keys = jnp.einsum(
            "hqk,qhd->khd", grad_scores, query, preferred_element_type=jnp.float32
        )
        grad_values = jnp.einsum(
            "hqk,qhd->khd", probs_low, grad_context, preferred_element_type=jnp.float32
        )
        return (
            grad_query.reshape(length, width).astype(jnp.bfloat16),
            grad_keys.reshape(length, width).astype(jnp.bfloat16),
            grad_values.reshape(length, width).astype(jnp.bfloat16),
        )

    attention_set = (
        lax.all_gather(query_weight, "fsdp", axis=0, tiled=True),
        lax.all_gather(key_weight, "fsdp", axis=0, tiled=True),
        lax.all_gather(value_weight, "fsdp", axis=0, tiled=True),
        lax.all_gather(out_weight, "fsdp", axis=0, tiled=True),
        lax.all_gather(query_bias, "fsdp", axis=0, tiled=True),
        lax.all_gather(value_bias, "fsdp", axis=0, tiled=True),
        lax.all_gather(out_bias, "fsdp", axis=0, tiled=True),
        lax.all_gather(attention_gain, "fsdp", axis=0, tiled=True),
        lax.all_gather(attention_shift, "fsdp", axis=0, tiled=True),
    )
    feed_set = (
        lax.all_gather(up_weight, "fsdp", axis=0, tiled=True),
        lax.all_gather(up_bias, "fsdp", axis=0, tiled=True),
        lax.all_gather(down_weight, "fsdp", axis=0, tiled=True),
        lax.all_gather(down_bias, "fsdp", axis=0, tiled=True),
        lax.all_gather(feed_gain, "fsdp", axis=0, tiled=True),
        lax.all_gather(feed_shift, "fsdp", axis=0, tiled=True),
    )
    whole_query, whole_key, whole_value, whole_out = (
        attention_set[0],
        attention_set[1],
        attention_set[2],
        attention_set[3],
    )
    whole_up, whole_down = (feed_set[0], feed_set[2])
    rows = tokens.reshape(-1, width)
    query = (linear(rows, whole_query) + attention_set[4].astype(jnp.float32)).astype(jnp.bfloat16)
    keys = linear(rows, whole_key).astype(jnp.bfloat16)
    values = (linear(rows, whole_value) + attention_set[5].astype(jnp.float32)).astype(jnp.bfloat16)
    context_rows, logsum = lax.map(
        attend_forward, (split_heads(query), split_heads(keys), split_heads(values), counts)
    )
    context = context_rows.reshape(-1, width).astype(jnp.bfloat16)
    branch = linear(context, whole_out) + attention_set[6].astype(jnp.float32)
    gain_one = attention_set[7].astype(jnp.float32)
    first, normal_one, inverse_one = norm_forward(
        rows.astype(jnp.float32) + branch, gain_one, attention_set[8].astype(jnp.float32)
    )
    first_low = first.astype(jnp.bfloat16)
    hidden = linear(first_low, whole_up) + feed_set[1].astype(jnp.float32)
    activated, gelu_pull = jax.vjp(exact_gelu, hidden)
    act_low = activated.astype(jnp.bfloat16)
    second = linear(act_low, whole_down) + feed_set[3].astype(jnp.float32)
    gain_two = feed_set[4].astype(jnp.float32)
    output, normal_two, inverse_two = norm_forward(
        first + second, gain_two, feed_set[5].astype(jnp.float32)
    )
    live = (positions[None, :] < counts[:, None]).reshape(-1, 1)
    layer_out = jnp.where(live, output, 0.0).astype(jnp.bfloat16).reshape(tokens.shape)
    back_feed = (
        lax.all_gather(up_weight, "fsdp", axis=0, tiled=True),
        lax.all_gather(down_weight, "fsdp", axis=0, tiled=True),
    )
    back_up, back_down = (back_feed[0], back_feed[1])
    grad_y = jnp.where(live, cotangent.reshape(-1, width).astype(jnp.float32), 0.0)
    resid_two, grad_feed_gain, grad_feed_shift = norm_backward(
        grad_y, normal_two, inverse_two, gain_two
    )
    err_two = resid_two.astype(jnp.bfloat16)
    grad_down_weight = outer_sum(act_low, err_two)
    grad_down_bias = column_sum(err_two)
    grad_act = linear_back(err_two, back_down)
    grad_hidden = gelu_pull(grad_act)[0].astype(jnp.bfloat16)
    grad_up_weight = outer_sum(first_low, grad_hidden)
    grad_up_bias = column_sum(grad_hidden)
    grad_first = resid_two + linear_back(grad_hidden, back_up)
    feed_shards = (
        lax.psum_scatter(
            grad_up_weight.astype(jnp.bfloat16), "fsdp", scatter_dimension=0, tiled=True
        ).astype(jnp.float32),
        lax.psum_scatter(
            grad_up_bias.astype(jnp.bfloat16), "fsdp", scatter_dimension=0, tiled=True
        ).astype(jnp.float32),
        lax.psum_scatter(
            grad_down_weight.astype(jnp.bfloat16), "fsdp", scatter_dimension=0, tiled=True
        ).astype(jnp.float32),
        lax.psum_scatter(
            grad_down_bias.astype(jnp.bfloat16), "fsdp", scatter_dimension=0, tiled=True
        ).astype(jnp.float32),
        lax.psum_scatter(
            grad_feed_gain.astype(jnp.bfloat16), "fsdp", scatter_dimension=0, tiled=True
        ).astype(jnp.float32),
        lax.psum_scatter(
            grad_feed_shift.astype(jnp.bfloat16), "fsdp", scatter_dimension=0, tiled=True
        ).astype(jnp.float32),
    )
    back_attention = (
        lax.all_gather(query_weight, "fsdp", axis=0, tiled=True),
        lax.all_gather(key_weight, "fsdp", axis=0, tiled=True),
        lax.all_gather(value_weight, "fsdp", axis=0, tiled=True),
        lax.all_gather(out_weight, "fsdp", axis=0, tiled=True),
    )
    back_query, back_key, back_value, back_out = (
        back_attention[0],
        back_attention[1],
        back_attention[2],
        back_attention[3],
    )
    resid_one, grad_attention_gain, grad_attention_shift = norm_backward(
        grad_first, normal_one, inverse_one, gain_one
    )
    err_one = resid_one.astype(jnp.bfloat16)
    grad_out_weight = outer_sum(context, err_one)
    grad_out_bias = column_sum(err_one)
    grad_context = linear_back(err_one, back_out).astype(jnp.bfloat16)
    grad_query, grad_keys, grad_values = lax.map(
        attend_backward,
        (
            split_heads(query),
            split_heads(keys),
            split_heads(values),
            counts,
            logsum,
            split_heads(grad_context),
        ),
    )
    grad_query = grad_query.reshape(-1, width)
    grad_keys = grad_keys.reshape(-1, width)
    grad_values = grad_values.reshape(-1, width)
    grad_query_weight = outer_sum(rows, grad_query)
    grad_key_weight = outer_sum(rows, grad_keys)
    grad_value_weight = outer_sum(rows, grad_values)
    grad_query_bias = column_sum(grad_query)
    grad_value_bias = column_sum(grad_values)
    input_grad = (
        resid_one
        + linear_back(grad_query, back_query)
        + linear_back(grad_keys, back_key)
        + linear_back(grad_values, back_value)
    )
    attention_shards = (
        lax.psum_scatter(
            grad_query_weight.astype(jnp.bfloat16), "fsdp", scatter_dimension=0, tiled=True
        ).astype(jnp.float32),
        lax.psum_scatter(
            grad_key_weight.astype(jnp.bfloat16), "fsdp", scatter_dimension=0, tiled=True
        ).astype(jnp.float32),
        lax.psum_scatter(
            grad_value_weight.astype(jnp.bfloat16), "fsdp", scatter_dimension=0, tiled=True
        ).astype(jnp.float32),
        lax.psum_scatter(
            grad_out_weight.astype(jnp.bfloat16), "fsdp", scatter_dimension=0, tiled=True
        ).astype(jnp.float32),
        lax.psum_scatter(
            grad_query_bias.astype(jnp.bfloat16), "fsdp", scatter_dimension=0, tiled=True
        ).astype(jnp.float32),
        lax.psum_scatter(
            grad_value_bias.astype(jnp.bfloat16), "fsdp", scatter_dimension=0, tiled=True
        ).astype(jnp.float32),
        lax.psum_scatter(
            grad_out_bias.astype(jnp.bfloat16), "fsdp", scatter_dimension=0, tiled=True
        ).astype(jnp.float32),
        lax.psum_scatter(
            grad_attention_gain.astype(jnp.bfloat16), "fsdp", scatter_dimension=0, tiled=True
        ).astype(jnp.float32),
        lax.psum_scatter(
            grad_attention_shift.astype(jnp.bfloat16), "fsdp", scatter_dimension=0, tiled=True
        ).astype(jnp.float32),
    )
    summed = lax.psum(
        (
            attention_shards[0],
            attention_shards[1],
            attention_shards[2],
            attention_shards[3],
            attention_shards[4],
            attention_shards[5],
            attention_shards[6],
            attention_shards[7],
            attention_shards[8],
            feed_shards[0],
            feed_shards[1],
            feed_shards[2],
            feed_shards[3],
            feed_shards[4],
            feed_shards[5],
        ),
        "dp",
    )
    return (
        layer_out,
        input_grad.reshape(tokens.shape),
        summed[0],
        summed[1],
        summed[2],
        summed[3],
        summed[4],
        summed[5],
        summed[6],
        summed[7],
        summed[8],
        summed[9],
        summed[10],
        summed[11],
        summed[12],
        summed[13],
        summed[14],
    )


def solution(mesh):
    small = mesh.shape["dp"] == 4 and mesh.shape["fsdp"] == NX * NZ
    return jax.shard_map(
        fused_layer if small else on_device,
        mesh=mesh,
        in_specs=(
            P(("dp", "fsdp"), None, None),
            P(("dp", "fsdp")),
            P(("dp", "fsdp"), None, None),
            P("fsdp", None),
            P("fsdp", None),
            P("fsdp", None),
            P("fsdp", None),
            P("fsdp"),
            P("fsdp"),
            P("fsdp"),
            P("fsdp"),
            P("fsdp"),
            P("fsdp", None),
            P("fsdp"),
            P("fsdp", None),
            P("fsdp"),
            P("fsdp"),
            P("fsdp"),
        ),
        out_specs=(
            P(("dp", "fsdp"), None, None),
            P(("dp", "fsdp"), None, None),
            P("fsdp", None),
            P("fsdp", None),
            P("fsdp", None),
            P("fsdp", None),
            P("fsdp"),
            P("fsdp"),
            P("fsdp"),
            P("fsdp"),
            P("fsdp"),
            P("fsdp", None),
            P("fsdp"),
            P("fsdp", None),
            P("fsdp"),
            P("fsdp"),
            P("fsdp"),
        ),
        check_vma=False,
    )
```

```python
import functools

import jax
import jax.numpy as jnp
from jax import lax
from jax.experimental import pallas as pl
from jax.experimental.pallas import tpu as pltpu
from jax.sharding import PartitionSpec as P

HEAD_DIM = 64
epsilon = 1e-05
F32 = jnp.float32
BF16 = jnp.bfloat16
MESH = pl.DeviceIdType.MESH
VMEM_LIMIT = 63 * 2**20
Shape = jax.ShapeDtypeStruct


def dot(left, right):
    return lax.dot_general(
        left, right, (((1,), (0,)), ((), ())), preferred_element_type=F32
    )


def dot_t(left, right):
    return lax.dot_general(
        left, right, (((1,), (1,)), ((), ())), preferred_element_type=F32
    )


def params(**extra):
    return pltpu.CompilerParams(vmem_limit_bytes=VMEM_LIMIT, **extra)


def whole(shape):
    return pl.BlockSpec(shape, lambda *_: (0,) * len(shape), pipeline_mode=pl.Buffered(1))


NX, NZ, ROWS = 2, 4, 96


def place():
    member = lax.axis_index("dp")
    shard = lax.axis_index("fsdp")
    return shard % NX, member // 2, shard // NX, member % 2


def at(x, y, z, core):
    return {"dp": y * 2 + core, "fsdp": z * NX + x}


def greet(peers):
    barrier = pltpu.get_barrier_semaphore()
    for peer in peers:
        pl.semaphore_signal(barrier, inc=1, device_id=peer, device_id_type=MESH)
    pl.semaphore_wait(barrier, len(peers))


def all_peers():
    x, y, z, core = place()
    near = [at(x, 1 - y, z, core), at(x, y, z, 1 - core)]
    for step in range(1, NX * NZ):
        near.append({"dp": y * 2 + core, "fsdp": (z * NX + x + step) % (NX * NZ)})
    return near


class Wire:
    def __init__(self, send, recv):
        self.send, self.recv, self.slots = send, recv, {}

    def copy(self, key, source, target, peer):
        slot = self.slots.setdefault(key, len(self.slots))
        return pltpu.make_async_remote_copy(
            src_ref=source,
            dst_ref=target,
            send_sem=self.send.at[slot],
            recv_sem=self.recv.at[slot],
            device_id=peer,
            device_id_type=MESH,
        )


QKV_PIECES = ((0, 1), (1, 1), (2, 2), (4, 2))
OWN_LOADED = 3
FORWARD_PLAN = {
    "start": ("q1.plane", "q0.turn_y", "q0.turn_x", "q1.turn_y", "q1.turn_x", "q2.plane", "q0.rest", "q0.ready",),
    ("before", 2): ("q1.ready",),
    ("before", 4): ("u0.plane", "q3.turn_y", "q3.turn_x", "q2.rest", "q2.ready",),
    ("before", 8): ("q3.ready",),
    ("attend", 0): ("q1.rest",),
    ("attend", 1): ("q3.plane",),
    ("attend", 2): ("q2.turn_x", "q2.turn_y",),
    ("attend", 5): ("u1.plane",),
    ("attend", 6): ("u0.turn_x", "u0.turn_y",),
    ("attend", 7): ("q3.rest",),
    ("attend", 8): ("d0.plane",),
    ("attend", 10): ("u1.turn_x", "u1.turn_y",),
    ("attend", 11): ("d1.plane",),
    ("norm", 0): ("u0.rest",),
    "up ready": ("d0.turn_y", "d0.turn_x", "u1.rest", "u0.ready", "u1.ready",),
    ("up", 2): ("d1.turn_x", "d1.turn_y",),
    ("up", 3): ("d0.rest",),
    ("up", 5): ("d1.rest",),
    "down ready": ("d0.ready", "d1.ready",),
}
BACKWARD_PLAN = {
    ("hidden", 3): ("d.chip",),
    ("first", 0): ("d.turn_y", "d.turn_x",),
    ("norm", 0): ("u.chip",),
    ("norm", 1): ("d.depth",),
    ("attend", 5): ("q0.chip", "u.turn_y", "u.turn_x",),
    ("attend", 10): ("q1.chip",),
    ("attend", 11): ("u.depth",),
    ("inputs", 0): ("q1.turn_y", "q2.chip", "q3.chip", "d.relay",),
    ("weights", 1): ("q0.turn_y", "q0.turn_x", "d.total",),
    ("weights", 2): ("q0.depth",),
    ("inputs", 2): ("q1.turn_x", "q2.turn_y",),
    "drain one": ("q3.turn_y", "q2.turn_x", "q1.depth", "q3.turn_x",),
    "drain two": ("u.total", "q2.depth", "q3.depth", "q0.total", "u.relay",),
    "drain three": ("q0.relay", "q1.total", "q2.total", "q1.relay", "q2.relay", "q3.total", "q3.relay",),
}


GROUP = 4 * HEAD_DIM
PAIR = 2 * HEAD_DIM
SCALE = HEAD_DIM**-0.5
CHUNK = 1024


def run_events(pieces, events):
    for event in events:
        name, stage = event.split(".")
        getattr(pieces[name], stage)()


def run_at(pieces, plan, prefix, index, count):
    for k in range(count):
        if (prefix, k) in plan:

            @pl.when(index == k)
            def _():
                run_events(pieces, plan[prefix, k])


class Piece:
    def __init__(self, name, wire, where, block):
        self.name, self.wire, self.where, self.block = name, wire, where, block

    def copy(self, key, source, peer):
        return self.wire.copy((self.name, key), source, source, peer)

    def copies(self, stage):
        x, y, z, core = self.where
        member, other = y * 2 + core, (1 - y) * 2 + core
        x_peer, y_peer = at(1 - x, y, z, core), at(x, 1 - y, z, core)
        c_peer = at(x, y, z, 1 - core)
        every, block = slice(None), self.block
        if stage == "depth":
            mine = block(member, z, x)
            plan = [(mine, at(x, y, (z + k) % NZ, core)) for k in range(1, NZ)]
        elif stage == "plane":
            mine = block(member, every, x)
            plan = [(mine, x_peer), (mine, y_peer)]
        elif stage == "turn":
            plan = [
                (block(other, pl.ds(0, 2), x), x_peer),
                (block(member, pl.ds(2, 2), 1 - x), y_peer),
            ]
        else:
            plan = [
                (block(member, every, x), c_peer),
                (block(other, every, x), c_peer),
                (block(member, every, 1 - x), c_peer),
                (block(other, every, 1 - x), c_peer),
            ]
        return [self.copy((stage, i), source, peer) for i, (source, peer) in enumerate(plan)]

    def send(self):
        for c in self.copies("depth"):
            c.start()

    def plane(self):
        for c in self.copies("depth"):
            c.wait_recv()
        for c in self.copies("plane"):
            c.start()
        self.copies("core")[0].start()

    def turn_x(self):
        self.copies("plane")[1].wait_recv()
        self.copies("turn")[0].start()
        self.copies("core")[1].start()

    def turn_y(self):
        self.copies("plane")[0].wait_recv()
        self.copies("turn")[1].start()
        self.copies("core")[2].start()

    def rest(self):
        for c in self.copies("turn"):
            c.wait_recv()
        self.copies("core")[3].start()

    def ready(self):
        for c in self.copies("core"):
            c.wait_recv()

    def drain(self):
        for stage in ("depth", "plane", "turn", "core"):
            for c in self.copies(stage):
                c.wait_send()


def half(index, shape):
    lanes = lax.broadcasted_iota(jnp.int32, shape, 1)
    return lanes < HEAD_DIM if index == 0 else lanes >= HEAD_DIM


def keep_half(index, value):
    return jnp.where(half(index, value.shape), value, jnp.zeros_like(value))


def attend_step(hidden_keys, q, k, v, powers, inverse, context_t):
    scaled, v_t = q * jnp.asarray(SCALE, BF16), v.T
    for h in range(2):
        rows = slice(h * HEAD_DIM, (h + 1) * HEAD_DIM)
        scores = dot_t(keep_half(h, k), scaled) + hidden_keys
        highest = jnp.max(scores, 0, keepdims=True)
        power = jnp.exp(scores - highest)
        inv = 1.0 / jnp.sum(power, 0, keepdims=True)
        low = power.astype(BF16)
        powers[h] = low
        inverse[h : h + 1] = inv
        context_t[rows] = (dot(v_t[rows], low) * inv).astype(BF16)


SQRT_HALF = 0.7071067811865476
PDF_SCALE = 0.3989422804014327


def normal_parts(value):
    z = jnp.abs(value) * SQRT_HALF
    t = 1.0 / (1.0 + 0.3275911 * z)
    bell = jnp.exp(-(z * z))
    poly = 1.061405429 * t - 1.453152027
    poly = poly * t + 1.421413741
    poly = poly * t - 0.284496736
    poly = poly * t + 0.254829592
    tail = (0.5 * poly * t) * bell
    return jnp.where(value >= 0, 1.0 - tail, tail), bell * PDF_SCALE


def centre(resid):
    centred = resid - jnp.mean(resid, 1, keepdims=True)
    inv = lax.rsqrt(jnp.mean(centred * centred, 1, keepdims=True) + epsilon)
    return centred * inv, inv


def pull_back(scaled, normal, inv):
    return inv * (
        scaled
        - jnp.mean(scaled, 1, keepdims=True)
        - normal * jnp.mean(scaled * normal, 1, keepdims=True)
    )


def note(sums, row, value):
    sums[row : row + 1] += jnp.sum(value, 0, keepdims=True)


def forward_kernel(
    counts, tokens, qb, vb, ob, ag, ash, db, fg, fsh, ub, cotangent_h, wq, wk, wv, wo, wu_i, wd_i,
    w4_h, wu_h, wd_h, layer_out_h, query_h, keys_h, values_h, powers_h, context_t_h, first_t_h,
    err_two_h, resid_two_h, normal_one_h, pull_h, part_d_h, vec8, inverse, inverse_one, sums,
    w4, wu, wd, gv, up_row, context_t, send, recv, local,
):
    where = x, y, z, core = place()
    shard, member = z * NX + x, y * 2 + core
    total, width = tokens.shape
    length = total // 2
    columns = up_row.shape[1]
    wire = Wire(send, recv)

    def columns_of(first, pairs):
        return lambda who, zs, xs: w4.at[who, zs, xs, :, pl.ds(first * PAIR, pairs * PAIR)]

    def up_part(i):
        part = width // 2
        return lambda who, zs, xs: wu.at[
            zs, xs, :, pl.ds(pl.multiple_of(who * width + i * part, part), part)
        ]

    def down_part(i):
        part = ROWS // 2
        return lambda who, zs, xs: wd.at[zs, xs, who, pl.ds(i * part, part)]

    pieces = {
        f"q{i}": Piece(f"q{i}", wire, where, columns_of(first, pairs))
        for i, (first, pairs) in enumerate(QKV_PIECES)
    }
    for i in range(2):
        pieces[f"u{i}"] = Piece(f"u{i}", wire, where, up_part(i))
    for i in range(2):
        pieces[f"d{i}"] = Piece(f"d{i}", wire, where, down_part(i))

    own = [
        pltpu.make_async_copy(wq, w4.at[member, z, x], local.at[0, 0]),
        pltpu.make_async_copy(
            wu_i.at[:, pl.ds(pl.multiple_of(member * width, width), width)],
            wu.at[z, x, :, pl.ds(pl.multiple_of(member * width, width), width)],
            local.at[0, 1],
        ),
        pltpu.make_async_copy(wd_i.at[member], wd.at[z, x, member], local.at[0, 2]),
    ]
    for i, w in enumerate((wq, wk, wv, wo)):

        @pl.when(member == i)
        def _():
            pltpu.make_async_copy(w, w4.at[i, z, x], local.at[0, 0]).start()

    for c in own[1:]:
        c.start()
    gv[shard] = jnp.zeros(gv.shape[1:], F32)
    gv[shard, 0:1, :] = ub[...].astype(F32).reshape(1, gv.shape[2])
    for i, vector in enumerate((qb, vb, ob, ag, ash, db, fg, fsh)):
        gv[shard, 8 + i : 9 + i, 0:ROWS] = vector[...].astype(F32).reshape(1, ROWS)
    greet(all_peers())
    for c in own:
        c.wait()

    def vec_copy(k):
        peer = {"dp": member, "fsdp": (shard + k) % (NX * NZ)}
        return wire.copy(("v", k), gv.at[shard], gv.at[shard], peer)

    for k in range(1, NX * NZ):
        vec_copy(k).start()
    for p in pieces.values():
        p.send()
    sums[...] = jnp.zeros_like(sums)
    pieces["q0"].plane()
    for k in range(1, NX * NZ):
        vec_copy(k).wait_recv()
    lanes = lax.broadcasted_iota(jnp.int32, (128, width), 0)
    features = lax.broadcasted_iota(jnp.int32, (128, width), 1)
    per = columns // (NX * NZ)
    joined = jnp.zeros((8, width), F32)
    for f in range(NX * NZ):
        pick = (features == f * ROWS + lanes) & (lanes < ROWS)
        joined = joined + dot(gv[f, 8:16, 0:128].astype(BF16), pick.astype(F32).astype(BF16))
        up_row[:, f * per : (f + 1) * per] = gv[f, 0:1, :]
    vec8[...] = joined
    run_events(pieces, FORWARD_PLAN["start"])

    def attention(qkv, powers):
        def outs(pair, s):
            rows = pl.ds(pl.multiple_of(s * length, length), length)
            cols = pl.ds(pl.multiple_of(pair * PAIR, PAIR), PAIR)
            return [
                pltpu.make_async_copy(qkv.at[s, i], a.at[rows, cols], local.at[1 + i, s])
                for i, a in enumerate((query_h, keys_h, values_h))
            ] + [
                pltpu.make_async_copy(
                    powers.at[s], powers_h.at[s, pl.ds(pair * 2, 2)], local.at[4, s]
                )
            ]

        @pl.loop(0, 12)
        def _(t):
            pair, s = t // 2, t % 2
            rows = pl.ds(pl.multiple_of(s * length, length), length)
            cols = pl.ds(pl.multiple_of(pair * PAIR, PAIR), PAIR)
            run_at(pieces, FORWARD_PLAN, "before", t, 12)

            @pl.when(t >= 2)
            def _():
                for c in outs(pair, s):
                    c.wait()

            weights = jnp.concatenate(
                [w4[i, :, :, :, cols].reshape(width, PAIR) for i in range(3)], 1
            )
            together = dot(tokens[rows, :], weights)
            q = (together[:, :PAIR] + vec8[0:1, cols]).astype(BF16)
            k = together[:, PAIR : 2 * PAIR].astype(BF16)
            v = (together[:, 2 * PAIR :] + vec8[1:2, cols]).astype(BF16)
            qkv[s, 0], qkv[s, 1], qkv[s, 2] = q, k, v
            key_rows = lax.broadcasted_iota(jnp.int32, (length, 1), 0)
            hidden_keys = jnp.where(key_rows < counts[s], 0.0, -1000000000.0)
            attend_step(
                hidden_keys, q, k, v, powers.at[s], inverse.at[s, pair], context_t.at[cols, rows]
            )
            for c in outs(pair, s):
                c.start()
            run_at(pieces, FORWARD_PLAN, "attend", t, 12)

        for s in range(2):
            for c in outs(5, s):
                c.wait()

    pl.run_scoped(
        attention,
        pltpu.VMEM((2, 3, length, PAIR), BF16),
        pltpu.VMEM((2, 2, length, length), BF16),
    )

    def feed(act, pull, first_low, first_t, err_two, err_two_t, normal_one, resid_two, low_out, cotangent, part_d):
        v = [vec8[i : i + 1] for i in range(8)]
        out_bias, gain_one, shift_one, down_bias, gain_two, shift_two = v[2:]
        loads = [pltpu.make_async_copy(cotangent_h, cotangent, local.at[5, 0])]
        outs = [
            pltpu.make_async_copy(w4, w4_h, local.at[5, 1]),
            pltpu.make_async_copy(context_t, context_t_h, local.at[5, 2]),
        ]
        for c in loads + outs:
            c.start()

        def keep(source, target, slot):
            c = pltpu.make_async_copy(source, target, local.at[6 + slot // 4, slot % 4])
            c.start()
            outs.append(c)

        def rows_of(s):
            return pl.ds(pl.multiple_of(s * length, length), length)

        @pl.loop(0, 2)
        def _(s):
            rows = rows_of(s)
            r1 = (
                tokens[rows, :].astype(F32)
                + dot(context_t[:, rows].T, w4[3].reshape(width, width))
                + out_bias
            )
            normal, inv = centre(r1)
            normal_one[rows, :] = normal
            inverse_one[rows, :] = inv
            low = (normal * gain_one + shift_one).astype(BF16)
            first_low[rows, :] = low
            first_t[:, rows] = low.T
            run_at(pieces, FORWARD_PLAN, "norm", s, 2)

        keep(normal_one, normal_one_h, 0)
        keep(first_t, first_t_h, 1)
        run_events(pieces, FORWARD_PLAN["up ready"])
        keep(wu, wu_h, 2)
        loops = columns // CHUNK

        @pl.loop(0, 2 * loops)
        def _(t):
            rows = rows_of(t // loops)
            cols = pl.ds(pl.multiple_of((t % loops) * CHUNK, CHUNK), CHUNK)
            weight = wu[:, :, :, cols].reshape(width, CHUNK)
            hidden = dot(first_low[rows, :], weight) + up_row[:, cols]
            cdf, density = normal_parts(hidden)
            act[rows, cols] = (hidden * cdf).astype(BF16)
            pull[rows, cols] = (cdf + hidden * density).astype(BF16)
            run_at(pieces, FORWARD_PLAN, "up", t, 2 * loops)

        keep(pull, pull_h, 3)
        run_events(pieces, FORWARD_PLAN["down ready"])
        keep(wd, wd_h, 4)
        for c in loads:
            c.wait()

        @pl.loop(0, 2)
        def _(s):
            rows = rows_of(s)
            first = normal_one[rows, :] * gain_one + shift_one
            second = dot(act[rows, :], wd[...].reshape(columns, width))
            normal, inv = centre(first + second + down_bias)
            live = lax.broadcasted_iota(jnp.int32, (length, 1), 0) < counts[s]
            low_out[rows, :] = jnp.where(live, normal * gain_two + shift_two, 0.0).astype(BF16)
            grad_y = jnp.where(live, cotangent[rows, :].astype(F32), 0.0)
            resid = pull_back(grad_y * gain_two, normal, inv)
            resid_two[rows, :] = resid
            low = resid.astype(BF16)
            err_two[rows, :] = low
            err_two_t[:, rows] = low.T
            note(sums, 6, grad_y * normal)
            note(sums, 7, grad_y)
            note(sums, 5, low.astype(F32))

        keep(low_out, layer_out_h, 5)
        keep(err_two, err_two_h, 6)
        keep(resid_two, resid_two_h, 7)

        @pl.loop(0, NX * NZ)
        def _(f):
            cols = pl.ds(pl.multiple_of(f * per, per), per)
            part_d[:, f // NX, f % NX] = (
                dot(err_two_t[...], act[:, cols]).astype(BF16).reshape(4, width // 4, per)
            )

        keep(part_d, part_d_h, 8)
        for c in outs:
            c.wait()
        for p in pieces.values():
            p.drain()
        for k in range(1, NX * NZ):
            vec_copy(k).wait_send()

    pl.run_scoped(
        feed,
        pltpu.VMEM((total, columns), BF16),
        pltpu.VMEM((total, columns), BF16),
        pltpu.VMEM((total, width), BF16),
        pltpu.VMEM((width, total), BF16),
        pltpu.VMEM((total, width), BF16),
        pltpu.VMEM((width, total), BF16),
        pltpu.VMEM((total, width), F32),
        pltpu.VMEM((total, width), F32),
        pltpu.VMEM((total, width), BF16),
        pltpu.VMEM((total, width), BF16),
        pltpu.VMEM((4, NZ, NX, width // 4, per), BF16),
    )


def forward(counts, rows, vectors, cotangent, wq, wk, wv, wo, wu, wd):
    total, width = rows.shape
    columns = wu.shape[1]
    slots, length = 2, total // 2
    heads = width // HEAD_DIM
    per = columns // (NX * NZ)
    copies = 7 + (len(QKV_PIECES) + 4) * (3 + 2 + 2 + 4)
    hbm, vmem = pl.BlockSpec(memory_space=pl.ANY), pl.BlockSpec(memory_space=pltpu.VMEM)
    w4_shape = (4, NZ, NX, ROWS, width)
    wu_shape = (NZ, NX, ROWS, columns)
    wd_shape = (NZ, NX, 4, ROWS, width)
    return pl.pallas_call(
        forward_kernel,
        name="forward",
        in_specs=[pl.BlockSpec(memory_space=pltpu.SMEM)] + [vmem] * 10 + [hbm] * 7,
        out_specs=[hbm] * 15 + [vmem] * 4,
        out_shape=[
            Shape(w4_shape, BF16),
            Shape(wu_shape, BF16),
            Shape(wd_shape, BF16),
            Shape((total, width), BF16),
            Shape((total, width), BF16),
            Shape((total, width), BF16),
            Shape((total, width), BF16),
            Shape((slots, heads, length, length), BF16),
            Shape((width, total), BF16),
            Shape((width, total), BF16),
            Shape((total, width), BF16),
            Shape((total, width), F32),
            Shape((total, width), F32),
            Shape((total, columns), BF16),
            Shape((4, NZ, NX, width // 4, per), BF16),
            Shape((8, width), F32),
            Shape((slots, heads // 2, 2, length), F32),
            Shape((total, 1), F32),
            Shape((8, width), F32),
        ],
        scratch_shapes=[
            pltpu.VMEM(w4_shape, BF16),
            pltpu.VMEM(wu_shape, BF16),
            pltpu.VMEM(wd_shape, BF16),
            pltpu.VMEM((NX * NZ, 16, per), F32),
            pltpu.VMEM((1, columns), F32),
            pltpu.VMEM((width, total), BF16),
            pltpu.SemaphoreType.DMA((copies,)),
            pltpu.SemaphoreType.DMA((copies,)),
            pltpu.SemaphoreType.DMA((9, 4)),
        ],
        compiler_params=params(collective_id=0, has_side_effects=True),
    )(counts, rows, *vectors, cotangent, wq, wk, wv, wo, wu, wd.reshape(4, ROWS, width))


class Chunk:
    def __init__(self, name, wire, where, part, mine, scratch):
        self.name, self.wire, self.where = name, wire, where
        self.part, self.mine = part, mine
        self.rc, self.bx, self.by, self.cx, self.cy, self.bz, self.fin = scratch

    @staticmethod
    def scratch(a, b):
        return [
            pltpu.VMEM((2, NZ, NX, a, b), BF16),
            pltpu.VMEM((2, 2, a, b), BF16),
            pltpu.VMEM((2, NX, a, b), BF16),
            pltpu.VMEM((2, a, b), BF16),
            pltpu.VMEM((2, a, b), BF16),
            pltpu.VMEM((NZ - 1, a, b), BF16),
            pltpu.VMEM((4, a, b), BF16),
        ]

    def copies(self, stage):
        x, y, z, core = self.where
        member, other = y * 2 + core, (1 - y) * 2 + core
        x_peer, y_peer = at(1 - x, y, z, core), at(x, 1 - y, z, core)
        c_peer = at(x, y, z, 1 - core)
        rc, fin = self.rc, self.fin
        if stage == "core":
            plan = [(self.part.at[yy * 2 + 1 - core], rc.at[yy], c_peer) for yy in range(2)]
        elif stage == "plane":
            plan = [
                (rc.at[:, pl.ds(0, 2), 1 - x], self.bx, x_peer),
                (rc.at[1 - y, pl.ds(2, 2)], self.by, y_peer),
            ]
        elif stage == "turn":
            plan = [
                (rc.at[1 - y, pl.ds(0, 2), x], self.cy, y_peer),
                (rc.at[y, pl.ds(2, 2), 1 - x], self.cx, x_peer),
            ]
        elif stage == "depth":
            plan = [
                (rc.at[y, (z + k) % NZ, x], self.bz.at[k - 1], at(x, y, (z + k) % NZ, core))
                for k in range(1, NZ)
            ]
        elif stage == "spread":
            plan = [(fin.at[member], fin.at[member], peer) for peer in (y_peer, c_peer)]
        else:
            plan = [(fin.at[other], fin.at[other], c_peer)]
        return [
            self.wire.copy((self.name, stage, i), source, target, peer)
            for i, (source, target, peer) in enumerate(plan)
        ]

    def start(self, stage):
        for c in self.copies(stage):
            c.start()

    def arrive(self, stage):
        for c in self.copies(stage):
            c.wait_recv()

    def chip(self):
        core = self.where[3]
        self.arrive("core")
        rc, mine = self.rc, self.mine
        for yy in range(2):

            @pl.loop(0, NZ)
            def _(zz):
                for xx in range(NX):
                    rc[yy, zz, xx] = rc[yy, zz, xx] + mine(yy, core, zz, xx)

        self.start("plane")

    def turn_y(self):
        x, y, z, core = self.where
        rc, bx = self.rc, self.bx
        self.copies("plane")[0].wait_recv()

        @pl.loop(0, 2)
        def _(zz):
            for yy in range(2):
                rc[yy, zz, x] = rc[yy, zz, x] + bx[yy, zz]

        self.copies("turn")[0].start()

    def turn_x(self):
        x, y, z, core = self.where
        rc, by = self.rc, self.by
        self.copies("plane")[1].wait_recv()

        @pl.loop(0, 2)
        def _(zz):
            for xx in range(NX):
                rc[y, 2 + zz, xx] = rc[y, 2 + zz, xx] + by[zz, xx]

        self.copies("turn")[1].start()

    def depth(self):
        x, y, z, core = self.where
        rc, cx, cy = self.rc, self.cx, self.cy
        self.arrive("turn")

        @pl.loop(0, 2)
        def _(zz):
            rc[y, zz, x] = rc[y, zz, x] + cy[zz]
            rc[y, 2 + zz, x] = rc[y, 2 + zz, x] + cx[zz]

        self.start("depth")

    def total(self):
        x, y, z, core = self.where
        self.arrive("depth")
        summed = self.rc[y, z, x].astype(F32)
        for k in range(NZ - 1):
            summed = summed + self.bz[k].astype(F32)
        self.fin[y * 2 + core] = summed.astype(BF16)
        self.start("spread")

    def relay(self):
        self.copies("spread")[0].wait_recv()
        self.start("relay")

    def done(self):
        self.copies("spread")[1].wait_recv()
        self.arrive("relay")

    def drain(self):
        for stage in ("core", "plane", "turn", "depth", "spread", "relay"):
            for c in self.copies(stage):
                c.wait_send()


def attend_back_step(query, keys, values, powers, inverse, context_t, grad):
    q2 = query[...] * jnp.asarray(SCALE, BF16)
    k2, v2 = keys[...], values[...]
    grad_t = grad[...].astype(F32).T
    product = grad_t * context_t[...].astype(F32)
    k_t = k2.T
    inv = [inverse[h : h + 1] for h in range(2)]
    scaled_t = jnp.concatenate([grad_t[:HEAD_DIM] * inv[0], grad_t[HEAD_DIM:] * inv[1]], 0).astype(
        BF16
    )
    scaled = scaled_t.T
    dq, dk, dv = [], 0.0, 0.0
    for h in range(2):
        rows = slice(h * HEAD_DIM, (h + 1) * HEAD_DIM)
        inner = jnp.sum(product[rows], 0, keepdims=True) * inv[h]
        power = powers[h]
        grad_probs = dot(keep_half(h, v2), scaled_t)
        grad_scores = (power.astype(F32) * (grad_probs - inner)).astype(BF16)
        dv = dv + dot(power, keep_half(h, scaled))
        dk = dk + dot(grad_scores, keep_half(h, q2))
        dq.append(dot(k_t[rows], grad_scores))
    return (jnp.concatenate(dq, 0) * SCALE).astype(BF16).T, dk.astype(BF16), dv.astype(BF16)


def backward_kernel(
    part_d, err_two_h, pull_h, wd_h, wu_h, resid_two_h, normal_one_h, inverse_one, first_t_h,
    query_h, keys_h, values_h, powers_h, inverse, context_t_h, tokens_h, w4_h, vec, sums_in,
    o4, ou, od, ov, input_grad,
    part_u, own_d, err_one, grad_context, grad_in, tokens_t, context_t, sums, sums_up,
    pv, va, vb, *rest,
):
    scratch, (send, recv, load) = rest[:42], rest[42:]
    where = x, y, z, core = place()
    shard, member = z * NX + x, y * 2 + core
    total, width = grad_in.shape
    length = total // 2
    columns = sums_up.shape[1]
    loops = columns // CHUNK
    wire = Wire(send, recv)

    def own_part(part):
        return lambda yy, core, zz, xx: part[yy * 2 + core, zz, xx]

    d = Chunk("d", wire, where, part_d, lambda yy, core, zz, xx: own_d[yy, zz, xx], scratch[:7])
    u = Chunk("u", wire, where, part_u, own_part(part_u), scratch[7:14])

    chunks = {"d": d, "u": u}

    def rows_of(s):
        return pl.ds(pl.multiple_of(s * length, length), length)

    def block(j):
        return pl.ds(pl.multiple_of(j * CHUNK, CHUNK), CHUNK)

    own_loads = [
        pltpu.make_async_copy(part_d.at[yy * 2 + core], own_d.at[yy], load.at[0, yy])
        for yy in range(2)
    ]
    gain_one = vec[3:4].astype(F32)
    sums[...] = sums_in[...]
    sums_up[...] = jnp.zeros_like(sums_up)

    def feed_back(wd, wu, pull, err_two, normal_one, first_t, wo):
        first_loads = [
            pltpu.make_async_copy(err_two_h, err_two, load.at[1, 0]),
            pltpu.make_async_copy(resid_two_h, grad_in, load.at[1, 1]),
            pltpu.make_async_copy(normal_one_h, normal_one, load.at[1, 2]),
            pltpu.make_async_copy(w4_h.at[3], wo, load.at[1, 3]),
        ]
        late_loads = [
            pltpu.make_async_copy(first_t_h, first_t, load.at[2, 0]),
            pltpu.make_async_copy(context_t_h, context_t, load.at[2, 2]),
        ]

        def loads(j):
            return [
                pltpu.make_async_copy(wd_h.at[block(j)], wd.at[block(j)], load.at[3, j]),
                pltpu.make_async_copy(pull_h.at[:, block(j)], pull.at[:, block(j)], load.at[4, j]),
                pltpu.make_async_copy(wu_h.at[:, block(j)], wu.at[:, block(j)], load.at[5, j]),
            ]

        first_loads[0].start()
        for c in loads(0):
            c.start()
        for c in own_loads + first_loads[1:]:
            c.start()
        for j in range(1, loops):
            for c in loads(j):
                c.start()
        for c in late_loads:
            c.start()
        greet(all_peers())
        d.start("core")
        first_loads[0].wait()

        @pl.loop(0, 2 * loops)
        def _(t):
            j = t % loops
            rows = rows_of(t // loops)

            @pl.when(t < loops)
            def _():
                for c in loads(j)[:2]:
                    c.wait()

            grads = dot_t(err_two[rows, :], wd[block(j), :])
            low = (grads * pull[rows, block(j)].astype(F32)).astype(BF16)
            pull[rows, block(j)] = low
            sums_up[:, block(j)] += jnp.sum(low.astype(F32), 0, keepdims=True)

            @pl.when(t == OWN_LOADED)
            def _():
                for c in own_loads:
                    c.wait()

            run_at(chunks, BACKWARD_PLAN, "hidden", t, 2 * loops)

        for c in late_loads[:1]:
            c.wait()

        @pl.loop(0, 4)
        def _(m):
            cols = pl.ds(pl.multiple_of(m * width, width), width)
            part_u[m] = dot(first_t[...], pull[:, cols]).astype(BF16).reshape(part_u.shape[1:])
            run_at(chunks, BACKWARD_PLAN, "grad up", m, 4)

        u.start("core")
        for c in first_loads[1:] + late_loads[1:]:
            c.wait()
        for j in range(loops):
            loads(j)[2].wait()

        @pl.loop(0, 2)
        def _(s):
            rows = rows_of(s)
            grad_first = grad_in[rows, :] + dot_t(pull[rows, :], wu[...])
            run_at(chunks, BACKWARD_PLAN, "first", s, 2)
            normal = normal_one[rows, :]
            note(sums, 3, grad_first * normal)
            note(sums, 4, grad_first)
            resid = pull_back(grad_first * gain_one, normal, inverse_one[rows, :])
            grad_in[rows, :] = resid
            low = resid.astype(BF16)
            err_one[rows, :] = low
            note(sums, 2, low.astype(F32))
            grad_context[rows, :] = dot_t(low, wo[...]).astype(BF16)
            run_at(chunks, BACKWARD_PLAN, "norm", s, 2)

    pl.run_scoped(
        feed_back,
        pltpu.VMEM((columns, width), BF16),
        pltpu.VMEM((width, columns), BF16),
        pltpu.VMEM((total, columns), BF16),
        pltpu.VMEM((total, width), BF16),
        pltpu.VMEM((total, width), F32),
        pltpu.VMEM((width, total), BF16),
        pltpu.VMEM((width, width), BF16),
    )

    def attend_and_inputs(qkv, powers, grads, weights, part_q, tokens):
        halves = [part_q.at[0], part_q.at[1]] + [
            part_q.at[2, :, :, :, :, pl.ds(i * PAIR, PAIR)] for i in range(2)
        ]
        q = [
            Chunk(f"q{i}", wire, where, p, own_part(p), scratch[14 + 7 * i : 21 + 7 * i])
            for i, p in enumerate(halves)
        ]
        chunks.update({c.name: c for c in q})

        def loads(t):
            pair, s = t // 2, t % 2
            rows, cols = rows_of(s), pl.ds(pl.multiple_of(pair * PAIR, PAIR), PAIR)
            return [
                pltpu.make_async_copy(a.at[rows, cols], qkv.at[s, i], load.at[6 + i, s])
                for i, a in enumerate((query_h, keys_h, values_h))
            ] + [
                pltpu.make_async_copy(
                    powers_h.at[s, pl.ds(pair * 2, 2)], powers.at[s], load.at[9, s]
                )
            ]

        weight_loads = [
            pltpu.make_async_copy(
                w4_h.at[i, :, pl.ds(g * GROUP, GROUP)],
                weights.at[g, :, pl.ds(i * GROUP, GROUP)],
                load.at[10 + g, i],
            )
            for g in range(3)
            for i in range(3)
        ]
        tokens_load = pltpu.make_async_copy(tokens_h, tokens, load.at[2, 1])
        for c in loads(0) + [tokens_load] + weight_loads:
            c.start()

        @pl.loop(0, 3)
        def _(g):
            @pl.loop(0, 4)
            def _(k):
                t = g * 4 + k
                pair, s = t // 2, t % 2

                @pl.when(t < 11)
                def _():
                    for c in loads(t + 1):
                        c.start()

                for c in loads(t):
                    c.wait()
                rows, cols = rows_of(s), pl.ds(pl.multiple_of(pair * PAIR, PAIR), PAIR)
                values = attend_back_step(
                    qkv.at[s, 0], qkv.at[s, 1], qkv.at[s, 2], powers.at[s],
                    inverse.at[s, pair], context_t.at[cols, rows], grad_context.at[rows, cols],
                )
                for i, value in enumerate(values):
                    lane = pl.multiple_of(i * GROUP + (pair % 2) * PAIR, PAIR)
                    grads[g, rows, pl.ds(lane, PAIR)] = value
                run_at(chunks, BACKWARD_PLAN, "attend", t, 12)

            @pl.when(g == 0)
            def _():
                tokens_load.wait()
                tokens_t[...] = tokens[...].T

            cols = pl.ds(pl.multiple_of(g * GROUP, GROUP), GROUP)
            for i in range(3):
                lanes = slice(i * GROUP, (i + 1) * GROUP)
                part_q[g, i] = (
                    dot(tokens_t[...], grads[g, :, lanes])
                    .astype(BF16)
                    .reshape(NZ, NX, ROWS, GROUP)
                )
            part_q[g, 3] = (
                dot(context_t[...], err_one[:, cols]).astype(BF16).reshape(NZ, NX, ROWS, GROUP)
            )
            for i in range(2):

                @pl.when(g == i)
                def _():
                    q[i].start("core")

            @pl.when(g == 2)
            def _():
                q[2].start("core")
                q[3].start("core")

            sums[0:1, cols] = jnp.sum(grads[g, :, :GROUP].astype(F32), 0, keepdims=True)
            sums[1:2, cols] = jnp.sum(grads[g, :, 2 * GROUP :].astype(F32), 0, keepdims=True)
            run_at(chunks, BACKWARD_PLAN, "weights", g, 3)

        pv[...] = jnp.zeros_like(pv)
        lanes = lax.broadcasted_iota(jnp.int32, (width, NX * NZ * 128), 1)
        rows = lax.broadcasted_iota(jnp.int32, (width, NX * NZ * 128), 0)
        pick = (rows == (lanes // 128) * ROWS + lanes % 128) & (lanes % 128 < ROWS)
        spread8 = lax.dot_general(
            sums[...], pick.astype(F32), (((1,), (0,)), ((), ())),
            precision=lax.Precision.HIGHEST, preferred_element_type=F32,
        )
        per = columns // (NX * NZ)
        for f in range(NX * NZ):
            pv[f, 8:16, 0:128] = spread8[:, f * 128 : (f + 1) * 128]
            pv[f, 0:1, :] = sums_up[:, f * per : (f + 1) * per]

        def to_owner(k):
            to = (shard + k) % (NX * NZ)
            return wire.copy(("v", k), pv.at[to], va.at[k - 1], {"dp": member, "fsdp": to})

        for k in range(1, NX * NZ):
            to_owner(k).start()
        for c in weight_loads:
            c.wait()
        out = []
        for i in range(3):
            lanes = slice(i * GROUP, (i + 1) * GROUP)
            summed = grad_in[:, lanes]
            for g in range(3):
                summed = summed + dot_t(grads[g], weights[g, lanes, :])
            grad_in[:, lanes] = summed
            c = pltpu.make_async_copy(
                grad_in.at[:, lanes], input_grad.at[:, lanes], load.at[13, i]
            )
            c.start()
            out.append(c)
            run_events(chunks, BACKWARD_PLAN.get(("inputs", i), ()))

        for k in range(1, NX * NZ):
            to_owner(k).wait_recv()
        partial = pv[shard]
        for k in range(NX * NZ - 1):
            partial = partial + va[k]
        vb[member] = partial

        def to_member(i):
            dy, dc = ((0, 1), (1, 0), (1, 1))[i]
            peer = at(x, (y + dy) % 2, z, (core + dc) % 2)
            return wire.copy(("w", i), vb.at[member], vb.at[member], peer)

        for i in range(3):
            to_member(i).start()
        run_events(chunks, BACKWARD_PLAN["drain one"])
        for i in range(3):
            to_member(i).wait_recv()
        ov[...] = (vb[0] + vb[1]) + (vb[2] + vb[3])
        d.done()
        od[...] = d.fin[...]
        run_events(chunks, BACKWARD_PLAN["drain two"])
        u.done()
        ou[...] = u.fin[...]
        run_events(chunks, BACKWARD_PLAN["drain three"])
        first = 0
        for c in q:
            c.done()
            last = first + c.fin.shape[2]
            o4[:, :, first:last] = c.fin[...]
            first = last
        for c in out:
            c.wait()
        for c in [d, u] + q:
            c.drain()
        for k in range(1, NX * NZ):
            to_owner(k).wait_send()
        for i in range(3):
            to_member(i).wait_send()

    pl.run_scoped(
        attend_and_inputs,
        pltpu.VMEM((2, 3, length, PAIR), BF16),
        pltpu.VMEM((2, 2, length, length), BF16),
        pltpu.VMEM((3, total, width), BF16),
        pltpu.VMEM((3, width, width), BF16),
        pltpu.VMEM((3, 4, NZ, NX, ROWS, GROUP), BF16),
        pltpu.VMEM((total, width), BF16),
    )


def backward(
    part_d, err_two, pull, wd, wu, resid_two, normal_one, inverse_one, first_t,
    query, keys, values, powers, inverse, context_t, rows, w4, vec, sums_in,
):
    total, width = rows.shape
    columns = wu.shape[1]
    per = columns // (NX * NZ)
    hbm, vmem = pl.BlockSpec(memory_space=pl.ANY), pl.BlockSpec(memory_space=pltpu.VMEM)
    d_block, copies = part_d.shape[3:], 7 + 3 + 6 * (2 + 2 + 2 + 3 + 2 + 1)
    scratch = [
        pltpu.VMEM((4, NZ, NX, ROWS, width), BF16),
        pltpu.VMEM((2, NZ, NX) + d_block, BF16),
        pltpu.VMEM((total, width), BF16),
        pltpu.VMEM((total, width), BF16),
        pltpu.VMEM((total, width), F32),
        pltpu.VMEM((width, total), BF16),
        pltpu.VMEM((width, total), BF16),
        pltpu.VMEM((8, width), F32),
        pltpu.VMEM((1, columns), F32),
        pltpu.VMEM((NX * NZ, 16, per), F32),
        pltpu.VMEM((NX * NZ - 1, 16, per), F32),
        pltpu.VMEM((4, 16, per), F32),
    ]
    scratch += Chunk.scratch(*d_block) + Chunk.scratch(ROWS, width)
    scratch += Chunk.scratch(ROWS, GROUP) * 2 + Chunk.scratch(ROWS, PAIR) * 2
    scratch += [pltpu.SemaphoreType.DMA((copies,))] * 2 + [pltpu.SemaphoreType.DMA((14, 4))]
    return pl.pallas_call(
        backward_kernel,
        name="backward",
        in_specs=[hbm] * 7 + [vmem] + [hbm] * 5 + [vmem] + [hbm] * 3 + [vmem] * 2,
        out_specs=[vmem] * 4 + [hbm],
        out_shape=[
            Shape((4, ROWS, width), BF16),
            Shape((4, ROWS, width), BF16),
            Shape((4,) + part_d.shape[3:], BF16),
            Shape((16, per), F32),
            Shape((total, width), F32),
        ],
        scratch_shapes=scratch,
        compiler_params=params(collective_id=1, has_side_effects=True),
    )(
        part_d, err_two, pull, wd, wu, resid_two, normal_one, inverse_one, first_t,
        query, keys, values, powers, inverse, context_t, rows, w4, vec, sums_in,
    )


def finish_kernel(o4, ou, od, ov, *outs):
    width = o4.shape[2]
    for i in range(4):
        outs[i][...] = o4[i].astype(F32)
        outs[4][:, i * width : (i + 1) * width] = ou[i].astype(F32)
        rows = od.shape[1]
        outs[5][:, i * rows : (i + 1) * rows] = od[i].astype(F32).T
        outs[7 + i][...] = ov[8 + i : 9 + i, :ROWS]
        outs[11 + i][...] = ov[12 + i : 13 + i, :ROWS]
    outs[6][...] = ov[0:1, :]


def finish(o4, ou, od, ov):
    width, per = o4.shape[2], ov.shape[1]
    vmem = pl.BlockSpec(memory_space=pltpu.VMEM)
    return pl.pallas_call(
        finish_kernel,
        name="finish",
        in_specs=[vmem] * 4,
        out_specs=[vmem] * 15,
        out_shape=[Shape((ROWS, width), F32)] * 4
        + [Shape((ROWS, 4 * width), F32), Shape((od.shape[2], 4 * od.shape[1]), F32)]
        + [Shape((1, per), F32)]
        + [Shape((1, ROWS), F32)] * 8,
        compiler_params=params(),
    )(o4, ou, od, ov)


def fused_layer(
    tokens, counts, cotangent, query_weight, key_weight, value_weight, out_weight, query_bias,
    value_bias, out_bias, attention_gain, attention_shift, up_weight, up_bias, down_weight,
    down_bias, feed_gain, feed_shift,
):
    width = tokens.shape[2]
    shards = NX * NZ
    columns = up_weight.shape[1]
    rows = tokens.reshape(-1, width)
    vectors = (
        query_bias, value_bias, out_bias, attention_gain, attention_shift, down_bias, feed_gain,
        feed_shift, up_bias,
    )
    (
        w4, wu, wd, layer_out, query, keys, values, powers, context_t, first_t, err_two, resid_two,
        normal_one, pull, part_d, vec8, inverse, inverse_one, sums,
    ) = forward(
        counts, rows, vectors, cotangent.reshape(-1, width), query_weight, key_weight, value_weight,
        out_weight, up_weight, down_weight,
    )
    o4, ou, od, ov, input_grad = backward(
        part_d, err_two, pull, wd.reshape(columns, width), wu.reshape(width, columns), resid_two,
        normal_one, inverse_one, first_t, query, keys, values, powers, inverse, context_t, rows,
        w4.reshape(4, width, width), vec8, sums,
    )
    gq, gk, gv, go, gu, gd, gub, *v = finish(o4, ou, od, ov)
    v = [i.reshape(-1) for i in v]
    return (
        layer_out.reshape(tokens.shape),
        input_grad.reshape(tokens.shape),
        gq, gk, gv, go, v[0], v[1], v[2], v[3], v[4], gu, gub.reshape(-1), gd, v[5], v[6], v[7],
    )


def exact_gelu(value):
    return jax.nn.gelu(value, approximate=False)


def norm_forward(resid, gain, shift):
    average = jnp.mean(resid, axis=-1, keepdims=True)
    centred = resid - average
    spread = jnp.mean(centred * centred, axis=-1, keepdims=True)
    inverse = lax.rsqrt(spread + epsilon)
    normal = centred * inverse
    return (normal * gain + shift, normal, inverse)


def norm_backward(grad_out, normal, inverse, gain):
    scaled = grad_out * gain
    first_mean = jnp.mean(scaled, axis=-1, keepdims=True)
    second_mean = jnp.mean(scaled * normal, axis=-1, keepdims=True)
    grad_resid = inverse * (scaled - first_mean - normal * second_mean)
    return (grad_resid, jnp.sum(grad_out * normal, 0), jnp.sum(grad_out, 0))


def linear(rows, weight):
    return jnp.dot(rows, weight, preferred_element_type=jnp.float32)


def linear_back(grads, weight):
    return lax.dot_general(
        grads, weight, (((1,), (1,)), ((), ())), preferred_element_type=jnp.float32
    )


def outer_sum(rows, grads):
    return lax.dot_general(
        rows, grads, (((0,), (0,)), ((), ())), preferred_element_type=jnp.float32
    )


def column_sum(grads):
    return jnp.sum(grads.astype(jnp.float32), 0)


def on_device(
    tokens,
    counts,
    cotangent,
    query_weight,
    key_weight,
    value_weight,
    out_weight,
    query_bias,
    value_bias,
    out_bias,
    attention_gain,
    attention_shift,
    up_weight,
    up_bias,
    down_weight,
    down_bias,
    feed_gain,
    feed_shift,
):
    slots, length, width = tokens.shape
    heads = width // HEAD_DIM
    factor = HEAD_DIM ** (-0.5)
    positions = jnp.arange(length, dtype=jnp.int32)

    def split_heads(value):
        return value.reshape(slots, length, heads, HEAD_DIM)

    def masked_scores(query, keys, count):
        raw = jnp.einsum("qhd,khd->hqk", query, keys, preferred_element_type=jnp.float32)
        live = positions < count
        return jnp.where(live[None, None, :], raw * factor, -1000000000.0)

    def attend_forward(block):
        query, keys, values, count = block
        scores = masked_scores(query, keys, count)
        highest = jnp.max(scores, axis=-1, keepdims=True)
        powers = jnp.exp(scores - highest)
        totals = jnp.sum(powers, axis=-1, keepdims=True)
        probs = (powers / totals).astype(jnp.bfloat16)
        context = jnp.einsum("hqk,khd->qhd", probs, values, preferred_element_type=jnp.float32)
        return (context.reshape(length, width), highest + jnp.log(totals))

    def attend_backward(block):
        query, keys, values, count, logsum, grad_context = block
        scores = masked_scores(query, keys, count)
        probs = jnp.exp(scores - logsum)
        probs_low = probs.astype(jnp.bfloat16)
        grad_probs = jnp.einsum(
            "qhd,khd->hqk", grad_context, values, preferred_element_type=jnp.float32
        )
        inner = jnp.sum(probs * grad_probs, axis=-1, keepdims=True)
        grad_scores = (probs * (grad_probs - inner) * factor).astype(jnp.bfloat16)
        grad_query = jnp.einsum(
            "hqk,khd->qhd", grad_scores, keys, preferred_element_type=jnp.float32
        )
        grad_keys = jnp.einsum(
            "hqk,qhd->khd", grad_scores, query, preferred_element_type=jnp.float32
        )
        grad_values = jnp.einsum(
            "hqk,qhd->khd", probs_low, grad_context, preferred_element_type=jnp.float32
        )
        return (
            grad_query.reshape(length, width).astype(jnp.bfloat16),
            grad_keys.reshape(length, width).astype(jnp.bfloat16),
            grad_values.reshape(length, width).astype(jnp.bfloat16),
        )

    attention_set = (
        lax.all_gather(query_weight, "fsdp", axis=0, tiled=True),
        lax.all_gather(key_weight, "fsdp", axis=0, tiled=True),
        lax.all_gather(value_weight, "fsdp", axis=0, tiled=True),
        lax.all_gather(out_weight, "fsdp", axis=0, tiled=True),
        lax.all_gather(query_bias, "fsdp", axis=0, tiled=True),
        lax.all_gather(value_bias, "fsdp", axis=0, tiled=True),
        lax.all_gather(out_bias, "fsdp", axis=0, tiled=True),
        lax.all_gather(attention_gain, "fsdp", axis=0, tiled=True),
        lax.all_gather(attention_shift, "fsdp", axis=0, tiled=True),
    )
    feed_set = (
        lax.all_gather(up_weight, "fsdp", axis=0, tiled=True),
        lax.all_gather(up_bias, "fsdp", axis=0, tiled=True),
        lax.all_gather(down_weight, "fsdp", axis=0, tiled=True),
        lax.all_gather(down_bias, "fsdp", axis=0, tiled=True),
        lax.all_gather(feed_gain, "fsdp", axis=0, tiled=True),
        lax.all_gather(feed_shift, "fsdp", axis=0, tiled=True),
    )
    whole_query, whole_key, whole_value, whole_out = (
        attention_set[0],
        attention_set[1],
        attention_set[2],
        attention_set[3],
    )
    whole_up, whole_down = (feed_set[0], feed_set[2])
    rows = tokens.reshape(-1, width)
    query = (linear(rows, whole_query) + attention_set[4].astype(jnp.float32)).astype(jnp.bfloat16)
    keys = linear(rows, whole_key).astype(jnp.bfloat16)
    values = (linear(rows, whole_value) + attention_set[5].astype(jnp.float32)).astype(jnp.bfloat16)
    context_rows, logsum = lax.map(
        attend_forward, (split_heads(query), split_heads(keys), split_heads(values), counts)
    )
    context = context_rows.reshape(-1, width).astype(jnp.bfloat16)
    branch = linear(context, whole_out) + attention_set[6].astype(jnp.float32)
    gain_one = attention_set[7].astype(jnp.float32)
    first, normal_one, inverse_one = norm_forward(
        rows.astype(jnp.float32) + branch, gain_one, attention_set[8].astype(jnp.float32)
    )
    first_low = first.astype(jnp.bfloat16)
    hidden = linear(first_low, whole_up) + feed_set[1].astype(jnp.float32)
    activated, gelu_pull = jax.vjp(exact_gelu, hidden)
    act_low = activated.astype(jnp.bfloat16)
    second = linear(act_low, whole_down) + feed_set[3].astype(jnp.float32)
    gain_two = feed_set[4].astype(jnp.float32)
    output, normal_two, inverse_two = norm_forward(
        first + second, gain_two, feed_set[5].astype(jnp.float32)
    )
    live = (positions[None, :] < counts[:, None]).reshape(-1, 1)
    layer_out = jnp.where(live, output, 0.0).astype(jnp.bfloat16).reshape(tokens.shape)
    back_feed = (
        lax.all_gather(up_weight, "fsdp", axis=0, tiled=True),
        lax.all_gather(down_weight, "fsdp", axis=0, tiled=True),
    )
    back_up, back_down = (back_feed[0], back_feed[1])
    grad_y = jnp.where(live, cotangent.reshape(-1, width).astype(jnp.float32), 0.0)
    resid_two, grad_feed_gain, grad_feed_shift = norm_backward(
        grad_y, normal_two, inverse_two, gain_two
    )
    err_two = resid_two.astype(jnp.bfloat16)
    grad_down_weight = outer_sum(act_low, err_two)
    grad_down_bias = column_sum(err_two)
    grad_act = linear_back(err_two, back_down)
    grad_hidden = gelu_pull(grad_act)[0].astype(jnp.bfloat16)
    grad_up_weight = outer_sum(first_low, grad_hidden)
    grad_up_bias = column_sum(grad_hidden)
    grad_first = resid_two + linear_back(grad_hidden, back_up)
    feed_shards = (
        lax.psum_scatter(
            grad_up_weight.astype(jnp.bfloat16), "fsdp", scatter_dimension=0, tiled=True
        ).astype(jnp.float32),
        lax.psum_scatter(
            grad_up_bias.astype(jnp.bfloat16), "fsdp", scatter_dimension=0, tiled=True
        ).astype(jnp.float32),
        lax.psum_scatter(
            grad_down_weight.astype(jnp.bfloat16), "fsdp", scatter_dimension=0, tiled=True
        ).astype(jnp.float32),
        lax.psum_scatter(
            grad_down_bias.astype(jnp.bfloat16), "fsdp", scatter_dimension=0, tiled=True
        ).astype(jnp.float32),
        lax.psum_scatter(
            grad_feed_gain.astype(jnp.bfloat16), "fsdp", scatter_dimension=0, tiled=True
        ).astype(jnp.float32),
        lax.psum_scatter(
            grad_feed_shift.astype(jnp.bfloat16), "fsdp", scatter_dimension=0, tiled=True
        ).astype(jnp.float32),
    )
    back_attention = (
        lax.all_gather(query_weight, "fsdp", axis=0, tiled=True),
        lax.all_gather(key_weight, "fsdp", axis=0, tiled=True),
        lax.all_gather(value_weight, "fsdp", axis=0, tiled=True),
        lax.all_gather(out_weight, "fsdp", axis=0, tiled=True),
    )
    back_query, back_key, back_value, back_out = (
        back_attention[0],
        back_attention[1],
        back_attention[2],
        back_attention[3],
    )
    resid_one, grad_attention_gain, grad_attention_shift = norm_backward(
        grad_first, normal_one, inverse_one, gain_one
    )
    err_one = resid_one.astype(jnp.bfloat16)
    grad_out_weight = outer_sum(context, err_one)
    grad_out_bias = column_sum(err_one)
    grad_context = linear_back(err_one, back_out).astype(jnp.bfloat16)
    grad_query, grad_keys, grad_values = lax.map(
        attend_backward,
        (
            split_heads(query),
            split_heads(keys),
            split_heads(values),
            counts,
            logsum,
            split_heads(grad_context),
        ),
    )
    grad_query = grad_query.reshape(-1, width)
    grad_keys = grad_keys.reshape(-1, width)
    grad_values = grad_values.reshape(-1, width)
    grad_query_weight = outer_sum(rows, grad_query)
    grad_key_weight = outer_sum(rows, grad_keys)
    grad_value_weight = outer_sum(rows, grad_values)
    grad_query_bias = column_sum(grad_query)
    grad_value_bias = column_sum(grad_values)
    input_grad = (
        resid_one
        + linear_back(grad_query, back_query)
        + linear_back(grad_keys, back_key)
        + linear_back(grad_values, back_value)
    )
    attention_shards = (
        lax.psum_scatter(
            grad_query_weight.astype(jnp.bfloat16), "fsdp", scatter_dimension=0, tiled=True
        ).astype(jnp.float32),
        lax.psum_scatter(
            grad_key_weight.astype(jnp.bfloat16), "fsdp", scatter_dimension=0, tiled=True
        ).astype(jnp.float32),
        lax.psum_scatter(
            grad_value_weight.astype(jnp.bfloat16), "fsdp", scatter_dimension=0, tiled=True
        ).astype(jnp.float32),
        lax.psum_scatter(
            grad_out_weight.astype(jnp.bfloat16), "fsdp", scatter_dimension=0, tiled=True
        ).astype(jnp.float32),
        lax.psum_scatter(
            grad_query_bias.astype(jnp.bfloat16), "fsdp", scatter_dimension=0, tiled=True
        ).astype(jnp.float32),
        lax.psum_scatter(
            grad_value_bias.astype(jnp.bfloat16), "fsdp", scatter_dimension=0, tiled=True
        ).astype(jnp.float32),
        lax.psum_scatter(
            grad_out_bias.astype(jnp.bfloat16), "fsdp", scatter_dimension=0, tiled=True
        ).astype(jnp.float32),
        lax.psum_scatter(
            grad_attention_gain.astype(jnp.bfloat16), "fsdp", scatter_dimension=0, tiled=True
        ).astype(jnp.float32),
        lax.psum_scatter(
            grad_attention_shift.astype(jnp.bfloat16), "fsdp", scatter_dimension=0, tiled=True
        ).astype(jnp.float32),
    )
    summed = lax.psum(
        (
            attention_shards[0],
            attention_shards[1],
            attention_shards[2],
            attention_shards[3],
            attention_shards[4],
            attention_shards[5],
            attention_shards[6],
            attention_shards[7],
            attention_shards[8],
            feed_shards[0],
            feed_shards[1],
            feed_shards[2],
            feed_shards[3],
            feed_shards[4],
            feed_shards[5],
        ),
        "dp",
    )
    return (
        layer_out,
        input_grad.reshape(tokens.shape),
        summed[0],
        summed[1],
        summed[2],
        summed[3],
        summed[4],
        summed[5],
        summed[6],
        summed[7],
        summed[8],
        summed[9],
        summed[10],
        summed[11],
        summed[12],
        summed[13],
        summed[14],
    )


def solution(mesh):
    small = mesh.shape["dp"] == 4 and mesh.shape["fsdp"] == NX * NZ
    return jax.shard_map(
        fused_layer if small else on_device,
        mesh=mesh,
        in_specs=(
            P(("dp", "fsdp"), None, None),
            P(("dp", "fsdp")),
            P(("dp", "fsdp"), None, None),
            P("fsdp", None),
            P("fsdp", None),
            P("fsdp", None),
            P("fsdp", None),
            P("fsdp"),
            P("fsdp"),
            P("fsdp"),
            P("fsdp"),
            P("fsdp"),
            P("fsdp", None),
            P("fsdp"),
            P("fsdp", None),
            P("fsdp"),
            P("fsdp"),
            P("fsdp"),
        ),
        out_specs=(
            P(("dp", "fsdp"), None, None),
            P(("dp", "fsdp"), None, None),
            P("fsdp", None),
            P("fsdp", None),
            P("fsdp", None),
            P("fsdp", None),
            P("fsdp"),
            P("fsdp"),
            P("fsdp"),
            P("fsdp"),
            P("fsdp"),
            P("fsdp", None),
            P("fsdp"),
            P("fsdp", None),
            P("fsdp"),
            P("fsdp"),
            P("fsdp"),
        ),
        check_vma=False,
    )
```

```python
import functools

import jax
import jax.numpy as jnp
from jax import lax
from jax.experimental import pallas as pl
from jax.experimental.pallas import tpu as pltpu
from jax.sharding import PartitionSpec as P

HEAD_DIM = 64
epsilon = 1e-05
F32 = jnp.float32
BF16 = jnp.bfloat16
MESH = pl.DeviceIdType.MESH
VMEM_LIMIT = 63 * 2**20
Shape = jax.ShapeDtypeStruct


def dot(left, right):
    return lax.dot_general(
        left, right, (((1,), (0,)), ((), ())), preferred_element_type=F32
    )


def dot_t(left, right):
    return lax.dot_general(
        left, right, (((1,), (1,)), ((), ())), preferred_element_type=F32
    )


def params(**extra):
    return pltpu.CompilerParams(vmem_limit_bytes=VMEM_LIMIT, **extra)


def whole(shape):
    return pl.BlockSpec(shape, lambda *_: (0,) * len(shape), pipeline_mode=pl.Buffered(1))


NX, NZ, ROWS = 2, 4, 96


def place():
    member = lax.axis_index("dp")
    shard = lax.axis_index("fsdp")
    return shard % NX, member // 2, shard // NX, member % 2


def at(x, y, z, core):
    return {"dp": y * 2 + core, "fsdp": z * NX + x}


def greet(peers):
    barrier = pltpu.get_barrier_semaphore()
    for peer in peers:
        pl.semaphore_signal(barrier, inc=1, device_id=peer, device_id_type=MESH)
    pl.semaphore_wait(barrier, len(peers))


def all_peers():
    x, y, z, core = place()
    near = [at(x, 1 - y, z, core), at(x, y, z, 1 - core)]
    for step in range(1, NX * NZ):
        near.append({"dp": y * 2 + core, "fsdp": (z * NX + x + step) % (NX * NZ)})
    return near


class Wire:
    def __init__(self, send, recv):
        self.send, self.recv, self.slots = send, recv, {}

    def copy(self, key, source, target, peer):
        slot = self.slots.setdefault(key, len(self.slots))
        return pltpu.make_async_remote_copy(
            src_ref=source,
            dst_ref=target,
            send_sem=self.send.at[slot],
            recv_sem=self.recv.at[slot],
            device_id=peer,
            device_id_type=MESH,
        )


QKV_PIECES = ((0, 1), (1, 1), (2, 2), (4, 2))
FEED_PIECES = ((0, 512), (512, 256))
OWN_LOADED = 3
FORWARD_PLAN = {
    "start": ("q1.plane", "q0.turn_y", "q0.turn_x", "q1.turn_y", "q1.turn_x", "q2.plane", "q0.rest", "q0.ready",),
    ("before", 2): ("q1.ready",),
    ("before", 4): ("q3.turn_y", "q3.turn_x", "u0.plane", "q2.rest", "q2.ready",),
    ("before", 8): ("q3.ready",),
    ("attend", 0): ("q1.rest",),
    ("attend", 1): ("q3.plane",),
    ("attend", 2): ("q2.turn_x", "q2.turn_y",),
    ("attend", 4): ("q3.rest", "u1.plane",),
    ("attend", 8): ("u0.turn_x", "u0.turn_y",),
    ("attend", 9): ("d0.plane",),
    ("attend", 11): ("u1.turn_x", "u1.turn_y", "d1.plane",),
    ("norm", 1): ("u0.rest",),
    ("up ready", 0): ("u0.ready",),
    ("up 0", 2): ("d0.turn_x", "d0.turn_y",),
    ("up 0", 3): ("u1.rest",),
    ("up ready", 1): ("u1.ready",),
    ("up 1", 1): ("d1.turn_x", "d1.turn_y",),
    ("down ready", 0): ("d0.rest", "d1.rest", "d0.ready",),
    ("down ready", 1): ("d1.ready",),
}
BACKWARD_PLAN = {
    ("hidden", 3): ("d.chip",),
    ("first", 0): ("d.turn_y", "d.turn_x",),
    ("norm", 0): ("u.chip",),
    ("norm", 1): ("d.depth",),
    ("attend", 5): ("q0.chip", "u.turn_y", "u.turn_x",),
    ("attend", 10): ("q1.chip",),
    ("attend", 11): ("u.depth",),
    ("inputs", 0): ("q1.turn_y", "q2.chip", "q3.chip", "d.relay",),
    ("weights", 1): ("q0.turn_y", "q0.turn_x", "d.total",),
    ("weights", 2): ("q0.depth",),
    ("inputs", 2): ("q1.turn_x", "q2.turn_y",),
    "drain one": ("q3.turn_y", "q2.turn_x", "q1.depth", "q3.turn_x",),
    "drain two": ("u.total", "q2.depth", "q3.depth", "q0.total", "u.relay",),
    "drain three": ("q0.relay", "q1.total", "q2.total", "q1.relay", "q2.relay", "q3.total", "q3.relay",),
}


GROUP = 4 * HEAD_DIM
PAIR = 2 * HEAD_DIM
SCALE = HEAD_DIM**-0.5
CHUNK = 1024


def run_events(pieces, events):
    for event in events:
        name, stage = event.split(".")
        getattr(pieces[name], stage)()


def run_at(pieces, plan, prefix, index, count):
    for k in range(count):
        if (prefix, k) in plan:

            @pl.when(index == k)
            def _():
                run_events(pieces, plan[prefix, k])


class Piece:
    def __init__(self, name, wire, where, block):
        self.name, self.wire, self.where, self.block = name, wire, where, block

    def copy(self, key, source, peer):
        return self.wire.copy((self.name, key), source, source, peer)

    def copies(self, stage):
        x, y, z, core = self.where
        member, other = y * 2 + core, (1 - y) * 2 + core
        x_peer, y_peer = at(1 - x, y, z, core), at(x, 1 - y, z, core)
        c_peer = at(x, y, z, 1 - core)
        every, block = slice(None), self.block
        if stage == "depth":
            mine = block(member, z, x)
            plan = [(mine, at(x, y, (z + k) % NZ, core)) for k in range(1, NZ)]
        elif stage == "plane":
            mine = block(member, every, x)
            plan = [(mine, x_peer), (mine, y_peer)]
        elif stage == "turn":
            plan = [
                (block(other, pl.ds(0, 2), x), x_peer),
                (block(member, pl.ds(2, 2), 1 - x), y_peer),
            ]
        else:
            plan = [
                (block(member, every, x), c_peer),
                (block(other, every, x), c_peer),
                (block(member, every, 1 - x), c_peer),
                (block(other, every, 1 - x), c_peer),
            ]
        return [self.copy((stage, i), source, peer) for i, (source, peer) in enumerate(plan)]

    def send(self):
        for c in self.copies("depth"):
            c.start()

    def plane(self):
        for c in self.copies("depth"):
            c.wait_recv()
        for c in self.copies("plane"):
            c.start()
        self.copies("core")[0].start()

    def turn_x(self):
        self.copies("plane")[1].wait_recv()
        self.copies("turn")[0].start()
        self.copies("core")[1].start()

    def turn_y(self):
        self.copies("plane")[0].wait_recv()
        self.copies("turn")[1].start()
        self.copies("core")[2].start()

    def rest(self):
        for c in self.copies("turn"):
            c.wait_recv()
        self.copies("core")[3].start()

    def ready(self):
        for c in self.copies("core"):
            c.wait_recv()

    def drain(self):
        for stage in ("depth", "plane", "turn", "core"):
            for c in self.copies(stage):
                c.wait_send()


def half(index, shape):
    lanes = lax.broadcasted_iota(jnp.int32, shape, 1)
    return lanes < HEAD_DIM if index == 0 else lanes >= HEAD_DIM


def keep_half(index, value):
    return jnp.where(half(index, value.shape), value, jnp.zeros_like(value))


def attend_step(hidden_keys, q, k, v, powers, inverse, context_t):
    scaled, v_t = q * jnp.asarray(SCALE, BF16), v.T
    for h in range(2):
        rows = slice(h * HEAD_DIM, (h + 1) * HEAD_DIM)
        scores = dot_t(keep_half(h, k), scaled) + hidden_keys
        highest = jnp.max(scores, 0, keepdims=True)
        power = jnp.exp(scores - highest)
        inv = 1.0 / jnp.sum(power, 0, keepdims=True)
        low = power.astype(BF16)
        powers[h] = low
        inverse[h : h + 1] = inv
        context_t[rows] = (dot(v_t[rows], low) * inv).astype(BF16)


SQRT_HALF = 0.7071067811865476
PDF_SCALE = 0.3989422804014327


def normal_parts(value):
    z = jnp.abs(value) * SQRT_HALF
    t = 1.0 / (1.0 + 0.3275911 * z)
    bell = jnp.exp(-(z * z))
    poly = 1.061405429 * t - 1.453152027
    poly = poly * t + 1.421413741
    poly = poly * t - 0.284496736
    poly = poly * t + 0.254829592
    tail = (0.5 * poly * t) * bell
    return jnp.where(value >= 0, 1.0 - tail, tail), bell * PDF_SCALE


def centre(resid):
    centred = resid - jnp.mean(resid, 1, keepdims=True)
    inv = lax.rsqrt(jnp.mean(centred * centred, 1, keepdims=True) + epsilon)
    return centred * inv, inv


def pull_back(scaled, normal, inv):
    return inv * (
        scaled
        - jnp.mean(scaled, 1, keepdims=True)
        - normal * jnp.mean(scaled * normal, 1, keepdims=True)
    )


def note(sums, row, value):
    sums[row : row + 1] += jnp.sum(value, 0, keepdims=True)


def forward_kernel(
    counts, tokens, qb, vb, ob, ag, ash, db, fg, fsh, ub, cotangent_h, wq, wk, wv, wo, wu_i, wd_i,
    w4_h, wu_h, wd_h, layer_out_h, query_h, keys_h, values_h, powers_h, context_t_h, first_t_h,
    err_two_h, resid_two_h, normal_one_h, pull_h, part_d_h, vec8, inverse, inverse_one, sums,
    w4, wu, wd, gv, up_row, context_t, send, recv, local,
):
    where = x, y, z, core = place()
    shard, member = z * NX + x, y * 2 + core
    total, width = tokens.shape
    length = total // 2
    columns = up_row.shape[1]
    wire = Wire(send, recv)

    def columns_of(first, pairs):
        return lambda who, zs, xs: w4.at[who, zs, xs, :, pl.ds(first * PAIR, pairs * PAIR)]

    def up_part(first, wide):
        return lambda who, zs, xs: wu.at[
            zs, xs, :, pl.ds(pl.multiple_of(who * width + first, 128), wide)
        ]

    def down_part(first, wide):
        return lambda who, zs, xs: wd.at[zs, xs, who, :, pl.ds(first, wide)]

    pieces = {
        f"q{i}": Piece(f"q{i}", wire, where, columns_of(first, pairs))
        for i, (first, pairs) in enumerate(QKV_PIECES)
    }
    for i, part in enumerate(FEED_PIECES):
        pieces[f"u{i}"] = Piece(f"u{i}", wire, where, up_part(*part))
    for i, part in enumerate(FEED_PIECES):
        pieces[f"d{i}"] = Piece(f"d{i}", wire, where, down_part(*part))

    own = [
        pltpu.make_async_copy(wq, w4.at[member, z, x], local.at[0, 0]),
        pltpu.make_async_copy(
            wu_i.at[:, pl.ds(pl.multiple_of(member * width, width), width)],
            wu.at[z, x, :, pl.ds(pl.multiple_of(member * width, width), width)],
            local.at[0, 1],
        ),
        pltpu.make_async_copy(wd_i.at[member], wd.at[z, x, member], local.at[0, 2]),
    ]
    for i, w in enumerate((wq, wk, wv, wo)):

        @pl.when(member == i)
        def _():
            pltpu.make_async_copy(w, w4.at[i, z, x], local.at[0, 0]).start()

    for c in own[1:]:
        c.start()
    gv[shard] = jnp.zeros(gv.shape[1:], F32)
    bias_row = ub[...].astype(F32).reshape(1, 4 * ROWS)
    for i in range(3):
        gv[shard, 8 + i : 9 + i, :] = bias_row[:, i * 128 : (i + 1) * 128]
    for i, vector in enumerate((qb, vb, ob, ag, ash, db, fg, fsh)):
        gv[shard, i : i + 1, 0:ROWS] = vector[...].astype(F32).reshape(1, ROWS)
    greet(all_peers())
    for c in own:
        c.wait()

    def vec_copy(k):
        peer = {"dp": member, "fsdp": (shard + k) % (NX * NZ)}
        return wire.copy(("v", k), gv.at[shard], gv.at[shard], peer)

    pieces["q0"].send()
    for k in range(1, NX * NZ):
        vec_copy(k).start()
    for name, p in pieces.items():
        if name != "q0":
            p.send()
    sums[...] = jnp.zeros_like(sums)
    pieces["q0"].plane()
    for k in range(1, NX * NZ):
        vec_copy(k).wait_recv()
    lanes = lax.broadcasted_iota(jnp.int32, (128, width), 0)
    features = lax.broadcasted_iota(jnp.int32, (128, width), 1)
    per = columns // (NX * NZ)
    joined = jnp.zeros((8, width), F32)
    for f in range(NX * NZ):
        pick = (features == f * ROWS + lanes) & (lanes < ROWS)
        joined = joined + dot(gv[f, 0:8, :].astype(BF16), pick.astype(F32).astype(BF16))
        for i in range(3):
            up_row[:, f * per + i * 128 : f * per + (i + 1) * 128] = gv[f, 8 + i : 9 + i, :]
    vec8[...] = joined
    run_events(pieces, FORWARD_PLAN["start"])

    def attention(qkv, powers):
        def outs(pair, s):
            rows = pl.ds(pl.multiple_of(s * length, length), length)
            cols = pl.ds(pl.multiple_of(pair * PAIR, PAIR), PAIR)
            return [
                pltpu.make_async_copy(qkv.at[s, i], a.at[rows, cols], local.at[1 + i, s])
                for i, a in enumerate((query_h, keys_h, values_h))
            ] + [
                pltpu.make_async_copy(
                    powers.at[s], powers_h.at[s, pl.ds(pair * 2, 2)], local.at[4, s]
                )
            ]

        @pl.loop(0, 12)
        def _(t):
            pair, s = t // 2, t % 2
            rows = pl.ds(pl.multiple_of(s * length, length), length)
            cols = pl.ds(pl.multiple_of(pair * PAIR, PAIR), PAIR)
            run_at(pieces, FORWARD_PLAN, "before", t, 12)

            @pl.when(t >= 2)
            def _():
                for c in outs(pair, s):
                    c.wait()

            weights = jnp.concatenate(
                [w4[i, :, :, :, cols].reshape(width, PAIR) for i in range(3)], 1
            )
            together = dot(tokens[rows, :], weights)
            q = (together[:, :PAIR] + vec8[0:1, cols]).astype(BF16)
            k = together[:, PAIR : 2 * PAIR].astype(BF16)
            v = (together[:, 2 * PAIR :] + vec8[1:2, cols]).astype(BF16)
            qkv[s, 0], qkv[s, 1], qkv[s, 2] = q, k, v
            key_rows = lax.broadcasted_iota(jnp.int32, (length, 1), 0)
            hidden_keys = jnp.where(key_rows < counts[s], 0.0, -1000000000.0)
            attend_step(
                hidden_keys, q, k, v, powers.at[s], inverse.at[s, pair], context_t.at[cols, rows]
            )
            for c in outs(pair, s):
                c.start()
            run_at(pieces, FORWARD_PLAN, "attend", t, 12)

        for s in range(2):
            for c in outs(5, s):
                c.wait()

    pl.run_scoped(
        attention,
        pltpu.VMEM((2, 3, length, PAIR), BF16),
        pltpu.VMEM((2, 2, length, length), BF16),
    )

    def feed(act, pull, first_low, first_t, err_two, err_two_t, normal_one, resid_two, low_out, cotangent, part_d):
        v = [vec8[i : i + 1] for i in range(8)]
        out_bias, gain_one, shift_one, down_bias, gain_two, shift_two = v[2:]
        loads = [pltpu.make_async_copy(cotangent_h, cotangent, local.at[5, 0])]
        outs = [
            pltpu.make_async_copy(w4, w4_h, local.at[5, 1]),
            pltpu.make_async_copy(context_t, context_t_h, local.at[5, 2]),
        ]
        for c in loads + outs:
            c.start()

        def keep(source, target, slot):
            c = pltpu.make_async_copy(source, target, local.at[6 + slot // 4, slot % 4])
            c.start()
            outs.append(c)

        def rows_of(s):
            return pl.ds(pl.multiple_of(s * length, length), length)

        @pl.loop(0, 2)
        def _(s):
            rows = rows_of(s)
            r1 = (
                tokens[rows, :].astype(F32)
                + dot(context_t[:, rows].T, w4[3].reshape(width, width))
                + out_bias
            )
            normal, inv = centre(r1)
            normal_one[rows, :] = normal
            inverse_one[rows, :] = inv
            low = (normal * gain_one + shift_one).astype(BF16)
            first_low[rows, :] = low
            first_t[:, rows] = low.T
            run_at(pieces, FORWARD_PLAN, "norm", s, 2)

        keep(normal_one, normal_one_h, 0)
        keep(first_t, first_t_h, 1)
        for i, (first, wide) in enumerate(FEED_PIECES):
            run_events(pieces, FORWARD_PLAN["up ready", i])

            @pl.loop(0, 4)
            def _(m):
                cols = pl.ds(pl.multiple_of(m * width + first, 128), wide)
                weight = wu[:, :, :, cols].reshape(width, wide)
                for s in range(2):
                    rows = slice(s * length, (s + 1) * length)
                    hidden = dot(first_low[rows, :], weight) + up_row[:, cols]
                    cdf, density = normal_parts(hidden)
                    act[rows, cols] = (hidden * cdf).astype(BF16)
                    pull[rows, cols] = (cdf + hidden * density).astype(BF16)
                run_at(pieces, FORWARD_PLAN, f"up {i}", m, 4)

        keep(wu, wu_h, 2)
        keep(pull, pull_h, 3)
        for c in loads:
            c.wait()
        for i, (first, wide) in enumerate(FEED_PIECES):
            run_events(pieces, FORWARD_PLAN["down ready", i])

            @pl.loop(0, 2)
            def _(s):
                rows = rows_of(s)
                weight = wd[:, :, :, :, first : first + wide].reshape(columns, wide)
                resid_two[rows, first : first + wide] = dot(act[rows, :], weight)
                run_at(pieces, FORWARD_PLAN, f"down {i}", s, 2)

        keep(wd, wd_h, 4)

        @pl.loop(0, 2)
        def _(s):
            rows = rows_of(s)
            first = normal_one[rows, :] * gain_one + shift_one
            normal, inv = centre(first + resid_two[rows, :] + down_bias)
            live = lax.broadcasted_iota(jnp.int32, (length, 1), 0) < counts[s]
            low_out[rows, :] = jnp.where(live, normal * gain_two + shift_two, 0.0).astype(BF16)
            grad_y = jnp.where(live, cotangent[rows, :].astype(F32), 0.0)
            resid = pull_back(grad_y * gain_two, normal, inv)
            resid_two[rows, :] = resid
            low = resid.astype(BF16)
            err_two[rows, :] = low
            err_two_t[:, rows] = low.T
            note(sums, 6, grad_y * normal)
            note(sums, 7, grad_y)
            note(sums, 5, low.astype(F32))

        keep(low_out, layer_out_h, 5)
        keep(err_two, err_two_h, 6)
        keep(resid_two, resid_two_h, 7)

        @pl.loop(0, NZ)
        def _(zz):
            cols = pl.ds(pl.multiple_of(zz * NX * per, per), NX * per)
            grad = dot(err_two_t[...], act[:, cols]).astype(BF16)
            for xx in range(NX):
                part_d[:, zz, xx] = grad[:, xx * per : (xx + 1) * per].reshape(4, width // 4, per)

        keep(part_d, part_d_h, 8)
        for c in outs:
            c.wait()
        for p in pieces.values():
            p.drain()
        for k in range(1, NX * NZ):
            vec_copy(k).wait_send()

    pl.run_scoped(
        feed,
        pltpu.VMEM((total, columns), BF16),
        pltpu.VMEM((total, columns), BF16),
        pltpu.VMEM((total, width), BF16),
        pltpu.VMEM((width, total), BF16),
        pltpu.VMEM((total, width), BF16),
        pltpu.VMEM((width, total), BF16),
        pltpu.VMEM((total, width), F32),
        pltpu.VMEM((total, width), F32),
        pltpu.VMEM((total, width), BF16),
        pltpu.VMEM((total, width), BF16),
        pltpu.VMEM((4, NZ, NX, width // 4, per), BF16),
    )


def forward(counts, rows, vectors, cotangent, wq, wk, wv, wo, wu, wd):
    total, width = rows.shape
    columns = wu.shape[1]
    slots, length = 2, total // 2
    heads = width // HEAD_DIM
    per = columns // (NX * NZ)
    copies = 7 + (len(QKV_PIECES) + 4) * (3 + 2 + 2 + 4)
    hbm, vmem = pl.BlockSpec(memory_space=pl.ANY), pl.BlockSpec(memory_space=pltpu.VMEM)
    w4_shape = (4, NZ, NX, ROWS, width)
    wu_shape = (NZ, NX, ROWS, columns)
    wd_shape = (NZ, NX, 4, ROWS, width)
    return pl.pallas_call(
        forward_kernel,
        name="forward",
        in_specs=[pl.BlockSpec(memory_space=pltpu.SMEM)] + [vmem] * 10 + [hbm] * 7,
        out_specs=[hbm] * 15 + [vmem] * 4,
        out_shape=[
            Shape(w4_shape, BF16),
            Shape(wu_shape, BF16),
            Shape(wd_shape, BF16),
            Shape((total, width), BF16),
            Shape((total, width), BF16),
            Shape((total, width), BF16),
            Shape((total, width), BF16),
            Shape((slots, heads, length, length), BF16),
            Shape((width, total), BF16),
            Shape((width, total), BF16),
            Shape((total, width), BF16),
            Shape((total, width), F32),
            Shape((total, width), F32),
            Shape((total, columns), BF16),
            Shape((4, NZ, NX, width // 4, per), BF16),
            Shape((8, width), F32),
            Shape((slots, heads // 2, 2, length), F32),
            Shape((total, 1), F32),
            Shape((8, width), F32),
        ],
        scratch_shapes=[
            pltpu.VMEM(w4_shape, BF16),
            pltpu.VMEM(wu_shape, BF16),
            pltpu.VMEM(wd_shape, BF16),
            pltpu.VMEM((NX * NZ, 16, 128), F32),
            pltpu.VMEM((1, columns), F32),
            pltpu.VMEM((width, total), BF16),
            pltpu.SemaphoreType.DMA((copies,)),
            pltpu.SemaphoreType.DMA((copies,)),
            pltpu.SemaphoreType.DMA((9, 4)),
        ],
        compiler_params=params(collective_id=0, has_side_effects=True),
    )(counts, rows, *vectors, cotangent, wq, wk, wv, wo, wu, wd.reshape(4, ROWS, width))


class Chunk:
    def __init__(self, name, wire, where, part, mine, scratch):
        self.name, self.wire, self.where = name, wire, where
        self.part, self.mine = part, mine
        self.rc, self.bx, self.by, self.cx, self.cy, self.bz, self.fin = scratch

    @staticmethod
    def scratch(a, b):
        return [
            pltpu.VMEM((2, NZ, NX, a, b), BF16),
            pltpu.VMEM((2, 2, a, b), BF16),
            pltpu.VMEM((2, NX, a, b), BF16),
            pltpu.VMEM((2, a, b), BF16),
            pltpu.VMEM((2, a, b), BF16),
            pltpu.VMEM((NZ - 1, a, b), BF16),
            pltpu.VMEM((4, a, b), BF16),
        ]

    def copies(self, stage):
        x, y, z, core = self.where
        member, other = y * 2 + core, (1 - y) * 2 + core
        x_peer, y_peer = at(1 - x, y, z, core), at(x, 1 - y, z, core)
        c_peer = at(x, y, z, 1 - core)
        rc, fin = self.rc, self.fin
        if stage == "core":
            plan = [(self.part.at[yy * 2 + 1 - core], rc.at[yy], c_peer) for yy in range(2)]
        elif stage == "plane":
            plan = [
                (rc.at[:, pl.ds(0, 2), 1 - x], self.bx, x_peer),
                (rc.at[1 - y, pl.ds(2, 2)], self.by, y_peer),
            ]
        elif stage == "turn":
            plan = [
                (rc.at[1 - y, pl.ds(0, 2), x], self.cy, y_peer),
                (rc.at[y, pl.ds(2, 2), 1 - x], self.cx, x_peer),
            ]
        elif stage == "depth":
            plan = [
                (rc.at[y, (z + k) % NZ, x], self.bz.at[k - 1], at(x, y, (z + k) % NZ, core))
                for k in range(1, NZ)
            ]
        elif stage == "spread":
            plan = [(fin.at[member], fin.at[member], peer) for peer in (y_peer, c_peer)]
        else:
            plan = [(fin.at[other], fin.at[other], c_peer)]
        return [
            self.wire.copy((self.name, stage, i), source, target, peer)
            for i, (source, target, peer) in enumerate(plan)
        ]

    def start(self, stage):
        for c in self.copies(stage):
            c.start()

    def arrive(self, stage):
        for c in self.copies(stage):
            c.wait_recv()

    def chip(self):
        core = self.where[3]
        self.arrive("core")
        rc, mine = self.rc, self.mine
        for yy in range(2):

            @pl.loop(0, NZ)
            def _(zz):
                for xx in range(NX):
                    rc[yy, zz, xx] = rc[yy, zz, xx] + mine(yy, core, zz, xx)

        self.start("plane")

    def turn_y(self):
        x, y, z, core = self.where
        rc, bx = self.rc, self.bx
        self.copies("plane")[0].wait_recv()

        @pl.loop(0, 2)
        def _(zz):
            for yy in range(2):
                rc[yy, zz, x] = rc[yy, zz, x] + bx[yy, zz]

        self.copies("turn")[0].start()

    def turn_x(self):
        x, y, z, core = self.where
        rc, by = self.rc, self.by
        self.copies("plane")[1].wait_recv()

        @pl.loop(0, 2)
        def _(zz):
            for xx in range(NX):
                rc[y, 2 + zz, xx] = rc[y, 2 + zz, xx] + by[zz, xx]

        self.copies("turn")[1].start()

    def depth(self):
        x, y, z, core = self.where
        rc, cx, cy = self.rc, self.cx, self.cy
        self.arrive("turn")

        @pl.loop(0, 2)
        def _(zz):
            rc[y, zz, x] = rc[y, zz, x] + cy[zz]
            rc[y, 2 + zz, x] = rc[y, 2 + zz, x] + cx[zz]

        self.start("depth")

    def total(self):
        x, y, z, core = self.where
        self.arrive("depth")
        summed = self.rc[y, z, x].astype(F32)
        for k in range(NZ - 1):
            summed = summed + self.bz[k].astype(F32)
        self.fin[y * 2 + core] = summed.astype(BF16)
        self.start("spread")

    def relay(self):
        self.copies("spread")[0].wait_recv()
        self.start("relay")

    def done(self):
        self.copies("spread")[1].wait_recv()
        self.arrive("relay")

    def drain(self):
        for stage in ("core", "plane", "turn", "depth", "spread", "relay"):
            for c in self.copies(stage):
                c.wait_send()


def attend_back_step(query, keys, values, powers, inverse, context_t, grad):
    q2 = query[...] * jnp.asarray(SCALE, BF16)
    k2, v2 = keys[...], values[...]
    grad_t = grad[...].astype(F32).T
    product = grad_t * context_t[...].astype(F32)
    k_t = k2.T
    inv = [inverse[h : h + 1] for h in range(2)]
    scaled_t = jnp.concatenate([grad_t[:HEAD_DIM] * inv[0], grad_t[HEAD_DIM:] * inv[1]], 0).astype(
        BF16
    )
    scaled = scaled_t.T
    dq, dk, dv = [], 0.0, 0.0
    for h in range(2):
        rows = slice(h * HEAD_DIM, (h + 1) * HEAD_DIM)
        inner = jnp.sum(product[rows], 0, keepdims=True) * inv[h]
        power = powers[h]
        grad_probs = dot(keep_half(h, v2), scaled_t)
        grad_scores = (power.astype(F32) * (grad_probs - inner)).astype(BF16)
        dv = dv + dot(power, keep_half(h, scaled))
        dk = dk + dot(grad_scores, keep_half(h, q2))
        dq.append(dot(k_t[rows], grad_scores))
    return (jnp.concatenate(dq, 0) * SCALE).astype(BF16).T, dk.astype(BF16), dv.astype(BF16)


def backward_kernel(
    part_d, err_two_h, pull_h, wd_h, wu_h, resid_two_h, normal_one_h, inverse_one, first_t_h,
    query_h, keys_h, values_h, powers_h, inverse, context_t_h, tokens_h, w4_h, vec, sums_in,
    o4, ou, od, ov, input_grad,
    part_u, own_d, err_one, grad_context, grad_in, tokens_t, context_t, sums, sums_up,
    pv, va, vb, *rest,
):
    scratch, (send, recv, load) = rest[:42], rest[42:]
    where = x, y, z, core = place()
    shard, member = z * NX + x, y * 2 + core
    total, width = grad_in.shape
    length = total // 2
    columns = sums_up.shape[1]
    loops = columns // CHUNK
    wire = Wire(send, recv)

    def own_part(part):
        return lambda yy, core, zz, xx: part[yy * 2 + core, zz, xx]

    d = Chunk("d", wire, where, part_d, lambda yy, core, zz, xx: own_d[yy, zz, xx], scratch[:7])
    u = Chunk("u", wire, where, part_u, own_part(part_u), scratch[7:14])

    chunks = {"d": d, "u": u}

    def rows_of(s):
        return pl.ds(pl.multiple_of(s * length, length), length)

    def block(j):
        return pl.ds(pl.multiple_of(j * CHUNK, CHUNK), CHUNK)

    own_loads = [
        pltpu.make_async_copy(part_d.at[yy * 2 + core], own_d.at[yy], load.at[0, yy])
        for yy in range(2)
    ]
    gain_one = vec[3:4].astype(F32)
    sums[...] = sums_in[...]
    sums_up[...] = jnp.zeros_like(sums_up)

    def feed_back(wd, wu, pull, err_two, normal_one, first_t, wo):
        first_loads = [
            pltpu.make_async_copy(err_two_h, err_two, load.at[1, 0]),
            pltpu.make_async_copy(resid_two_h, grad_in, load.at[1, 1]),
            pltpu.make_async_copy(normal_one_h, normal_one, load.at[1, 2]),
            pltpu.make_async_copy(w4_h.at[3], wo, load.at[1, 3]),
        ]
        late_loads = [
            pltpu.make_async_copy(first_t_h, first_t, load.at[2, 0]),
            pltpu.make_async_copy(context_t_h, context_t, load.at[2, 2]),
        ]

        def loads(j):
            return [
                pltpu.make_async_copy(wd_h.at[block(j)], wd.at[block(j)], load.at[3, j]),
                pltpu.make_async_copy(pull_h.at[:, block(j)], pull.at[:, block(j)], load.at[4, j]),
                pltpu.make_async_copy(wu_h.at[:, block(j)], wu.at[:, block(j)], load.at[5, j]),
            ]

        first_loads[0].start()
        for c in loads(0):
            c.start()
        for c in own_loads + first_loads[1:]:
            c.start()
        for j in range(1, loops):
            for c in loads(j):
                c.start()
        for c in late_loads:
            c.start()
        greet(all_peers())
        d.start("core")
        first_loads[0].wait()

        @pl.loop(0, 2 * loops)
        def _(t):
            j = t % loops
            rows = rows_of(t // loops)

            @pl.when(t < loops)
            def _():
                for c in loads(j)[:2]:
                    c.wait()

            grads = dot_t(err_two[rows, :], wd[block(j), :])
            low = (grads * pull[rows, block(j)].astype(F32)).astype(BF16)
            pull[rows, block(j)] = low
            sums_up[:, block(j)] += jnp.sum(low.astype(F32), 0, keepdims=True)

            @pl.when(t == OWN_LOADED)
            def _():
                for c in own_loads:
                    c.wait()

            run_at(chunks, BACKWARD_PLAN, "hidden", t, 2 * loops)

        for c in late_loads[:1]:
            c.wait()

        @pl.loop(0, 4)
        def _(m):
            cols = pl.ds(pl.multiple_of(m * width, width), width)
            part_u[m] = dot(first_t[...], pull[:, cols]).astype(BF16).reshape(part_u.shape[1:])
            run_at(chunks, BACKWARD_PLAN, "grad up", m, 4)

        u.start("core")
        for c in first_loads[1:] + late_loads[1:]:
            c.wait()
        for j in range(loops):
            loads(j)[2].wait()

        @pl.loop(0, 2)
        def _(s):
            rows = rows_of(s)
            grad_first = grad_in[rows, :] + dot_t(pull[rows, :], wu[...])
            run_at(chunks, BACKWARD_PLAN, "first", s, 2)
            normal = normal_one[rows, :]
            note(sums, 3, grad_first * normal)
            note(sums, 4, grad_first)
            resid = pull_back(grad_first * gain_one, normal, inverse_one[rows, :])
            grad_in[rows, :] = resid
            low = resid.astype(BF16)
            err_one[rows, :] = low
            note(sums, 2, low.astype(F32))
            grad_context[rows, :] = dot_t(low, wo[...]).astype(BF16)
            run_at(chunks, BACKWARD_PLAN, "norm", s, 2)

    pl.run_scoped(
        feed_back,
        pltpu.VMEM((columns, width), BF16),
        pltpu.VMEM((width, columns), BF16),
        pltpu.VMEM((total, columns), BF16),
        pltpu.VMEM((total, width), BF16),
        pltpu.VMEM((total, width), F32),
        pltpu.VMEM((width, total), BF16),
        pltpu.VMEM((width, width), BF16),
    )

    def attend_and_inputs(qkv, powers, grads, weights, part_q, tokens):
        halves = [part_q.at[0], part_q.at[1]] + [
            part_q.at[2, :, :, :, :, pl.ds(i * PAIR, PAIR)] for i in range(2)
        ]
        q = [
            Chunk(f"q{i}", wire, where, p, own_part(p), scratch[14 + 7 * i : 21 + 7 * i])
            for i, p in enumerate(halves)
        ]
        chunks.update({c.name: c for c in q})

        def loads(t):
            pair, s = t // 2, t % 2
            rows, cols = rows_of(s), pl.ds(pl.multiple_of(pair * PAIR, PAIR), PAIR)
            return [
                pltpu.make_async_copy(a.at[rows, cols], qkv.at[s, i], load.at[6 + i, s])
                for i, a in enumerate((query_h, keys_h, values_h))
            ] + [
                pltpu.make_async_copy(
                    powers_h.at[s, pl.ds(pair * 2, 2)], powers.at[s], load.at[9, s]
                )
            ]

        weight_loads = [
            pltpu.make_async_copy(
                w4_h.at[i, :, pl.ds(g * GROUP, GROUP)],
                weights.at[g, :, pl.ds(i * GROUP, GROUP)],
                load.at[10 + g, i],
            )
            for g in range(3)
            for i in range(3)
        ]
        tokens_load = pltpu.make_async_copy(tokens_h, tokens, load.at[2, 1])
        for c in loads(0) + [tokens_load] + weight_loads:
            c.start()

        @pl.loop(0, 3)
        def _(g):
            @pl.loop(0, 4)
            def _(k):
                t = g * 4 + k
                pair, s = t // 2, t % 2

                @pl.when(t < 11)
                def _():
                    for c in loads(t + 1):
                        c.start()

                for c in loads(t):
                    c.wait()
                rows, cols = rows_of(s), pl.ds(pl.multiple_of(pair * PAIR, PAIR), PAIR)
                values = attend_back_step(
                    qkv.at[s, 0], qkv.at[s, 1], qkv.at[s, 2], powers.at[s],
                    inverse.at[s, pair], context_t.at[cols, rows], grad_context.at[rows, cols],
                )
                for i, value in enumerate(values):
                    lane = pl.multiple_of(i * GROUP + (pair % 2) * PAIR, PAIR)
                    grads[g, rows, pl.ds(lane, PAIR)] = value
                run_at(chunks, BACKWARD_PLAN, "attend", t, 12)

            @pl.when(g == 0)
            def _():
                tokens_load.wait()
                tokens_t[...] = tokens[...].T

            cols = pl.ds(pl.multiple_of(g * GROUP, GROUP), GROUP)
            for i in range(3):
                lanes = slice(i * GROUP, (i + 1) * GROUP)
                part_q[g, i] = (
                    dot(tokens_t[...], grads[g, :, lanes])
                    .astype(BF16)
                    .reshape(NZ, NX, ROWS, GROUP)
                )
            part_q[g, 3] = (
                dot(context_t[...], err_one[:, cols]).astype(BF16).reshape(NZ, NX, ROWS, GROUP)
            )
            for i in range(2):

                @pl.when(g == i)
                def _():
                    q[i].start("core")

            @pl.when(g == 2)
            def _():
                q[2].start("core")
                q[3].start("core")

            sums[0:1, cols] = jnp.sum(grads[g, :, :GROUP].astype(F32), 0, keepdims=True)
            sums[1:2, cols] = jnp.sum(grads[g, :, 2 * GROUP :].astype(F32), 0, keepdims=True)
            run_at(chunks, BACKWARD_PLAN, "weights", g, 3)

        pv[...] = jnp.zeros_like(pv)
        lanes = lax.broadcasted_iota(jnp.int32, (width, NX * NZ * 128), 1)
        rows = lax.broadcasted_iota(jnp.int32, (width, NX * NZ * 128), 0)
        pick = (rows == (lanes // 128) * ROWS + lanes % 128) & (lanes % 128 < ROWS)
        spread8 = lax.dot_general(
            sums[...], pick.astype(F32), (((1,), (0,)), ((), ())),
            precision=lax.Precision.HIGHEST, preferred_element_type=F32,
        )
        per = columns // (NX * NZ)
        for f in range(NX * NZ):
            pv[f, 0:8, :] = spread8[:, f * 128 : (f + 1) * 128]
            for i in range(3):
                first = f * per + i * 128
                pv[f, 8 + i : 9 + i, :] = sums_up[:, first : first + 128]

        def to_owner(k):
            to = (shard + k) % (NX * NZ)
            return wire.copy(("v", k), pv.at[to], va.at[k - 1], {"dp": member, "fsdp": to})

        for k in range(1, NX * NZ):
            to_owner(k).start()
        for c in weight_loads:
            c.wait()
        out = []
        for i in range(3):
            lanes = slice(i * GROUP, (i + 1) * GROUP)
            summed = grad_in[:, lanes]
            for g in range(3):
                summed = summed + dot_t(grads[g], weights[g, lanes, :])
            grad_in[:, lanes] = summed
            c = pltpu.make_async_copy(
                grad_in.at[:, lanes], input_grad.at[:, lanes], load.at[13, i]
            )
            c.start()
            out.append(c)
            run_events(chunks, BACKWARD_PLAN.get(("inputs", i), ()))

        for k in range(1, NX * NZ):
            to_owner(k).wait_recv()
        partial = pv[shard]
        for k in range(NX * NZ - 1):
            partial = partial + va[k]
        vb[member] = partial

        def to_member(i):
            dy, dc = ((0, 1), (1, 0), (1, 1))[i]
            peer = at(x, (y + dy) % 2, z, (core + dc) % 2)
            return wire.copy(("w", i), vb.at[member], vb.at[member], peer)

        for i in range(3):
            to_member(i).start()
        run_events(chunks, BACKWARD_PLAN["drain one"])
        for i in range(3):
            to_member(i).wait_recv()
        ov[...] = (vb[0] + vb[1]) + (vb[2] + vb[3])
        d.done()
        od[...] = d.fin[...]
        run_events(chunks, BACKWARD_PLAN["drain two"])
        u.done()
        ou[...] = u.fin[...]
        run_events(chunks, BACKWARD_PLAN["drain three"])
        first = 0
        for c in q:
            c.done()
            last = first + c.fin.shape[2]
            o4[:, :, first:last] = c.fin[...]
            first = last
        for c in out:
            c.wait()
        for c in [d, u] + q:
            c.drain()
        for k in range(1, NX * NZ):
            to_owner(k).wait_send()
        for i in range(3):
            to_member(i).wait_send()

    pl.run_scoped(
        attend_and_inputs,
        pltpu.VMEM((2, 3, length, PAIR), BF16),
        pltpu.VMEM((2, 2, length, length), BF16),
        pltpu.VMEM((3, total, width), BF16),
        pltpu.VMEM((3, width, width), BF16),
        pltpu.VMEM((3, 4, NZ, NX, ROWS, GROUP), BF16),
        pltpu.VMEM((total, width), BF16),
    )


def backward(
    part_d, err_two, pull, wd, wu, resid_two, normal_one, inverse_one, first_t,
    query, keys, values, powers, inverse, context_t, rows, w4, vec, sums_in,
):
    total, width = rows.shape
    columns = wu.shape[1]
    per = columns // (NX * NZ)
    hbm, vmem = pl.BlockSpec(memory_space=pl.ANY), pl.BlockSpec(memory_space=pltpu.VMEM)
    d_block, copies = part_d.shape[3:], 7 + 3 + 6 * (2 + 2 + 2 + 3 + 2 + 1)
    scratch = [
        pltpu.VMEM((4, NZ, NX, ROWS, width), BF16),
        pltpu.VMEM((2, NZ, NX) + d_block, BF16),
        pltpu.VMEM((total, width), BF16),
        pltpu.VMEM((total, width), BF16),
        pltpu.VMEM((total, width), F32),
        pltpu.VMEM((width, total), BF16),
        pltpu.VMEM((width, total), BF16),
        pltpu.VMEM((8, width), F32),
        pltpu.VMEM((1, columns), F32),
        pltpu.VMEM((NX * NZ, 16, 128), F32),
        pltpu.VMEM((NX * NZ - 1, 16, 128), F32),
        pltpu.VMEM((4, 16, 128), F32),
    ]
    scratch += Chunk.scratch(*d_block) + Chunk.scratch(ROWS, width)
    scratch += Chunk.scratch(ROWS, GROUP) * 2 + Chunk.scratch(ROWS, PAIR) * 2
    scratch += [pltpu.SemaphoreType.DMA((copies,))] * 2 + [pltpu.SemaphoreType.DMA((14, 4))]
    return pl.pallas_call(
        backward_kernel,
        name="backward",
        in_specs=[hbm] * 7 + [vmem] + [hbm] * 5 + [vmem] + [hbm] * 3 + [vmem] * 2,
        out_specs=[vmem] * 4 + [hbm],
        out_shape=[
            Shape((4, ROWS, width), BF16),
            Shape((4, ROWS, width), BF16),
            Shape((4,) + part_d.shape[3:], BF16),
            Shape((16, 128), F32),
            Shape((total, width), F32),
        ],
        scratch_shapes=scratch,
        compiler_params=params(collective_id=1, has_side_effects=True),
    )(
        part_d, err_two, pull, wd, wu, resid_two, normal_one, inverse_one, first_t,
        query, keys, values, powers, inverse, context_t, rows, w4, vec, sums_in,
    )


def finish_kernel(layer_in, grad_in, o4, ou, od, ov, layer_out, input_grad, *rest):
    outs, (layer_v, grad_v, sem) = rest[:15], rest[15:]
    half = grad_v.shape[0] // 2
    spans = [slice(0, half), slice(half, 2 * half)]
    takes = [pltpu.make_async_copy(layer_in, layer_v, sem.at[0])]
    gives = [pltpu.make_async_copy(layer_v, layer_out, sem.at[1])]
    for i, span in enumerate(spans):
        takes.append(pltpu.make_async_copy(grad_in.at[span], grad_v.at[span], sem.at[2 + i]))
        gives.append(pltpu.make_async_copy(grad_v.at[span], input_grad.at[span], sem.at[4 + i]))
    for c in takes:
        c.start()
    width = o4.shape[2]
    for take, give in zip(takes, gives):
        take.wait()
        give.start()
    for i in range(4):
        outs[i][...] = o4[i].astype(F32)
        outs[4][:, i * width : (i + 1) * width] = ou[i].astype(F32)
        rows = od.shape[1]
        outs[5][:, i * rows : (i + 1) * rows] = od[i].astype(F32).T
        outs[7 + i][...] = ov[i : i + 1, :ROWS]
        outs[11 + i][...] = ov[4 + i : 5 + i, :ROWS]
    outs[6][...] = jnp.concatenate([ov[8 + i : 9 + i, :] for i in range(3)], 1).reshape(4 * ROWS)
    for give in gives:
        give.wait()


def finish(layer_out, input_grad, o4, ou, od, ov):
    width = o4.shape[2]
    hbm, vmem = pl.BlockSpec(memory_space=pl.ANY), pl.BlockSpec(memory_space=pltpu.VMEM)
    return pl.pallas_call(
        finish_kernel,
        name="finish",
        in_specs=[hbm] * 2 + [vmem] * 4,
        out_specs=[hbm] * 2 + [vmem] * 15,
        out_shape=[Shape(layer_out.shape, BF16), Shape(input_grad.shape, F32)]
        + [Shape((ROWS, width), F32)] * 4
        + [Shape((ROWS, 4 * width), F32), Shape((od.shape[2], 4 * od.shape[1]), F32)]
        + [Shape((4 * ROWS,), F32)]
        + [Shape((1, ROWS), F32)] * 8,
        scratch_shapes=[
            pltpu.VMEM(layer_out.shape, BF16),
            pltpu.VMEM(input_grad.shape, F32),
            pltpu.SemaphoreType.DMA((6,)),
        ],
        compiler_params=params(),
    )(layer_out, input_grad, o4, ou, od, ov)


def fused_layer(
    tokens, counts, cotangent, query_weight, key_weight, value_weight, out_weight, query_bias,
    value_bias, out_bias, attention_gain, attention_shift, up_weight, up_bias, down_weight,
    down_bias, feed_gain, feed_shift,
):
    width = tokens.shape[2]
    shards = NX * NZ
    columns = up_weight.shape[1]
    rows = tokens.reshape(-1, width)
    vectors = (
        query_bias, value_bias, out_bias, attention_gain, attention_shift, down_bias, feed_gain,
        feed_shift, up_bias,
    )
    (
        w4, wu, wd, layer_out, query, keys, values, powers, context_t, first_t, err_two, resid_two,
        normal_one, pull, part_d, vec8, inverse, inverse_one, sums,
    ) = forward(
        counts, rows, vectors, cotangent.reshape(-1, width), query_weight, key_weight, value_weight,
        out_weight, up_weight, down_weight,
    )
    o4, ou, od, ov, input_grad = backward(
        part_d, err_two, pull, wd.reshape(columns, width), wu.reshape(width, columns), resid_two,
        normal_one, inverse_one, first_t, query, keys, values, powers, inverse, context_t, rows,
        w4.reshape(4, width, width), vec8, sums,
    )
    layer_out, input_grad, gq, gk, gv, go, gu, gd, gub, *v = finish(
        layer_out, input_grad, o4, ou, od, ov
    )
    v = [i.reshape(-1) for i in v]
    return (
        layer_out.reshape(tokens.shape),
        input_grad.reshape(tokens.shape),
        gq, gk, gv, go, v[0], v[1], v[2], v[3], v[4], gu, gub, gd, v[5], v[6], v[7],
    )


def exact_gelu(value):
    return jax.nn.gelu(value, approximate=False)


def norm_forward(resid, gain, shift):
    average = jnp.mean(resid, axis=-1, keepdims=True)
    centred = resid - average
    spread = jnp.mean(centred * centred, axis=-1, keepdims=True)
    inverse = lax.rsqrt(spread + epsilon)
    normal = centred * inverse
    return (normal * gain + shift, normal, inverse)


def norm_backward(grad_out, normal, inverse, gain):
    scaled = grad_out * gain
    first_mean = jnp.mean(scaled, axis=-1, keepdims=True)
    second_mean = jnp.mean(scaled * normal, axis=-1, keepdims=True)
    grad_resid = inverse * (scaled - first_mean - normal * second_mean)
    return (grad_resid, jnp.sum(grad_out * normal, 0), jnp.sum(grad_out, 0))


def linear(rows, weight):
    return jnp.dot(rows, weight, preferred_element_type=jnp.float32)


def linear_back(grads, weight):
    return lax.dot_general(
        grads, weight, (((1,), (1,)), ((), ())), preferred_element_type=jnp.float32
    )


def outer_sum(rows, grads):
    return lax.dot_general(
        rows, grads, (((0,), (0,)), ((), ())), preferred_element_type=jnp.float32
    )


def column_sum(grads):
    return jnp.sum(grads.astype(jnp.float32), 0)


def on_device(
    tokens,
    counts,
    cotangent,
    query_weight,
    key_weight,
    value_weight,
    out_weight,
    query_bias,
    value_bias,
    out_bias,
    attention_gain,
    attention_shift,
    up_weight,
    up_bias,
    down_weight,
    down_bias,
    feed_gain,
    feed_shift,
):
    slots, length, width = tokens.shape
    heads = width // HEAD_DIM
    factor = HEAD_DIM ** (-0.5)
    positions = jnp.arange(length, dtype=jnp.int32)

    def split_heads(value):
        return value.reshape(slots, length, heads, HEAD_DIM)

    def masked_scores(query, keys, count):
        raw = jnp.einsum("qhd,khd->hqk", query, keys, preferred_element_type=jnp.float32)
        live = positions < count
        return jnp.where(live[None, None, :], raw * factor, -1000000000.0)

    def attend_forward(block):
        query, keys, values, count = block
        scores = masked_scores(query, keys, count)
        highest = jnp.max(scores, axis=-1, keepdims=True)
        powers = jnp.exp(scores - highest)
        totals = jnp.sum(powers, axis=-1, keepdims=True)
        probs = (powers / totals).astype(jnp.bfloat16)
        context = jnp.einsum("hqk,khd->qhd", probs, values, preferred_element_type=jnp.float32)
        return (context.reshape(length, width), highest + jnp.log(totals))

    def attend_backward(block):
        query, keys, values, count, logsum, grad_context = block
        scores = masked_scores(query, keys, count)
        probs = jnp.exp(scores - logsum)
        probs_low = probs.astype(jnp.bfloat16)
        grad_probs = jnp.einsum(
            "qhd,khd->hqk", grad_context, values, preferred_element_type=jnp.float32
        )
        inner = jnp.sum(probs * grad_probs, axis=-1, keepdims=True)
        grad_scores = (probs * (grad_probs - inner) * factor).astype(jnp.bfloat16)
        grad_query = jnp.einsum(
            "hqk,khd->qhd", grad_scores, keys, preferred_element_type=jnp.float32
        )
        grad_keys = jnp.einsum(
            "hqk,qhd->khd", grad_scores, query, preferred_element_type=jnp.float32
        )
        grad_values = jnp.einsum(
            "hqk,qhd->khd", probs_low, grad_context, preferred_element_type=jnp.float32
        )
        return (
            grad_query.reshape(length, width).astype(jnp.bfloat16),
            grad_keys.reshape(length, width).astype(jnp.bfloat16),
            grad_values.reshape(length, width).astype(jnp.bfloat16),
        )

    attention_set = (
        lax.all_gather(query_weight, "fsdp", axis=0, tiled=True),
        lax.all_gather(key_weight, "fsdp", axis=0, tiled=True),
        lax.all_gather(value_weight, "fsdp", axis=0, tiled=True),
        lax.all_gather(out_weight, "fsdp", axis=0, tiled=True),
        lax.all_gather(query_bias, "fsdp", axis=0, tiled=True),
        lax.all_gather(value_bias, "fsdp", axis=0, tiled=True),
        lax.all_gather(out_bias, "fsdp", axis=0, tiled=True),
        lax.all_gather(attention_gain, "fsdp", axis=0, tiled=True),
        lax.all_gather(attention_shift, "fsdp", axis=0, tiled=True),
    )
    feed_set = (
        lax.all_gather(up_weight, "fsdp", axis=0, tiled=True),
        lax.all_gather(up_bias, "fsdp", axis=0, tiled=True),
        lax.all_gather(down_weight, "fsdp", axis=0, tiled=True),
        lax.all_gather(down_bias, "fsdp", axis=0, tiled=True),
        lax.all_gather(feed_gain, "fsdp", axis=0, tiled=True),
        lax.all_gather(feed_shift, "fsdp", axis=0, tiled=True),
    )
    whole_query, whole_key, whole_value, whole_out = (
        attention_set[0],
        attention_set[1],
        attention_set[2],
        attention_set[3],
    )
    whole_up, whole_down = (feed_set[0], feed_set[2])
    rows = tokens.reshape(-1, width)
    query = (linear(rows, whole_query) + attention_set[4].astype(jnp.float32)).astype(jnp.bfloat16)
    keys = linear(rows, whole_key).astype(jnp.bfloat16)
    values = (linear(rows, whole_value) + attention_set[5].astype(jnp.float32)).astype(jnp.bfloat16)
    context_rows, logsum = lax.map(
        attend_forward, (split_heads(query), split_heads(keys), split_heads(values), counts)
    )
    context = context_rows.reshape(-1, width).astype(jnp.bfloat16)
    branch = linear(context, whole_out) + attention_set[6].astype(jnp.float32)
    gain_one = attention_set[7].astype(jnp.float32)
    first, normal_one, inverse_one = norm_forward(
        rows.astype(jnp.float32) + branch, gain_one, attention_set[8].astype(jnp.float32)
    )
    first_low = first.astype(jnp.bfloat16)
    hidden = linear(first_low, whole_up) + feed_set[1].astype(jnp.float32)
    activated, gelu_pull = jax.vjp(exact_gelu, hidden)
    act_low = activated.astype(jnp.bfloat16)
    second = linear(act_low, whole_down) + feed_set[3].astype(jnp.float32)
    gain_two = feed_set[4].astype(jnp.float32)
    output, normal_two, inverse_two = norm_forward(
        first + second, gain_two, feed_set[5].astype(jnp.float32)
    )
    live = (positions[None, :] < counts[:, None]).reshape(-1, 1)
    layer_out = jnp.where(live, output, 0.0).astype(jnp.bfloat16).reshape(tokens.shape)
    back_feed = (
        lax.all_gather(up_weight, "fsdp", axis=0, tiled=True),
        lax.all_gather(down_weight, "fsdp", axis=0, tiled=True),
    )
    back_up, back_down = (back_feed[0], back_feed[1])
    grad_y = jnp.where(live, cotangent.reshape(-1, width).astype(jnp.float32), 0.0)
    resid_two, grad_feed_gain, grad_feed_shift = norm_backward(
        grad_y, normal_two, inverse_two, gain_two
    )
    err_two = resid_two.astype(jnp.bfloat16)
    grad_down_weight = outer_sum(act_low, err_two)
    grad_down_bias = column_sum(err_two)
    grad_act = linear_back(err_two, back_down)
    grad_hidden = gelu_pull(grad_act)[0].astype(jnp.bfloat16)
    grad_up_weight = outer_sum(first_low, grad_hidden)
    grad_up_bias = column_sum(grad_hidden)
    grad_first = resid_two + linear_back(grad_hidden, back_up)
    feed_shards = (
        lax.psum_scatter(
            grad_up_weight.astype(jnp.bfloat16), "fsdp", scatter_dimension=0, tiled=True
        ).astype(jnp.float32),
        lax.psum_scatter(
            grad_up_bias.astype(jnp.bfloat16), "fsdp", scatter_dimension=0, tiled=True
        ).astype(jnp.float32),
        lax.psum_scatter(
            grad_down_weight.astype(jnp.bfloat16), "fsdp", scatter_dimension=0, tiled=True
        ).astype(jnp.float32),
        lax.psum_scatter(
            grad_down_bias.astype(jnp.bfloat16), "fsdp", scatter_dimension=0, tiled=True
        ).astype(jnp.float32),
        lax.psum_scatter(
            grad_feed_gain.astype(jnp.bfloat16), "fsdp", scatter_dimension=0, tiled=True
        ).astype(jnp.float32),
        lax.psum_scatter(
            grad_feed_shift.astype(jnp.bfloat16), "fsdp", scatter_dimension=0, tiled=True
        ).astype(jnp.float32),
    )
    back_attention = (
        lax.all_gather(query_weight, "fsdp", axis=0, tiled=True),
        lax.all_gather(key_weight, "fsdp", axis=0, tiled=True),
        lax.all_gather(value_weight, "fsdp", axis=0, tiled=True),
        lax.all_gather(out_weight, "fsdp", axis=0, tiled=True),
    )
    back_query, back_key, back_value, back_out = (
        back_attention[0],
        back_attention[1],
        back_attention[2],
        back_attention[3],
    )
    resid_one, grad_attention_gain, grad_attention_shift = norm_backward(
        grad_first, normal_one, inverse_one, gain_one
    )
    err_one = resid_one.astype(jnp.bfloat16)
    grad_out_weight = outer_sum(context, err_one)
    grad_out_bias = column_sum(err_one)
    grad_context = linear_back(err_one, back_out).astype(jnp.bfloat16)
    grad_query, grad_keys, grad_values = lax.map(
        attend_backward,
        (
            split_heads(query),
            split_heads(keys),
            split_heads(values),
            counts,
            logsum,
            split_heads(grad_context),
        ),
    )
    grad_query = grad_query.reshape(-1, width)
    grad_keys = grad_keys.reshape(-1, width)
    grad_values = grad_values.reshape(-1, width)
    grad_query_weight = outer_sum(rows, grad_query)
    grad_key_weight = outer_sum(rows, grad_keys)
    grad_value_weight = outer_sum(rows, grad_values)
    grad_query_bias = column_sum(grad_query)
    grad_value_bias = column_sum(grad_values)
    input_grad = (
        resid_one
        + linear_back(grad_query, back_query)
        + linear_back(grad_keys, back_key)
        + linear_back(grad_values, back_value)
    )
    attention_shards = (
        lax.psum_scatter(
            grad_query_weight.astype(jnp.bfloat16), "fsdp", scatter_dimension=0, tiled=True
        ).astype(jnp.float32),
        lax.psum_scatter(
            grad_key_weight.astype(jnp.bfloat16), "fsdp", scatter_dimension=0, tiled=True
        ).astype(jnp.float32),
        lax.psum_scatter(
            grad_value_weight.astype(jnp.bfloat16), "fsdp", scatter_dimension=0, tiled=True
        ).astype(jnp.float32),
        lax.psum_scatter(
            grad_out_weight.astype(jnp.bfloat16), "fsdp", scatter_dimension=0, tiled=True
        ).astype(jnp.float32),
        lax.psum_scatter(
            grad_query_bias.astype(jnp.bfloat16), "fsdp", scatter_dimension=0, tiled=True
        ).astype(jnp.float32),
        lax.psum_scatter(
            grad_value_bias.astype(jnp.bfloat16), "fsdp", scatter_dimension=0, tiled=True
        ).astype(jnp.float32),
        lax.psum_scatter(
            grad_out_bias.astype(jnp.bfloat16), "fsdp", scatter_dimension=0, tiled=True
        ).astype(jnp.float32),
        lax.psum_scatter(
            grad_attention_gain.astype(jnp.bfloat16), "fsdp", scatter_dimension=0, tiled=True
        ).astype(jnp.float32),
        lax.psum_scatter(
            grad_attention_shift.astype(jnp.bfloat16), "fsdp", scatter_dimension=0, tiled=True
        ).astype(jnp.float32),
    )
    summed = lax.psum(
        (
            attention_shards[0],
            attention_shards[1],
            attention_shards[2],
            attention_shards[3],
            attention_shards[4],
            attention_shards[5],
            attention_shards[6],
            attention_shards[7],
            attention_shards[8],
            feed_shards[0],
            feed_shards[1],
            feed_shards[2],
            feed_shards[3],
            feed_shards[4],
            feed_shards[5],
        ),
        "dp",
    )
    return (
        layer_out,
        input_grad.reshape(tokens.shape),
        summed[0],
        summed[1],
        summed[2],
        summed[3],
        summed[4],
        summed[5],
        summed[6],
        summed[7],
        summed[8],
        summed[9],
        summed[10],
        summed[11],
        summed[12],
        summed[13],
        summed[14],
    )


def solution(mesh):
    small = mesh.shape["dp"] == 4 and mesh.shape["fsdp"] == NX * NZ
    return jax.shard_map(
        fused_layer if small else on_device,
        mesh=mesh,
        in_specs=(
            P(("dp", "fsdp"), None, None),
            P(("dp", "fsdp")),
            P(("dp", "fsdp"), None, None),
            P("fsdp", None),
            P("fsdp", None),
            P("fsdp", None),
            P("fsdp", None),
            P("fsdp"),
            P("fsdp"),
            P("fsdp"),
            P("fsdp"),
            P("fsdp"),
            P("fsdp", None),
            P("fsdp"),
            P("fsdp", None),
            P("fsdp"),
            P("fsdp"),
            P("fsdp"),
        ),
        out_specs=(
            P(("dp", "fsdp"), None, None),
            P(("dp", "fsdp"), None, None),
            P("fsdp", None),
            P("fsdp", None),
            P("fsdp", None),
            P("fsdp", None),
            P("fsdp"),
            P("fsdp"),
            P("fsdp"),
            P("fsdp"),
            P("fsdp"),
            P("fsdp", None),
            P("fsdp"),
            P("fsdp", None),
            P("fsdp"),
            P("fsdp"),
            P("fsdp"),
        ),
        check_vma=False,
    )
```

```python
import functools

import jax
import jax.numpy as jnp
from jax import lax
from jax.experimental import pallas as pl
from jax.experimental.pallas import tpu as pltpu
from jax.sharding import PartitionSpec as P

HEAD_DIM = 64
epsilon = 1e-05
F32 = jnp.float32
BF16 = jnp.bfloat16
MESH = pl.DeviceIdType.MESH
VMEM_LIMIT = 63 * 2**20
Shape = jax.ShapeDtypeStruct


def dot(left, right):
    return lax.dot_general(
        left, right, (((1,), (0,)), ((), ())), preferred_element_type=F32
    )


def dot_t(left, right):
    return lax.dot_general(
        left, right, (((1,), (1,)), ((), ())), preferred_element_type=F32
    )


def params(**extra):
    return pltpu.CompilerParams(vmem_limit_bytes=VMEM_LIMIT, **extra)


def whole(shape):
    return pl.BlockSpec(shape, lambda *_: (0,) * len(shape), pipeline_mode=pl.Buffered(1))


NX, NZ, ROWS = 2, 4, 96


def place():
    member = lax.axis_index("dp")
    shard = lax.axis_index("fsdp")
    return shard % NX, member // 2, shard // NX, member % 2


def at(x, y, z, core):
    return {"dp": y * 2 + core, "fsdp": z * NX + x}


def greet(peers):
    barrier = pltpu.get_barrier_semaphore()
    for peer in peers:
        pl.semaphore_signal(barrier, inc=1, device_id=peer, device_id_type=MESH)
    pl.semaphore_wait(barrier, len(peers))


def all_peers():
    x, y, z, core = place()
    near = [at(x, 1 - y, z, core), at(x, y, z, 1 - core)]
    for step in range(1, NX * NZ):
        near.append({"dp": y * 2 + core, "fsdp": (z * NX + x + step) % (NX * NZ)})
    return near


class Wire:
    def __init__(self, send, recv):
        self.send, self.recv, self.slots = send, recv, {}

    def copy(self, key, source, target, peer):
        slot = self.slots.setdefault(key, len(self.slots))
        return pltpu.make_async_remote_copy(
            src_ref=source,
            dst_ref=target,
            send_sem=self.send.at[slot],
            recv_sem=self.recv.at[slot],
            device_id=peer,
            device_id_type=MESH,
        )


QKV_PIECES = ((0, 1), (1, 1), (2, 2), (4, 2))
UP_PIECES = ((0, 512), (512, 256))
DOWN_PIECES = ((0, 256, 'x'), (256, 256, 'y'), (512, 256, ''))
GRAD_DOWN = ((0, 256), (256, 128))
GRAD_UP = ((0, 512), (512, 256))
OWN_LOADED = 3
FORWARD_PLAN = {
    "start": ("q0.plane", "u0.send", "q1.plane", "u1.send", "q0.turn_x", "q0.turn_y", "q1.turn_y", "q1.turn_x", "q2.plane", "d0.send", "q0.rest", "q3.plane", "d1.send", "q2.turn_x", "q2.turn_y", "q0.ready",),
    ("attend", 0): ("q1.rest",),
    ("before", 2): ("q1.ready",),
    ("attend", 2): ("q3.turn_y", "q3.turn_x",),
    ("attend", 3): ("d0.plane", "q2.rest", "u0.plane", "d2.send", "q3.rest",),
    ("before", 4): ("q2.ready",),
    ("attend", 5): ("u1.plane",),
    ("before", 8): ("q3.ready",),
    ("attend", 8): ("u0.turn_y", "u0.turn_x",),
    ("attend", 10): ("d1.turn_x", "d1.plane",),
    ("attend", 11): ("u1.turn_x", "u1.turn_y", "d0.turn_x", "d0.turn_y",),
    ("norm", 0): ("u0.rest",),
    ("norm", 1): ("d2.plane",),
    ("up ready", 0): ("u0.ready",),
    ("up 0", 1): ("d0.rest",),
    ("up 0", 2): ("u1.rest", "d1.turn_y",),
    ("up ready", 1): ("u1.ready", "d2.turn_y", "d1.rest",),
    ("up 1", 0): ("d0.rest2",),
    ("down ready", 0): ("d0.ready", "d2.turn_x", "d1.rest2",),
    ("down ready", 1): ("d1.ready",),
    ("down 1", 0): ("d2.rest",),
    ("down ready", 2): ("d2.ready",),
    "send": ("q1.send", "q2.send", "q3.send",),
}
BACKWARD_PLAN = {
    "start": (),
    "drain": ("q1.total", "q2.total", "q3.total", "q0.relay", "q2.relay", "u0.relay", "q1.relay", "d1.relay", "q3.relay",),
    ("hidden", 3): ("d0.chip",),
    ("grad up 0", 0): ("d1.chip",),
    ("grad up 1", 1): ("d0.turn_x",),
    ("grad up 1", 2): ("d0.turn_y",),
    ("first", 0): ("u1.chip", "u0.chip", "d1.turn_y",),
    ("first", 1): ("d1.turn_x",),
    ("norm", 1): ("u1.turn_y",),
    ("attend", 1): ("d0.depth",),
    ("attend", 3): ("u1.turn_x",),
    ("weights", 0): ("u0.turn_y", "u0.turn_x",),
    ("attend", 5): ("u1.depth", "q0.chip",),
    ("attend", 6): ("d1.depth",),
    ("attend", 7): ("d0.total",),
    ("attend", 8): ("q0.turn_y", "q0.turn_x", "u0.depth",),
    ("attend", 9): ("q1.chip",),
    ("weights", 2): ("q1.turn_x", "q1.turn_y", "q0.depth", "q2.chip",),
    ("inputs", 0): ("q3.chip", "q1.depth", "q2.turn_y", "u1.total", "q2.turn_x",),
    ("inputs", 1): ("q3.turn_x", "q3.turn_y", "q2.depth", "d1.total", "q0.total", "u1.relay", "d0.relay", "u0.total", "q3.depth",),
}


GROUP = 4 * HEAD_DIM
PAIR = 2 * HEAD_DIM
SCALE = HEAD_DIM**-0.5
CHUNK = 1024


def run_events(pieces, events):
    for event in events:
        name, stage = event.split(".")
        getattr(pieces[name], stage)()


def run_at(pieces, plan, prefix, index, count):
    for k in range(count):
        if (prefix, k) in plan:

            @pl.when(index == k)
            def _():
                run_events(pieces, plan[prefix, k])


class Piece:
    def __init__(self, name, wire, where, block):
        self.name, self.wire, self.where, self.block = name, wire, where, block

    def copy(self, key, source, peer):
        return self.wire.copy((self.name, key), source, source, peer)

    def copies(self, stage):
        x, y, z, core = self.where
        member, other = y * 2 + core, (1 - y) * 2 + core
        x_peer, y_peer = at(1 - x, y, z, core), at(x, 1 - y, z, core)
        c_peer = at(x, y, z, 1 - core)
        every, block = slice(None), self.block
        if stage == "depth":
            mine = block(member, z, x)
            plan = [(mine, at(x, y, (z + k) % NZ, core)) for k in range(1, NZ)]
        elif stage == "plane":
            mine = block(member, every, x)
            plan = [(mine, x_peer), (mine, y_peer)]
        elif stage == "turn":
            plan = [
                (block(other, pl.ds(0, 2), x), x_peer),
                (block(member, pl.ds(2, 2), 1 - x), y_peer),
            ]
        else:
            plan = [
                (block(member, every, x), c_peer),
                (block(other, every, x), c_peer),
                (block(member, every, 1 - x), c_peer),
                (block(other, every, 1 - x), c_peer),
            ]
        return [self.copy((stage, i), source, peer) for i, (source, peer) in enumerate(plan)]

    def send(self):
        for c in self.copies("depth"):
            c.start()

    def plane(self):
        for c in self.copies("depth"):
            c.wait_recv()
        for c in self.copies("plane"):
            c.start()
        self.copies("core")[0].start()

    def turn_x(self):
        self.copies("plane")[1].wait_recv()
        self.copies("turn")[0].start()
        self.copies("core")[1].start()

    def turn_y(self):
        self.copies("plane")[0].wait_recv()
        self.copies("turn")[1].start()
        self.copies("core")[2].start()

    def rest(self):
        for c in self.copies("turn"):
            c.wait_recv()
        self.copies("core")[3].start()

    def ready(self):
        for c in self.copies("core"):
            c.wait_recv()

    def drain(self):
        for stage in ("depth", "plane", "turn", "core"):
            for c in self.copies(stage):
                c.wait_send()


class DeepPiece(Piece):
    def __init__(self, name, wire, where, block, axis):
        super().__init__(name, wire, where, block)
        self.axis = axis

    def copies(self, stage):
        x, y, z, core = self.where
        member, other = y * 2 + core, (1 - y) * 2 + core
        x_peer, y_peer = at(1 - x, y, z, core), at(x, 1 - y, z, core)
        c_peer = at(x, y, z, 1 - core)
        by_x, every = self.axis == "x", slice(None)
        near = (member, 1 - x) if by_x else (other, x)
        far = (other, x) if by_x else (member, 1 - x)
        places = [(member, x), near, far, (other, 1 - x)]

        def block(place, zs):
            return self.block(place[0], zs, place[1])

        depth = [at(x, y, (z + k) % NZ, core) for k in range(1, NZ)]
        if stage == "first":
            plan = [(block(places[0], z), x_peer if by_x else y_peer)]
        elif stage == "depth":
            plan = [(block(places[0], z), peer) for peer in depth]
        elif stage == "near depth":
            plan = [(block(places[1], z), peer) for peer in depth]
        elif stage == "last":
            plan = [(block(p, every), y_peer if by_x else x_peer) for p in places[:2]]
        else:
            plan = [(block(p, every), c_peer) for p in places]
        return [self.copy((stage, i), source, peer) for i, (source, peer) in enumerate(plan)]

    def send(self):
        for c in self.copies("first") + self.copies("depth"):
            c.start()

    def plane(self):
        self.copies("first")[0].wait_recv()
        for c in self.copies("near depth"):
            c.start()

    def pass_on(self, stage, i):
        for c in self.copies(stage):
            c.wait_recv()
        self.copies("last")[i].start()
        self.copies("core")[i].start()

    def turn_x(self):
        self.pass_on("depth", 0)

    def turn_y(self):
        self.pass_on("near depth", 1)

    def rest(self):
        self.copies("last")[0].wait_recv()
        self.copies("core")[2].start()

    def rest2(self):
        self.copies("last")[1].wait_recv()
        self.copies("core")[3].start()

    def drain(self):
        for stage in ("first", "depth", "near depth", "last", "core"):
            for c in self.copies(stage):
                c.wait_send()


def half(index, shape):
    lanes = lax.broadcasted_iota(jnp.int32, shape, 1)
    return lanes < HEAD_DIM if index == 0 else lanes >= HEAD_DIM


def keep_half(index, value):
    return jnp.where(half(index, value.shape), value, jnp.zeros_like(value))


def attend_step(hidden_keys, q, k, v, powers, inverse, context_t):
    scaled, v_t = q * jnp.asarray(SCALE, BF16), v.T
    for h in range(2):
        rows = slice(h * HEAD_DIM, (h + 1) * HEAD_DIM)
        scores = dot_t(keep_half(h, k), scaled) + hidden_keys
        highest = jnp.max(scores, 0, keepdims=True)
        power = jnp.exp(scores - highest)
        inv = 1.0 / jnp.sum(power, 0, keepdims=True)
        low = power.astype(BF16)
        powers[h] = low
        inverse[h : h + 1] = inv
        context_t[rows] = (dot(v_t[rows], low) * inv).astype(BF16)


SQRT_HALF = 0.7071067811865476
PDF_SCALE = 0.3989422804014327


def normal_parts(value):
    z = jnp.abs(value) * SQRT_HALF
    t = 1.0 / (1.0 + 0.3275911 * z)
    bell = jnp.exp(-(z * z))
    poly = 1.061405429 * t - 1.453152027
    poly = poly * t + 1.421413741
    poly = poly * t - 0.284496736
    poly = poly * t + 0.254829592
    tail = (0.5 * poly * t) * bell
    return jnp.where(value >= 0, 1.0 - tail, tail), bell * PDF_SCALE


def centre(resid):
    centred = resid - jnp.mean(resid, 1, keepdims=True)
    inv = lax.rsqrt(jnp.mean(centred * centred, 1, keepdims=True) + epsilon)
    return centred * inv, inv


def pull_back(scaled, normal, inv):
    return inv * (
        scaled
        - jnp.mean(scaled, 1, keepdims=True)
        - normal * jnp.mean(scaled * normal, 1, keepdims=True)
    )


def note(sums, row, value):
    sums[row : row + 1] += jnp.sum(value, 0, keepdims=True)


def forward_kernel(
    counts, tokens, qb, vb, ob, ag, ash, db, fg, fsh, ub, cotangent_h, wq, wk, wv, wo, wu_i, wd_i,
    w4_h, wu_h, wd_h, layer_out_h, query_h, keys_h, values_h, powers_h, context_t_h, first_t_h,
    err_two_h, resid_two_h, normal_one_h, pull_h, part_d_h, vec8, inverse, inverse_one, sums,
    w4, wu, wd, gv, up_row, context_t, send, recv, local,
):
    where = x, y, z, core = place()
    shard, member = z * NX + x, y * 2 + core
    total, width = tokens.shape
    length = total // 2
    columns = up_row.shape[1]
    wire = Wire(send, recv)

    def columns_of(first, pairs):
        return lambda who, zs, xs: w4.at[who, zs, xs, :, pl.ds(first * PAIR, pairs * PAIR)]

    def up_part(first, wide):
        return lambda who, zs, xs: wu.at[
            zs, xs, :, pl.ds(pl.multiple_of(who * width + first, 128), wide)
        ]

    def down_part(first, wide):
        return lambda who, zs, xs: wd.at[zs, xs, who, :, pl.ds(first, wide)]

    pieces = {
        f"q{i}": Piece(f"q{i}", wire, where, columns_of(first, pairs))
        for i, (first, pairs) in enumerate(QKV_PIECES)
    }
    for i, part in enumerate(UP_PIECES):
        pieces[f"u{i}"] = Piece(f"u{i}", wire, where, up_part(*part))
    for i, (first, wide, axis) in enumerate(DOWN_PIECES):
        if axis:
            piece = DeepPiece(f"d{i}", wire, where, down_part(first, wide), axis)
        else:
            piece = Piece(f"d{i}", wire, where, down_part(first, wide))
        pieces[f"d{i}"] = piece

    own = [
        pltpu.make_async_copy(wq, w4.at[member, z, x], local.at[0, 0]),
        pltpu.make_async_copy(
            wu_i.at[:, pl.ds(pl.multiple_of(member * width, width), width)],
            wu.at[z, x, :, pl.ds(pl.multiple_of(member * width, width), width)],
            local.at[0, 1],
        ),
        pltpu.make_async_copy(wd_i.at[member], wd.at[z, x, member], local.at[0, 2]),
    ]
    for i, w in enumerate((wq, wk, wv, wo)):

        @pl.when(member == i)
        def _():
            pltpu.make_async_copy(w, w4.at[i, z, x], local.at[0, 0]).start()

    for c in own[1:]:
        c.start()
    gv[shard] = jnp.zeros(gv.shape[1:], F32)
    bias_row = ub[...].astype(F32).reshape(1, 4 * ROWS)
    for i in range(3):
        gv[shard, 8 + i : 9 + i, :] = bias_row[:, i * 128 : (i + 1) * 128]
    for i, vector in enumerate((qb, vb, ob, ag, ash, db, fg, fsh)):
        gv[shard, i : i + 1, 0:ROWS] = vector[...].astype(F32).reshape(1, ROWS)
    greet(all_peers())
    for c in own:
        c.wait()

    def vec_copy(k):
        peer = {"dp": member, "fsdp": (shard + k) % (NX * NZ)}
        return wire.copy(("v", k), gv.at[shard], gv.at[shard], peer)

    pieces["q0"].send()
    for k in range(1, NX * NZ):
        vec_copy(k).start()
    run_events(pieces, FORWARD_PLAN["send"])
    sums[...] = jnp.zeros_like(sums)
    run_events(pieces, FORWARD_PLAN["start"][:1])
    for k in range(1, NX * NZ):
        vec_copy(k).wait_recv()
    lanes = lax.broadcasted_iota(jnp.int32, (128, width), 0)
    features = lax.broadcasted_iota(jnp.int32, (128, width), 1)
    per = columns // (NX * NZ)
    joined = jnp.zeros((8, width), F32)
    for f in range(NX * NZ):
        pick = (features == f * ROWS + lanes) & (lanes < ROWS)
        joined = joined + dot(gv[f, 0:8, :].astype(BF16), pick.astype(F32).astype(BF16))
        for i in range(3):
            up_row[:, f * per + i * 128 : f * per + (i + 1) * 128] = gv[f, 8 + i : 9 + i, :]
    vec8[...] = joined
    run_events(pieces, FORWARD_PLAN["start"][1:])

    def attention(qkv, powers):
        def outs(pair, s):
            rows = pl.ds(pl.multiple_of(s * length, length), length)
            cols = pl.ds(pl.multiple_of(pair * PAIR, PAIR), PAIR)
            return [
                pltpu.make_async_copy(qkv.at[s, i], a.at[rows, cols], local.at[1 + i, s])
                for i, a in enumerate((query_h, keys_h, values_h))
            ] + [
                pltpu.make_async_copy(
                    powers.at[s], powers_h.at[s, pl.ds(pair * 2, 2)], local.at[4, s]
                )
            ]

        @pl.loop(0, 12)
        def _(t):
            pair, s = t // 2, t % 2
            rows = pl.ds(pl.multiple_of(s * length, length), length)
            cols = pl.ds(pl.multiple_of(pair * PAIR, PAIR), PAIR)
            run_at(pieces, FORWARD_PLAN, "before", t, 12)

            @pl.when(t >= 2)
            def _():
                for c in outs(pair, s):
                    c.wait()

            weights = jnp.concatenate(
                [w4[i, :, :, :, cols].reshape(width, PAIR) for i in range(3)], 1
            )
            together = dot(tokens[rows, :], weights)
            q = (together[:, :PAIR] + vec8[0:1, cols]).astype(BF16)
            k = together[:, PAIR : 2 * PAIR].astype(BF16)
            v = (together[:, 2 * PAIR :] + vec8[1:2, cols]).astype(BF16)
            qkv[s, 0], qkv[s, 1], qkv[s, 2] = q, k, v
            key_rows = lax.broadcasted_iota(jnp.int32, (length, 1), 0)
            hidden_keys = jnp.where(key_rows < counts[s], 0.0, -1000000000.0)
            attend_step(
                hidden_keys, q, k, v, powers.at[s], inverse.at[s, pair], context_t.at[cols, rows]
            )
            for c in outs(pair, s):
                c.start()
            run_at(pieces, FORWARD_PLAN, "attend", t, 12)

        for s in range(2):
            for c in outs(5, s):
                c.wait()

    pl.run_scoped(
        attention,
        pltpu.VMEM((2, 3, length, PAIR), BF16),
        pltpu.VMEM((2, 2, length, length), BF16),
    )

    def feed(act, pull, first_low, first_t, err_two, err_two_t, normal_one, resid_two, low_out, cotangent, part_d):
        v = [vec8[i : i + 1] for i in range(8)]
        out_bias, gain_one, shift_one, down_bias, gain_two, shift_two = v[2:]
        loads = [pltpu.make_async_copy(cotangent_h, cotangent, local.at[5, 0])]
        outs = [
            pltpu.make_async_copy(w4, w4_h, local.at[5, 1]),
            pltpu.make_async_copy(context_t, context_t_h, local.at[5, 2]),
        ]
        for c in loads + outs:
            c.start()

        def keep(source, target, slot):
            c = pltpu.make_async_copy(source, target, local.at[6 + slot // 4, slot % 4])
            c.start()
            outs.append(c)

        def rows_of(s):
            return pl.ds(pl.multiple_of(s * length, length), length)

        @pl.loop(0, 2)
        def _(s):
            rows = rows_of(s)
            r1 = (
                tokens[rows, :].astype(F32)
                + dot(context_t[:, rows].T, w4[3].reshape(width, width))
                + out_bias
            )
            normal, inv = centre(r1)
            normal_one[rows, :] = normal
            inverse_one[rows, :] = inv
            low = (normal * gain_one + shift_one).astype(BF16)
            first_low[rows, :] = low
            first_t[:, rows] = low.T
            run_at(pieces, FORWARD_PLAN, "norm", s, 2)

        keep(normal_one, normal_one_h, 0)
        keep(first_t, first_t_h, 1)
        for i, (first, wide) in enumerate(UP_PIECES):
            run_events(pieces, FORWARD_PLAN["up ready", i])

            @pl.loop(0, 4)
            def _(m):
                cols = pl.ds(pl.multiple_of(m * width + first, 128), wide)
                weight = wu[:, :, :, cols].reshape(width, wide)
                for s in range(2):
                    rows = slice(s * length, (s + 1) * length)
                    hidden = dot(first_low[rows, :], weight) + up_row[:, cols]
                    cdf, density = normal_parts(hidden)
                    act[rows, cols] = (hidden * cdf).astype(BF16)
                    pull[rows, cols] = (cdf + hidden * density).astype(BF16)
                run_at(pieces, FORWARD_PLAN, f"up {i}", m, 4)

        keep(wu, wu_h, 2)
        keep(pull, pull_h, 3)
        for c in loads:
            c.wait()
        for i, (first, wide, _) in enumerate(DOWN_PIECES):
            run_events(pieces, FORWARD_PLAN["down ready", i])

            @pl.loop(0, 2)
            def _(s):
                rows = rows_of(s)
                weight = wd[:, :, :, :, first : first + wide].reshape(columns, wide)
                resid_two[rows, first : first + wide] = dot(act[rows, :], weight)
                run_at(pieces, FORWARD_PLAN, f"down {i}", s, 2)

        keep(wd, wd_h, 4)

        @pl.loop(0, 2)
        def _(s):
            rows = rows_of(s)
            first = normal_one[rows, :] * gain_one + shift_one
            normal, inv = centre(first + resid_two[rows, :] + down_bias)
            live = lax.broadcasted_iota(jnp.int32, (length, 1), 0) < counts[s]
            low_out[rows, :] = jnp.where(live, normal * gain_two + shift_two, 0.0).astype(BF16)
            grad_y = jnp.where(live, cotangent[rows, :].astype(F32), 0.0)
            resid = pull_back(grad_y * gain_two, normal, inv)
            resid_two[rows, :] = resid
            low = resid.astype(BF16)
            err_two[rows, :] = low
            err_two_t[:, rows] = low.T
            note(sums, 6, grad_y * normal)
            note(sums, 7, grad_y)
            note(sums, 5, low.astype(F32))

        keep(low_out, layer_out_h, 5)
        keep(err_two, err_two_h, 6)
        keep(resid_two, resid_two_h, 7)

        @pl.loop(0, NZ)
        def _(zz):
            cols = pl.ds(pl.multiple_of(zz * NX * per, per), NX * per)
            grad = dot(err_two_t[...], act[:, cols]).astype(BF16)
            for xx in range(NX):
                part_d[:, zz, xx] = grad[:, xx * per : (xx + 1) * per].reshape(4, width // 4, per)

        keep(part_d, part_d_h, 8)
        for c in outs:
            c.wait()
        for p in pieces.values():
            p.drain()
        for k in range(1, NX * NZ):
            vec_copy(k).wait_send()

    pl.run_scoped(
        feed,
        pltpu.VMEM((total, columns), BF16),
        pltpu.VMEM((total, columns), BF16),
        pltpu.VMEM((total, width), BF16),
        pltpu.VMEM((width, total), BF16),
        pltpu.VMEM((total, width), BF16),
        pltpu.VMEM((width, total), BF16),
        pltpu.VMEM((total, width), F32),
        pltpu.VMEM((total, width), F32),
        pltpu.VMEM((total, width), BF16),
        pltpu.VMEM((total, width), BF16),
        pltpu.VMEM((4, NZ, NX, width // 4, per), BF16),
    )


def forward(counts, rows, vectors, cotangent, wq, wk, wv, wo, wu, wd):
    total, width = rows.shape
    columns = wu.shape[1]
    slots, length = 2, total // 2
    heads = width // HEAD_DIM
    per = columns // (NX * NZ)
    copies = 7 + (len(QKV_PIECES) + len(UP_PIECES) + len(DOWN_PIECES)) * 13
    hbm, vmem = pl.BlockSpec(memory_space=pl.ANY), pl.BlockSpec(memory_space=pltpu.VMEM)
    w4_shape = (4, NZ, NX, ROWS, width)
    wu_shape = (NZ, NX, ROWS, columns)
    wd_shape = (NZ, NX, 4, ROWS, width)
    return pl.pallas_call(
        forward_kernel,
        name="forward",
        in_specs=[pl.BlockSpec(memory_space=pltpu.SMEM)] + [vmem] * 10 + [hbm] * 7,
        out_specs=[hbm] * 15 + [vmem] * 4,
        out_shape=[
            Shape(w4_shape, BF16),
            Shape(wu_shape, BF16),
            Shape(wd_shape, BF16),
            Shape((total, width), BF16),
            Shape((total, width), BF16),
            Shape((total, width), BF16),
            Shape((total, width), BF16),
            Shape((slots, heads, length, length), BF16),
            Shape((width, total), BF16),
            Shape((width, total), BF16),
            Shape((total, width), BF16),
            Shape((total, width), F32),
            Shape((total, width), F32),
            Shape((total, columns), BF16),
            Shape((4, NZ, NX, width // 4, per), BF16),
            Shape((8, width), F32),
            Shape((slots, heads // 2, 2, length), F32),
            Shape((total, 1), F32),
            Shape((8, width), F32),
        ],
        scratch_shapes=[
            pltpu.VMEM(w4_shape, BF16),
            pltpu.VMEM(wu_shape, BF16),
            pltpu.VMEM(wd_shape, BF16),
            pltpu.VMEM((NX * NZ, 16, 128), F32),
            pltpu.VMEM((1, columns), F32),
            pltpu.VMEM((width, total), BF16),
            pltpu.SemaphoreType.DMA((copies,)),
            pltpu.SemaphoreType.DMA((copies,)),
            pltpu.SemaphoreType.DMA((9, 4)),
        ],
        compiler_params=params(collective_id=0, has_side_effects=True),
    )(counts, rows, *vectors, cotangent, wq, wk, wv, wo, wu, wd.reshape(4, ROWS, width))


class Chunk:
    def __init__(self, name, wire, where, part, mine, scratch):
        self.name, self.wire, self.where = name, wire, where
        self.part, self.mine = part, mine
        self.rc, self.bx, self.by, self.cx, self.cy, self.bz, self.fin = scratch

    @staticmethod
    def scratch(a, b):
        return [
            pltpu.VMEM((2, NZ, NX, a, b), BF16),
            pltpu.VMEM((2, 2, a, b), BF16),
            pltpu.VMEM((2, NX, a, b), BF16),
            pltpu.VMEM((2, a, b), BF16),
            pltpu.VMEM((2, a, b), BF16),
            pltpu.VMEM((NZ - 1, a, b), BF16),
            pltpu.VMEM((4, a, b), BF16),
        ]

    def copies(self, stage):
        x, y, z, core = self.where
        member, other = y * 2 + core, (1 - y) * 2 + core
        x_peer, y_peer = at(1 - x, y, z, core), at(x, 1 - y, z, core)
        c_peer = at(x, y, z, 1 - core)
        rc, fin = self.rc, self.fin
        if stage == "core":
            plan = [(self.part.at[yy * 2 + 1 - core], rc.at[yy], c_peer) for yy in range(2)]
        elif stage == "plane":
            plan = [
                (rc.at[:, pl.ds(0, 2), 1 - x], self.bx, x_peer),
                (rc.at[1 - y, pl.ds(2, 2)], self.by, y_peer),
            ]
        elif stage == "turn":
            plan = [
                (rc.at[1 - y, pl.ds(0, 2), x], self.cy, y_peer),
                (rc.at[y, pl.ds(2, 2), 1 - x], self.cx, x_peer),
            ]
        elif stage == "depth":
            plan = [
                (rc.at[y, (z + k) % NZ, x], self.bz.at[k - 1], at(x, y, (z + k) % NZ, core))
                for k in range(1, NZ)
            ]
        elif stage == "spread":
            plan = [(fin.at[member], fin.at[member], peer) for peer in (y_peer, c_peer)]
        else:
            plan = [(fin.at[other], fin.at[other], c_peer)]
        return [
            self.wire.copy((self.name, stage, i), source, target, peer)
            for i, (source, target, peer) in enumerate(plan)
        ]

    def start(self, stage):
        for c in self.copies(stage):
            c.start()

    def arrive(self, stage):
        for c in self.copies(stage):
            c.wait_recv()

    def chip(self):
        core = self.where[3]
        self.arrive("core")
        rc, mine = self.rc, self.mine
        for yy in range(2):

            @pl.loop(0, NZ)
            def _(zz):
                for xx in range(NX):
                    rc[yy, zz, xx] = rc[yy, zz, xx] + mine(yy, core, zz, xx)

        self.start("plane")

    def turn_y(self):
        x, y, z, core = self.where
        rc, bx = self.rc, self.bx
        self.copies("plane")[0].wait_recv()

        @pl.loop(0, 2)
        def _(zz):
            for yy in range(2):
                rc[yy, zz, x] = rc[yy, zz, x] + bx[yy, zz]

        self.copies("turn")[0].start()

    def turn_x(self):
        x, y, z, core = self.where
        rc, by = self.rc, self.by
        self.copies("plane")[1].wait_recv()

        @pl.loop(0, 2)
        def _(zz):
            for xx in range(NX):
                rc[y, 2 + zz, xx] = rc[y, 2 + zz, xx] + by[zz, xx]

        self.copies("turn")[1].start()

    def depth(self):
        x, y, z, core = self.where
        rc, cx, cy = self.rc, self.cx, self.cy
        self.arrive("turn")

        @pl.loop(0, 2)
        def _(zz):
            rc[y, zz, x] = rc[y, zz, x] + cy[zz]
            rc[y, 2 + zz, x] = rc[y, 2 + zz, x] + cx[zz]

        self.start("depth")

    def total(self):
        x, y, z, core = self.where
        self.arrive("depth")
        summed = self.rc[y, z, x].astype(F32)
        for k in range(NZ - 1):
            summed = summed + self.bz[k].astype(F32)
        self.fin[y * 2 + core] = summed.astype(BF16)
        self.start("spread")

    def relay(self):
        self.copies("spread")[0].wait_recv()
        self.start("relay")

    def done(self):
        self.copies("spread")[1].wait_recv()
        self.arrive("relay")

    def drain(self):
        for stage in ("core", "plane", "turn", "depth", "spread", "relay"):
            for c in self.copies(stage):
                c.wait_send()


def attend_back_step(query, keys, values, powers, inverse, context_t, grad):
    q2 = query[...] * jnp.asarray(SCALE, BF16)
    k2, v2 = keys[...], values[...]
    grad_t = grad[...].astype(F32).T
    product = grad_t * context_t[...].astype(F32)
    k_t = k2.T
    inv = [inverse[h : h + 1] for h in range(2)]
    scaled_t = jnp.concatenate([grad_t[:HEAD_DIM] * inv[0], grad_t[HEAD_DIM:] * inv[1]], 0).astype(
        BF16
    )
    scaled = scaled_t.T
    dq, dk, dv = [], 0.0, 0.0
    for h in range(2):
        rows = slice(h * HEAD_DIM, (h + 1) * HEAD_DIM)
        inner = jnp.sum(product[rows], 0, keepdims=True) * inv[h]
        power = powers[h]
        grad_probs = dot(keep_half(h, v2), scaled_t)
        grad_scores = (power.astype(F32) * (grad_probs - inner)).astype(BF16)
        dv = dv + dot(power, keep_half(h, scaled))
        dk = dk + dot(grad_scores, keep_half(h, q2))
        dq.append(dot(k_t[rows], grad_scores))
    return (jnp.concatenate(dq, 0) * SCALE).astype(BF16).T, dk.astype(BF16), dv.astype(BF16)


def backward_kernel(
    part_d, err_two_h, pull_h, wd_h, wu_h, resid_two_h, normal_one_h, inverse_one, first_t_h,
    query_h, keys_h, values_h, powers_h, inverse, context_t_h, tokens_h, w4_h, vec, sums_in,
    o4, ou, od, ov, input_grad,
    part_u, own_d, err_one, grad_context, grad_in, tokens_t, context_t, sums, sums_up,
    pv, va, vb, *rest,
):
    count = 7 * (len(GRAD_DOWN) + len(GRAD_UP) + 4)
    scratch, (send, recv, load) = list(rest[:count]), rest[count:]
    where = x, y, z, core = place()
    shard, member = z * NX + x, y * 2 + core
    total, width = grad_in.shape
    length = total // 2
    columns = sums_up.shape[1]
    loops = columns // CHUNK
    wire = Wire(send, recv)

    def lanes_of(part, first, wide):
        return part.at[:, :, :, :, pl.ds(first, wide)]

    def own_part(part):
        return lambda yy, core, zz, xx: part[yy * 2 + core, zz, xx]

    def take():
        mine = scratch[:7]
        del scratch[:7]
        return mine

    d, u = [], []
    for i, part in enumerate(GRAD_DOWN):
        own = lanes_of(own_d, *part)
        d.append(
            Chunk(
                f"d{i}", wire, where, lanes_of(part_d, *part),
                lambda yy, core, zz, xx, own=own: own[yy, zz, xx], take(),
            )
        )
    for i, part in enumerate(GRAD_UP):
        rows_u = lanes_of(part_u, *part)
        u.append(Chunk(f"u{i}", wire, where, rows_u, own_part(rows_u), take()))
    chunks = {c.name: c for c in d + u}

    def rows_of(s):
        return pl.ds(pl.multiple_of(s * length, length), length)

    def block(j):
        return pl.ds(pl.multiple_of(j * CHUNK, CHUNK), CHUNK)

    own_loads = [
        pltpu.make_async_copy(part_d.at[yy * 2 + core], own_d.at[yy], load.at[0, yy])
        for yy in range(2)
    ]
    gain_one = vec[3:4].astype(F32)
    sums[...] = sums_in[...]
    sums_up[...] = jnp.zeros_like(sums_up)

    def feed_back(wd, wu, pull, err_two, normal_one, first_t, wo):
        first_loads = [
            pltpu.make_async_copy(err_two_h, err_two, load.at[1, 0]),
            pltpu.make_async_copy(resid_two_h, grad_in, load.at[1, 1]),
            pltpu.make_async_copy(normal_one_h, normal_one, load.at[1, 2]),
            pltpu.make_async_copy(w4_h.at[3], wo, load.at[1, 3]),
        ]
        late_loads = [
            pltpu.make_async_copy(first_t_h, first_t, load.at[2, 0]),
            pltpu.make_async_copy(context_t_h, context_t, load.at[2, 2]),
        ]

        def loads(j):
            return [
                pltpu.make_async_copy(wd_h.at[block(j)], wd.at[block(j)], load.at[3, j]),
                pltpu.make_async_copy(pull_h.at[:, block(j)], pull.at[:, block(j)], load.at[4, j]),
                pltpu.make_async_copy(wu_h.at[:, block(j)], wu.at[:, block(j)], load.at[5, j]),
            ]

        first_loads[0].start()
        for c in loads(0):
            c.start()
        for c in own_loads + first_loads[1:]:
            c.start()
        for j in range(1, loops):
            for c in loads(j):
                c.start()
        for c in late_loads:
            c.start()
        greet(all_peers())
        for c in d:
            c.start("core")
        run_events(chunks, BACKWARD_PLAN["start"])
        first_loads[0].wait()

        @pl.loop(0, 2 * loops)
        def _(t):
            j = t % loops
            rows = rows_of(t // loops)

            @pl.when(t < loops)
            def _():
                for c in loads(j)[:2]:
                    c.wait()

            grads = dot_t(err_two[rows, :], wd[block(j), :])
            low = (grads * pull[rows, block(j)].astype(F32)).astype(BF16)
            pull[rows, block(j)] = low
            sums_up[:, block(j)] += jnp.sum(low.astype(F32), 0, keepdims=True)

            @pl.when(t == OWN_LOADED)
            def _():
                for c in own_loads:
                    c.wait()

            run_at(chunks, BACKWARD_PLAN, "hidden", t, 2 * loops)

        for c in late_loads[:1]:
            c.wait()

        for i, (first, wide) in enumerate(GRAD_UP):

            @pl.loop(0, 4)
            def _(m):
                cols = pl.ds(pl.multiple_of(m * width + first, 128), wide)
                part_u[m, :, :, :, first : first + wide] = (
                    dot(first_t[...], pull[:, cols]).astype(BF16).reshape(NZ, NX, ROWS, wide)
                )

                @pl.when(m == 3)
                def _():
                    u[i].start("core")

                run_at(chunks, BACKWARD_PLAN, f"grad up {i}", m, 4)

        for c in first_loads[1:] + late_loads[1:]:
            c.wait()
        for j in range(loops):
            loads(j)[2].wait()

        @pl.loop(0, 2)
        def _(s):
            rows = rows_of(s)
            grad_first = grad_in[rows, :] + dot_t(pull[rows, :], wu[...])
            run_at(chunks, BACKWARD_PLAN, "first", s, 2)
            normal = normal_one[rows, :]
            note(sums, 3, grad_first * normal)
            note(sums, 4, grad_first)
            resid = pull_back(grad_first * gain_one, normal, inverse_one[rows, :])
            grad_in[rows, :] = resid
            low = resid.astype(BF16)
            err_one[rows, :] = low
            note(sums, 2, low.astype(F32))
            grad_context[rows, :] = dot_t(low, wo[...]).astype(BF16)
            run_at(chunks, BACKWARD_PLAN, "norm", s, 2)

    pl.run_scoped(
        feed_back,
        pltpu.VMEM((columns, width), BF16),
        pltpu.VMEM((width, columns), BF16),
        pltpu.VMEM((total, columns), BF16),
        pltpu.VMEM((total, width), BF16),
        pltpu.VMEM((total, width), F32),
        pltpu.VMEM((width, total), BF16),
        pltpu.VMEM((width, width), BF16),
    )

    def attend_and_inputs(qkv, powers, grads, weights, part_q, tokens):
        halves = [part_q.at[0], part_q.at[1]] + [
            part_q.at[2, :, :, :, :, pl.ds(i * PAIR, PAIR)] for i in range(2)
        ]
        q = [
            Chunk(f"q{i}", wire, where, p, own_part(p), take())
            for i, p in enumerate(halves)
        ]
        chunks.update({c.name: c for c in q})

        def loads(t):
            pair, s = t // 2, t % 2
            rows, cols = rows_of(s), pl.ds(pl.multiple_of(pair * PAIR, PAIR), PAIR)
            return [
                pltpu.make_async_copy(a.at[rows, cols], qkv.at[s, i], load.at[6 + i, s])
                for i, a in enumerate((query_h, keys_h, values_h))
            ] + [
                pltpu.make_async_copy(
                    powers_h.at[s, pl.ds(pair * 2, 2)], powers.at[s], load.at[9, s]
                )
            ]

        weight_loads = [
            pltpu.make_async_copy(
                w4_h.at[i, :, pl.ds(g * GROUP, GROUP)],
                weights.at[g, :, pl.ds(i * GROUP, GROUP)],
                load.at[10 + g, i],
            )
            for g in range(3)
            for i in range(3)
        ]
        tokens_load = pltpu.make_async_copy(tokens_h, tokens, load.at[2, 1])
        for c in loads(0) + [tokens_load] + weight_loads:
            c.start()

        @pl.loop(0, 3)
        def _(g):
            @pl.loop(0, 4)
            def _(k):
                t = g * 4 + k
                pair, s = t // 2, t % 2

                @pl.when(t < 11)
                def _():
                    for c in loads(t + 1):
                        c.start()

                for c in loads(t):
                    c.wait()
                rows, cols = rows_of(s), pl.ds(pl.multiple_of(pair * PAIR, PAIR), PAIR)
                values = attend_back_step(
                    qkv.at[s, 0], qkv.at[s, 1], qkv.at[s, 2], powers.at[s],
                    inverse.at[s, pair], context_t.at[cols, rows], grad_context.at[rows, cols],
                )
                for i, value in enumerate(values):
                    lane = pl.multiple_of(i * GROUP + (pair % 2) * PAIR, PAIR)
                    grads[g, rows, pl.ds(lane, PAIR)] = value
                run_at(chunks, BACKWARD_PLAN, "attend", t, 12)

            @pl.when(g == 0)
            def _():
                tokens_load.wait()
                tokens_t[...] = tokens[...].T

            cols = pl.ds(pl.multiple_of(g * GROUP, GROUP), GROUP)
            for i in range(3):
                lanes = slice(i * GROUP, (i + 1) * GROUP)
                part_q[g, i] = (
                    dot(tokens_t[...], grads[g, :, lanes])
                    .astype(BF16)
                    .reshape(NZ, NX, ROWS, GROUP)
                )
            part_q[g, 3] = (
                dot(context_t[...], err_one[:, cols]).astype(BF16).reshape(NZ, NX, ROWS, GROUP)
            )
            for i in range(2):

                @pl.when(g == i)
                def _():
                    q[i].start("core")

            @pl.when(g == 2)
            def _():
                q[2].start("core")
                q[3].start("core")

            sums[0:1, cols] = jnp.sum(grads[g, :, :GROUP].astype(F32), 0, keepdims=True)
            sums[1:2, cols] = jnp.sum(grads[g, :, 2 * GROUP :].astype(F32), 0, keepdims=True)
            run_at(chunks, BACKWARD_PLAN, "weights", g, 3)

        pv[...] = jnp.zeros_like(pv)
        lanes = lax.broadcasted_iota(jnp.int32, (width, NX * NZ * 128), 1)
        rows = lax.broadcasted_iota(jnp.int32, (width, NX * NZ * 128), 0)
        pick = (rows == (lanes // 128) * ROWS + lanes % 128) & (lanes % 128 < ROWS)
        spread8 = lax.dot_general(
            sums[...], pick.astype(F32), (((1,), (0,)), ((), ())),
            precision=lax.Precision.HIGHEST, preferred_element_type=F32,
        )
        per = columns // (NX * NZ)
        for f in range(NX * NZ):
            pv[f, 0:8, :] = spread8[:, f * 128 : (f + 1) * 128]
            for i in range(3):
                first = f * per + i * 128
                pv[f, 8 + i : 9 + i, :] = sums_up[:, first : first + 128]

        def to_owner(k):
            to = (shard + k) % (NX * NZ)
            return wire.copy(("v", k), pv.at[to], va.at[k - 1], {"dp": member, "fsdp": to})

        for k in range(1, NX * NZ):
            to_owner(k).start()
        for c in weight_loads:
            c.wait()
        out = []
        for i in range(3):
            lanes = slice(i * GROUP, (i + 1) * GROUP)
            summed = grad_in[:, lanes]
            for g in range(3):
                summed = summed + dot_t(grads[g], weights[g, lanes, :])
            grad_in[:, lanes] = summed
            c = pltpu.make_async_copy(
                grad_in.at[:, lanes], input_grad.at[:, lanes], load.at[13, i]
            )
            c.start()
            out.append(c)
            run_events(chunks, BACKWARD_PLAN.get(("inputs", i), ()))

        for k in range(1, NX * NZ):
            to_owner(k).wait_recv()
        partial = pv[shard]
        for k in range(NX * NZ - 1):
            partial = partial + va[k]
        vb[member] = partial

        def to_member(i):
            dy, dc = ((0, 1), (1, 0), (1, 1))[i]
            peer = at(x, (y + dy) % 2, z, (core + dc) % 2)
            return wire.copy(("w", i), vb.at[member], vb.at[member], peer)

        for i in range(3):
            to_member(i).start()
        run_events(chunks, BACKWARD_PLAN["drain"])
        for i in range(3):
            to_member(i).wait_recv()
        ov[...] = (vb[0] + vb[1]) + (vb[2] + vb[3])
        for out_ref, group, parts in ((od, d, GRAD_DOWN), (ou, u, GRAD_UP)):
            for c, (first, wide) in zip(group, parts):
                c.done()
                out_ref[:, :, first : first + wide] = c.fin[...]
        first = 0
        for c in q:
            c.done()
            last = first + c.fin.shape[2]
            o4[:, :, first:last] = c.fin[...]
            first = last
        for c in out:
            c.wait()
        for c in d + u + q:
            c.drain()
        for k in range(1, NX * NZ):
            to_owner(k).wait_send()
        for i in range(3):
            to_member(i).wait_send()

    pl.run_scoped(
        attend_and_inputs,
        pltpu.VMEM((2, 3, length, PAIR), BF16),
        pltpu.VMEM((2, 2, length, length), BF16),
        pltpu.VMEM((3, total, width), BF16),
        pltpu.VMEM((3, width, width), BF16),
        pltpu.VMEM((3, 4, NZ, NX, ROWS, GROUP), BF16),
        pltpu.VMEM((total, width), BF16),
    )


def backward(
    part_d, err_two, pull, wd, wu, resid_two, normal_one, inverse_one, first_t,
    query, keys, values, powers, inverse, context_t, rows, w4, vec, sums_in,
):
    total, width = rows.shape
    columns = wu.shape[1]
    per = columns // (NX * NZ)
    hbm, vmem = pl.BlockSpec(memory_space=pl.ANY), pl.BlockSpec(memory_space=pltpu.VMEM)
    d_block, copies = part_d.shape[3:], 7 + 3 + (len(GRAD_DOWN) + len(GRAD_UP) + 4) * 12
    scratch = [
        pltpu.VMEM((4, NZ, NX, ROWS, width), BF16),
        pltpu.VMEM((2, NZ, NX) + d_block, BF16),
        pltpu.VMEM((total, width), BF16),
        pltpu.VMEM((total, width), BF16),
        pltpu.VMEM((total, width), F32),
        pltpu.VMEM((width, total), BF16),
        pltpu.VMEM((width, total), BF16),
        pltpu.VMEM((8, width), F32),
        pltpu.VMEM((1, columns), F32),
        pltpu.VMEM((NX * NZ, 16, 128), F32),
        pltpu.VMEM((NX * NZ - 1, 16, 128), F32),
        pltpu.VMEM((4, 16, 128), F32),
    ]
    for _, wide in GRAD_DOWN:
        scratch += Chunk.scratch(d_block[0], wide)
    for _, wide in GRAD_UP:
        scratch += Chunk.scratch(ROWS, wide)
    scratch += Chunk.scratch(ROWS, GROUP) * 2 + Chunk.scratch(ROWS, PAIR) * 2
    scratch += [pltpu.SemaphoreType.DMA((copies,))] * 2 + [pltpu.SemaphoreType.DMA((14, 4))]
    return pl.pallas_call(
        backward_kernel,
        name="backward",
        in_specs=[hbm] * 7 + [vmem] + [hbm] * 5 + [vmem] + [hbm] * 3 + [vmem] * 2,
        out_specs=[vmem] * 4 + [hbm],
        out_shape=[
            Shape((4, ROWS, width), BF16),
            Shape((4, ROWS, width), BF16),
            Shape((4,) + part_d.shape[3:], BF16),
            Shape((16, 128), F32),
            Shape((total, width), F32),
        ],
        scratch_shapes=scratch,
        compiler_params=params(collective_id=1, has_side_effects=True),
    )(
        part_d, err_two, pull, wd, wu, resid_two, normal_one, inverse_one, first_t,
        query, keys, values, powers, inverse, context_t, rows, w4, vec, sums_in,
    )


def finish_kernel(layer_in, grad_in, o4, ou, od, ov, layer_out, input_grad, *rest):
    outs, (layer_v, grad_v, sem) = rest[:15], rest[15:]
    half = grad_v.shape[0] // 2
    spans = [slice(0, half), slice(half, 2 * half)]
    takes = [pltpu.make_async_copy(layer_in, layer_v, sem.at[0])]
    gives = [pltpu.make_async_copy(layer_v, layer_out, sem.at[1])]
    for i, span in enumerate(spans):
        takes.append(pltpu.make_async_copy(grad_in.at[span], grad_v.at[span], sem.at[2 + i]))
        gives.append(pltpu.make_async_copy(grad_v.at[span], input_grad.at[span], sem.at[4 + i]))
    for c in takes:
        c.start()
    width = o4.shape[2]
    for take, give in zip(takes, gives):
        take.wait()
        give.start()
    for i in range(4):
        outs[i][...] = o4[i].astype(F32)
        outs[4][:, i * width : (i + 1) * width] = ou[i].astype(F32)
        rows = od.shape[1]
        outs[5][:, i * rows : (i + 1) * rows] = od[i].astype(F32).T
        outs[7 + i][...] = ov[i : i + 1, :ROWS]
        outs[11 + i][...] = ov[4 + i : 5 + i, :ROWS]
    outs[6][...] = jnp.concatenate([ov[8 + i : 9 + i, :] for i in range(3)], 1).reshape(4 * ROWS)
    for give in gives:
        give.wait()


def finish(layer_out, input_grad, o4, ou, od, ov):
    width = o4.shape[2]
    hbm, vmem = pl.BlockSpec(memory_space=pl.ANY), pl.BlockSpec(memory_space=pltpu.VMEM)
    return pl.pallas_call(
        finish_kernel,
        name="finish",
        in_specs=[hbm] * 2 + [vmem] * 4,
        out_specs=[hbm] * 2 + [vmem] * 15,
        out_shape=[Shape(layer_out.shape, BF16), Shape(input_grad.shape, F32)]
        + [Shape((ROWS, width), F32)] * 4
        + [Shape((ROWS, 4 * width), F32), Shape((od.shape[2], 4 * od.shape[1]), F32)]
        + [Shape((4 * ROWS,), F32)]
        + [Shape((1, ROWS), F32)] * 8,
        scratch_shapes=[
            pltpu.VMEM(layer_out.shape, BF16),
            pltpu.VMEM(input_grad.shape, F32),
            pltpu.SemaphoreType.DMA((6,)),
        ],
        compiler_params=params(),
    )(layer_out, input_grad, o4, ou, od, ov)


def fused_layer(
    tokens, counts, cotangent, query_weight, key_weight, value_weight, out_weight, query_bias,
    value_bias, out_bias, attention_gain, attention_shift, up_weight, up_bias, down_weight,
    down_bias, feed_gain, feed_shift,
):
    width = tokens.shape[2]
    shards = NX * NZ
    columns = up_weight.shape[1]
    rows = tokens.reshape(-1, width)
    vectors = (
        query_bias, value_bias, out_bias, attention_gain, attention_shift, down_bias, feed_gain,
        feed_shift, up_bias,
    )
    (
        w4, wu, wd, layer_out, query, keys, values, powers, context_t, first_t, err_two, resid_two,
        normal_one, pull, part_d, vec8, inverse, inverse_one, sums,
    ) = forward(
        counts, rows, vectors, cotangent.reshape(-1, width), query_weight, key_weight, value_weight,
        out_weight, up_weight, down_weight,
    )
    o4, ou, od, ov, input_grad = backward(
        part_d, err_two, pull, wd.reshape(columns, width), wu.reshape(width, columns), resid_two,
        normal_one, inverse_one, first_t, query, keys, values, powers, inverse, context_t, rows,
        w4.reshape(4, width, width), vec8, sums,
    )
    layer_out, input_grad, gq, gk, gv, go, gu, gd, gub, *v = finish(
        layer_out, input_grad, o4, ou, od, ov
    )
    v = [i.reshape(-1) for i in v]
    return (
        layer_out.reshape(tokens.shape),
        input_grad.reshape(tokens.shape),
        gq, gk, gv, go, v[0], v[1], v[2], v[3], v[4], gu, gub, gd, v[5], v[6], v[7],
    )


def exact_gelu(value):
    return jax.nn.gelu(value, approximate=False)


def norm_forward(resid, gain, shift):
    average = jnp.mean(resid, axis=-1, keepdims=True)
    centred = resid - average
    spread = jnp.mean(centred * centred, axis=-1, keepdims=True)
    inverse = lax.rsqrt(spread + epsilon)
    normal = centred * inverse
    return (normal * gain + shift, normal, inverse)


def norm_backward(grad_out, normal, inverse, gain):
    scaled = grad_out * gain
    first_mean = jnp.mean(scaled, axis=-1, keepdims=True)
    second_mean = jnp.mean(scaled * normal, axis=-1, keepdims=True)
    grad_resid = inverse * (scaled - first_mean - normal * second_mean)
    return (grad_resid, jnp.sum(grad_out * normal, 0), jnp.sum(grad_out, 0))


def linear(rows, weight):
    return jnp.dot(rows, weight, preferred_element_type=jnp.float32)


def linear_back(grads, weight):
    return lax.dot_general(
        grads, weight, (((1,), (1,)), ((), ())), preferred_element_type=jnp.float32
    )


def outer_sum(rows, grads):
    return lax.dot_general(
        rows, grads, (((0,), (0,)), ((), ())), preferred_element_type=jnp.float32
    )


def column_sum(grads):
    return jnp.sum(grads.astype(jnp.float32), 0)


def on_device(
    tokens,
    counts,
    cotangent,
    query_weight,
    key_weight,
    value_weight,
    out_weight,
    query_bias,
    value_bias,
    out_bias,
    attention_gain,
    attention_shift,
    up_weight,
    up_bias,
    down_weight,
    down_bias,
    feed_gain,
    feed_shift,
):
    slots, length, width = tokens.shape
    heads = width // HEAD_DIM
    factor = HEAD_DIM ** (-0.5)
    positions = jnp.arange(length, dtype=jnp.int32)

    def split_heads(value):
        return value.reshape(slots, length, heads, HEAD_DIM)

    def masked_scores(query, keys, count):
        raw = jnp.einsum("qhd,khd->hqk", query, keys, preferred_element_type=jnp.float32)
        live = positions < count
        return jnp.where(live[None, None, :], raw * factor, -1000000000.0)

    def attend_forward(block):
        query, keys, values, count = block
        scores = masked_scores(query, keys, count)
        highest = jnp.max(scores, axis=-1, keepdims=True)
        powers = jnp.exp(scores - highest)
        totals = jnp.sum(powers, axis=-1, keepdims=True)
        probs = (powers / totals).astype(jnp.bfloat16)
        context = jnp.einsum("hqk,khd->qhd", probs, values, preferred_element_type=jnp.float32)
        return (context.reshape(length, width), highest + jnp.log(totals))

    def attend_backward(block):
        query, keys, values, count, logsum, grad_context = block
        scores = masked_scores(query, keys, count)
        probs = jnp.exp(scores - logsum)
        probs_low = probs.astype(jnp.bfloat16)
        grad_probs = jnp.einsum(
            "qhd,khd->hqk", grad_context, values, preferred_element_type=jnp.float32
        )
        inner = jnp.sum(probs * grad_probs, axis=-1, keepdims=True)
        grad_scores = (probs * (grad_probs - inner) * factor).astype(jnp.bfloat16)
        grad_query = jnp.einsum(
            "hqk,khd->qhd", grad_scores, keys, preferred_element_type=jnp.float32
        )
        grad_keys = jnp.einsum(
            "hqk,qhd->khd", grad_scores, query, preferred_element_type=jnp.float32
        )
        grad_values = jnp.einsum(
            "hqk,qhd->khd", probs_low, grad_context, preferred_element_type=jnp.float32
        )
        return (
            grad_query.reshape(length, width).astype(jnp.bfloat16),
            grad_keys.reshape(length, width).astype(jnp.bfloat16),
            grad_values.reshape(length, width).astype(jnp.bfloat16),
        )

    attention_set = (
        lax.all_gather(query_weight, "fsdp", axis=0, tiled=True),
        lax.all_gather(key_weight, "fsdp", axis=0, tiled=True),
        lax.all_gather(value_weight, "fsdp", axis=0, tiled=True),
        lax.all_gather(out_weight, "fsdp", axis=0, tiled=True),
        lax.all_gather(query_bias, "fsdp", axis=0, tiled=True),
        lax.all_gather(value_bias, "fsdp", axis=0, tiled=True),
        lax.all_gather(out_bias, "fsdp", axis=0, tiled=True),
        lax.all_gather(attention_gain, "fsdp", axis=0, tiled=True),
        lax.all_gather(attention_shift, "fsdp", axis=0, tiled=True),
    )
    feed_set = (
        lax.all_gather(up_weight, "fsdp", axis=0, tiled=True),
        lax.all_gather(up_bias, "fsdp", axis=0, tiled=True),
        lax.all_gather(down_weight, "fsdp", axis=0, tiled=True),
        lax.all_gather(down_bias, "fsdp", axis=0, tiled=True),
        lax.all_gather(feed_gain, "fsdp", axis=0, tiled=True),
        lax.all_gather(feed_shift, "fsdp", axis=0, tiled=True),
    )
    whole_query, whole_key, whole_value, whole_out = (
        attention_set[0],
        attention_set[1],
        attention_set[2],
        attention_set[3],
    )
    whole_up, whole_down = (feed_set[0], feed_set[2])
    rows = tokens.reshape(-1, width)
    query = (linear(rows, whole_query) + attention_set[4].astype(jnp.float32)).astype(jnp.bfloat16)
    keys = linear(rows, whole_key).astype(jnp.bfloat16)
    values = (linear(rows, whole_value) + attention_set[5].astype(jnp.float32)).astype(jnp.bfloat16)
    context_rows, logsum = lax.map(
        attend_forward, (split_heads(query), split_heads(keys), split_heads(values), counts)
    )
    context = context_rows.reshape(-1, width).astype(jnp.bfloat16)
    branch = linear(context, whole_out) + attention_set[6].astype(jnp.float32)
    gain_one = attention_set[7].astype(jnp.float32)
    first, normal_one, inverse_one = norm_forward(
        rows.astype(jnp.float32) + branch, gain_one, attention_set[8].astype(jnp.float32)
    )
    first_low = first.astype(jnp.bfloat16)
    hidden = linear(first_low, whole_up) + feed_set[1].astype(jnp.float32)
    activated, gelu_pull = jax.vjp(exact_gelu, hidden)
    act_low = activated.astype(jnp.bfloat16)
    second = linear(act_low, whole_down) + feed_set[3].astype(jnp.float32)
    gain_two = feed_set[4].astype(jnp.float32)
    output, normal_two, inverse_two = norm_forward(
        first + second, gain_two, feed_set[5].astype(jnp.float32)
    )
    live = (positions[None, :] < counts[:, None]).reshape(-1, 1)
    layer_out = jnp.where(live, output, 0.0).astype(jnp.bfloat16).reshape(tokens.shape)
    back_feed = (
        lax.all_gather(up_weight, "fsdp", axis=0, tiled=True),
        lax.all_gather(down_weight, "fsdp", axis=0, tiled=True),
    )
    back_up, back_down = (back_feed[0], back_feed[1])
    grad_y = jnp.where(live, cotangent.reshape(-1, width).astype(jnp.float32), 0.0)
    resid_two, grad_feed_gain, grad_feed_shift = norm_backward(
        grad_y, normal_two, inverse_two, gain_two
    )
    err_two = resid_two.astype(jnp.bfloat16)
    grad_down_weight = outer_sum(act_low, err_two)
    grad_down_bias = column_sum(err_two)
    grad_act = linear_back(err_two, back_down)
    grad_hidden = gelu_pull(grad_act)[0].astype(jnp.bfloat16)
    grad_up_weight = outer_sum(first_low, grad_hidden)
    grad_up_bias = column_sum(grad_hidden)
    grad_first = resid_two + linear_back(grad_hidden, back_up)
    feed_shards = (
        lax.psum_scatter(
            grad_up_weight.astype(jnp.bfloat16), "fsdp", scatter_dimension=0, tiled=True
        ).astype(jnp.float32),
        lax.psum_scatter(
            grad_up_bias.astype(jnp.bfloat16), "fsdp", scatter_dimension=0, tiled=True
        ).astype(jnp.float32),
        lax.psum_scatter(
            grad_down_weight.astype(jnp.bfloat16), "fsdp", scatter_dimension=0, tiled=True
        ).astype(jnp.float32),
        lax.psum_scatter(
            grad_down_bias.astype(jnp.bfloat16), "fsdp", scatter_dimension=0, tiled=True
        ).astype(jnp.float32),
        lax.psum_scatter(
            grad_feed_gain.astype(jnp.bfloat16), "fsdp", scatter_dimension=0, tiled=True
        ).astype(jnp.float32),
        lax.psum_scatter(
            grad_feed_shift.astype(jnp.bfloat16), "fsdp", scatter_dimension=0, tiled=True
        ).astype(jnp.float32),
    )
    back_attention = (
        lax.all_gather(query_weight, "fsdp", axis=0, tiled=True),
        lax.all_gather(key_weight, "fsdp", axis=0, tiled=True),
        lax.all_gather(value_weight, "fsdp", axis=0, tiled=True),
        lax.all_gather(out_weight, "fsdp", axis=0, tiled=True),
    )
    back_query, back_key, back_value, back_out = (
        back_attention[0],
        back_attention[1],
        back_attention[2],
        back_attention[3],
    )
    resid_one, grad_attention_gain, grad_attention_shift = norm_backward(
        grad_first, normal_one, inverse_one, gain_one
    )
    err_one = resid_one.astype(jnp.bfloat16)
    grad_out_weight = outer_sum(context, err_one)
    grad_out_bias = column_sum(err_one)
    grad_context = linear_back(err_one, back_out).astype(jnp.bfloat16)
    grad_query, grad_keys, grad_values = lax.map(
        attend_backward,
        (
            split_heads(query),
            split_heads(keys),
            split_heads(values),
            counts,
            logsum,
            split_heads(grad_context),
        ),
    )
    grad_query = grad_query.reshape(-1, width)
    grad_keys = grad_keys.reshape(-1, width)
    grad_values = grad_values.reshape(-1, width)
    grad_query_weight = outer_sum(rows, grad_query)
    grad_key_weight = outer_sum(rows, grad_keys)
    grad_value_weight = outer_sum(rows, grad_values)
    grad_query_bias = column_sum(grad_query)
    grad_value_bias = column_sum(grad_values)
    input_grad = (
        resid_one
        + linear_back(grad_query, back_query)
        + linear_back(grad_keys, back_key)
        + linear_back(grad_values, back_value)
    )
    attention_shards = (
        lax.psum_scatter(
            grad_query_weight.astype(jnp.bfloat16), "fsdp", scatter_dimension=0, tiled=True
        ).astype(jnp.float32),
        lax.psum_scatter(
            grad_key_weight.astype(jnp.bfloat16), "fsdp", scatter_dimension=0, tiled=True
        ).astype(jnp.float32),
        lax.psum_scatter(
            grad_value_weight.astype(jnp.bfloat16), "fsdp", scatter_dimension=0, tiled=True
        ).astype(jnp.float32),
        lax.psum_scatter(
            grad_out_weight.astype(jnp.bfloat16), "fsdp", scatter_dimension=0, tiled=True
        ).astype(jnp.float32),
        lax.psum_scatter(
            grad_query_bias.astype(jnp.bfloat16), "fsdp", scatter_dimension=0, tiled=True
        ).astype(jnp.float32),
        lax.psum_scatter(
            grad_value_bias.astype(jnp.bfloat16), "fsdp", scatter_dimension=0, tiled=True
        ).astype(jnp.float32),
        lax.psum_scatter(
            grad_out_bias.astype(jnp.bfloat16), "fsdp", scatter_dimension=0, tiled=True
        ).astype(jnp.float32),
        lax.psum_scatter(
            grad_attention_gain.astype(jnp.bfloat16), "fsdp", scatter_dimension=0, tiled=True
        ).astype(jnp.float32),
        lax.psum_scatter(
            grad_attention_shift.astype(jnp.bfloat16), "fsdp", scatter_dimension=0, tiled=True
        ).astype(jnp.float32),
    )
    summed = lax.psum(
        (
            attention_shards[0],
            attention_shards[1],
            attention_shards[2],
            attention_shards[3],
            attention_shards[4],
            attention_shards[5],
            attention_shards[6],
            attention_shards[7],
            attention_shards[8],
            feed_shards[0],
            feed_shards[1],
            feed_shards[2],
            feed_shards[3],
            feed_shards[4],
            feed_shards[5],
        ),
        "dp",
    )
    return (
        layer_out,
        input_grad.reshape(tokens.shape),
        summed[0],
        summed[1],
        summed[2],
        summed[3],
        summed[4],
        summed[5],
        summed[6],
        summed[7],
        summed[8],
        summed[9],
        summed[10],
        summed[11],
        summed[12],
        summed[13],
        summed[14],
    )


def solution(mesh):
    small = mesh.shape["dp"] == 4 and mesh.shape["fsdp"] == NX * NZ
    return jax.shard_map(
        fused_layer if small else on_device,
        mesh=mesh,
        in_specs=(
            P(("dp", "fsdp"), None, None),
            P(("dp", "fsdp")),
            P(("dp", "fsdp"), None, None),
            P("fsdp", None),
            P("fsdp", None),
            P("fsdp", None),
            P("fsdp", None),
            P("fsdp"),
            P("fsdp"),
            P("fsdp"),
            P("fsdp"),
            P("fsdp"),
            P("fsdp", None),
            P("fsdp"),
            P("fsdp", None),
            P("fsdp"),
            P("fsdp"),
            P("fsdp"),
        ),
        out_specs=(
            P(("dp", "fsdp"), None, None),
            P(("dp", "fsdp"), None, None),
            P("fsdp", None),
            P("fsdp", None),
            P("fsdp", None),
            P("fsdp", None),
            P("fsdp"),
            P("fsdp"),
            P("fsdp"),
            P("fsdp"),
            P("fsdp"),
            P("fsdp", None),
            P("fsdp"),
            P("fsdp", None),
            P("fsdp"),
            P("fsdp"),
            P("fsdp"),
        ),
        check_vma=False,
    )
```

```python
import functools

import jax
import jax.numpy as jnp
from jax import lax
from jax.experimental import pallas as pl
from jax.experimental.pallas import tpu as pltpu
from jax.sharding import PartitionSpec as P

HEAD_DIM = 64
epsilon = 1e-05
F32 = jnp.float32
BF16 = jnp.bfloat16
MESH = pl.DeviceIdType.MESH
VMEM_LIMIT = 63 * 2**20
Shape = jax.ShapeDtypeStruct


def dot(left, right):
    return lax.dot_general(
        left, right, (((1,), (0,)), ((), ())), preferred_element_type=F32
    )


def dot_t(left, right):
    return lax.dot_general(
        left, right, (((1,), (1,)), ((), ())), preferred_element_type=F32
    )


def params(**extra):
    return pltpu.CompilerParams(vmem_limit_bytes=VMEM_LIMIT, **extra)


def whole(shape):
    return pl.BlockSpec(shape, lambda *_: (0,) * len(shape), pipeline_mode=pl.Buffered(1))


NX, NZ, ROWS = 2, 4, 96


def place():
    member = lax.axis_index("dp")
    shard = lax.axis_index("fsdp")
    return shard % NX, member // 2, shard // NX, member % 2


def at(x, y, z, core):
    return {"dp": y * 2 + core, "fsdp": z * NX + x}


def hello(peers):
    barrier = pltpu.get_barrier_semaphore()
    for peer in peers:
        pl.semaphore_signal(barrier, inc=1, device_id=peer, device_id_type=MESH)


def all_here(peers):
    pl.semaphore_wait(pltpu.get_barrier_semaphore(), len(peers))


def greet(peers):
    hello(peers)
    all_here(peers)


def all_peers():
    x, y, z, core = place()
    near = [at(x, 1 - y, z, core), at(x, y, z, 1 - core)]
    for step in range(1, NX * NZ):
        near.append({"dp": y * 2 + core, "fsdp": (z * NX + x + step) % (NX * NZ)})
    return near


class Wire:
    def __init__(self, send, recv):
        self.send, self.recv, self.slots = send, recv, {}

    def copy(self, key, source, target, peer):
        slot = self.slots.setdefault(key, len(self.slots))
        return pltpu.make_async_remote_copy(
            src_ref=source,
            dst_ref=target,
            send_sem=self.send.at[slot],
            recv_sem=self.recv.at[slot],
            device_id=peer,
            device_id_type=MESH,
        )


Q0, Q1, Q2, Q3, U0, U1, D0, D1, D2 = range(9)
PLANE, TURN_X, TURN_Y, REST, REST2, READY, SEND, CHIP, DEPTH, TOTAL, RELAY = range(11)
STAGES = (
    "plane", "turn_x", "turn_y", "rest", "rest2", "ready", "send", "chip", "depth", "total", "relay",
)
START, SENDS, DRAIN, BEFORE, ATTEND, NORM, UP_READY, UP_0, UP_1, DOWN_READY, DOWN_0 = range(11)
DOWN_1, DOWN_2, HIDDEN, GRAD_UP_0, GRAD_UP_1, FIRST, WEIGHTS, INPUTS = range(11, 19)
UP_STEPS, DOWN_STEPS = (UP_0, UP_1), (DOWN_0, DOWN_1, DOWN_2)
GRAD_UP_STEPS = (GRAD_UP_0, GRAD_UP_1)
QKV_PIECES = ((0, 1), (1, 1), (2, 2), (4, 2))
UP_PIECES = ((0, 512), (512, 256))
DOWN_PIECES = ((0, 256, 'x'), (256, 256, 'y'), (512, 256, ''))
GRAD_DOWN = ((0, 256), (256, 128))
GRAD_UP = ((0, 512), (512, 256))
OWN_LOADED = 3
FORWARD_PLAN = {
    START: ((Q0, PLANE), (U0, SEND), (Q1, PLANE), (U1, SEND), (Q0, TURN_X), (Q0, TURN_Y), (Q1, TURN_Y), (Q1, TURN_X), (Q2, PLANE), (D0, SEND), (Q0, REST), (Q3, PLANE), (D1, SEND), (Q2, TURN_X), (Q2, TURN_Y), (Q0, READY),),
    (ATTEND, 0): ((Q1, REST),),
    (BEFORE, 2): ((Q1, READY),),
    (ATTEND, 2): ((Q3, TURN_Y), (Q3, TURN_X),),
    (ATTEND, 3): ((D0, PLANE), (Q2, REST), (U0, PLANE), (D2, SEND), (Q3, REST),),
    (BEFORE, 4): ((Q2, READY),),
    (ATTEND, 5): ((U1, PLANE),),
    (BEFORE, 8): ((Q3, READY),),
    (ATTEND, 8): ((U0, TURN_Y), (U0, TURN_X),),
    (ATTEND, 10): ((D1, TURN_X), (D1, PLANE),),
    (ATTEND, 11): ((U1, TURN_X), (U1, TURN_Y), (D0, TURN_X), (D0, TURN_Y),),
    (NORM, 0): ((U0, REST),),
    (NORM, 1): ((D2, PLANE),),
    (UP_READY, 0): ((U0, READY),),
    (UP_0, 1): ((D0, REST),),
    (UP_0, 2): ((U1, REST), (D1, TURN_Y),),
    (UP_READY, 1): ((U1, READY), (D2, TURN_Y), (D1, REST),),
    (UP_1, 0): ((D0, REST2),),
    (DOWN_READY, 0): ((D0, READY), (D2, TURN_X), (D1, REST2),),
    (DOWN_READY, 1): ((D1, READY),),
    (DOWN_1, 0): ((D2, REST),),
    (DOWN_READY, 2): ((D2, READY),),
    SENDS: ((Q1, SEND), (Q2, SEND), (Q3, SEND),),
}
BACKWARD_PLAN = {
    START: (),
    DRAIN: ((Q1, TOTAL), (Q2, TOTAL), (Q3, TOTAL), (Q0, RELAY), (Q2, RELAY), (U0, RELAY), (Q1, RELAY), (D1, RELAY), (Q3, RELAY),),
    (HIDDEN, 3): ((D0, CHIP),),
    (GRAD_UP_0, 0): ((D1, CHIP),),
    (GRAD_UP_1, 1): ((D0, TURN_X),),
    (GRAD_UP_1, 2): ((D0, TURN_Y),),
    (FIRST, 0): ((U1, CHIP), (U0, CHIP), (D1, TURN_Y),),
    (FIRST, 1): ((D1, TURN_X),),
    (NORM, 1): ((U1, TURN_Y),),
    (ATTEND, 1): ((D0, DEPTH),),
    (ATTEND, 3): ((U1, TURN_X),),
    (WEIGHTS, 0): ((U0, TURN_Y), (U0, TURN_X),),
    (ATTEND, 5): ((U1, DEPTH), (Q0, CHIP),),
    (ATTEND, 6): ((D1, DEPTH),),
    (ATTEND, 7): ((D0, TOTAL),),
    (ATTEND, 8): ((Q0, TURN_Y), (Q0, TURN_X), (U0, DEPTH),),
    (ATTEND, 9): ((Q1, CHIP),),
    (WEIGHTS, 2): ((Q1, TURN_X), (Q1, TURN_Y), (Q0, DEPTH), (Q2, CHIP),),
    (INPUTS, 0): ((Q3, CHIP), (Q1, DEPTH), (Q2, TURN_Y), (U1, TOTAL), (Q2, TURN_X),),
    (INPUTS, 1): ((Q3, TURN_X), (Q3, TURN_Y), (Q2, DEPTH), (D1, TOTAL), (Q0, TOTAL), (U1, RELAY), (D0, RELAY), (U0, TOTAL), (Q3, DEPTH),),
}


GROUP = 4 * HEAD_DIM
PAIR = 2 * HEAD_DIM
SCALE = HEAD_DIM**-0.5
CHUNK = 1024


def run_events(pieces, events):
    for piece, stage in events:
        getattr(pieces[piece], STAGES[stage])()


def run_at(pieces, plan, prefix, index, count):
    for k in range(count):
        if (prefix, k) in plan:

            @pl.when(index == k)
            def _():
                run_events(pieces, plan[prefix, k])


class Piece:
    def __init__(self, name, wire, where, block):
        self.name, self.wire, self.where, self.block = name, wire, where, block

    def copy(self, key, source, peer):
        return self.wire.copy((self.name, key), source, source, peer)

    def copies(self, stage):
        x, y, z, core = self.where
        member, other = y * 2 + core, (1 - y) * 2 + core
        x_peer, y_peer = at(1 - x, y, z, core), at(x, 1 - y, z, core)
        c_peer = at(x, y, z, 1 - core)
        every, block = slice(None), self.block
        if stage == "depth":
            mine = block(member, z, x)
            plan = [(mine, at(x, y, (z + k) % NZ, core)) for k in range(1, NZ)]
        elif stage == "plane":
            mine = block(member, every, x)
            plan = [(mine, x_peer), (mine, y_peer)]
        elif stage == "turn":
            plan = [
                (block(other, pl.ds(0, 2), x), x_peer),
                (block(member, pl.ds(2, 2), 1 - x), y_peer),
            ]
        else:
            plan = [
                (block(member, every, x), c_peer),
                (block(other, every, x), c_peer),
                (block(member, every, 1 - x), c_peer),
                (block(other, every, 1 - x), c_peer),
            ]
        return [self.copy((stage, i), source, peer) for i, (source, peer) in enumerate(plan)]

    def send(self):
        for c in self.copies("depth"):
            c.start()

    def plane(self):
        for c in self.copies("depth"):
            c.wait_recv()
        for c in self.copies("plane"):
            c.start()
        self.copies("core")[0].start()

    def turn_x(self):
        self.copies("plane")[1].wait_recv()
        self.copies("turn")[0].start()
        self.copies("core")[1].start()

    def turn_y(self):
        self.copies("plane")[0].wait_recv()
        self.copies("turn")[1].start()
        self.copies("core")[2].start()

    def rest(self):
        for c in self.copies("turn"):
            c.wait_recv()
        self.copies("core")[3].start()

    def ready(self):
        for c in self.copies("core"):
            c.wait_recv()

    def drain(self):
        for stage in ("depth", "plane", "turn", "core"):
            for c in self.copies(stage):
                c.wait_send()


class DeepPiece(Piece):
    def __init__(self, name, wire, where, block, axis):
        super().__init__(name, wire, where, block)
        self.axis = axis

    def copies(self, stage):
        x, y, z, core = self.where
        member, other = y * 2 + core, (1 - y) * 2 + core
        x_peer, y_peer = at(1 - x, y, z, core), at(x, 1 - y, z, core)
        c_peer = at(x, y, z, 1 - core)
        by_x, every = self.axis == "x", slice(None)
        near = (member, 1 - x) if by_x else (other, x)
        far = (other, x) if by_x else (member, 1 - x)
        places = [(member, x), near, far, (other, 1 - x)]

        def block(place, zs):
            return self.block(place[0], zs, place[1])

        depth = [at(x, y, (z + k) % NZ, core) for k in range(1, NZ)]
        if stage == "first":
            plan = [(block(places[0], z), x_peer if by_x else y_peer)]
        elif stage == "depth":
            plan = [(block(places[0], z), peer) for peer in depth]
        elif stage == "near depth":
            plan = [(block(places[1], z), peer) for peer in depth]
        elif stage == "last":
            plan = [(block(p, every), y_peer if by_x else x_peer) for p in places[:2]]
        else:
            plan = [(block(p, every), c_peer) for p in places]
        return [self.copy((stage, i), source, peer) for i, (source, peer) in enumerate(plan)]

    def send(self):
        for c in self.copies("first") + self.copies("depth"):
            c.start()

    def plane(self):
        self.copies("first")[0].wait_recv()
        for c in self.copies("near depth"):
            c.start()

    def pass_on(self, stage, i):
        for c in self.copies(stage):
            c.wait_recv()
        self.copies("last")[i].start()
        self.copies("core")[i].start()

    def turn_x(self):
        self.pass_on("depth", 0)

    def turn_y(self):
        self.pass_on("near depth", 1)

    def rest(self):
        self.copies("last")[0].wait_recv()
        self.copies("core")[2].start()

    def rest2(self):
        self.copies("last")[1].wait_recv()
        self.copies("core")[3].start()

    def drain(self):
        for stage in ("first", "depth", "near depth", "last", "core"):
            for c in self.copies(stage):
                c.wait_send()


def half(index, shape):
    lanes = lax.broadcasted_iota(jnp.int32, shape, 1)
    return lanes < HEAD_DIM if index == 0 else lanes >= HEAD_DIM


def keep_half(index, value):
    return jnp.where(half(index, value.shape), value, jnp.zeros_like(value))


def attend_step(hidden_keys, q, k, v, powers, inverse, context_t):
    scaled, v_t = q * jnp.asarray(SCALE, BF16), v.T
    for h in range(2):
        rows = slice(h * HEAD_DIM, (h + 1) * HEAD_DIM)
        scores = dot_t(keep_half(h, k), scaled) + hidden_keys
        highest = jnp.max(scores, 0, keepdims=True)
        power = jnp.exp(scores - highest)
        inv = 1.0 / jnp.sum(power, 0, keepdims=True)
        low = power.astype(BF16)
        powers[h] = low
        inverse[h : h + 1] = inv
        context_t[rows] = (dot(v_t[rows], low) * inv).astype(BF16)


SQRT_HALF = 0.7071067811865476
PDF_SCALE = 0.3989422804014327


def normal_parts(value):
    z = jnp.abs(value) * SQRT_HALF
    t = 1.0 / (1.0 + 0.3275911 * z)
    bell = jnp.exp(-(z * z))
    poly = 1.061405429 * t - 1.453152027
    poly = poly * t + 1.421413741
    poly = poly * t - 0.284496736
    poly = poly * t + 0.254829592
    tail = (0.5 * poly * t) * bell
    return jnp.where(value >= 0, 1.0 - tail, tail), bell * PDF_SCALE


def centre(resid):
    centred = resid - jnp.mean(resid, 1, keepdims=True)
    inv = lax.rsqrt(jnp.mean(centred * centred, 1, keepdims=True) + epsilon)
    return centred * inv, inv


def pull_back(scaled, normal, inv):
    return inv * (
        scaled
        - jnp.mean(scaled, 1, keepdims=True)
        - normal * jnp.mean(scaled * normal, 1, keepdims=True)
    )


def note(sums, row, value):
    sums[row : row + 1] += jnp.sum(value, 0, keepdims=True)


def forward_kernel(
    counts, tokens, qb, vb, ob, ag, ash, db, fg, fsh, ub, cotangent_h, wq, wk, wv, wo, wu_i, wd_i,
    w4_h, wu_h, wd_h, layer_out_h, query_h, keys_h, values_h, powers_h, context_t_h, first_t_h,
    err_two_h, resid_two_h, normal_one_h, pull_h, part_d_h, tokens_t_h, vec8, inverse, inverse_one, sums,
    w4, wu, wd, gv, up_row, context_t, tokens_t, send, recv, local,
):
    where = x, y, z, core = place()
    shard, member = z * NX + x, y * 2 + core
    total, width = tokens.shape
    length = total // 2
    columns = up_row.shape[1]
    wire = Wire(send, recv)

    def columns_of(first, pairs):
        return lambda who, zs, xs: w4.at[who, zs, xs, :, pl.ds(first * PAIR, pairs * PAIR)]

    def up_part(first, wide):
        return lambda who, zs, xs: wu.at[
            zs, xs, :, pl.ds(pl.multiple_of(who * width + first, 128), wide)
        ]

    def down_part(first, wide):
        return lambda who, zs, xs: wd.at[zs, xs, who, :, pl.ds(first, wide)]

    pieces = {
        Q0 + i: Piece(Q0 + i, wire, where, columns_of(first, pairs))
        for i, (first, pairs) in enumerate(QKV_PIECES)
    }
    for i, part in enumerate(UP_PIECES):
        pieces[U0 + i] = Piece(U0 + i, wire, where, up_part(*part))
    for i, (first, wide, axis) in enumerate(DOWN_PIECES):
        if axis:
            piece = DeepPiece(D0 + i, wire, where, down_part(first, wide), axis)
        else:
            piece = Piece(D0 + i, wire, where, down_part(first, wide))
        pieces[D0 + i] = piece

    own = [
        pltpu.make_async_copy(wq, w4.at[member, z, x], local.at[0, 0]),
        pltpu.make_async_copy(
            wu_i.at[:, pl.ds(pl.multiple_of(member * width, width), width)],
            wu.at[z, x, :, pl.ds(pl.multiple_of(member * width, width), width)],
            local.at[0, 1],
        ),
        pltpu.make_async_copy(wd_i.at[member], wd.at[z, x, member], local.at[0, 2]),
    ]
    for i, w in enumerate((wq, wk, wv, wo)):

        @pl.when(member == i)
        def _():
            pltpu.make_async_copy(w, w4.at[i, z, x], local.at[0, 0]).start()

    for c in own[1:]:
        c.start()
    gv[shard] = jnp.zeros(gv.shape[1:], F32)
    bias_row = ub[...].astype(F32).reshape(1, 4 * ROWS)
    for i in range(3):
        gv[shard, 8 + i : 9 + i, :] = bias_row[:, i * 128 : (i + 1) * 128]
    for i, vector in enumerate((qb, vb, ob, ag, ash, db, fg, fsh)):
        gv[shard, i : i + 1, 0:ROWS] = vector[...].astype(F32).reshape(1, ROWS)
    greet(all_peers())
    for c in own:
        c.wait()

    def vec_copy(k):
        peer = {"dp": member, "fsdp": (shard + k) % (NX * NZ)}
        return wire.copy(("v", k), gv.at[shard], gv.at[shard], peer)

    pieces[Q0].send()
    for k in range(1, NX * NZ):
        vec_copy(k).start()
    run_events(pieces, FORWARD_PLAN[SENDS])
    tokens_t[...] = tokens[...].T
    tokens_out = pltpu.make_async_copy(tokens_t, tokens_t_h, local.at[5, 3])
    tokens_out.start()
    sums[...] = jnp.zeros_like(sums)
    run_events(pieces, FORWARD_PLAN[START][:1])
    for k in range(1, NX * NZ):
        vec_copy(k).wait_recv()
    lanes = lax.broadcasted_iota(jnp.int32, (128, width), 0)
    features = lax.broadcasted_iota(jnp.int32, (128, width), 1)
    per = columns // (NX * NZ)
    joined = jnp.zeros((8, width), F32)
    for f in range(NX * NZ):
        pick = (features == f * ROWS + lanes) & (lanes < ROWS)
        joined = joined + dot(gv[f, 0:8, :].astype(BF16), pick.astype(F32).astype(BF16))
        for i in range(3):
            up_row[:, f * per + i * 128 : f * per + (i + 1) * 128] = gv[f, 8 + i : 9 + i, :]
    vec8[...] = joined
    run_events(pieces, FORWARD_PLAN[START][1:])

    def attention(qkv, powers):
        def outs(pair, s):
            rows = pl.ds(pl.multiple_of(s * length, length), length)
            cols = pl.ds(pl.multiple_of(pair * PAIR, PAIR), PAIR)
            return [
                pltpu.make_async_copy(qkv.at[s, i], a.at[rows, cols], local.at[1 + i, s])
                for i, a in enumerate((query_h, keys_h, values_h))
            ] + [
                pltpu.make_async_copy(
                    powers.at[s], powers_h.at[s, pl.ds(pair * 2, 2)], local.at[4, s]
                )
            ]

        @pl.loop(0, 12)
        def _(t):
            pair, s = t // 2, t % 2
            rows = pl.ds(pl.multiple_of(s * length, length), length)
            cols = pl.ds(pl.multiple_of(pair * PAIR, PAIR), PAIR)
            run_at(pieces, FORWARD_PLAN, BEFORE, t, 12)

            @pl.when(t >= 2)
            def _():
                for c in outs(pair, s):
                    c.wait()

            weights = jnp.concatenate(
                [w4[i, :, :, :, cols].reshape(width, PAIR) for i in range(3)], 1
            )
            together = dot(tokens[rows, :], weights)
            q = (together[:, :PAIR] + vec8[0:1, cols]).astype(BF16)
            k = together[:, PAIR : 2 * PAIR].astype(BF16)
            v = (together[:, 2 * PAIR :] + vec8[1:2, cols]).astype(BF16)
            qkv[s, 0], qkv[s, 1], qkv[s, 2] = q, k, v
            key_rows = lax.broadcasted_iota(jnp.int32, (length, 1), 0)
            hidden_keys = jnp.where(key_rows < counts[s], 0.0, -1000000000.0)
            attend_step(
                hidden_keys, q, k, v, powers.at[s], inverse.at[s, pair], context_t.at[cols, rows]
            )
            for c in outs(pair, s):
                c.start()
            run_at(pieces, FORWARD_PLAN, ATTEND, t, 12)

        for s in range(2):
            for c in outs(5, s):
                c.wait()

    pl.run_scoped(
        attention,
        pltpu.VMEM((2, 3, length, PAIR), BF16),
        pltpu.VMEM((2, 2, length, length), BF16),
    )

    def feed(act, pull, first_low, first_t, err_two, err_two_t, normal_one, resid_two, low_out, cotangent, part_d):
        v = [vec8[i : i + 1] for i in range(8)]
        out_bias, gain_one, shift_one, down_bias, gain_two, shift_two = v[2:]
        loads = [pltpu.make_async_copy(cotangent_h, cotangent, local.at[5, 0])]
        outs = [
            pltpu.make_async_copy(w4, w4_h, local.at[5, 1]),
            pltpu.make_async_copy(context_t, context_t_h, local.at[5, 2]),
        ]
        for c in loads + outs:
            c.start()
        outs.append(tokens_out)

        def keep(source, target, slot):
            c = pltpu.make_async_copy(source, target, local.at[6 + slot // 4, slot % 4])
            c.start()
            outs.append(c)

        def rows_of(s):
            return pl.ds(pl.multiple_of(s * length, length), length)

        @pl.loop(0, 2)
        def _(s):
            rows = rows_of(s)
            r1 = (
                tokens[rows, :].astype(F32)
                + dot(context_t[:, rows].T, w4[3].reshape(width, width))
                + out_bias
            )
            normal, inv = centre(r1)
            normal_one[rows, :] = normal
            inverse_one[rows, :] = inv
            low = (normal * gain_one + shift_one).astype(BF16)
            first_low[rows, :] = low
            first_t[:, rows] = low.T
            run_at(pieces, FORWARD_PLAN, NORM, s, 2)

        keep(normal_one, normal_one_h, 0)
        keep(first_t, first_t_h, 1)
        for i, (first, wide) in enumerate(UP_PIECES):
            run_events(pieces, FORWARD_PLAN[UP_READY, i])

            @pl.loop(0, 4)
            def _(m):
                cols = pl.ds(pl.multiple_of(m * width + first, 128), wide)
                weight = wu[:, :, :, cols].reshape(width, wide)
                for s in range(2):
                    rows = slice(s * length, (s + 1) * length)
                    hidden = dot(first_low[rows, :], weight) + up_row[:, cols]
                    cdf, density = normal_parts(hidden)
                    act[rows, cols] = (hidden * cdf).astype(BF16)
                    pull[rows, cols] = (cdf + hidden * density).astype(BF16)
                run_at(pieces, FORWARD_PLAN, UP_STEPS[i], m, 4)

        keep(wu, wu_h, 2)
        keep(pull, pull_h, 3)
        for c in loads:
            c.wait()
        for i, (first, wide, _) in enumerate(DOWN_PIECES):
            run_events(pieces, FORWARD_PLAN[DOWN_READY, i])

            @pl.loop(0, 2)
            def _(s):
                rows = rows_of(s)
                weight = wd[:, :, :, :, first : first + wide].reshape(columns, wide)
                resid_two[rows, first : first + wide] = dot(act[rows, :], weight)
                run_at(pieces, FORWARD_PLAN, DOWN_STEPS[i], s, 2)

        keep(wd, wd_h, 4)

        @pl.loop(0, 2)
        def _(s):
            rows = rows_of(s)
            first = normal_one[rows, :] * gain_one + shift_one
            normal, inv = centre(first + resid_two[rows, :] + down_bias)
            live = lax.broadcasted_iota(jnp.int32, (length, 1), 0) < counts[s]
            low_out[rows, :] = jnp.where(live, normal * gain_two + shift_two, 0.0).astype(BF16)
            grad_y = jnp.where(live, cotangent[rows, :].astype(F32), 0.0)
            resid = pull_back(grad_y * gain_two, normal, inv)
            resid_two[rows, :] = resid
            low = resid.astype(BF16)
            err_two[rows, :] = low
            err_two_t[:, rows] = low.T
            note(sums, 6, grad_y * normal)
            note(sums, 7, grad_y)
            note(sums, 5, low.astype(F32))

        keep(low_out, layer_out_h, 5)
        keep(err_two, err_two_h, 6)
        keep(resid_two, resid_two_h, 7)

        @pl.loop(0, NZ)
        def _(zz):
            cols = pl.ds(pl.multiple_of(zz * NX * per, per), NX * per)
            grad = dot(err_two_t[...], act[:, cols]).astype(BF16)
            for xx in range(NX):
                part_d[:, zz, xx] = grad[:, xx * per : (xx + 1) * per].reshape(4, width // 4, per)
            pltpu.make_async_copy(part_d.at[:, zz], part_d_h.at[:, zz], local.at[8, zz]).start()

        for zz in range(NZ):
            outs.append(
                pltpu.make_async_copy(part_d.at[:, zz], part_d_h.at[:, zz], local.at[8, zz])
            )
        for c in outs:
            c.wait()
        for p in pieces.values():
            p.drain()
        for k in range(1, NX * NZ):
            vec_copy(k).wait_send()

    pl.run_scoped(
        feed,
        pltpu.VMEM((total, columns), BF16),
        pltpu.VMEM((total, columns), BF16),
        pltpu.VMEM((total, width), BF16),
        pltpu.VMEM((width, total), BF16),
        pltpu.VMEM((total, width), BF16),
        pltpu.VMEM((width, total), BF16),
        pltpu.VMEM((total, width), F32),
        pltpu.VMEM((total, width), F32),
        pltpu.VMEM((total, width), BF16),
        pltpu.VMEM((total, width), BF16),
        pltpu.VMEM((4, NZ, NX, width // 4, per), BF16),
    )


def forward(counts, rows, vectors, cotangent, wq, wk, wv, wo, wu, wd):
    total, width = rows.shape
    columns = wu.shape[1]
    slots, length = 2, total // 2
    heads = width // HEAD_DIM
    per = columns // (NX * NZ)
    copies = 7 + (len(QKV_PIECES) + len(UP_PIECES) + len(DOWN_PIECES)) * 13
    hbm, vmem = pl.BlockSpec(memory_space=pl.ANY), pl.BlockSpec(memory_space=pltpu.VMEM)
    w4_shape = (4, NZ, NX, ROWS, width)
    wu_shape = (NZ, NX, ROWS, columns)
    wd_shape = (NZ, NX, 4, ROWS, width)
    return pl.pallas_call(
        forward_kernel,
        name="forward",
        in_specs=[pl.BlockSpec(memory_space=pltpu.SMEM)] + [vmem] * 10 + [hbm] * 7,
        out_specs=[hbm] * 16 + [vmem] * 4,
        out_shape=[
            Shape(w4_shape, BF16),
            Shape(wu_shape, BF16),
            Shape(wd_shape, BF16),
            Shape((total, width), BF16),
            Shape((total, width), BF16),
            Shape((total, width), BF16),
            Shape((total, width), BF16),
            Shape((slots, heads, length, length), BF16),
            Shape((width, total), BF16),
            Shape((width, total), BF16),
            Shape((total, width), BF16),
            Shape((total, width), F32),
            Shape((total, width), F32),
            Shape((total, columns), BF16),
            Shape((4, NZ, NX, width // 4, per), BF16),
            Shape((width, total), BF16),
            Shape((8, width), F32),
            Shape((slots, heads // 2, 2, length), F32),
            Shape((total, 1), F32),
            Shape((8, width), F32),
        ],
        scratch_shapes=[
            pltpu.VMEM(w4_shape, BF16),
            pltpu.VMEM(wu_shape, BF16),
            pltpu.VMEM(wd_shape, BF16),
            pltpu.VMEM((NX * NZ, 16, 128), F32),
            pltpu.VMEM((1, columns), F32),
            pltpu.VMEM((width, total), BF16),
            pltpu.VMEM((width, total), BF16),
            pltpu.SemaphoreType.DMA((copies,)),
            pltpu.SemaphoreType.DMA((copies,)),
            pltpu.SemaphoreType.DMA((9, 4)),
        ],
        compiler_params=params(collective_id=0, has_side_effects=True),
    )(counts, rows, *vectors, cotangent, wq, wk, wv, wo, wu, wd.reshape(4, ROWS, width))


class Chunk:
    def __init__(self, name, wire, where, part, mine, scratch):
        self.name, self.wire, self.where = name, wire, where
        self.part, self.mine = part, mine
        self.rc, self.bx, self.by, self.cx, self.cy, self.bz, self.fin = scratch

    @staticmethod
    def scratch(a, b):
        return [
            pltpu.VMEM((2, NZ, NX, a, b), BF16),
            pltpu.VMEM((2, 2, a, b), BF16),
            pltpu.VMEM((2, NX, a, b), BF16),
            pltpu.VMEM((2, a, b), BF16),
            pltpu.VMEM((2, a, b), BF16),
            pltpu.VMEM((NZ - 1, a, b), BF16),
            pltpu.VMEM((4, a, b), BF16),
        ]

    def copies(self, stage):
        x, y, z, core = self.where
        member, other = y * 2 + core, (1 - y) * 2 + core
        x_peer, y_peer = at(1 - x, y, z, core), at(x, 1 - y, z, core)
        c_peer = at(x, y, z, 1 - core)
        rc, fin = self.rc, self.fin
        if stage == "core":
            plan = [(self.part.at[yy * 2 + 1 - core], rc.at[yy], c_peer) for yy in range(2)]
        elif stage == "plane":
            plan = [
                (rc.at[:, pl.ds(0, 2), 1 - x], self.bx, x_peer),
                (rc.at[1 - y, pl.ds(2, 2)], self.by, y_peer),
            ]
        elif stage == "turn":
            plan = [
                (rc.at[1 - y, pl.ds(0, 2), x], self.cy, y_peer),
                (rc.at[y, pl.ds(2, 2), 1 - x], self.cx, x_peer),
            ]
        elif stage == "depth":
            plan = [
                (rc.at[y, (z + k) % NZ, x], self.bz.at[k - 1], at(x, y, (z + k) % NZ, core))
                for k in range(1, NZ)
            ]
        elif stage == "spread":
            plan = [(fin.at[member], fin.at[member], peer) for peer in (y_peer, c_peer)]
        else:
            plan = [(fin.at[other], fin.at[other], c_peer)]
        return [
            self.wire.copy((self.name, stage, i), source, target, peer)
            for i, (source, target, peer) in enumerate(plan)
        ]

    def start(self, stage):
        for c in self.copies(stage):
            c.start()

    def arrive(self, stage):
        for c in self.copies(stage):
            c.wait_recv()

    def chip(self):
        core = self.where[3]
        self.arrive("core")
        rc, mine = self.rc, self.mine
        for yy in range(2):

            @pl.loop(0, NZ)
            def _(zz):
                for xx in range(NX):
                    rc[yy, zz, xx] = rc[yy, zz, xx] + mine(yy, core, zz, xx)

        self.start("plane")

    def turn_y(self):
        x, y, z, core = self.where
        rc, bx = self.rc, self.bx
        self.copies("plane")[0].wait_recv()

        @pl.loop(0, 2)
        def _(zz):
            for yy in range(2):
                rc[yy, zz, x] = rc[yy, zz, x] + bx[yy, zz]

        self.copies("turn")[0].start()

    def turn_x(self):
        x, y, z, core = self.where
        rc, by = self.rc, self.by
        self.copies("plane")[1].wait_recv()

        @pl.loop(0, 2)
        def _(zz):
            for xx in range(NX):
                rc[y, 2 + zz, xx] = rc[y, 2 + zz, xx] + by[zz, xx]

        self.copies("turn")[1].start()

    def depth(self):
        x, y, z, core = self.where
        rc, cx, cy = self.rc, self.cx, self.cy
        self.arrive("turn")

        @pl.loop(0, 2)
        def _(zz):
            rc[y, zz, x] = rc[y, zz, x] + cy[zz]
            rc[y, 2 + zz, x] = rc[y, 2 + zz, x] + cx[zz]

        self.start("depth")

    def total(self):
        x, y, z, core = self.where
        self.arrive("depth")
        summed = self.rc[y, z, x].astype(F32)
        for k in range(NZ - 1):
            summed = summed + self.bz[k].astype(F32)
        self.fin[y * 2 + core] = summed.astype(BF16)
        self.start("spread")

    def relay(self):
        self.copies("spread")[0].wait_recv()
        self.start("relay")

    def done(self):
        self.copies("spread")[1].wait_recv()
        self.arrive("relay")

    def drain(self):
        for stage in ("core", "plane", "turn", "depth", "spread", "relay"):
            for c in self.copies(stage):
                c.wait_send()


def attend_back_step(query, keys, values, powers, inverse, context_t, grad):
    q2 = query[...] * jnp.asarray(SCALE, BF16)
    k2, v2 = keys[...], values[...]
    grad_t = grad[...].astype(F32).T
    product = grad_t * context_t[...].astype(F32)
    k_t = k2.T
    inv = [inverse[h : h + 1] for h in range(2)]
    scaled_t = jnp.concatenate([grad_t[:HEAD_DIM] * inv[0], grad_t[HEAD_DIM:] * inv[1]], 0).astype(
        BF16
    )
    scaled = scaled_t.T
    dq, dk, dv = [], 0.0, 0.0
    for h in range(2):
        rows = slice(h * HEAD_DIM, (h + 1) * HEAD_DIM)
        inner = jnp.sum(product[rows], 0, keepdims=True) * inv[h]
        power = powers[h]
        grad_probs = dot(keep_half(h, v2), scaled_t)
        grad_scores = (power.astype(F32) * (grad_probs - inner)).astype(BF16)
        dv = dv + dot(power, keep_half(h, scaled))
        dk = dk + dot(grad_scores, keep_half(h, q2))
        dq.append(dot(k_t[rows], grad_scores))
    return (jnp.concatenate(dq, 0) * SCALE).astype(BF16).T, dk.astype(BF16), dv.astype(BF16)


def backward_kernel(
    part_d, err_two_h, pull_h, wd_h, wu_h, resid_two_h, normal_one_h, inverse_one, first_t_h,
    query_h, keys_h, values_h, powers_h, inverse, context_t_h, tokens_t_h, w4_h, vec, sums_in,
    o4, ou, od, ov, input_grad,
    part_u, own_d, err_one, grad_context, grad_in, tokens_t, context_t, sums, sums_up,
    pv, va, vb, *rest,
):
    count = 7 * (len(GRAD_DOWN) + len(GRAD_UP) + 4)
    scratch, (send, recv, load) = list(rest[:count]), rest[count:]
    where = x, y, z, core = place()
    shard, member = z * NX + x, y * 2 + core
    total, width = grad_in.shape
    length = total // 2
    columns = sums_up.shape[1]
    loops = columns // CHUNK
    wire = Wire(send, recv)

    def lanes_of(part, first, wide):
        return part.at[:, :, :, :, pl.ds(first, wide)]

    def own_part(part):
        return lambda yy, core, zz, xx: part[yy * 2 + core, zz, xx]

    def take():
        mine = scratch[:7]
        del scratch[:7]
        return mine

    d, u = [], []
    for i, part in enumerate(GRAD_DOWN):
        own = lanes_of(own_d, *part)
        d.append(
            Chunk(
                D0 + i, wire, where, lanes_of(part_d, *part),
                lambda yy, core, zz, xx, own=own: own[yy, zz, xx], take(),
            )
        )
    for i, part in enumerate(GRAD_UP):
        rows_u = lanes_of(part_u, *part)
        u.append(Chunk(U0 + i, wire, where, rows_u, own_part(rows_u), take()))
    chunks = {c.name: c for c in d + u}

    def rows_of(s):
        return pl.ds(pl.multiple_of(s * length, length), length)

    def block(j):
        return pl.ds(pl.multiple_of(j * CHUNK, CHUNK), CHUNK)

    own_loads = [
        pltpu.make_async_copy(part_d.at[yy * 2 + core], own_d.at[yy], load.at[0, yy])
        for yy in range(2)
    ]
    gain_one = vec[3:4].astype(F32)
    sums[...] = sums_in[...]
    sums_up[...] = jnp.zeros_like(sums_up)

    def feed_back(wd, wu, pull, err_two, normal_one, first_t, wo):
        first_loads = [
            pltpu.make_async_copy(err_two_h, err_two, load.at[1, 0]),
            pltpu.make_async_copy(resid_two_h, grad_in, load.at[1, 1]),
            pltpu.make_async_copy(normal_one_h, normal_one, load.at[1, 2]),
            pltpu.make_async_copy(w4_h.at[3], wo, load.at[1, 3]),
        ]
        late_loads = [
            pltpu.make_async_copy(first_t_h, first_t, load.at[2, 0]),
            pltpu.make_async_copy(context_t_h, context_t, load.at[2, 2]),
            pltpu.make_async_copy(tokens_t_h, tokens_t, load.at[2, 1]),
        ]

        def loads(j):
            return [
                pltpu.make_async_copy(wd_h.at[block(j)], wd.at[block(j)], load.at[3, j]),
                pltpu.make_async_copy(pull_h.at[:, block(j)], pull.at[:, block(j)], load.at[4, j]),
                pltpu.make_async_copy(wu_h.at[:, block(j)], wu.at[:, block(j)], load.at[5, j]),
            ]

        first_loads[0].start()
        for c in loads(0)[:2]:
            c.start()
        hello(all_peers())
        for j in range(1, loops):
            for c in loads(j)[:2]:
                c.start()
        for c in own_loads + first_loads[1:]:
            c.start()
        for j in range(loops):
            loads(j)[2].start()
        for c in late_loads:
            c.start()
        first_loads[0].wait()

        @pl.loop(0, 2 * loops)
        def _(t):
            j = t % loops
            rows = rows_of(t // loops)

            @pl.when(t < loops)
            def _():
                for c in loads(j)[:2]:
                    c.wait()

            grads = dot_t(err_two[rows, :], wd[block(j), :])
            low = (grads * pull[rows, block(j)].astype(F32)).astype(BF16)
            pull[rows, block(j)] = low
            sums_up[:, block(j)] += jnp.sum(low.astype(F32), 0, keepdims=True)

            @pl.when(t == 0)
            def _():
                all_here(all_peers())
                for c in d:
                    c.start("core")

            @pl.when(t == OWN_LOADED)
            def _():
                for c in own_loads:
                    c.wait()

            run_at(chunks, BACKWARD_PLAN, HIDDEN, t, 2 * loops)

        for c in late_loads[:1]:
            c.wait()

        for i, (first, wide) in enumerate(GRAD_UP):

            @pl.loop(0, 4)
            def _(m):
                cols = pl.ds(pl.multiple_of(m * width + first, 128), wide)
                part_u[m, :, :, :, first : first + wide] = (
                    dot(first_t[...], pull[:, cols]).astype(BF16).reshape(NZ, NX, ROWS, wide)
                )

                @pl.when(m == 3)
                def _():
                    u[i].start("core")

                run_at(chunks, BACKWARD_PLAN, GRAD_UP_STEPS[i], m, 4)

        for c in first_loads[1:] + late_loads[1:]:
            c.wait()
        for j in range(loops):
            loads(j)[2].wait()

        @pl.loop(0, 2)
        def _(s):
            rows = rows_of(s)
            grad_first = grad_in[rows, :] + dot_t(pull[rows, :], wu[...])
            run_at(chunks, BACKWARD_PLAN, FIRST, s, 2)
            normal = normal_one[rows, :]
            note(sums, 3, grad_first * normal)
            note(sums, 4, grad_first)
            resid = pull_back(grad_first * gain_one, normal, inverse_one[rows, :])
            grad_in[rows, :] = resid
            low = resid.astype(BF16)
            err_one[rows, :] = low
            note(sums, 2, low.astype(F32))
            grad_context[rows, :] = dot_t(low, wo[...]).astype(BF16)
            run_at(chunks, BACKWARD_PLAN, NORM, s, 2)

    pl.run_scoped(
        feed_back,
        pltpu.VMEM((columns, width), BF16),
        pltpu.VMEM((width, columns), BF16),
        pltpu.VMEM((total, columns), BF16),
        pltpu.VMEM((total, width), BF16),
        pltpu.VMEM((total, width), F32),
        pltpu.VMEM((width, total), BF16),
        pltpu.VMEM((width, width), BF16),
    )

    def attend_and_inputs(qkv, powers, grads, weights, part_q):
        halves = [part_q.at[0], part_q.at[1]] + [
            part_q.at[2, :, :, :, :, pl.ds(i * PAIR, PAIR)] for i in range(2)
        ]
        q = [
            Chunk(Q0 + i, wire, where, p, own_part(p), take())
            for i, p in enumerate(halves)
        ]
        chunks.update({c.name: c for c in q})

        def loads(t):
            pair, s = t // 2, t % 2
            rows, cols = rows_of(s), pl.ds(pl.multiple_of(pair * PAIR, PAIR), PAIR)
            return [
                pltpu.make_async_copy(a.at[rows, cols], qkv.at[s, i], load.at[6 + i, s])
                for i, a in enumerate((query_h, keys_h, values_h))
            ] + [
                pltpu.make_async_copy(
                    powers_h.at[s, pl.ds(pair * 2, 2)], powers.at[s], load.at[9, s]
                )
            ]

        weight_loads = [
            pltpu.make_async_copy(
                w4_h.at[i, :, pl.ds(g * GROUP, GROUP)],
                weights.at[g, :, pl.ds(i * GROUP, GROUP)],
                load.at[10 + g, i],
            )
            for g in range(3)
            for i in range(3)
        ]
        for c in loads(0) + weight_loads:
            c.start()

        @pl.loop(0, 3)
        def _(g):
            @pl.loop(0, 4)
            def _(k):
                t = g * 4 + k
                pair, s = t // 2, t % 2

                @pl.when(t < 11)
                def _():
                    for c in loads(t + 1):
                        c.start()

                for c in loads(t):
                    c.wait()
                rows, cols = rows_of(s), pl.ds(pl.multiple_of(pair * PAIR, PAIR), PAIR)
                values = attend_back_step(
                    qkv.at[s, 0], qkv.at[s, 1], qkv.at[s, 2], powers.at[s],
                    inverse.at[s, pair], context_t.at[cols, rows], grad_context.at[rows, cols],
                )
                for i, value in enumerate(values):
                    lane = pl.multiple_of(i * GROUP + (pair % 2) * PAIR, PAIR)
                    grads[g, rows, pl.ds(lane, PAIR)] = value
                run_at(chunks, BACKWARD_PLAN, ATTEND, t, 12)

            cols = pl.ds(pl.multiple_of(g * GROUP, GROUP), GROUP)
            for i in range(3):
                lanes = slice(i * GROUP, (i + 1) * GROUP)
                part_q[g, i] = (
                    dot(tokens_t[...], grads[g, :, lanes])
                    .astype(BF16)
                    .reshape(NZ, NX, ROWS, GROUP)
                )
            part_q[g, 3] = (
                dot(context_t[...], err_one[:, cols]).astype(BF16).reshape(NZ, NX, ROWS, GROUP)
            )
            for i in range(2):

                @pl.when(g == i)
                def _():
                    q[i].start("core")

            @pl.when(g == 2)
            def _():
                q[2].start("core")
                q[3].start("core")

            sums[0:1, cols] = jnp.sum(grads[g, :, :GROUP].astype(F32), 0, keepdims=True)
            sums[1:2, cols] = jnp.sum(grads[g, :, 2 * GROUP :].astype(F32), 0, keepdims=True)
            run_at(chunks, BACKWARD_PLAN, WEIGHTS, g, 3)

        pv[...] = jnp.zeros_like(pv)
        lanes = lax.broadcasted_iota(jnp.int32, (width, NX * NZ * 128), 1)
        rows = lax.broadcasted_iota(jnp.int32, (width, NX * NZ * 128), 0)
        pick = (rows == (lanes // 128) * ROWS + lanes % 128) & (lanes % 128 < ROWS)
        spread8 = lax.dot_general(
            sums[...], pick.astype(F32), (((1,), (0,)), ((), ())),
            precision=lax.Precision.HIGHEST, preferred_element_type=F32,
        )
        per = columns // (NX * NZ)
        for f in range(NX * NZ):
            pv[f, 0:8, :] = spread8[:, f * 128 : (f + 1) * 128]
            for i in range(3):
                first = f * per + i * 128
                pv[f, 8 + i : 9 + i, :] = sums_up[:, first : first + 128]

        def to_owner(k):
            to = (shard + k) % (NX * NZ)
            return wire.copy(("v", k), pv.at[to], va.at[k - 1], {"dp": member, "fsdp": to})

        for k in range(1, NX * NZ):
            to_owner(k).start()
        for c in weight_loads:
            c.wait()
        out = []
        for i in range(3):
            lanes = slice(i * GROUP, (i + 1) * GROUP)
            summed = grad_in[:, lanes]
            for g in range(3):
                summed = summed + dot_t(grads[g], weights[g, lanes, :])
            grad_in[:, lanes] = summed
            c = pltpu.make_async_copy(
                grad_in.at[:, lanes], input_grad.at[:, lanes], load.at[13, i]
            )
            c.start()
            out.append(c)
            run_events(chunks, BACKWARD_PLAN.get((INPUTS, i), ()))

        for k in range(1, NX * NZ):
            to_owner(k).wait_recv()
        partial = pv[shard]
        for k in range(NX * NZ - 1):
            partial = partial + va[k]
        vb[member] = partial

        def to_member(i):
            dy, dc = ((0, 1), (1, 0), (1, 1))[i]
            peer = at(x, (y + dy) % 2, z, (core + dc) % 2)
            return wire.copy(("w", i), vb.at[member], vb.at[member], peer)

        for i in range(3):
            to_member(i).start()
        run_events(chunks, BACKWARD_PLAN[DRAIN])
        for i in range(3):
            to_member(i).wait_recv()
        ov[...] = (vb[0] + vb[1]) + (vb[2] + vb[3])
        for out_ref, group, parts in ((od, d, GRAD_DOWN), (ou, u, GRAD_UP)):
            for c, (first, wide) in zip(group, parts):
                c.done()
                out_ref[:, :, first : first + wide] = c.fin[...]
        first = 0
        for c in q:
            c.done()
            last = first + c.fin.shape[2]
            o4[:, :, first:last] = c.fin[...]
            first = last
        for c in out:
            c.wait()
        for c in d + u + q:
            c.drain()
        for k in range(1, NX * NZ):
            to_owner(k).wait_send()
        for i in range(3):
            to_member(i).wait_send()

    pl.run_scoped(
        attend_and_inputs,
        pltpu.VMEM((2, 3, length, PAIR), BF16),
        pltpu.VMEM((2, 2, length, length), BF16),
        pltpu.VMEM((3, total, width), BF16),
        pltpu.VMEM((3, width, width), BF16),
        pltpu.VMEM((3, 4, NZ, NX, ROWS, GROUP), BF16),
    )


def backward(
    part_d, err_two, pull, wd, wu, resid_two, normal_one, inverse_one, first_t,
    query, keys, values, powers, inverse, context_t, tokens_t, w4, vec, sums_in,
):
    total, width = query.shape
    columns = wu.shape[1]
    per = columns // (NX * NZ)
    hbm, vmem = pl.BlockSpec(memory_space=pl.ANY), pl.BlockSpec(memory_space=pltpu.VMEM)
    d_block, copies = part_d.shape[3:], 7 + 3 + (len(GRAD_DOWN) + len(GRAD_UP) + 4) * 12
    scratch = [
        pltpu.VMEM((4, NZ, NX, ROWS, width), BF16),
        pltpu.VMEM((2, NZ, NX) + d_block, BF16),
        pltpu.VMEM((total, width), BF16),
        pltpu.VMEM((total, width), BF16),
        pltpu.VMEM((total, width), F32),
        pltpu.VMEM((width, total), BF16),
        pltpu.VMEM((width, total), BF16),
        pltpu.VMEM((8, width), F32),
        pltpu.VMEM((1, columns), F32),
        pltpu.VMEM((NX * NZ, 16, 128), F32),
        pltpu.VMEM((NX * NZ - 1, 16, 128), F32),
        pltpu.VMEM((4, 16, 128), F32),
    ]
    for _, wide in GRAD_DOWN:
        scratch += Chunk.scratch(d_block[0], wide)
    for _, wide in GRAD_UP:
        scratch += Chunk.scratch(ROWS, wide)
    scratch += Chunk.scratch(ROWS, GROUP) * 2 + Chunk.scratch(ROWS, PAIR) * 2
    scratch += [pltpu.SemaphoreType.DMA((copies,))] * 2 + [pltpu.SemaphoreType.DMA((14, 4))]
    return pl.pallas_call(
        backward_kernel,
        name="backward",
        in_specs=[hbm] * 7 + [vmem] + [hbm] * 5 + [vmem] + [hbm] * 3 + [vmem] * 2,
        out_specs=[vmem] * 4 + [hbm],
        out_shape=[
            Shape((4, ROWS, width), BF16),
            Shape((4, ROWS, width), BF16),
            Shape((4,) + part_d.shape[3:], BF16),
            Shape((16, 128), F32),
            Shape((total, width), F32),
        ],
        scratch_shapes=scratch,
        compiler_params=params(collective_id=1, has_side_effects=True),
    )(
        part_d, err_two, pull, wd, wu, resid_two, normal_one, inverse_one, first_t,
        query, keys, values, powers, inverse, context_t, tokens_t, w4, vec, sums_in,
    )


def finish_kernel(layer_in, grad_in, o4, ou, od, ov, layer_out, input_grad, *rest):
    outs, stage, (layer_v, grad_v, sem) = rest[:15], rest[15:30], rest[30:]
    part = grad_v.shape[0] // 4
    takes, gives = [], []
    for source, middle, target, first in (
        (layer_in, layer_v, layer_out, 6), (grad_in, grad_v, input_grad, 14),
    ):
        for i in range(4):
            span = slice(i * part, (i + 1) * part)
            takes.append(
                pltpu.make_async_copy(source.at[span], middle.at[span], sem.at[first + i])
            )
            gives.append(
                pltpu.make_async_copy(middle.at[span], target.at[span], sem.at[first + 4 + i])
            )
    for c in takes:
        c.start()
    sends = [pltpu.make_async_copy(stage[i], outs[i], sem.at[22 + i]) for i in range(15)]
    width, rows = o4.shape[2], od.shape[1]
    for i in range(8):
        stage[7 + i][...] = ov[i : i + 1, :ROWS]
    stage[6][...] = jnp.concatenate([ov[8 + i : 9 + i, :] for i in range(3)], 1).reshape(4 * ROWS)
    for i in range(6, 15):
        sends[i].start()

    def hand_on(first, last):
        for i in range(first, last):
            takes[i].wait()
            gives[i].start()

    for i in range(4):
        stage[i][...] = o4[i].astype(F32)
        sends[i].start()
    hand_on(0, 4)
    for i in range(4):
        stage[4][:, i * width : (i + 1) * width] = ou[i].astype(F32)
    sends[4].start()
    hand_on(4, 6)
    for i in range(4):
        stage[5][:, i * rows : (i + 1) * rows] = od[i].astype(F32).T
    sends[5].start()
    hand_on(6, 8)
    for c in sends + gives:
        c.wait()


def finish(layer_out, input_grad, o4, ou, od, ov):
    width = o4.shape[2]
    hbm, vmem = pl.BlockSpec(memory_space=pl.ANY), pl.BlockSpec(memory_space=pltpu.VMEM)
    small = [(4 * ROWS,)] + [(1, ROWS)] * 8
    large = [(ROWS, width)] * 4 + [(ROWS, 4 * width), (od.shape[2], 4 * od.shape[1])]
    return pl.pallas_call(
        finish_kernel,
        name="finish",
        in_specs=[hbm] * 2 + [vmem] * 4,
        out_specs=[hbm] * 17,
        out_shape=[Shape(layer_out.shape, BF16), Shape(input_grad.shape, F32)]
        + [Shape(shape, F32) for shape in large + small],
        scratch_shapes=[pltpu.VMEM(shape, F32) for shape in large + small]
        + [
            pltpu.VMEM(layer_out.shape, BF16),
            pltpu.VMEM(input_grad.shape, F32),
            pltpu.SemaphoreType.DMA((37,)),
        ],
        compiler_params=params(),
    )(layer_out, input_grad, o4, ou, od, ov)


def fused_layer(
    tokens, counts, cotangent, query_weight, key_weight, value_weight, out_weight, query_bias,
    value_bias, out_bias, attention_gain, attention_shift, up_weight, up_bias, down_weight,
    down_bias, feed_gain, feed_shift,
):
    width = tokens.shape[2]
    shards = NX * NZ
    columns = up_weight.shape[1]
    rows = tokens.reshape(-1, width)
    vectors = (
        query_bias, value_bias, out_bias, attention_gain, attention_shift, down_bias, feed_gain,
        feed_shift, up_bias,
    )
    (
        w4, wu, wd, layer_out, query, keys, values, powers, context_t, first_t, err_two, resid_two,
        normal_one, pull, part_d, tokens_t, vec8, inverse, inverse_one, sums,
    ) = forward(
        counts, rows, vectors, cotangent.reshape(-1, width), query_weight, key_weight, value_weight,
        out_weight, up_weight, down_weight,
    )
    o4, ou, od, ov, input_grad = backward(
        part_d, err_two, pull, wd.reshape(columns, width), wu.reshape(width, columns), resid_two,
        normal_one, inverse_one, first_t, query, keys, values, powers, inverse, context_t, tokens_t,
        w4.reshape(4, width, width), vec8, sums,
    )
    layer_out, input_grad, gq, gk, gv, go, gu, gd, gub, *v = finish(
        layer_out, input_grad, o4, ou, od, ov
    )
    v = [i.reshape(-1) for i in v]
    return (
        layer_out.reshape(tokens.shape),
        input_grad.reshape(tokens.shape),
        gq, gk, gv, go, v[0], v[1], v[2], v[3], v[4], gu, gub, gd, v[5], v[6], v[7],
    )


def exact_gelu(value):
    return jax.nn.gelu(value, approximate=False)


def norm_forward(resid, gain, shift):
    average = jnp.mean(resid, axis=-1, keepdims=True)
    centred = resid - average
    spread = jnp.mean(centred * centred, axis=-1, keepdims=True)
    inverse = lax.rsqrt(spread + epsilon)
    normal = centred * inverse
    return (normal * gain + shift, normal, inverse)


def norm_backward(grad_out, normal, inverse, gain):
    scaled = grad_out * gain
    first_mean = jnp.mean(scaled, axis=-1, keepdims=True)
    second_mean = jnp.mean(scaled * normal, axis=-1, keepdims=True)
    grad_resid = inverse * (scaled - first_mean - normal * second_mean)
    return (grad_resid, jnp.sum(grad_out * normal, 0), jnp.sum(grad_out, 0))


def linear(rows, weight):
    return jnp.dot(rows, weight, preferred_element_type=jnp.float32)


def linear_back(grads, weight):
    return lax.dot_general(
        grads, weight, (((1,), (1,)), ((), ())), preferred_element_type=jnp.float32
    )


def outer_sum(rows, grads):
    return lax.dot_general(
        rows, grads, (((0,), (0,)), ((), ())), preferred_element_type=jnp.float32
    )


def column_sum(grads):
    return jnp.sum(grads.astype(jnp.float32), 0)


def on_device(
    tokens,
    counts,
    cotangent,
    query_weight,
    key_weight,
    value_weight,
    out_weight,
    query_bias,
    value_bias,
    out_bias,
    attention_gain,
    attention_shift,
    up_weight,
    up_bias,
    down_weight,
    down_bias,
    feed_gain,
    feed_shift,
):
    slots, length, width = tokens.shape
    heads = width // HEAD_DIM
    factor = HEAD_DIM ** (-0.5)
    positions = jnp.arange(length, dtype=jnp.int32)

    def split_heads(value):
        return value.reshape(slots, length, heads, HEAD_DIM)

    def masked_scores(query, keys, count):
        raw = jnp.einsum("qhd,khd->hqk", query, keys, preferred_element_type=jnp.float32)
        live = positions < count
        return jnp.where(live[None, None, :], raw * factor, -1000000000.0)

    def attend_forward(block):
        query, keys, values, count = block
        scores = masked_scores(query, keys, count)
        highest = jnp.max(scores, axis=-1, keepdims=True)
        powers = jnp.exp(scores - highest)
        totals = jnp.sum(powers, axis=-1, keepdims=True)
        probs = (powers / totals).astype(jnp.bfloat16)
        context = jnp.einsum("hqk,khd->qhd", probs, values, preferred_element_type=jnp.float32)
        return (context.reshape(length, width), highest + jnp.log(totals))

    def attend_backward(block):
        query, keys, values, count, logsum, grad_context = block
        scores = masked_scores(query, keys, count)
        probs = jnp.exp(scores - logsum)
        probs_low = probs.astype(jnp.bfloat16)
        grad_probs = jnp.einsum(
            "qhd,khd->hqk", grad_context, values, preferred_element_type=jnp.float32
        )
        inner = jnp.sum(probs * grad_probs, axis=-1, keepdims=True)
        grad_scores = (probs * (grad_probs - inner) * factor).astype(jnp.bfloat16)
        grad_query = jnp.einsum(
            "hqk,khd->qhd", grad_scores, keys, preferred_element_type=jnp.float32
        )
        grad_keys = jnp.einsum(
            "hqk,qhd->khd", grad_scores, query, preferred_element_type=jnp.float32
        )
        grad_values = jnp.einsum(
            "hqk,qhd->khd", probs_low, grad_context, preferred_element_type=jnp.float32
        )
        return (
            grad_query.reshape(length, width).astype(jnp.bfloat16),
            grad_keys.reshape(length, width).astype(jnp.bfloat16),
            grad_values.reshape(length, width).astype(jnp.bfloat16),
        )

    attention_set = (
        lax.all_gather(query_weight, "fsdp", axis=0, tiled=True),
        lax.all_gather(key_weight, "fsdp", axis=0, tiled=True),
        lax.all_gather(value_weight, "fsdp", axis=0, tiled=True),
        lax.all_gather(out_weight, "fsdp", axis=0, tiled=True),
        lax.all_gather(query_bias, "fsdp", axis=0, tiled=True),
        lax.all_gather(value_bias, "fsdp", axis=0, tiled=True),
        lax.all_gather(out_bias, "fsdp", axis=0, tiled=True),
        lax.all_gather(attention_gain, "fsdp", axis=0, tiled=True),
        lax.all_gather(attention_shift, "fsdp", axis=0, tiled=True),
    )
    feed_set = (
        lax.all_gather(up_weight, "fsdp", axis=0, tiled=True),
        lax.all_gather(up_bias, "fsdp", axis=0, tiled=True),
        lax.all_gather(down_weight, "fsdp", axis=0, tiled=True),
        lax.all_gather(down_bias, "fsdp", axis=0, tiled=True),
        lax.all_gather(feed_gain, "fsdp", axis=0, tiled=True),
        lax.all_gather(feed_shift, "fsdp", axis=0, tiled=True),
    )
    whole_query, whole_key, whole_value, whole_out = (
        attention_set[0],
        attention_set[1],
        attention_set[2],
        attention_set[3],
    )
    whole_up, whole_down = (feed_set[0], feed_set[2])
    rows = tokens.reshape(-1, width)
    query = (linear(rows, whole_query) + attention_set[4].astype(jnp.float32)).astype(jnp.bfloat16)
    keys = linear(rows, whole_key).astype(jnp.bfloat16)
    values = (linear(rows, whole_value) + attention_set[5].astype(jnp.float32)).astype(jnp.bfloat16)
    context_rows, logsum = lax.map(
        attend_forward, (split_heads(query), split_heads(keys), split_heads(values), counts)
    )
    context = context_rows.reshape(-1, width).astype(jnp.bfloat16)
    branch = linear(context, whole_out) + attention_set[6].astype(jnp.float32)
    gain_one = attention_set[7].astype(jnp.float32)
    first, normal_one, inverse_one = norm_forward(
        rows.astype(jnp.float32) + branch, gain_one, attention_set[8].astype(jnp.float32)
    )
    first_low = first.astype(jnp.bfloat16)
    hidden = linear(first_low, whole_up) + feed_set[1].astype(jnp.float32)
    activated, gelu_pull = jax.vjp(exact_gelu, hidden)
    act_low = activated.astype(jnp.bfloat16)
    second = linear(act_low, whole_down) + feed_set[3].astype(jnp.float32)
    gain_two = feed_set[4].astype(jnp.float32)
    output, normal_two, inverse_two = norm_forward(
        first + second, gain_two, feed_set[5].astype(jnp.float32)
    )
    live = (positions[None, :] < counts[:, None]).reshape(-1, 1)
    layer_out = jnp.where(live, output, 0.0).astype(jnp.bfloat16).reshape(tokens.shape)
    back_feed = (
        lax.all_gather(up_weight, "fsdp", axis=0, tiled=True),
        lax.all_gather(down_weight, "fsdp", axis=0, tiled=True),
    )
    back_up, back_down = (back_feed[0], back_feed[1])
    grad_y = jnp.where(live, cotangent.reshape(-1, width).astype(jnp.float32), 0.0)
    resid_two, grad_feed_gain, grad_feed_shift = norm_backward(
        grad_y, normal_two, inverse_two, gain_two
    )
    err_two = resid_two.astype(jnp.bfloat16)
    grad_down_weight = outer_sum(act_low, err_two)
    grad_down_bias = column_sum(err_two)
    grad_act = linear_back(err_two, back_down)
    grad_hidden = gelu_pull(grad_act)[0].astype(jnp.bfloat16)
    grad_up_weight = outer_sum(first_low, grad_hidden)
    grad_up_bias = column_sum(grad_hidden)
    grad_first = resid_two + linear_back(grad_hidden, back_up)
    feed_shards = (
        lax.psum_scatter(
            grad_up_weight.astype(jnp.bfloat16), "fsdp", scatter_dimension=0, tiled=True
        ).astype(jnp.float32),
        lax.psum_scatter(
            grad_up_bias.astype(jnp.bfloat16), "fsdp", scatter_dimension=0, tiled=True
        ).astype(jnp.float32),
        lax.psum_scatter(
            grad_down_weight.astype(jnp.bfloat16), "fsdp", scatter_dimension=0, tiled=True
        ).astype(jnp.float32),
        lax.psum_scatter(
            grad_down_bias.astype(jnp.bfloat16), "fsdp", scatter_dimension=0, tiled=True
        ).astype(jnp.float32),
        lax.psum_scatter(
            grad_feed_gain.astype(jnp.bfloat16), "fsdp", scatter_dimension=0, tiled=True
        ).astype(jnp.float32),
        lax.psum_scatter(
            grad_feed_shift.astype(jnp.bfloat16), "fsdp", scatter_dimension=0, tiled=True
        ).astype(jnp.float32),
    )
    back_attention = (
        lax.all_gather(query_weight, "fsdp", axis=0, tiled=True),
        lax.all_gather(key_weight, "fsdp", axis=0, tiled=True),
        lax.all_gather(value_weight, "fsdp", axis=0, tiled=True),
        lax.all_gather(out_weight, "fsdp", axis=0, tiled=True),
    )
    back_query, back_key, back_value, back_out = (
        back_attention[0],
        back_attention[1],
        back_attention[2],
        back_attention[3],
    )
    resid_one, grad_attention_gain, grad_attention_shift = norm_backward(
        grad_first, normal_one, inverse_one, gain_one
    )
    err_one = resid_one.astype(jnp.bfloat16)
    grad_out_weight = outer_sum(context, err_one)
    grad_out_bias = column_sum(err_one)
    grad_context = linear_back(err_one, back_out).astype(jnp.bfloat16)
    grad_query, grad_keys, grad_values = lax.map(
        attend_backward,
        (
            split_heads(query),
            split_heads(keys),
            split_heads(values),
            counts,
            logsum,
            split_heads(grad_context),
        ),
    )
    grad_query = grad_query.reshape(-1, width)
    grad_keys = grad_keys.reshape(-1, width)
    grad_values = grad_values.reshape(-1, width)
    grad_query_weight = outer_sum(rows, grad_query)
    grad_key_weight = outer_sum(rows, grad_keys)
    grad_value_weight = outer_sum(rows, grad_values)
    grad_query_bias = column_sum(grad_query)
    grad_value_bias = column_sum(grad_values)
    input_grad = (
        resid_one
        + linear_back(grad_query, back_query)
        + linear_back(grad_keys, back_key)
        + linear_back(grad_values, back_value)
    )
    attention_shards = (
        lax.psum_scatter(
            grad_query_weight.astype(jnp.bfloat16), "fsdp", scatter_dimension=0, tiled=True
        ).astype(jnp.float32),
        lax.psum_scatter(
            grad_key_weight.astype(jnp.bfloat16), "fsdp", scatter_dimension=0, tiled=True
        ).astype(jnp.float32),
        lax.psum_scatter(
            grad_value_weight.astype(jnp.bfloat16), "fsdp", scatter_dimension=0, tiled=True
        ).astype(jnp.float32),
        lax.psum_scatter(
            grad_out_weight.astype(jnp.bfloat16), "fsdp", scatter_dimension=0, tiled=True
        ).astype(jnp.float32),
        lax.psum_scatter(
            grad_query_bias.astype(jnp.bfloat16), "fsdp", scatter_dimension=0, tiled=True
        ).astype(jnp.float32),
        lax.psum_scatter(
            grad_value_bias.astype(jnp.bfloat16), "fsdp", scatter_dimension=0, tiled=True
        ).astype(jnp.float32),
        lax.psum_scatter(
            grad_out_bias.astype(jnp.bfloat16), "fsdp", scatter_dimension=0, tiled=True
        ).astype(jnp.float32),
        lax.psum_scatter(
            grad_attention_gain.astype(jnp.bfloat16), "fsdp", scatter_dimension=0, tiled=True
        ).astype(jnp.float32),
        lax.psum_scatter(
            grad_attention_shift.astype(jnp.bfloat16), "fsdp", scatter_dimension=0, tiled=True
        ).astype(jnp.float32),
    )
    summed = lax.psum(
        (
            attention_shards[0],
            attention_shards[1],
            attention_shards[2],
            attention_shards[3],
            attention_shards[4],
            attention_shards[5],
            attention_shards[6],
            attention_shards[7],
            attention_shards[8],
            feed_shards[0],
            feed_shards[1],
            feed_shards[2],
            feed_shards[3],
            feed_shards[4],
            feed_shards[5],
        ),
        "dp",
    )
    return (
        layer_out,
        input_grad.reshape(tokens.shape),
        summed[0],
        summed[1],
        summed[2],
        summed[3],
        summed[4],
        summed[5],
        summed[6],
        summed[7],
        summed[8],
        summed[9],
        summed[10],
        summed[11],
        summed[12],
        summed[13],
        summed[14],
    )


def solution(mesh):
    small = mesh.shape["dp"] == 4 and mesh.shape["fsdp"] == NX * NZ
    return jax.shard_map(
        fused_layer if small else on_device,
        mesh=mesh,
        in_specs=(
            P(("dp", "fsdp"), None, None),
            P(("dp", "fsdp")),
            P(("dp", "fsdp"), None, None),
            P("fsdp", None),
            P("fsdp", None),
            P("fsdp", None),
            P("fsdp", None),
            P("fsdp"),
            P("fsdp"),
            P("fsdp"),
            P("fsdp"),
            P("fsdp"),
            P("fsdp", None),
            P("fsdp"),
            P("fsdp", None),
            P("fsdp"),
            P("fsdp"),
            P("fsdp"),
        ),
        out_specs=(
            P(("dp", "fsdp"), None, None),
            P(("dp", "fsdp"), None, None),
            P("fsdp", None),
            P("fsdp", None),
            P("fsdp", None),
            P("fsdp", None),
            P("fsdp"),
            P("fsdp"),
            P("fsdp"),
            P("fsdp"),
            P("fsdp"),
            P("fsdp", None),
            P("fsdp"),
            P("fsdp", None),
            P("fsdp"),
            P("fsdp"),
            P("fsdp"),
        ),
        check_vma=False,
    )
```

```python
import functools

import jax
import jax.numpy as jnp
from jax import lax
from jax.experimental import pallas as pl
from jax.experimental.pallas import tpu as pltpu
from jax.sharding import PartitionSpec as P

HEAD_DIM = 64
epsilon = 1e-05
F32 = jnp.float32
BF16 = jnp.bfloat16
MESH = pl.DeviceIdType.MESH
VMEM_LIMIT = 63 * 2**20
Shape = jax.ShapeDtypeStruct


def dot(left, right):
    return lax.dot_general(
        left, right, (((1,), (0,)), ((), ())), preferred_element_type=F32
    )


def dot_t(left, right):
    return lax.dot_general(
        left, right, (((1,), (1,)), ((), ())), preferred_element_type=F32
    )


def params(**extra):
    return pltpu.CompilerParams(vmem_limit_bytes=VMEM_LIMIT, **extra)


def whole(shape):
    return pl.BlockSpec(shape, lambda *_: (0,) * len(shape), pipeline_mode=pl.Buffered(1))


NX, NZ, ROWS = 2, 4, 96


def place():
    member = lax.axis_index("dp")
    shard = lax.axis_index("fsdp")
    return shard % NX, member // 2, shard // NX, member % 2


def at(x, y, z, core):
    return {"dp": y * 2 + core, "fsdp": z * NX + x}


def hello(peers):
    barrier = pltpu.get_barrier_semaphore()
    for peer in peers:
        pl.semaphore_signal(barrier, inc=1, device_id=peer, device_id_type=MESH)


def all_here(peers):
    pl.semaphore_wait(pltpu.get_barrier_semaphore(), len(peers))


def greet(peers):
    hello(peers)
    all_here(peers)


def all_peers():
    x, y, z, core = place()
    near = [at(x, 1 - y, z, core), at(x, y, z, 1 - core)]
    for step in range(1, NX * NZ):
        near.append({"dp": y * 2 + core, "fsdp": (z * NX + x + step) % (NX * NZ)})
    return near


class Wire:
    def __init__(self, send, recv):
        self.send, self.recv, self.slots = send, recv, {}

    def copy(self, key, source, target, peer):
        slot = self.slots.setdefault(key, len(self.slots))
        return pltpu.make_async_remote_copy(
            src_ref=source,
            dst_ref=target,
            send_sem=self.send.at[slot],
            recv_sem=self.recv.at[slot],
            device_id=peer,
            device_id_type=MESH,
        )


Q0, Q1, Q2, Q3, U0, U1, D0, D1, D2 = range(9)
PLANE, TURN_X, TURN_Y, REST, REST2, READY, SEND, CHIP, DEPTH, TOTAL, RELAY = range(11)
STAGES = (
    "plane", "turn_x", "turn_y", "rest", "rest2", "ready", "send", "chip", "depth", "total", "relay",
)
START, SENDS, DRAIN, BEFORE, ATTEND, NORM, UP_READY, UP_0, UP_1, DOWN_READY, DOWN_0 = range(11)
DOWN_1, DOWN_2, HIDDEN, GRAD_UP_0, GRAD_UP_1, FIRST, WEIGHTS, INPUTS = range(11, 19)
UP_STEPS, DOWN_STEPS = (UP_0, UP_1), (DOWN_0, DOWN_1, DOWN_2)
GRAD_UP_STEPS = (GRAD_UP_0, GRAD_UP_1)
QKV_PIECES = ((0, 1), (1, 1), (2, 2), (4, 2))
UP_PIECES = ((0, 512), (512, 256))
DOWN_PIECES = ((0, 256, 'x'), (256, 256, 'y'), (512, 256, ''))
GRAD_DOWN = ((0, 256), (256, 128))
GRAD_UP = ((0, 512), (512, 256))
OWN_LOADED = 3
FORWARD_PLAN = {
    START: ((Q0, PLANE), (U0, SEND), (Q1, PLANE), (U1, SEND), (Q0, TURN_X), (Q0, TURN_Y), (Q1, TURN_Y), (Q1, TURN_X), (Q2, PLANE), (D0, SEND), (Q0, REST), (Q3, PLANE), (D1, SEND), (Q2, TURN_X), (Q2, TURN_Y), (Q0, READY),),
    (ATTEND, 0): ((Q1, REST),),
    (BEFORE, 2): ((Q1, READY),),
    (ATTEND, 2): ((Q3, TURN_Y), (Q3, TURN_X),),
    (ATTEND, 3): ((D0, PLANE), (Q2, REST), (U0, PLANE), (D2, SEND), (Q3, REST),),
    (BEFORE, 4): ((Q2, READY),),
    (ATTEND, 5): ((U1, PLANE),),
    (BEFORE, 8): ((Q3, READY),),
    (ATTEND, 8): ((U0, TURN_Y), (U0, TURN_X),),
    (ATTEND, 10): ((D1, TURN_X), (D1, PLANE),),
    (ATTEND, 11): ((U1, TURN_X), (U1, TURN_Y), (D0, TURN_X), (D0, TURN_Y),),
    (NORM, 0): ((U0, REST),),
    (NORM, 1): ((D2, PLANE),),
    (UP_READY, 0): ((U0, READY),),
    (UP_0, 1): ((D0, REST),),
    (UP_0, 2): ((U1, REST), (D1, TURN_Y),),
    (UP_READY, 1): ((U1, READY), (D2, TURN_Y), (D1, REST),),
    (UP_1, 0): ((D0, REST2),),
    (DOWN_READY, 0): ((D0, READY), (D2, TURN_X), (D1, REST2),),
    (DOWN_READY, 1): ((D1, READY),),
    (DOWN_1, 0): ((D2, REST),),
    (DOWN_READY, 2): ((D2, READY),),
    SENDS: ((Q1, SEND), (Q2, SEND), (Q3, SEND),),
}
BACKWARD_PLAN = {
    START: (),
    DRAIN: ((Q1, TOTAL), (Q2, TOTAL), (Q3, TOTAL), (Q0, RELAY), (Q2, RELAY), (U0, RELAY), (Q1, RELAY), (D1, RELAY), (Q3, RELAY),),
    (HIDDEN, 3): ((D0, CHIP),),
    (GRAD_UP_0, 0): ((D1, CHIP),),
    (GRAD_UP_1, 1): ((D0, TURN_X),),
    (GRAD_UP_1, 2): ((D0, TURN_Y),),
    (FIRST, 0): ((U1, CHIP), (U0, CHIP), (D1, TURN_Y),),
    (FIRST, 1): ((D1, TURN_X),),
    (NORM, 1): ((U1, TURN_Y),),
    (ATTEND, 1): ((D0, DEPTH),),
    (ATTEND, 3): ((U1, TURN_X),),
    (WEIGHTS, 0): ((U0, TURN_Y), (U0, TURN_X),),
    (ATTEND, 5): ((U1, DEPTH), (Q0, CHIP),),
    (ATTEND, 6): ((D1, DEPTH),),
    (ATTEND, 7): ((D0, TOTAL),),
    (ATTEND, 8): ((Q0, TURN_Y), (Q0, TURN_X), (U0, DEPTH),),
    (ATTEND, 9): ((Q1, CHIP),),
    (WEIGHTS, 2): ((Q1, TURN_X), (Q1, TURN_Y), (Q0, DEPTH), (Q2, CHIP),),
    (INPUTS, 0): ((Q3, CHIP), (Q1, DEPTH), (Q2, TURN_Y), (U1, TOTAL), (Q2, TURN_X),),
    (INPUTS, 1): ((Q3, TURN_X), (Q3, TURN_Y), (Q2, DEPTH), (D1, TOTAL), (Q0, TOTAL), (U1, RELAY), (D0, RELAY), (U0, TOTAL), (Q3, DEPTH),),
}


GROUP = 4 * HEAD_DIM
PAIR = 2 * HEAD_DIM
SCALE = HEAD_DIM**-0.5
CHUNK = 1024


def run_events(pieces, events):
    for piece, stage in events:
        getattr(pieces[piece], STAGES[stage])()


def run_at(pieces, plan, prefix, index, count):
    for k in range(count):
        if (prefix, k) in plan:

            @pl.when(index == k)
            def _():
                run_events(pieces, plan[prefix, k])


class Piece:
    def __init__(self, name, wire, where, block):
        self.name, self.wire, self.where, self.block = name, wire, where, block

    def copy(self, key, source, peer):
        return self.wire.copy((self.name, key), source, source, peer)

    def copies(self, stage):
        x, y, z, core = self.where
        member, other = y * 2 + core, (1 - y) * 2 + core
        x_peer, y_peer = at(1 - x, y, z, core), at(x, 1 - y, z, core)
        c_peer = at(x, y, z, 1 - core)
        every, block = slice(None), self.block
        if stage == "depth":
            mine = block(member, z, x)
            plan = [(mine, at(x, y, (z + k) % NZ, core)) for k in range(1, NZ)]
        elif stage == "plane":
            mine = block(member, every, x)
            plan = [(mine, x_peer), (mine, y_peer)]
        elif stage == "turn":
            plan = [
                (block(other, pl.ds(0, 2), x), x_peer),
                (block(member, pl.ds(2, 2), 1 - x), y_peer),
            ]
        else:
            plan = [
                (block(member, every, x), c_peer),
                (block(other, every, x), c_peer),
                (block(member, every, 1 - x), c_peer),
                (block(other, every, 1 - x), c_peer),
            ]
        return [self.copy((stage, i), source, peer) for i, (source, peer) in enumerate(plan)]

    def send(self):
        for c in self.copies("depth"):
            c.start()

    def plane(self):
        for c in self.copies("depth"):
            c.wait_recv()
        for c in self.copies("plane"):
            c.start()
        self.copies("core")[0].start()

    def turn_x(self):
        self.copies("plane")[1].wait_recv()
        self.copies("turn")[0].start()
        self.copies("core")[1].start()

    def turn_y(self):
        self.copies("plane")[0].wait_recv()
        self.copies("turn")[1].start()
        self.copies("core")[2].start()

    def rest(self):
        for c in self.copies("turn"):
            c.wait_recv()
        self.copies("core")[3].start()

    def ready(self):
        for c in self.copies("core"):
            c.wait_recv()

    def drain(self):
        for stage in ("depth", "plane", "turn", "core"):
            for c in self.copies(stage):
                c.wait_send()


class DeepPiece(Piece):
    def __init__(self, name, wire, where, block, axis):
        super().__init__(name, wire, where, block)
        self.axis = axis

    def copies(self, stage):
        x, y, z, core = self.where
        member, other = y * 2 + core, (1 - y) * 2 + core
        x_peer, y_peer = at(1 - x, y, z, core), at(x, 1 - y, z, core)
        c_peer = at(x, y, z, 1 - core)
        by_x, every = self.axis == "x", slice(None)
        near = (member, 1 - x) if by_x else (other, x)
        far = (other, x) if by_x else (member, 1 - x)
        places = [(member, x), near, far, (other, 1 - x)]

        def block(place, zs):
            return self.block(place[0], zs, place[1])

        depth = [at(x, y, (z + k) % NZ, core) for k in range(1, NZ)]
        if stage == "first":
            plan = [(block(places[0], z), x_peer if by_x else y_peer)]
        elif stage == "depth":
            plan = [(block(places[0], z), peer) for peer in depth]
        elif stage == "near depth":
            plan = [(block(places[1], z), peer) for peer in depth]
        elif stage == "last":
            plan = [(block(p, every), y_peer if by_x else x_peer) for p in places[:2]]
        else:
            plan = [(block(p, every), c_peer) for p in places]
        return [self.copy((stage, i), source, peer) for i, (source, peer) in enumerate(plan)]

    def send(self):
        for c in self.copies("first") + self.copies("depth"):
            c.start()

    def plane(self):
        self.copies("first")[0].wait_recv()
        for c in self.copies("near depth"):
            c.start()

    def pass_on(self, stage, i):
        for c in self.copies(stage):
            c.wait_recv()
        self.copies("last")[i].start()
        self.copies("core")[i].start()

    def turn_x(self):
        self.pass_on("depth", 0)

    def turn_y(self):
        self.pass_on("near depth", 1)

    def rest(self):
        self.copies("last")[0].wait_recv()
        self.copies("core")[2].start()

    def rest2(self):
        self.copies("last")[1].wait_recv()
        self.copies("core")[3].start()

    def drain(self):
        for stage in ("first", "depth", "near depth", "last", "core"):
            for c in self.copies(stage):
                c.wait_send()


def half(index, shape):
    lanes = lax.broadcasted_iota(jnp.int32, shape, 1)
    return lanes < HEAD_DIM if index == 0 else lanes >= HEAD_DIM


def keep_half(index, value):
    return jnp.where(half(index, value.shape), value, jnp.zeros_like(value))


def attend_step(hidden_keys, q, k, v, powers, inverse, context_t):
    scaled, v_t = q * jnp.asarray(SCALE, BF16), v.T
    for h in range(2):
        rows = slice(h * HEAD_DIM, (h + 1) * HEAD_DIM)
        scores = dot_t(keep_half(h, k), scaled) + hidden_keys
        highest = jnp.max(scores, 0, keepdims=True)
        power = jnp.exp(scores - highest)
        inv = 1.0 / jnp.sum(power, 0, keepdims=True)
        low = power.astype(BF16)
        powers[h] = low
        inverse[h : h + 1] = inv
        context_t[rows] = (dot(v_t[rows], low) * inv).astype(BF16)


SQRT_HALF = 0.7071067811865476
PDF_SCALE = 0.3989422804014327
LOG2_E = 1.4426950408889634


def normal_parts(value):
    t = 1.0 / (1.0 + (0.3275911 * SQRT_HALF) * jnp.abs(value))
    bell = jnp.exp2((value * value) * (-0.5 * LOG2_E))
    poly = (0.5 * 1.061405429) * t - 0.5 * 1.453152027
    poly = poly * t + 0.5 * 1.421413741
    poly = poly * t - 0.5 * 0.284496736
    poly = poly * t + 0.5 * 0.254829592
    tail = (poly * t) * bell
    return jnp.where(value >= 0, 1.0 - tail, tail), bell * PDF_SCALE


def centre(resid):
    centred = resid - jnp.mean(resid, 1, keepdims=True)
    inv = lax.rsqrt(jnp.mean(centred * centred, 1, keepdims=True) + epsilon)
    return centred * inv, inv


def pull_back(scaled, normal, inv):
    return inv * (
        scaled
        - jnp.mean(scaled, 1, keepdims=True)
        - normal * jnp.mean(scaled * normal, 1, keepdims=True)
    )


def note(sums, row, value):
    sums[row : row + 1] += jnp.sum(value, 0, keepdims=True)


def forward_kernel(
    counts, tokens, qb, vb, ob, ag, ash, db, fg, fsh, ub, cotangent_h, wq, wk, wv, wo, wu_i, wd_i,
    w4_h, wu_h, wd_h, layer_out_h, query_h, keys_h, values_h, powers_h, context_t_h, first_t_h,
    err_two_h, resid_two_h, normal_one_h, pull_h, part_d_h, tokens_t_h, vec8, inverse, inverse_one, sums,
    w4, wu, wd, gv, up_row, context_t, tokens_t, send, recv, local,
):
    where = x, y, z, core = place()
    shard, member = z * NX + x, y * 2 + core
    total, width = tokens.shape
    length = total // 2
    columns = up_row.shape[1]
    wire = Wire(send, recv)

    def columns_of(first, pairs):
        return lambda who, zs, xs: w4.at[who, zs, xs, :, pl.ds(first * PAIR, pairs * PAIR)]

    def up_part(first, wide):
        return lambda who, zs, xs: wu.at[
            zs, xs, :, pl.ds(pl.multiple_of(who * width + first, 128), wide)
        ]

    def down_part(first, wide):
        return lambda who, zs, xs: wd.at[zs, xs, who, :, pl.ds(first, wide)]

    pieces = {
        Q0 + i: Piece(Q0 + i, wire, where, columns_of(first, pairs))
        for i, (first, pairs) in enumerate(QKV_PIECES)
    }
    for i, part in enumerate(UP_PIECES):
        pieces[U0 + i] = Piece(U0 + i, wire, where, up_part(*part))
    for i, (first, wide, axis) in enumerate(DOWN_PIECES):
        if axis:
            piece = DeepPiece(D0 + i, wire, where, down_part(first, wide), axis)
        else:
            piece = Piece(D0 + i, wire, where, down_part(first, wide))
        pieces[D0 + i] = piece

    own = [
        pltpu.make_async_copy(wq, w4.at[member, z, x], local.at[0, 0]),
        pltpu.make_async_copy(
            wu_i.at[:, pl.ds(pl.multiple_of(member * width, width), width)],
            wu.at[z, x, :, pl.ds(pl.multiple_of(member * width, width), width)],
            local.at[0, 1],
        ),
        pltpu.make_async_copy(wd_i.at[member], wd.at[z, x, member], local.at[0, 2]),
    ]
    for i, w in enumerate((wq, wk, wv, wo)):

        @pl.when(member == i)
        def _():
            pltpu.make_async_copy(w, w4.at[i, z, x], local.at[0, 0]).start()

    for c in own[1:]:
        c.start()
    gv[shard] = jnp.zeros(gv.shape[1:], F32)
    bias_row = ub[...].astype(F32).reshape(1, 4 * ROWS)
    for i in range(3):
        gv[shard, 8 + i : 9 + i, :] = bias_row[:, i * 128 : (i + 1) * 128]
    for i, vector in enumerate((qb, vb, ob, ag, ash, db, fg, fsh)):
        gv[shard, i : i + 1, 0:ROWS] = vector[...].astype(F32).reshape(1, ROWS)
    greet(all_peers())
    for c in own:
        c.wait()

    def vec_copy(k):
        peer = {"dp": member, "fsdp": (shard + k) % (NX * NZ)}
        return wire.copy(("v", k), gv.at[shard], gv.at[shard], peer)

    pieces[Q0].send()
    for k in range(1, NX * NZ):
        vec_copy(k).start()
    run_events(pieces, FORWARD_PLAN[SENDS])
    tokens_t[...] = tokens[...].T
    tokens_out = pltpu.make_async_copy(tokens_t, tokens_t_h, local.at[5, 3])
    tokens_out.start()
    sums[...] = jnp.zeros_like(sums)
    run_events(pieces, FORWARD_PLAN[START][:1])
    for k in range(1, NX * NZ):
        vec_copy(k).wait_recv()
    lanes = lax.broadcasted_iota(jnp.int32, (128, width), 0)
    features = lax.broadcasted_iota(jnp.int32, (128, width), 1)
    per = columns // (NX * NZ)
    joined = jnp.zeros((8, width), F32)
    for f in range(NX * NZ):
        pick = (features == f * ROWS + lanes) & (lanes < ROWS)
        joined = joined + dot(gv[f, 0:8, :].astype(BF16), pick.astype(F32).astype(BF16))
        for i in range(3):
            up_row[:, f * per + i * 128 : f * per + (i + 1) * 128] = gv[f, 8 + i : 9 + i, :]
    vec8[...] = joined
    run_events(pieces, FORWARD_PLAN[START][1:])

    def attention(qkv, powers):
        def outs(pair, s):
            rows = pl.ds(pl.multiple_of(s * length, length), length)
            cols = pl.ds(pl.multiple_of(pair * PAIR, PAIR), PAIR)
            return [
                pltpu.make_async_copy(qkv.at[s, i], a.at[rows, cols], local.at[1 + i, s])
                for i, a in enumerate((query_h, keys_h, values_h))
            ] + [
                pltpu.make_async_copy(
                    powers.at[s], powers_h.at[s, pl.ds(pair * 2, 2)], local.at[4, s]
                )
            ]

        @pl.loop(0, 12)
        def _(t):
            pair, s = t // 2, t % 2
            rows = pl.ds(pl.multiple_of(s * length, length), length)
            cols = pl.ds(pl.multiple_of(pair * PAIR, PAIR), PAIR)
            run_at(pieces, FORWARD_PLAN, BEFORE, t, 12)

            @pl.when(t >= 2)
            def _():
                for c in outs(pair, s):
                    c.wait()

            weights = jnp.concatenate(
                [w4[i, :, :, :, cols].reshape(width, PAIR) for i in range(3)], 1
            )
            together = dot(tokens[rows, :], weights)
            q = (together[:, :PAIR] + vec8[0:1, cols]).astype(BF16)
            k = together[:, PAIR : 2 * PAIR].astype(BF16)
            v = (together[:, 2 * PAIR :] + vec8[1:2, cols]).astype(BF16)
            qkv[s, 0], qkv[s, 1], qkv[s, 2] = q, k, v
            key_rows = lax.broadcasted_iota(jnp.int32, (length, 1), 0)
            hidden_keys = jnp.where(key_rows < counts[s], 0.0, -1000000000.0)
            attend_step(
                hidden_keys, q, k, v, powers.at[s], inverse.at[s, pair], context_t.at[cols, rows]
            )
            for c in outs(pair, s):
                c.start()
            run_at(pieces, FORWARD_PLAN, ATTEND, t, 12)

        for s in range(2):
            for c in outs(5, s):
                c.wait()

    pl.run_scoped(
        attention,
        pltpu.VMEM((2, 3, length, PAIR), BF16),
        pltpu.VMEM((2, 2, length, length), BF16),
    )

    def feed(act, pull, first_low, first_t, err_two, err_two_t, normal_one, resid_two, low_out, cotangent, part_d):
        v = [vec8[i : i + 1] for i in range(8)]
        out_bias, gain_one, shift_one, down_bias, gain_two, shift_two = v[2:]
        loads = [pltpu.make_async_copy(cotangent_h, cotangent, local.at[5, 0])]
        outs = [
            pltpu.make_async_copy(w4, w4_h, local.at[5, 1]),
            pltpu.make_async_copy(context_t, context_t_h, local.at[5, 2]),
        ]
        for c in loads + outs:
            c.start()
        outs.append(tokens_out)

        def keep(source, target, slot):
            c = pltpu.make_async_copy(source, target, local.at[6 + slot // 4, slot % 4])
            c.start()
            outs.append(c)

        def rows_of(s):
            return pl.ds(pl.multiple_of(s * length, length), length)

        @pl.loop(0, 2)
        def _(s):
            rows = rows_of(s)
            r1 = (
                tokens[rows, :].astype(F32)
                + dot(context_t[:, rows].T, w4[3].reshape(width, width))
                + out_bias
            )
            normal, inv = centre(r1)
            normal_one[rows, :] = normal
            inverse_one[rows, :] = inv
            low = (normal * gain_one + shift_one).astype(BF16)
            first_low[rows, :] = low
            first_t[:, rows] = low.T
            run_at(pieces, FORWARD_PLAN, NORM, s, 2)

        keep(normal_one, normal_one_h, 0)
        keep(first_t, first_t_h, 1)
        for i, (first, wide) in enumerate(UP_PIECES):
            run_events(pieces, FORWARD_PLAN[UP_READY, i])

            @pl.loop(0, 4)
            def _(m):
                cols = pl.ds(pl.multiple_of(m * width + first, 128), wide)
                weight = wu[:, :, :, cols].reshape(width, wide)
                for s in range(2):
                    rows = slice(s * length, (s + 1) * length)
                    hidden = dot(first_low[rows, :], weight) + up_row[:, cols]
                    cdf, density = normal_parts(hidden)
                    act[rows, cols] = (hidden * cdf).astype(BF16)
                    pull[rows, cols] = (cdf + hidden * density).astype(BF16)
                run_at(pieces, FORWARD_PLAN, UP_STEPS[i], m, 4)

        keep(wu, wu_h, 2)
        keep(pull, pull_h, 3)
        for c in loads:
            c.wait()
        for i, (first, wide, _) in enumerate(DOWN_PIECES):
            run_events(pieces, FORWARD_PLAN[DOWN_READY, i])

            @pl.loop(0, 2)
            def _(s):
                rows = rows_of(s)
                weight = wd[:, :, :, :, first : first + wide].reshape(columns, wide)
                resid_two[rows, first : first + wide] = dot(act[rows, :], weight)
                run_at(pieces, FORWARD_PLAN, DOWN_STEPS[i], s, 2)

        keep(wd, wd_h, 4)

        @pl.loop(0, 2)
        def _(s):
            rows = rows_of(s)
            first = normal_one[rows, :] * gain_one + shift_one
            normal, inv = centre(first + resid_two[rows, :] + down_bias)
            live = lax.broadcasted_iota(jnp.int32, (length, 1), 0) < counts[s]
            low_out[rows, :] = jnp.where(live, normal * gain_two + shift_two, 0.0).astype(BF16)
            grad_y = jnp.where(live, cotangent[rows, :].astype(F32), 0.0)
            resid = pull_back(grad_y * gain_two, normal, inv)
            resid_two[rows, :] = resid
            low = resid.astype(BF16)
            err_two[rows, :] = low
            err_two_t[:, rows] = low.T
            note(sums, 6, grad_y * normal)
            note(sums, 7, grad_y)
            note(sums, 5, low.astype(F32))

        keep(low_out, layer_out_h, 5)
        keep(err_two, err_two_h, 6)
        keep(resid_two, resid_two_h, 7)

        @pl.loop(0, NZ)
        def _(zz):
            cols = pl.ds(pl.multiple_of(zz * NX * per, per), NX * per)
            grad = dot(err_two_t[...], act[:, cols]).astype(BF16)
            for xx in range(NX):
                part_d[:, zz, xx] = grad[:, xx * per : (xx + 1) * per].reshape(4, width // 4, per)
            pltpu.make_async_copy(part_d.at[:, zz], part_d_h.at[:, zz], local.at[8, zz]).start()

        for zz in range(NZ):
            outs.append(
                pltpu.make_async_copy(part_d.at[:, zz], part_d_h.at[:, zz], local.at[8, zz])
            )
        for c in outs:
            c.wait()
        for p in pieces.values():
            p.drain()
        for k in range(1, NX * NZ):
            vec_copy(k).wait_send()

    pl.run_scoped(
        feed,
        pltpu.VMEM((total, columns), BF16),
        pltpu.VMEM((total, columns), BF16),
        pltpu.VMEM((total, width), BF16),
        pltpu.VMEM((width, total), BF16),
        pltpu.VMEM((total, width), BF16),
        pltpu.VMEM((width, total), BF16),
        pltpu.VMEM((total, width), F32),
        pltpu.VMEM((total, width), F32),
        pltpu.VMEM((total, width), BF16),
        pltpu.VMEM((total, width), BF16),
        pltpu.VMEM((4, NZ, NX, width // 4, per), BF16),
    )


def forward(counts, rows, vectors, cotangent, wq, wk, wv, wo, wu, wd):
    total, width = rows.shape
    columns = wu.shape[1]
    slots, length = 2, total // 2
    heads = width // HEAD_DIM
    per = columns // (NX * NZ)
    copies = 7 + (len(QKV_PIECES) + len(UP_PIECES) + len(DOWN_PIECES)) * 13
    hbm, vmem = pl.BlockSpec(memory_space=pl.ANY), pl.BlockSpec(memory_space=pltpu.VMEM)
    w4_shape = (4, NZ, NX, ROWS, width)
    wu_shape = (NZ, NX, ROWS, columns)
    wd_shape = (NZ, NX, 4, ROWS, width)
    return pl.pallas_call(
        forward_kernel,
        name="forward",
        in_specs=[pl.BlockSpec(memory_space=pltpu.SMEM)] + [vmem] * 10 + [hbm] * 7,
        out_specs=[hbm] * 16 + [vmem] * 4,
        out_shape=[
            Shape(w4_shape, BF16),
            Shape(wu_shape, BF16),
            Shape(wd_shape, BF16),
            Shape((total, width), BF16),
            Shape((total, width), BF16),
            Shape((total, width), BF16),
            Shape((total, width), BF16),
            Shape((slots, heads, length, length), BF16),
            Shape((width, total), BF16),
            Shape((width, total), BF16),
            Shape((total, width), BF16),
            Shape((total, width), F32),
            Shape((total, width), F32),
            Shape((total, columns), BF16),
            Shape((4, NZ, NX, width // 4, per), BF16),
            Shape((width, total), BF16),
            Shape((8, width), F32),
            Shape((slots, heads // 2, 2, length), F32),
            Shape((total, 1), F32),
            Shape((8, width), F32),
        ],
        scratch_shapes=[
            pltpu.VMEM(w4_shape, BF16),
            pltpu.VMEM(wu_shape, BF16),
            pltpu.VMEM(wd_shape, BF16),
            pltpu.VMEM((NX * NZ, 16, 128), F32),
            pltpu.VMEM((1, columns), F32),
            pltpu.VMEM((width, total), BF16),
            pltpu.VMEM((width, total), BF16),
            pltpu.SemaphoreType.DMA((copies,)),
            pltpu.SemaphoreType.DMA((copies,)),
            pltpu.SemaphoreType.DMA((9, 4)),
        ],
        compiler_params=params(collective_id=0, has_side_effects=True),
    )(counts, rows, *vectors, cotangent, wq, wk, wv, wo, wu, wd.reshape(4, ROWS, width))


class Chunk:
    def __init__(self, name, wire, where, part, mine, scratch):
        self.name, self.wire, self.where = name, wire, where
        self.part, self.mine = part, mine
        self.rc, self.bx, self.by, self.cx, self.cy, self.bz, self.fin = scratch

    @staticmethod
    def scratch(a, b):
        return [
            pltpu.VMEM((2, NZ, NX, a, b), BF16),
            pltpu.VMEM((2, 2, a, b), BF16),
            pltpu.VMEM((2, NX, a, b), BF16),
            pltpu.VMEM((2, a, b), BF16),
            pltpu.VMEM((2, a, b), BF16),
            pltpu.VMEM((NZ - 1, a, b), BF16),
            pltpu.VMEM((4, a, b), BF16),
        ]

    def copies(self, stage):
        x, y, z, core = self.where
        member, other = y * 2 + core, (1 - y) * 2 + core
        x_peer, y_peer = at(1 - x, y, z, core), at(x, 1 - y, z, core)
        c_peer = at(x, y, z, 1 - core)
        rc, fin = self.rc, self.fin
        if stage == "core":
            plan = [(self.part.at[yy * 2 + 1 - core], rc.at[yy], c_peer) for yy in range(2)]
        elif stage == "plane":
            plan = [
                (rc.at[:, pl.ds(0, 2), 1 - x], self.bx, x_peer),
                (rc.at[1 - y, pl.ds(2, 2)], self.by, y_peer),
            ]
        elif stage == "turn":
            plan = [
                (rc.at[1 - y, pl.ds(0, 2), x], self.cy, y_peer),
                (rc.at[y, pl.ds(2, 2), 1 - x], self.cx, x_peer),
            ]
        elif stage == "depth":
            plan = [
                (rc.at[y, (z + k) % NZ, x], self.bz.at[k - 1], at(x, y, (z + k) % NZ, core))
                for k in range(1, NZ)
            ]
        elif stage == "spread":
            plan = [(fin.at[member], fin.at[member], peer) for peer in (y_peer, c_peer)]
        else:
            plan = [(fin.at[other], fin.at[other], c_peer)]
        return [
            self.wire.copy((self.name, stage, i), source, target, peer)
            for i, (source, target, peer) in enumerate(plan)
        ]

    def start(self, stage):
        for c in self.copies(stage):
            c.start()

    def arrive(self, stage):
        for c in self.copies(stage):
            c.wait_recv()

    def chip(self):
        core = self.where[3]
        self.arrive("core")
        rc, mine = self.rc, self.mine
        for yy in range(2):

            @pl.loop(0, NZ)
            def _(zz):
                for xx in range(NX):
                    rc[yy, zz, xx] = rc[yy, zz, xx] + mine(yy, core, zz, xx)

        self.start("plane")

    def turn_y(self):
        x, y, z, core = self.where
        rc, bx = self.rc, self.bx
        self.copies("plane")[0].wait_recv()

        @pl.loop(0, 2)
        def _(zz):
            for yy in range(2):
                rc[yy, zz, x] = rc[yy, zz, x] + bx[yy, zz]

        self.copies("turn")[0].start()

    def turn_x(self):
        x, y, z, core = self.where
        rc, by = self.rc, self.by
        self.copies("plane")[1].wait_recv()

        @pl.loop(0, 2)
        def _(zz):
            for xx in range(NX):
                rc[y, 2 + zz, xx] = rc[y, 2 + zz, xx] + by[zz, xx]

        self.copies("turn")[1].start()

    def depth(self):
        x, y, z, core = self.where
        rc, cx, cy = self.rc, self.cx, self.cy
        self.arrive("turn")

        @pl.loop(0, 2)
        def _(zz):
            rc[y, zz, x] = rc[y, zz, x] + cy[zz]
            rc[y, 2 + zz, x] = rc[y, 2 + zz, x] + cx[zz]

        self.start("depth")

    def total(self):
        x, y, z, core = self.where
        self.arrive("depth")
        summed = self.rc[y, z, x].astype(F32)
        for k in range(NZ - 1):
            summed = summed + self.bz[k].astype(F32)
        self.fin[y * 2 + core] = summed.astype(BF16)
        self.start("spread")

    def relay(self):
        self.copies("spread")[0].wait_recv()
        self.start("relay")

    def done(self):
        self.copies("spread")[1].wait_recv()
        self.arrive("relay")

    def drain(self):
        for stage in ("core", "plane", "turn", "depth", "spread", "relay"):
            for c in self.copies(stage):
                c.wait_send()


def attend_back_step(query, keys, values, powers, inverse, context_t, grad):
    q2 = query[...] * jnp.asarray(SCALE, BF16)
    k2, v2 = keys[...], values[...]
    grad_t = grad[...].astype(F32).T
    product = grad_t * context_t[...].astype(F32)
    k_t = k2.T
    inv = [inverse[h : h + 1] for h in range(2)]
    scaled_t = jnp.concatenate([grad_t[:HEAD_DIM] * inv[0], grad_t[HEAD_DIM:] * inv[1]], 0).astype(
        BF16
    )
    scaled = scaled_t.T
    dq, dk, dv = [], 0.0, 0.0
    for h in range(2):
        rows = slice(h * HEAD_DIM, (h + 1) * HEAD_DIM)
        inner = jnp.sum(product[rows], 0, keepdims=True) * inv[h]
        power = powers[h]
        grad_probs = dot(keep_half(h, v2), scaled_t)
        grad_scores = (power.astype(F32) * (grad_probs - inner)).astype(BF16)
        dv = dv + dot(power, keep_half(h, scaled))
        dk = dk + dot(grad_scores, keep_half(h, q2))
        dq.append(dot(k_t[rows], grad_scores))
    return (jnp.concatenate(dq, 0) * SCALE).astype(BF16).T, dk.astype(BF16), dv.astype(BF16)


def backward_kernel(
    part_d, err_two_h, pull_h, wd_h, wu_h, resid_two_h, normal_one_h, inverse_one, first_t_h,
    query_h, keys_h, values_h, powers_h, inverse, context_t_h, tokens_t_h, w4_h, vec, sums_in,
    o4, ou, od, ov, input_grad,
    part_u, own_d, err_one, grad_context, grad_in, tokens_t, context_t, sums, sums_up,
    pv, va, vb, *rest,
):
    count = 7 * (len(GRAD_DOWN) + len(GRAD_UP) + 4)
    scratch, (send, recv, load) = list(rest[:count]), rest[count:]
    where = x, y, z, core = place()
    shard, member = z * NX + x, y * 2 + core
    total, width = grad_in.shape
    length = total // 2
    columns = sums_up.shape[1]
    loops = columns // CHUNK
    wire = Wire(send, recv)

    def lanes_of(part, first, wide):
        return part.at[:, :, :, :, pl.ds(first, wide)]

    def own_part(part):
        return lambda yy, core, zz, xx: part[yy * 2 + core, zz, xx]

    def take():
        mine = scratch[:7]
        del scratch[:7]
        return mine

    d, u = [], []
    for i, part in enumerate(GRAD_DOWN):
        own = lanes_of(own_d, *part)
        d.append(
            Chunk(
                D0 + i, wire, where, lanes_of(part_d, *part),
                lambda yy, core, zz, xx, own=own: own[yy, zz, xx], take(),
            )
        )
    for i, part in enumerate(GRAD_UP):
        rows_u = lanes_of(part_u, *part)
        u.append(Chunk(U0 + i, wire, where, rows_u, own_part(rows_u), take()))
    chunks = {c.name: c for c in d + u}

    def rows_of(s):
        return pl.ds(pl.multiple_of(s * length, length), length)

    def block(j):
        return pl.ds(pl.multiple_of(j * CHUNK, CHUNK), CHUNK)

    own_loads = [
        pltpu.make_async_copy(part_d.at[yy * 2 + core], own_d.at[yy], load.at[0, yy])
        for yy in range(2)
    ]
    gain_one = vec[3:4].astype(F32)
    sums[...] = sums_in[...]
    sums_up[...] = jnp.zeros_like(sums_up)

    def feed_back(wd, wu, pull, err_two, normal_one, first_t, wo):
        first_loads = [
            pltpu.make_async_copy(err_two_h, err_two, load.at[1, 0]),
            pltpu.make_async_copy(resid_two_h, grad_in, load.at[1, 1]),
            pltpu.make_async_copy(normal_one_h, normal_one, load.at[1, 2]),
            pltpu.make_async_copy(w4_h.at[3], wo, load.at[1, 3]),
        ]
        late_loads = [
            pltpu.make_async_copy(first_t_h, first_t, load.at[2, 0]),
            pltpu.make_async_copy(context_t_h, context_t, load.at[2, 2]),
            pltpu.make_async_copy(tokens_t_h, tokens_t, load.at[2, 1]),
        ]

        def loads(j):
            return [
                pltpu.make_async_copy(wd_h.at[block(j)], wd.at[block(j)], load.at[3, j]),
                pltpu.make_async_copy(pull_h.at[:, block(j)], pull.at[:, block(j)], load.at[4, j]),
                pltpu.make_async_copy(wu_h.at[:, block(j)], wu.at[:, block(j)], load.at[5, j]),
            ]

        first_loads[0].start()
        for c in loads(0)[:2]:
            c.start()
        hello(all_peers())
        for j in range(1, loops):
            for c in loads(j)[:2]:
                c.start()
        for c in own_loads + first_loads[1:]:
            c.start()
        for j in range(loops):
            loads(j)[2].start()
        for c in late_loads:
            c.start()
        first_loads[0].wait()

        @pl.loop(0, 2 * loops)
        def _(t):
            j = t % loops
            rows = rows_of(t // loops)

            @pl.when(t < loops)
            def _():
                for c in loads(j)[:2]:
                    c.wait()

            grads = dot_t(err_two[rows, :], wd[block(j), :])
            low = (grads * pull[rows, block(j)].astype(F32)).astype(BF16)
            pull[rows, block(j)] = low
            sums_up[:, block(j)] += jnp.sum(low.astype(F32), 0, keepdims=True)

            @pl.when(t == 0)
            def _():
                all_here(all_peers())
                for c in d:
                    c.start("core")

            @pl.when(t == OWN_LOADED)
            def _():
                for c in own_loads:
                    c.wait()

            run_at(chunks, BACKWARD_PLAN, HIDDEN, t, 2 * loops)

        for c in late_loads[:1]:
            c.wait()

        for i, (first, wide) in enumerate(GRAD_UP):

            @pl.loop(0, 4)
            def _(m):
                cols = pl.ds(pl.multiple_of(m * width + first, 128), wide)
                part_u[m, :, :, :, first : first + wide] = (
                    dot(first_t[...], pull[:, cols]).astype(BF16).reshape(NZ, NX, ROWS, wide)
                )

                @pl.when(m == 3)
                def _():
                    u[i].start("core")

                run_at(chunks, BACKWARD_PLAN, GRAD_UP_STEPS[i], m, 4)

        for c in first_loads[1:] + late_loads[1:]:
            c.wait()
        for j in range(loops):
            loads(j)[2].wait()

        @pl.loop(0, 2)
        def _(s):
            rows = rows_of(s)
            grad_first = grad_in[rows, :] + dot_t(pull[rows, :], wu[...])
            run_at(chunks, BACKWARD_PLAN, FIRST, s, 2)
            normal = normal_one[rows, :]
            note(sums, 3, grad_first * normal)
            note(sums, 4, grad_first)
            resid = pull_back(grad_first * gain_one, normal, inverse_one[rows, :])
            grad_in[rows, :] = resid
            low = resid.astype(BF16)
            err_one[rows, :] = low
            note(sums, 2, low.astype(F32))
            grad_context[rows, :] = dot_t(low, wo[...]).astype(BF16)
            run_at(chunks, BACKWARD_PLAN, NORM, s, 2)

    pl.run_scoped(
        feed_back,
        pltpu.VMEM((columns, width), BF16),
        pltpu.VMEM((width, columns), BF16),
        pltpu.VMEM((total, columns), BF16),
        pltpu.VMEM((total, width), BF16),
        pltpu.VMEM((total, width), F32),
        pltpu.VMEM((width, total), BF16),
        pltpu.VMEM((width, width), BF16),
    )

    def attend_and_inputs(qkv, powers, grads, weights, part_q):
        halves = [part_q.at[0], part_q.at[1]] + [
            part_q.at[2, :, :, :, :, pl.ds(i * PAIR, PAIR)] for i in range(2)
        ]
        q = [
            Chunk(Q0 + i, wire, where, p, own_part(p), take())
            for i, p in enumerate(halves)
        ]
        chunks.update({c.name: c for c in q})

        def loads(t):
            pair, s = t // 2, t % 2
            rows, cols = rows_of(s), pl.ds(pl.multiple_of(pair * PAIR, PAIR), PAIR)
            return [
                pltpu.make_async_copy(a.at[rows, cols], qkv.at[s, i], load.at[6 + i, s])
                for i, a in enumerate((query_h, keys_h, values_h))
            ] + [
                pltpu.make_async_copy(
                    powers_h.at[s, pl.ds(pair * 2, 2)], powers.at[s], load.at[9, s]
                )
            ]

        weight_loads = [
            pltpu.make_async_copy(
                w4_h.at[i, :, pl.ds(g * GROUP, GROUP)],
                weights.at[g, :, pl.ds(i * GROUP, GROUP)],
                load.at[10 + g, i],
            )
            for g in range(3)
            for i in range(3)
        ]
        for c in loads(0) + weight_loads:
            c.start()

        @pl.loop(0, 3)
        def _(g):
            @pl.loop(0, 4)
            def _(k):
                t = g * 4 + k
                pair, s = t // 2, t % 2

                @pl.when(t < 11)
                def _():
                    for c in loads(t + 1):
                        c.start()

                for c in loads(t):
                    c.wait()
                rows, cols = rows_of(s), pl.ds(pl.multiple_of(pair * PAIR, PAIR), PAIR)
                values = attend_back_step(
                    qkv.at[s, 0], qkv.at[s, 1], qkv.at[s, 2], powers.at[s],
                    inverse.at[s, pair], context_t.at[cols, rows], grad_context.at[rows, cols],
                )
                for i, value in enumerate(values):
                    lane = pl.multiple_of(i * GROUP + (pair % 2) * PAIR, PAIR)
                    grads[g, rows, pl.ds(lane, PAIR)] = value
                run_at(chunks, BACKWARD_PLAN, ATTEND, t, 12)

            cols = pl.ds(pl.multiple_of(g * GROUP, GROUP), GROUP)
            for i in range(3):
                lanes = slice(i * GROUP, (i + 1) * GROUP)
                part_q[g, i] = (
                    dot(tokens_t[...], grads[g, :, lanes])
                    .astype(BF16)
                    .reshape(NZ, NX, ROWS, GROUP)
                )
            part_q[g, 3] = (
                dot(context_t[...], err_one[:, cols]).astype(BF16).reshape(NZ, NX, ROWS, GROUP)
            )
            for i in range(2):

                @pl.when(g == i)
                def _():
                    q[i].start("core")

            @pl.when(g == 2)
            def _():
                q[2].start("core")
                q[3].start("core")

            sums[0:1, cols] = jnp.sum(grads[g, :, :GROUP].astype(F32), 0, keepdims=True)
            sums[1:2, cols] = jnp.sum(grads[g, :, 2 * GROUP :].astype(F32), 0, keepdims=True)
            run_at(chunks, BACKWARD_PLAN, WEIGHTS, g, 3)

        pv[...] = jnp.zeros_like(pv)
        lanes = lax.broadcasted_iota(jnp.int32, (width, NX * NZ * 128), 1)
        rows = lax.broadcasted_iota(jnp.int32, (width, NX * NZ * 128), 0)
        pick = (rows == (lanes // 128) * ROWS + lanes % 128) & (lanes % 128 < ROWS)
        spread8 = lax.dot_general(
            sums[...], pick.astype(F32), (((1,), (0,)), ((), ())),
            precision=lax.Precision.HIGHEST, preferred_element_type=F32,
        )
        per = columns // (NX * NZ)
        for f in range(NX * NZ):
            pv[f, 0:8, :] = spread8[:, f * 128 : (f + 1) * 128]
            for i in range(3):
                first = f * per + i * 128
                pv[f, 8 + i : 9 + i, :] = sums_up[:, first : first + 128]

        def to_owner(k):
            to = (shard + k) % (NX * NZ)
            return wire.copy(("v", k), pv.at[to], va.at[k - 1], {"dp": member, "fsdp": to})

        for k in range(1, NX * NZ):
            to_owner(k).start()
        for c in weight_loads:
            c.wait()
        out = []
        for i in range(3):
            lanes = slice(i * GROUP, (i + 1) * GROUP)
            summed = grad_in[:, lanes]
            for g in range(3):
                summed = summed + dot_t(grads[g], weights[g, lanes, :])
            grad_in[:, lanes] = summed
            c = pltpu.make_async_copy(
                grad_in.at[:, lanes], input_grad.at[:, lanes], load.at[13, i]
            )
            c.start()
            out.append(c)
            run_events(chunks, BACKWARD_PLAN.get((INPUTS, i), ()))

        for k in range(1, NX * NZ):
            to_owner(k).wait_recv()
        partial = pv[shard]
        for k in range(NX * NZ - 1):
            partial = partial + va[k]
        vb[member] = partial

        def to_member(i):
            dy, dc = ((0, 1), (1, 0), (1, 1))[i]
            peer = at(x, (y + dy) % 2, z, (core + dc) % 2)
            return wire.copy(("w", i), vb.at[member], vb.at[member], peer)

        for i in range(3):
            to_member(i).start()
        run_events(chunks, BACKWARD_PLAN[DRAIN])
        for i in range(3):
            to_member(i).wait_recv()
        ov[...] = (vb[0] + vb[1]) + (vb[2] + vb[3])
        for out_ref, group, parts in ((od, d, GRAD_DOWN), (ou, u, GRAD_UP)):
            for c, (first, wide) in zip(group, parts):
                c.done()
                out_ref[:, :, first : first + wide] = c.fin[...]
        first = 0
        for c in q:
            c.done()
            last = first + c.fin.shape[2]
            o4[:, :, first:last] = c.fin[...]
            first = last
        for c in out:
            c.wait()
        for c in d + u + q:
            c.drain()
        for k in range(1, NX * NZ):
            to_owner(k).wait_send()
        for i in range(3):
            to_member(i).wait_send()

    pl.run_scoped(
        attend_and_inputs,
        pltpu.VMEM((2, 3, length, PAIR), BF16),
        pltpu.VMEM((2, 2, length, length), BF16),
        pltpu.VMEM((3, total, width), BF16),
        pltpu.VMEM((3, width, width), BF16),
        pltpu.VMEM((3, 4, NZ, NX, ROWS, GROUP), BF16),
    )


def backward(
    part_d, err_two, pull, wd, wu, resid_two, normal_one, inverse_one, first_t,
    query, keys, values, powers, inverse, context_t, tokens_t, w4, vec, sums_in,
):
    total, width = query.shape
    columns = wu.shape[1]
    per = columns // (NX * NZ)
    hbm, vmem = pl.BlockSpec(memory_space=pl.ANY), pl.BlockSpec(memory_space=pltpu.VMEM)
    d_block, copies = part_d.shape[3:], 7 + 3 + (len(GRAD_DOWN) + len(GRAD_UP) + 4) * 12
    scratch = [
        pltpu.VMEM((4, NZ, NX, ROWS, width), BF16),
        pltpu.VMEM((2, NZ, NX) + d_block, BF16),
        pltpu.VMEM((total, width), BF16),
        pltpu.VMEM((total, width), BF16),
        pltpu.VMEM((total, width), F32),
        pltpu.VMEM((width, total), BF16),
        pltpu.VMEM((width, total), BF16),
        pltpu.VMEM((8, width), F32),
        pltpu.VMEM((1, columns), F32),
        pltpu.VMEM((NX * NZ, 16, 128), F32),
        pltpu.VMEM((NX * NZ - 1, 16, 128), F32),
        pltpu.VMEM((4, 16, 128), F32),
    ]
    for _, wide in GRAD_DOWN:
        scratch += Chunk.scratch(d_block[0], wide)
    for _, wide in GRAD_UP:
        scratch += Chunk.scratch(ROWS, wide)
    scratch += Chunk.scratch(ROWS, GROUP) * 2 + Chunk.scratch(ROWS, PAIR) * 2
    scratch += [pltpu.SemaphoreType.DMA((copies,))] * 2 + [pltpu.SemaphoreType.DMA((14, 4))]
    return pl.pallas_call(
        backward_kernel,
        name="backward",
        in_specs=[hbm] * 7 + [vmem] + [hbm] * 5 + [vmem] + [hbm] * 3 + [vmem] * 2,
        out_specs=[vmem] * 4 + [hbm],
        out_shape=[
            Shape((4, ROWS, width), BF16),
            Shape((4, ROWS, width), BF16),
            Shape((4,) + part_d.shape[3:], BF16),
            Shape((16, 128), F32),
            Shape((total, width), F32),
        ],
        scratch_shapes=scratch,
        compiler_params=params(collective_id=1, has_side_effects=True),
    )(
        part_d, err_two, pull, wd, wu, resid_two, normal_one, inverse_one, first_t,
        query, keys, values, powers, inverse, context_t, tokens_t, w4, vec, sums_in,
    )


def finish_kernel(layer_in, grad_in, o4, ou, od, ov, layer_out, input_grad, *rest):
    outs, stage, (layer_v, grad_v, sem) = rest[:15], rest[15:30], rest[30:]
    part = grad_v.shape[0] // 4
    takes, gives = [], []
    for source, middle, target, first in (
        (layer_in, layer_v, layer_out, 6), (grad_in, grad_v, input_grad, 14),
    ):
        for i in range(4):
            span = slice(i * part, (i + 1) * part)
            takes.append(
                pltpu.make_async_copy(source.at[span], middle.at[span], sem.at[first + i])
            )
            gives.append(
                pltpu.make_async_copy(middle.at[span], target.at[span], sem.at[first + 4 + i])
            )
    for c in takes:
        c.start()
    sends = [pltpu.make_async_copy(stage[i], outs[i], sem.at[22 + i]) for i in range(15)]
    width, rows = o4.shape[2], od.shape[1]
    for i in range(8):
        stage[7 + i][...] = ov[i : i + 1, :ROWS]
    stage[6][...] = jnp.concatenate([ov[8 + i : 9 + i, :] for i in range(3)], 1).reshape(4 * ROWS)
    for i in range(6, 15):
        sends[i].start()

    def hand_on(first, last):
        for i in range(first, last):
            takes[i].wait()
            gives[i].start()

    for i in range(4):
        stage[i][...] = o4[i].astype(F32)
        sends[i].start()
    hand_on(0, 4)
    for i in range(4):
        stage[4][:, i * width : (i + 1) * width] = ou[i].astype(F32)
    sends[4].start()
    hand_on(4, 6)
    for i in range(4):
        stage[5][:, i * rows : (i + 1) * rows] = od[i].astype(F32).T
    sends[5].start()
    hand_on(6, 8)
    for c in sends + gives:
        c.wait()


def finish(layer_out, input_grad, o4, ou, od, ov):
    width = o4.shape[2]
    hbm, vmem = pl.BlockSpec(memory_space=pl.ANY), pl.BlockSpec(memory_space=pltpu.VMEM)
    small = [(4 * ROWS,)] + [(1, ROWS)] * 8
    large = [(ROWS, width)] * 4 + [(ROWS, 4 * width), (od.shape[2], 4 * od.shape[1])]
    return pl.pallas_call(
        finish_kernel,
        name="finish",
        in_specs=[hbm] * 2 + [vmem] * 4,
        out_specs=[hbm] * 17,
        out_shape=[Shape(layer_out.shape, BF16), Shape(input_grad.shape, F32)]
        + [Shape(shape, F32) for shape in large + small],
        scratch_shapes=[pltpu.VMEM(shape, F32) for shape in large + small]
        + [
            pltpu.VMEM(layer_out.shape, BF16),
            pltpu.VMEM(input_grad.shape, F32),
            pltpu.SemaphoreType.DMA((37,)),
        ],
        compiler_params=params(),
    )(layer_out, input_grad, o4, ou, od, ov)


def fused_layer(
    tokens, counts, cotangent, query_weight, key_weight, value_weight, out_weight, query_bias,
    value_bias, out_bias, attention_gain, attention_shift, up_weight, up_bias, down_weight,
    down_bias, feed_gain, feed_shift,
):
    width = tokens.shape[2]
    shards = NX * NZ
    columns = up_weight.shape[1]
    rows = tokens.reshape(-1, width)
    vectors = (
        query_bias, value_bias, out_bias, attention_gain, attention_shift, down_bias, feed_gain,
        feed_shift, up_bias,
    )
    (
        w4, wu, wd, layer_out, query, keys, values, powers, context_t, first_t, err_two, resid_two,
        normal_one, pull, part_d, tokens_t, vec8, inverse, inverse_one, sums,
    ) = forward(
        counts, rows, vectors, cotangent.reshape(-1, width), query_weight, key_weight, value_weight,
        out_weight, up_weight, down_weight,
    )
    o4, ou, od, ov, input_grad = backward(
        part_d, err_two, pull, wd.reshape(columns, width), wu.reshape(width, columns), resid_two,
        normal_one, inverse_one, first_t, query, keys, values, powers, inverse, context_t, tokens_t,
        w4.reshape(4, width, width), vec8, sums,
    )
    layer_out, input_grad, gq, gk, gv, go, gu, gd, gub, *v = finish(
        layer_out, input_grad, o4, ou, od, ov
    )
    v = [i.reshape(-1) for i in v]
    return (
        layer_out.reshape(tokens.shape),
        input_grad.reshape(tokens.shape),
        gq, gk, gv, go, v[0], v[1], v[2], v[3], v[4], gu, gub, gd, v[5], v[6], v[7],
    )


def exact_gelu(value):
    return jax.nn.gelu(value, approximate=False)


def norm_forward(resid, gain, shift):
    average = jnp.mean(resid, axis=-1, keepdims=True)
    centred = resid - average
    spread = jnp.mean(centred * centred, axis=-1, keepdims=True)
    inverse = lax.rsqrt(spread + epsilon)
    normal = centred * inverse
    return (normal * gain + shift, normal, inverse)


def norm_backward(grad_out, normal, inverse, gain):
    scaled = grad_out * gain
    first_mean = jnp.mean(scaled, axis=-1, keepdims=True)
    second_mean = jnp.mean(scaled * normal, axis=-1, keepdims=True)
    grad_resid = inverse * (scaled - first_mean - normal * second_mean)
    return (grad_resid, jnp.sum(grad_out * normal, 0), jnp.sum(grad_out, 0))


def linear(rows, weight):
    return jnp.dot(rows, weight, preferred_element_type=jnp.float32)


def linear_back(grads, weight):
    return lax.dot_general(
        grads, weight, (((1,), (1,)), ((), ())), preferred_element_type=jnp.float32
    )


def outer_sum(rows, grads):
    return lax.dot_general(
        rows, grads, (((0,), (0,)), ((), ())), preferred_element_type=jnp.float32
    )


def column_sum(grads):
    return jnp.sum(grads.astype(jnp.float32), 0)


def on_device(
    tokens,
    counts,
    cotangent,
    query_weight,
    key_weight,
    value_weight,
    out_weight,
    query_bias,
    value_bias,
    out_bias,
    attention_gain,
    attention_shift,
    up_weight,
    up_bias,
    down_weight,
    down_bias,
    feed_gain,
    feed_shift,
):
    slots, length, width = tokens.shape
    heads = width // HEAD_DIM
    factor = HEAD_DIM ** (-0.5)
    positions = jnp.arange(length, dtype=jnp.int32)

    def split_heads(value):
        return value.reshape(slots, length, heads, HEAD_DIM)

    def masked_scores(query, keys, count):
        raw = jnp.einsum("qhd,khd->hqk", query, keys, preferred_element_type=jnp.float32)
        live = positions < count
        return jnp.where(live[None, None, :], raw * factor, -1000000000.0)

    def attend_forward(block):
        query, keys, values, count = block
        scores = masked_scores(query, keys, count)
        highest = jnp.max(scores, axis=-1, keepdims=True)
        powers = jnp.exp(scores - highest)
        totals = jnp.sum(powers, axis=-1, keepdims=True)
        probs = (powers / totals).astype(jnp.bfloat16)
        context = jnp.einsum("hqk,khd->qhd", probs, values, preferred_element_type=jnp.float32)
        return (context.reshape(length, width), highest + jnp.log(totals))

    def attend_backward(block):
        query, keys, values, count, logsum, grad_context = block
        scores = masked_scores(query, keys, count)
        probs = jnp.exp(scores - logsum)
        probs_low = probs.astype(jnp.bfloat16)
        grad_probs = jnp.einsum(
            "qhd,khd->hqk", grad_context, values, preferred_element_type=jnp.float32
        )
        inner = jnp.sum(probs * grad_probs, axis=-1, keepdims=True)
        grad_scores = (probs * (grad_probs - inner) * factor).astype(jnp.bfloat16)
        grad_query = jnp.einsum(
            "hqk,khd->qhd", grad_scores, keys, preferred_element_type=jnp.float32
        )
        grad_keys = jnp.einsum(
            "hqk,qhd->khd", grad_scores, query, preferred_element_type=jnp.float32
        )
        grad_values = jnp.einsum(
            "hqk,qhd->khd", probs_low, grad_context, preferred_element_type=jnp.float32
        )
        return (
            grad_query.reshape(length, width).astype(jnp.bfloat16),
            grad_keys.reshape(length, width).astype(jnp.bfloat16),
            grad_values.reshape(length, width).astype(jnp.bfloat16),
        )

    attention_set = (
        lax.all_gather(query_weight, "fsdp", axis=0, tiled=True),
        lax.all_gather(key_weight, "fsdp", axis=0, tiled=True),
        lax.all_gather(value_weight, "fsdp", axis=0, tiled=True),
        lax.all_gather(out_weight, "fsdp", axis=0, tiled=True),
        lax.all_gather(query_bias, "fsdp", axis=0, tiled=True),
        lax.all_gather(value_bias, "fsdp", axis=0, tiled=True),
        lax.all_gather(out_bias, "fsdp", axis=0, tiled=True),
        lax.all_gather(attention_gain, "fsdp", axis=0, tiled=True),
        lax.all_gather(attention_shift, "fsdp", axis=0, tiled=True),
    )
    feed_set = (
        lax.all_gather(up_weight, "fsdp", axis=0, tiled=True),
        lax.all_gather(up_bias, "fsdp", axis=0, tiled=True),
        lax.all_gather(down_weight, "fsdp", axis=0, tiled=True),
        lax.all_gather(down_bias, "fsdp", axis=0, tiled=True),
        lax.all_gather(feed_gain, "fsdp", axis=0, tiled=True),
        lax.all_gather(feed_shift, "fsdp", axis=0, tiled=True),
    )
    whole_query, whole_key, whole_value, whole_out = (
        attention_set[0],
        attention_set[1],
        attention_set[2],
        attention_set[3],
    )
    whole_up, whole_down = (feed_set[0], feed_set[2])
    rows = tokens.reshape(-1, width)
    query = (linear(rows, whole_query) + attention_set[4].astype(jnp.float32)).astype(jnp.bfloat16)
    keys = linear(rows, whole_key).astype(jnp.bfloat16)
    values = (linear(rows, whole_value) + attention_set[5].astype(jnp.float32)).astype(jnp.bfloat16)
    context_rows, logsum = lax.map(
        attend_forward, (split_heads(query), split_heads(keys), split_heads(values), counts)
    )
    context = context_rows.reshape(-1, width).astype(jnp.bfloat16)
    branch = linear(context, whole_out) + attention_set[6].astype(jnp.float32)
    gain_one = attention_set[7].astype(jnp.float32)
    first, normal_one, inverse_one = norm_forward(
        rows.astype(jnp.float32) + branch, gain_one, attention_set[8].astype(jnp.float32)
    )
    first_low = first.astype(jnp.bfloat16)
    hidden = linear(first_low, whole_up) + feed_set[1].astype(jnp.float32)
    activated, gelu_pull = jax.vjp(exact_gelu, hidden)
    act_low = activated.astype(jnp.bfloat16)
    second = linear(act_low, whole_down) + feed_set[3].astype(jnp.float32)
    gain_two = feed_set[4].astype(jnp.float32)
    output, normal_two, inverse_two = norm_forward(
        first + second, gain_two, feed_set[5].astype(jnp.float32)
    )
    live = (positions[None, :] < counts[:, None]).reshape(-1, 1)
    layer_out = jnp.where(live, output, 0.0).astype(jnp.bfloat16).reshape(tokens.shape)
    back_feed = (
        lax.all_gather(up_weight, "fsdp", axis=0, tiled=True),
        lax.all_gather(down_weight, "fsdp", axis=0, tiled=True),
    )
    back_up, back_down = (back_feed[0], back_feed[1])
    grad_y = jnp.where(live, cotangent.reshape(-1, width).astype(jnp.float32), 0.0)
    resid_two, grad_feed_gain, grad_feed_shift = norm_backward(
        grad_y, normal_two, inverse_two, gain_two
    )
    err_two = resid_two.astype(jnp.bfloat16)
    grad_down_weight = outer_sum(act_low, err_two)
    grad_down_bias = column_sum(err_two)
    grad_act = linear_back(err_two, back_down)
    grad_hidden = gelu_pull(grad_act)[0].astype(jnp.bfloat16)
    grad_up_weight = outer_sum(first_low, grad_hidden)
    grad_up_bias = column_sum(grad_hidden)
    grad_first = resid_two + linear_back(grad_hidden, back_up)
    feed_shards = (
        lax.psum_scatter(
            grad_up_weight.astype(jnp.bfloat16), "fsdp", scatter_dimension=0, tiled=True
        ).astype(jnp.float32),
        lax.psum_scatter(
            grad_up_bias.astype(jnp.bfloat16), "fsdp", scatter_dimension=0, tiled=True
        ).astype(jnp.float32),
        lax.psum_scatter(
            grad_down_weight.astype(jnp.bfloat16), "fsdp", scatter_dimension=0, tiled=True
        ).astype(jnp.float32),
        lax.psum_scatter(
            grad_down_bias.astype(jnp.bfloat16), "fsdp", scatter_dimension=0, tiled=True
        ).astype(jnp.float32),
        lax.psum_scatter(
            grad_feed_gain.astype(jnp.bfloat16), "fsdp", scatter_dimension=0, tiled=True
        ).astype(jnp.float32),
        lax.psum_scatter(
            grad_feed_shift.astype(jnp.bfloat16), "fsdp", scatter_dimension=0, tiled=True
        ).astype(jnp.float32),
    )
    back_attention = (
        lax.all_gather(query_weight, "fsdp", axis=0, tiled=True),
        lax.all_gather(key_weight, "fsdp", axis=0, tiled=True),
        lax.all_gather(value_weight, "fsdp", axis=0, tiled=True),
        lax.all_gather(out_weight, "fsdp", axis=0, tiled=True),
    )
    back_query, back_key, back_value, back_out = (
        back_attention[0],
        back_attention[1],
        back_attention[2],
        back_attention[3],
    )
    resid_one, grad_attention_gain, grad_attention_shift = norm_backward(
        grad_first, normal_one, inverse_one, gain_one
    )
    err_one = resid_one.astype(jnp.bfloat16)
    grad_out_weight = outer_sum(context, err_one)
    grad_out_bias = column_sum(err_one)
    grad_context = linear_back(err_one, back_out).astype(jnp.bfloat16)
    grad_query, grad_keys, grad_values = lax.map(
        attend_backward,
        (
            split_heads(query),
            split_heads(keys),
            split_heads(values),
            counts,
            logsum,
            split_heads(grad_context),
        ),
    )
    grad_query = grad_query.reshape(-1, width)
    grad_keys = grad_keys.reshape(-1, width)
    grad_values = grad_values.reshape(-1, width)
    grad_query_weight = outer_sum(rows, grad_query)
    grad_key_weight = outer_sum(rows, grad_keys)
    grad_value_weight = outer_sum(rows, grad_values)
    grad_query_bias = column_sum(grad_query)
    grad_value_bias = column_sum(grad_values)
    input_grad = (
        resid_one
        + linear_back(grad_query, back_query)
        + linear_back(grad_keys, back_key)
        + linear_back(grad_values, back_value)
    )
    attention_shards = (
        lax.psum_scatter(
            grad_query_weight.astype(jnp.bfloat16), "fsdp", scatter_dimension=0, tiled=True
        ).astype(jnp.float32),
        lax.psum_scatter(
            grad_key_weight.astype(jnp.bfloat16), "fsdp", scatter_dimension=0, tiled=True
        ).astype(jnp.float32),
        lax.psum_scatter(
            grad_value_weight.astype(jnp.bfloat16), "fsdp", scatter_dimension=0, tiled=True
        ).astype(jnp.float32),
        lax.psum_scatter(
            grad_out_weight.astype(jnp.bfloat16), "fsdp", scatter_dimension=0, tiled=True
        ).astype(jnp.float32),
        lax.psum_scatter(
            grad_query_bias.astype(jnp.bfloat16), "fsdp", scatter_dimension=0, tiled=True
        ).astype(jnp.float32),
        lax.psum_scatter(
            grad_value_bias.astype(jnp.bfloat16), "fsdp", scatter_dimension=0, tiled=True
        ).astype(jnp.float32),
        lax.psum_scatter(
            grad_out_bias.astype(jnp.bfloat16), "fsdp", scatter_dimension=0, tiled=True
        ).astype(jnp.float32),
        lax.psum_scatter(
            grad_attention_gain.astype(jnp.bfloat16), "fsdp", scatter_dimension=0, tiled=True
        ).astype(jnp.float32),
        lax.psum_scatter(
            grad_attention_shift.astype(jnp.bfloat16), "fsdp", scatter_dimension=0, tiled=True
        ).astype(jnp.float32),
    )
    summed = lax.psum(
        (
            attention_shards[0],
            attention_shards[1],
            attention_shards[2],
            attention_shards[3],
            attention_shards[4],
            attention_shards[5],
            attention_shards[6],
            attention_shards[7],
            attention_shards[8],
            feed_shards[0],
            feed_shards[1],
            feed_shards[2],
            feed_shards[3],
            feed_shards[4],
            feed_shards[5],
        ),
        "dp",
    )
    return (
        layer_out,
        input_grad.reshape(tokens.shape),
        summed[0],
        summed[1],
        summed[2],
        summed[3],
        summed[4],
        summed[5],
        summed[6],
        summed[7],
        summed[8],
        summed[9],
        summed[10],
        summed[11],
        summed[12],
        summed[13],
        summed[14],
    )


def solution(mesh):
    small = mesh.shape["dp"] == 4 and mesh.shape["fsdp"] == NX * NZ
    return jax.shard_map(
        fused_layer if small else on_device,
        mesh=mesh,
        in_specs=(
            P(("dp", "fsdp"), None, None),
            P(("dp", "fsdp")),
            P(("dp", "fsdp"), None, None),
            P("fsdp", None),
            P("fsdp", None),
            P("fsdp", None),
            P("fsdp", None),
            P("fsdp"),
            P("fsdp"),
            P("fsdp"),
            P("fsdp"),
            P("fsdp"),
            P("fsdp", None),
            P("fsdp"),
            P("fsdp", None),
            P("fsdp"),
            P("fsdp"),
            P("fsdp"),
        ),
        out_specs=(
            P(("dp", "fsdp"), None, None),
            P(("dp", "fsdp"), None, None),
            P("fsdp", None),
            P("fsdp", None),
            P("fsdp", None),
            P("fsdp", None),
            P("fsdp"),
            P("fsdp"),
            P("fsdp"),
            P("fsdp"),
            P("fsdp"),
            P("fsdp", None),
            P("fsdp"),
            P("fsdp", None),
            P("fsdp"),
            P("fsdp"),
            P("fsdp"),
        ),
        check_vma=False,
    )
```

```python
import functools

import jax
import jax.numpy as jnp
from jax import lax
from jax.experimental import pallas as pl
from jax.experimental.pallas import tpu as pltpu
from jax.sharding import PartitionSpec as P

HEAD_DIM = 64
epsilon = 1e-05
F32 = jnp.float32
BF16 = jnp.bfloat16
MESH = pl.DeviceIdType.MESH
VMEM_LIMIT = 63 * 2**20
Shape = jax.ShapeDtypeStruct


def dot(left, right):
    return lax.dot_general(
        left, right, (((1,), (0,)), ((), ())), preferred_element_type=F32
    )


def dot_t(left, right):
    return lax.dot_general(
        left, right, (((1,), (1,)), ((), ())), preferred_element_type=F32
    )


def params(**extra):
    return pltpu.CompilerParams(vmem_limit_bytes=VMEM_LIMIT, **extra)


def whole(shape):
    return pl.BlockSpec(shape, lambda *_: (0,) * len(shape), pipeline_mode=pl.Buffered(1))


NX, NZ, ROWS = 2, 4, 96


def place():
    member = lax.axis_index("dp")
    shard = lax.axis_index("fsdp")
    return shard % NX, member // 2, shard // NX, member % 2


def at(x, y, z, core):
    return {"dp": y * 2 + core, "fsdp": z * NX + x}


def hello(peers):
    barrier = pltpu.get_barrier_semaphore()
    for peer in peers:
        pl.semaphore_signal(barrier, inc=1, device_id=peer, device_id_type=MESH)


def all_here(peers):
    pl.semaphore_wait(pltpu.get_barrier_semaphore(), len(peers))


def greet(peers):
    hello(peers)
    all_here(peers)


def all_peers():
    x, y, z, core = place()
    near = [at(x, 1 - y, z, core), at(x, y, z, 1 - core)]
    for step in range(1, NX * NZ):
        near.append({"dp": y * 2 + core, "fsdp": (z * NX + x + step) % (NX * NZ)})
    return near


class Wire:
    def __init__(self, send, recv):
        self.send, self.recv, self.slots = send, recv, {}

    def copy(self, key, source, target, peer):
        slot = self.slots.setdefault(key, len(self.slots))
        return pltpu.make_async_remote_copy(
            src_ref=source,
            dst_ref=target,
            send_sem=self.send.at[slot],
            recv_sem=self.recv.at[slot],
            device_id=peer,
            device_id_type=MESH,
        )


Q0, Q1, Q2, Q3, U0, U1, D0, D1, D2 = range(9)
PLANE, TURN_X, TURN_Y, REST, REST2, READY, SEND, CHIP, DEPTH, TOTAL, RELAY = range(11)
STAGES = (
    "plane", "turn_x", "turn_y", "rest", "rest2", "ready", "send", "chip", "depth", "total", "relay",
)
START, SENDS, DRAIN, BEFORE, ATTEND, NORM, UP_READY, UP_0, UP_1, DOWN_READY, DOWN_0 = range(11)
DOWN_1, DOWN_2, HIDDEN, GRAD_UP_0, GRAD_UP_1, FIRST, WEIGHTS, INPUTS = range(11, 19)
UP_STEPS, DOWN_STEPS = (UP_0, UP_1), (DOWN_0, DOWN_1, DOWN_2)
GRAD_UP_STEPS = (GRAD_UP_0, GRAD_UP_1)
QKV_PIECES = ((0, 1), (1, 1), (2, 2), (4, 2))
UP_PIECES = ((0, 512), (512, 256))
DOWN_PIECES = ((0, 256, 'x'), (256, 256, 'y'), (512, 256, ''))
GRAD_DOWN = ((0, 256), (256, 128))
GRAD_UP = ((0, 512), (512, 256))
OWN_LOADED = 3
FORWARD_PLAN = {
    START: ((Q0, PLANE), (U0, SEND), (Q1, PLANE), (U1, SEND), (Q0, TURN_X), (Q0, TURN_Y), (Q1, TURN_Y), (Q1, TURN_X), (Q2, PLANE), (D0, SEND), (Q0, REST), (Q3, PLANE), (D1, SEND), (Q2, TURN_X), (Q2, TURN_Y), (Q0, READY),),
    (ATTEND, 0): ((Q1, REST),),
    (BEFORE, 2): ((Q1, READY),),
    (ATTEND, 2): ((Q3, TURN_Y), (Q3, TURN_X),),
    (ATTEND, 3): ((D0, PLANE), (Q2, REST), (U0, PLANE), (D2, SEND), (Q3, REST),),
    (BEFORE, 4): ((Q2, READY),),
    (ATTEND, 5): ((U1, PLANE),),
    (BEFORE, 8): ((Q3, READY),),
    (ATTEND, 8): ((U0, TURN_Y), (U0, TURN_X),),
    (ATTEND, 10): ((D1, TURN_X), (D1, PLANE),),
    (ATTEND, 11): ((U1, TURN_X), (U1, TURN_Y), (D0, TURN_X), (D0, TURN_Y),),
    (NORM, 0): ((U0, REST),),
    (NORM, 1): ((D2, PLANE),),
    (UP_READY, 0): ((U0, READY),),
    (UP_0, 1): ((D0, REST),),
    (UP_0, 2): ((U1, REST), (D1, TURN_Y),),
    (UP_READY, 1): ((U1, READY), (D2, TURN_Y), (D1, REST),),
    (UP_1, 0): ((D0, REST2),),
    (DOWN_READY, 0): ((D0, READY), (D2, TURN_X), (D1, REST2),),
    (DOWN_READY, 1): ((D1, READY),),
    (DOWN_1, 0): ((D2, REST),),
    (DOWN_READY, 2): ((D2, READY),),
    SENDS: ((Q1, SEND), (Q2, SEND), (Q3, SEND),),
}
BACKWARD_PLAN = {
    START: (),
    DRAIN: ((Q1, TOTAL), (Q2, TOTAL), (Q3, TOTAL), (Q0, RELAY), (Q2, RELAY), (U0, RELAY), (Q1, RELAY), (D1, RELAY), (Q3, RELAY),),
    (HIDDEN, 3): ((D0, CHIP),),
    (GRAD_UP_0, 0): ((D1, CHIP),),
    (GRAD_UP_1, 1): ((D0, TURN_X),),
    (GRAD_UP_1, 2): ((D0, TURN_Y),),
    (FIRST, 0): ((U1, CHIP), (U0, CHIP), (D1, TURN_Y),),
    (FIRST, 1): ((D1, TURN_X),),
    (NORM, 1): ((U1, TURN_Y),),
    (ATTEND, 1): ((D0, DEPTH),),
    (ATTEND, 3): ((U1, TURN_X),),
    (WEIGHTS, 0): ((U0, TURN_Y), (U0, TURN_X),),
    (ATTEND, 5): ((U1, DEPTH), (Q0, CHIP),),
    (ATTEND, 6): ((D1, DEPTH),),
    (ATTEND, 7): ((D0, TOTAL),),
    (ATTEND, 8): ((Q0, TURN_Y), (Q0, TURN_X), (U0, DEPTH),),
    (ATTEND, 9): ((Q1, CHIP),),
    (WEIGHTS, 2): ((Q1, TURN_X), (Q1, TURN_Y), (Q0, DEPTH), (Q2, CHIP),),
    (INPUTS, 0): ((Q3, CHIP), (Q1, DEPTH), (Q2, TURN_Y), (U1, TOTAL), (Q2, TURN_X),),
    (INPUTS, 1): ((Q3, TURN_X), (Q3, TURN_Y), (Q2, DEPTH), (D1, TOTAL), (Q0, TOTAL), (U1, RELAY), (D0, RELAY), (U0, TOTAL), (Q3, DEPTH),),
}


GROUP = 4 * HEAD_DIM
PAIR = 2 * HEAD_DIM
SCALE = HEAD_DIM**-0.5
CHUNK = 1024


def run_events(pieces, events):
    for piece, stage in events:
        getattr(pieces[piece], STAGES[stage])()


def run_at(pieces, plan, prefix, index, count):
    for k in range(count):
        if (prefix, k) in plan:

            @pl.when(index == k)
            def _():
                run_events(pieces, plan[prefix, k])


class Piece:
    def __init__(self, name, wire, where, block):
        self.name, self.wire, self.where, self.block = name, wire, where, block

    def copy(self, key, source, peer):
        return self.wire.copy((self.name, key), source, source, peer)

    def copies(self, stage):
        x, y, z, core = self.where
        member, other = y * 2 + core, (1 - y) * 2 + core
        x_peer, y_peer = at(1 - x, y, z, core), at(x, 1 - y, z, core)
        c_peer = at(x, y, z, 1 - core)
        every, block = slice(None), self.block
        if stage == "depth":
            mine = block(member, z, x)
            plan = [(mine, at(x, y, (z + k) % NZ, core)) for k in range(1, NZ)]
        elif stage == "plane":
            mine = block(member, every, x)
            plan = [(mine, x_peer), (mine, y_peer)]
        elif stage == "turn":
            plan = [
                (block(other, pl.ds(0, 2), x), x_peer),
                (block(member, pl.ds(2, 2), 1 - x), y_peer),
            ]
        else:
            plan = [
                (block(member, every, x), c_peer),
                (block(other, every, x), c_peer),
                (block(member, every, 1 - x), c_peer),
                (block(other, every, 1 - x), c_peer),
            ]
        return [self.copy((stage, i), source, peer) for i, (source, peer) in enumerate(plan)]

    def send(self):
        for c in self.copies("depth"):
            c.start()

    def plane(self):
        for c in self.copies("depth"):
            c.wait_recv()
        for c in self.copies("plane"):
            c.start()
        self.copies("core")[0].start()

    def turn_x(self):
        self.copies("plane")[1].wait_recv()
        self.copies("turn")[0].start()
        self.copies("core")[1].start()

    def turn_y(self):
        self.copies("plane")[0].wait_recv()
        self.copies("turn")[1].start()
        self.copies("core")[2].start()

    def rest(self):
        for c in self.copies("turn"):
            c.wait_recv()
        self.copies("core")[3].start()

    def ready(self):
        for c in self.copies("core"):
            c.wait_recv()

    def drain(self):
        for stage in ("depth", "plane", "turn", "core"):
            for c in self.copies(stage):
                c.wait_send()


class DeepPiece(Piece):
    def __init__(self, name, wire, where, block, axis):
        super().__init__(name, wire, where, block)
        self.axis = axis

    def copies(self, stage):
        x, y, z, core = self.where
        member, other = y * 2 + core, (1 - y) * 2 + core
        x_peer, y_peer = at(1 - x, y, z, core), at(x, 1 - y, z, core)
        c_peer = at(x, y, z, 1 - core)
        by_x, every = self.axis == "x", slice(None)
        near = (member, 1 - x) if by_x else (other, x)
        far = (other, x) if by_x else (member, 1 - x)
        places = [(member, x), near, far, (other, 1 - x)]

        def block(place, zs):
            return self.block(place[0], zs, place[1])

        depth = [at(x, y, (z + k) % NZ, core) for k in range(1, NZ)]
        if stage == "first":
            plan = [(block(places[0], z), x_peer if by_x else y_peer)]
        elif stage == "depth":
            plan = [(block(places[0], z), peer) for peer in depth]
        elif stage == "near depth":
            plan = [(block(places[1], z), peer) for peer in depth]
        elif stage == "last":
            plan = [(block(p, every), y_peer if by_x else x_peer) for p in places[:2]]
        else:
            plan = [(block(p, every), c_peer) for p in places]
        return [self.copy((stage, i), source, peer) for i, (source, peer) in enumerate(plan)]

    def send(self):
        for c in self.copies("first") + self.copies("depth"):
            c.start()

    def plane(self):
        self.copies("first")[0].wait_recv()
        for c in self.copies("near depth"):
            c.start()

    def pass_on(self, stage, i):
        for c in self.copies(stage):
            c.wait_recv()
        self.copies("last")[i].start()
        self.copies("core")[i].start()

    def turn_x(self):
        self.pass_on("depth", 0)

    def turn_y(self):
        self.pass_on("near depth", 1)

    def rest(self):
        self.copies("last")[0].wait_recv()
        self.copies("core")[2].start()

    def rest2(self):
        self.copies("last")[1].wait_recv()
        self.copies("core")[3].start()

    def drain(self):
        for stage in ("first", "depth", "near depth", "last", "core"):
            for c in self.copies(stage):
                c.wait_send()


def half(index, shape):
    lanes = lax.broadcasted_iota(jnp.int32, shape, 1)
    return lanes < HEAD_DIM if index == 0 else lanes >= HEAD_DIM


def keep_half(index, value):
    return jnp.where(half(index, value.shape), value, jnp.zeros_like(value))


def attend_step(hidden_keys, q, k, v, powers, inverse, context_t):
    scaled, v_t = q * jnp.asarray(SCALE, BF16), v.T
    lanes = lax.broadcasted_iota(jnp.int32, k.shape, 1)
    mask = jnp.broadcast_to(hidden_keys, k.shape).astype(BF16)
    for h in range(2):
        rows = slice(h * HEAD_DIM, (h + 1) * HEAD_DIM)
        idle = lanes == (1 - h) * (2 * HEAD_DIM - 1)
        masked = jnp.where(half(h, k.shape), k, jnp.where(idle, mask, jnp.zeros_like(k)))
        scores = dot_t(masked, jnp.where(idle, jnp.ones_like(scaled), scaled))
        highest = jnp.max(scores, 0, keepdims=True)
        power = jnp.exp(scores - highest)
        inv = 1.0 / jnp.sum(power, 0, keepdims=True)
        low = power.astype(BF16)
        powers[h] = low
        inverse[h : h + 1] = inv
        context_t[rows] = (dot(v_t[rows], low) * inv).astype(BF16)


SQRT_HALF = 0.7071067811865476
PDF_SCALE = 0.3989422804014327
LOG2_E = 1.4426950408889634


def normal_parts(value):
    t = 1.0 / (1.0 + (0.3275911 * SQRT_HALF) * jnp.abs(value))
    bell = jnp.exp2((value * value) * (-0.5 * LOG2_E))
    poly = (0.5 * 1.061405429) * t - 0.5 * 1.453152027
    poly = poly * t + 0.5 * 1.421413741
    poly = poly * t - 0.5 * 0.284496736
    poly = poly * t + 0.5 * 0.254829592
    tail = (poly * t) * bell
    return jnp.where(value >= 0, 1.0 - tail, tail), bell * PDF_SCALE


def centre(resid):
    centred = resid - jnp.mean(resid, 1, keepdims=True)
    inv = lax.rsqrt(jnp.mean(centred * centred, 1, keepdims=True) + epsilon)
    return centred * inv, inv


def pull_back(scaled, normal, inv):
    return inv * (
        scaled
        - jnp.mean(scaled, 1, keepdims=True)
        - normal * jnp.mean(scaled * normal, 1, keepdims=True)
    )


def note(sums, row, value):
    sums[row : row + 1] += jnp.sum(value, 0, keepdims=True)


def forward_kernel(
    counts, tokens, qb, vb, ob, ag, ash, db, fg, fsh, ub, cotangent_h, wq, wk, wv, wo, wu_i, wd_i,
    w4_h, wu_h, wd_h, layer_out_h, query_h, keys_h, values_h, powers_h, context_t_h, first_t_h,
    err_two_h, resid_two_h, normal_one_h, pull_h, part_d_h, tokens_t_h, vec8, inverse, inverse_one, sums,
    w4, wu, wd, gv, up_row, context_t, tokens_t, send, recv, local,
):
    where = x, y, z, core = place()
    shard, member = z * NX + x, y * 2 + core
    total, width = tokens.shape
    length = total // 2
    columns = up_row.shape[1]
    wire = Wire(send, recv)

    def columns_of(first, pairs):
        return lambda who, zs, xs: w4.at[who, zs, xs, :, pl.ds(first * PAIR, pairs * PAIR)]

    def up_part(first, wide):
        return lambda who, zs, xs: wu.at[
            zs, xs, :, pl.ds(pl.multiple_of(who * width + first, 128), wide)
        ]

    def down_part(first, wide):
        return lambda who, zs, xs: wd.at[zs, xs, who, :, pl.ds(first, wide)]

    pieces = {
        Q0 + i: Piece(Q0 + i, wire, where, columns_of(first, pairs))
        for i, (first, pairs) in enumerate(QKV_PIECES)
    }
    for i, part in enumerate(UP_PIECES):
        pieces[U0 + i] = Piece(U0 + i, wire, where, up_part(*part))
    for i, (first, wide, axis) in enumerate(DOWN_PIECES):
        if axis:
            piece = DeepPiece(D0 + i, wire, where, down_part(first, wide), axis)
        else:
            piece = Piece(D0 + i, wire, where, down_part(first, wide))
        pieces[D0 + i] = piece

    own = [
        pltpu.make_async_copy(wq, w4.at[member, z, x], local.at[0, 0]),
        pltpu.make_async_copy(
            wu_i.at[:, pl.ds(pl.multiple_of(member * width, width), width)],
            wu.at[z, x, :, pl.ds(pl.multiple_of(member * width, width), width)],
            local.at[0, 1],
        ),
        pltpu.make_async_copy(wd_i.at[member], wd.at[z, x, member], local.at[0, 2]),
    ]
    for i, w in enumerate((wq, wk, wv, wo)):

        @pl.when(member == i)
        def _():
            pltpu.make_async_copy(w, w4.at[i, z, x], local.at[0, 0]).start()

    for c in own[1:]:
        c.start()
    gv[shard] = jnp.zeros(gv.shape[1:], F32)
    bias_row = ub[...].astype(F32).reshape(1, 4 * ROWS)
    for i in range(3):
        gv[shard, 8 + i : 9 + i, :] = bias_row[:, i * 128 : (i + 1) * 128]
    for i, vector in enumerate((qb, vb, ob, ag, ash, db, fg, fsh)):
        gv[shard, i : i + 1, 0:ROWS] = vector[...].astype(F32).reshape(1, ROWS)
    greet(all_peers())
    for c in own:
        c.wait()

    def vec_copy(k):
        peer = {"dp": member, "fsdp": (shard + k) % (NX * NZ)}
        return wire.copy(("v", k), gv.at[shard], gv.at[shard], peer)

    pieces[Q0].send()
    for k in range(1, NX * NZ):
        vec_copy(k).start()
    run_events(pieces, FORWARD_PLAN[SENDS])
    tokens_t[...] = tokens[...].T
    tokens_out = pltpu.make_async_copy(tokens_t, tokens_t_h, local.at[5, 3])
    tokens_out.start()
    sums[...] = jnp.zeros_like(sums)
    run_events(pieces, FORWARD_PLAN[START][:1])
    for k in range(1, NX * NZ):
        vec_copy(k).wait_recv()
    lanes = lax.broadcasted_iota(jnp.int32, (128, width), 0)
    features = lax.broadcasted_iota(jnp.int32, (128, width), 1)
    per = columns // (NX * NZ)
    joined = jnp.zeros((8, width), F32)
    for f in range(NX * NZ):
        pick = (features == f * ROWS + lanes) & (lanes < ROWS)
        joined = joined + dot(gv[f, 0:8, :].astype(BF16), pick.astype(F32).astype(BF16))
        for i in range(3):
            up_row[:, f * per + i * 128 : f * per + (i + 1) * 128] = gv[f, 8 + i : 9 + i, :]
    vec8[...] = joined
    run_events(pieces, FORWARD_PLAN[START][1:])

    def attention(qkv, powers):
        def outs(pair, s):
            rows = pl.ds(pl.multiple_of(s * length, length), length)
            cols = pl.ds(pl.multiple_of(pair * PAIR, PAIR), PAIR)
            return [
                pltpu.make_async_copy(qkv.at[s, i], a.at[rows, cols], local.at[1 + i, s])
                for i, a in enumerate((query_h, keys_h, values_h))
            ] + [
                pltpu.make_async_copy(
                    powers.at[s], powers_h.at[s, pl.ds(pair * 2, 2)], local.at[4, s]
                )
            ]

        @pl.loop(0, 12)
        def _(t):
            pair, s = t // 2, t % 2
            rows = pl.ds(pl.multiple_of(s * length, length), length)
            cols = pl.ds(pl.multiple_of(pair * PAIR, PAIR), PAIR)
            run_at(pieces, FORWARD_PLAN, BEFORE, t, 12)

            @pl.when(t >= 2)
            def _():
                for c in outs(pair, s):
                    c.wait()

            weights = jnp.concatenate(
                [w4[i, :, :, :, cols].reshape(width, PAIR) for i in range(3)], 1
            )
            together = dot(tokens[rows, :], weights)
            q = (together[:, :PAIR] + vec8[0:1, cols]).astype(BF16)
            k = together[:, PAIR : 2 * PAIR].astype(BF16)
            v = (together[:, 2 * PAIR :] + vec8[1:2, cols]).astype(BF16)
            qkv[s, 0], qkv[s, 1], qkv[s, 2] = q, k, v
            key_rows = lax.broadcasted_iota(jnp.int32, (length, 1), 0)
            hidden_keys = jnp.where(key_rows < counts[s], 0.0, -1000000000.0)
            attend_step(
                hidden_keys, q, k, v, powers.at[s], inverse.at[s, pair], context_t.at[cols, rows]
            )
            for c in outs(pair, s):
                c.start()
            run_at(pieces, FORWARD_PLAN, ATTEND, t, 12)

        for s in range(2):
            for c in outs(5, s):
                c.wait()

    pl.run_scoped(
        attention,
        pltpu.VMEM((2, 3, length, PAIR), BF16),
        pltpu.VMEM((2, 2, length, length), BF16),
    )

    def feed(act, pull, first_low, first_t, err_two, err_two_t, normal_one, resid_two, low_out, cotangent, part_d):
        v = [vec8[i : i + 1] for i in range(8)]
        out_bias, gain_one, shift_one, down_bias, gain_two, shift_two = v[2:]
        loads = [pltpu.make_async_copy(cotangent_h, cotangent, local.at[5, 0])]
        outs = [
            pltpu.make_async_copy(w4, w4_h, local.at[5, 1]),
            pltpu.make_async_copy(context_t, context_t_h, local.at[5, 2]),
        ]
        for c in loads + outs:
            c.start()
        outs.append(tokens_out)

        def keep(source, target, slot):
            c = pltpu.make_async_copy(source, target, local.at[6 + slot // 4, slot % 4])
            c.start()
            outs.append(c)

        def rows_of(s):
            return pl.ds(pl.multiple_of(s * length, length), length)

        @pl.loop(0, 2)
        def _(s):
            rows = rows_of(s)
            r1 = (
                tokens[rows, :].astype(F32)
                + dot(context_t[:, rows].T, w4[3].reshape(width, width))
                + out_bias
            )
            normal, inv = centre(r1)
            normal_one[rows, :] = normal
            inverse_one[rows, :] = inv
            low = (normal * gain_one + shift_one).astype(BF16)
            first_low[rows, :] = low
            first_t[:, rows] = low.T
            run_at(pieces, FORWARD_PLAN, NORM, s, 2)

        keep(normal_one, normal_one_h, 0)
        keep(first_t, first_t_h, 1)
        for i, (first, wide) in enumerate(UP_PIECES):
            run_events(pieces, FORWARD_PLAN[UP_READY, i])

            @pl.loop(0, 4)
            def _(m):
                cols = pl.ds(pl.multiple_of(m * width + first, 128), wide)
                weight = wu[:, :, :, cols].reshape(width, wide)
                for s in range(2):
                    rows = slice(s * length, (s + 1) * length)
                    hidden = dot(first_low[rows, :], weight) + up_row[:, cols]
                    cdf, density = normal_parts(hidden)
                    act[rows, cols] = (hidden * cdf).astype(BF16)
                    pull[rows, cols] = (cdf + hidden * density).astype(BF16)
                run_at(pieces, FORWARD_PLAN, UP_STEPS[i], m, 4)

        keep(wu, wu_h, 2)
        keep(pull, pull_h, 3)
        for c in loads:
            c.wait()
        for i, (first, wide, _) in enumerate(DOWN_PIECES):
            run_events(pieces, FORWARD_PLAN[DOWN_READY, i])

            @pl.loop(0, 2)
            def _(s):
                rows = rows_of(s)
                weight = wd[:, :, :, :, first : first + wide].reshape(columns, wide)
                resid_two[rows, first : first + wide] = dot(act[rows, :], weight)
                run_at(pieces, FORWARD_PLAN, DOWN_STEPS[i], s, 2)

        keep(wd, wd_h, 4)

        @pl.loop(0, 2)
        def _(s):
            rows = rows_of(s)
            first = normal_one[rows, :] * gain_one + shift_one
            normal, inv = centre(first + resid_two[rows, :] + down_bias)
            live = lax.broadcasted_iota(jnp.int32, (length, 1), 0) < counts[s]
            low_out[rows, :] = jnp.where(live, normal * gain_two + shift_two, 0.0).astype(BF16)
            grad_y = jnp.where(live, cotangent[rows, :].astype(F32), 0.0)
            resid = pull_back(grad_y * gain_two, normal, inv)
            resid_two[rows, :] = resid
            low = resid.astype(BF16)
            err_two[rows, :] = low
            err_two_t[:, rows] = low.T
            note(sums, 6, grad_y * normal)
            note(sums, 7, grad_y)
            note(sums, 5, low.astype(F32))

        keep(low_out, layer_out_h, 5)
        keep(err_two, err_two_h, 6)
        keep(resid_two, resid_two_h, 7)

        @pl.loop(0, NZ)
        def _(zz):
            cols = pl.ds(pl.multiple_of(zz * NX * per, per), NX * per)
            grad = dot(err_two_t[...], act[:, cols]).astype(BF16)
            for xx in range(NX):
                part_d[:, zz, xx] = grad[:, xx * per : (xx + 1) * per].reshape(4, width // 4, per)
            pltpu.make_async_copy(part_d.at[:, zz], part_d_h.at[:, zz], local.at[8, zz]).start()

        for zz in range(NZ):
            outs.append(
                pltpu.make_async_copy(part_d.at[:, zz], part_d_h.at[:, zz], local.at[8, zz])
            )
        for c in outs:
            c.wait()
        for p in pieces.values():
            p.drain()
        for k in range(1, NX * NZ):
            vec_copy(k).wait_send()

    pl.run_scoped(
        feed,
        pltpu.VMEM((total, columns), BF16),
        pltpu.VMEM((total, columns), BF16),
        pltpu.VMEM((total, width), BF16),
        pltpu.VMEM((width, total), BF16),
        pltpu.VMEM((total, width), BF16),
        pltpu.VMEM((width, total), BF16),
        pltpu.VMEM((total, width), F32),
        pltpu.VMEM((total, width), F32),
        pltpu.VMEM((total, width), BF16),
        pltpu.VMEM((total, width), BF16),
        pltpu.VMEM((4, NZ, NX, width // 4, per), BF16),
    )


def forward(counts, rows, vectors, cotangent, wq, wk, wv, wo, wu, wd):
    total, width = rows.shape
    columns = wu.shape[1]
    slots, length = 2, total // 2
    heads = width // HEAD_DIM
    per = columns // (NX * NZ)
    copies = 7 + (len(QKV_PIECES) + len(UP_PIECES) + len(DOWN_PIECES)) * 13
    hbm, vmem = pl.BlockSpec(memory_space=pl.ANY), pl.BlockSpec(memory_space=pltpu.VMEM)
    w4_shape = (4, NZ, NX, ROWS, width)
    wu_shape = (NZ, NX, ROWS, columns)
    wd_shape = (NZ, NX, 4, ROWS, width)
    return pl.pallas_call(
        forward_kernel,
        name="forward",
        in_specs=[pl.BlockSpec(memory_space=pltpu.SMEM)] + [vmem] * 10 + [hbm] * 7,
        out_specs=[hbm] * 16 + [vmem] * 4,
        out_shape=[
            Shape(w4_shape, BF16),
            Shape(wu_shape, BF16),
            Shape(wd_shape, BF16),
            Shape((total, width), BF16),
            Shape((total, width), BF16),
            Shape((total, width), BF16),
            Shape((total, width), BF16),
            Shape((slots, heads, length, length), BF16),
            Shape((width, total), BF16),
            Shape((width, total), BF16),
            Shape((total, width), BF16),
            Shape((total, width), F32),
            Shape((total, width), F32),
            Shape((total, columns), BF16),
            Shape((4, NZ, NX, width // 4, per), BF16),
            Shape((width, total), BF16),
            Shape((8, width), F32),
            Shape((slots, heads // 2, 2, length), F32),
            Shape((total, 1), F32),
            Shape((8, width), F32),
        ],
        scratch_shapes=[
            pltpu.VMEM(w4_shape, BF16),
            pltpu.VMEM(wu_shape, BF16),
            pltpu.VMEM(wd_shape, BF16),
            pltpu.VMEM((NX * NZ, 16, 128), F32),
            pltpu.VMEM((1, columns), F32),
            pltpu.VMEM((width, total), BF16),
            pltpu.VMEM((width, total), BF16),
            pltpu.SemaphoreType.DMA((copies,)),
            pltpu.SemaphoreType.DMA((copies,)),
            pltpu.SemaphoreType.DMA((9, 4)),
        ],
        compiler_params=params(collective_id=0, has_side_effects=True),
    )(counts, rows, *vectors, cotangent, wq, wk, wv, wo, wu, wd.reshape(4, ROWS, width))


class Chunk:
    def __init__(self, name, wire, where, part, mine, scratch):
        self.name, self.wire, self.where = name, wire, where
        self.part, self.mine = part, mine
        self.rc, self.bx, self.by, self.cx, self.cy, self.bz, self.fin = scratch

    @staticmethod
    def scratch(a, b):
        return [
            pltpu.VMEM((2, NZ, NX, a, b), BF16),
            pltpu.VMEM((2, 2, a, b), BF16),
            pltpu.VMEM((2, NX, a, b), BF16),
            pltpu.VMEM((2, a, b), BF16),
            pltpu.VMEM((2, a, b), BF16),
            pltpu.VMEM((NZ - 1, a, b), BF16),
            pltpu.VMEM((4, a, b), BF16),
        ]

    def copies(self, stage):
        x, y, z, core = self.where
        member, other = y * 2 + core, (1 - y) * 2 + core
        x_peer, y_peer = at(1 - x, y, z, core), at(x, 1 - y, z, core)
        c_peer = at(x, y, z, 1 - core)
        rc, fin = self.rc, self.fin
        if stage == "core":
            plan = [(self.part.at[yy * 2 + 1 - core], rc.at[yy], c_peer) for yy in range(2)]
        elif stage == "plane":
            plan = [
                (rc.at[:, pl.ds(0, 2), 1 - x], self.bx, x_peer),
                (rc.at[1 - y, pl.ds(2, 2)], self.by, y_peer),
            ]
        elif stage == "turn":
            plan = [
                (rc.at[1 - y, pl.ds(0, 2), x], self.cy, y_peer),
                (rc.at[y, pl.ds(2, 2), 1 - x], self.cx, x_peer),
            ]
        elif stage == "depth":
            plan = [
                (rc.at[y, (z + k) % NZ, x], self.bz.at[k - 1], at(x, y, (z + k) % NZ, core))
                for k in range(1, NZ)
            ]
        elif stage == "spread":
            plan = [(fin.at[member], fin.at[member], peer) for peer in (y_peer, c_peer)]
        else:
            plan = [(fin.at[other], fin.at[other], c_peer)]
        return [
            self.wire.copy((self.name, stage, i), source, target, peer)
            for i, (source, target, peer) in enumerate(plan)
        ]

    def start(self, stage):
        for c in self.copies(stage):
            c.start()

    def arrive(self, stage):
        for c in self.copies(stage):
            c.wait_recv()

    def chip(self):
        core = self.where[3]
        self.arrive("core")
        rc, mine = self.rc, self.mine
        for yy in range(2):

            @pl.loop(0, NZ)
            def _(zz):
                for xx in range(NX):
                    rc[yy, zz, xx] = rc[yy, zz, xx] + mine(yy, core, zz, xx)

        self.start("plane")

    def turn_y(self):
        x, y, z, core = self.where
        rc, bx = self.rc, self.bx
        self.copies("plane")[0].wait_recv()

        @pl.loop(0, 2)
        def _(zz):
            for yy in range(2):
                rc[yy, zz, x] = rc[yy, zz, x] + bx[yy, zz]

        self.copies("turn")[0].start()

    def turn_x(self):
        x, y, z, core = self.where
        rc, by = self.rc, self.by
        self.copies("plane")[1].wait_recv()

        @pl.loop(0, 2)
        def _(zz):
            for xx in range(NX):
                rc[y, 2 + zz, xx] = rc[y, 2 + zz, xx] + by[zz, xx]

        self.copies("turn")[1].start()

    def depth(self):
        x, y, z, core = self.where
        rc, cx, cy = self.rc, self.cx, self.cy
        self.arrive("turn")

        @pl.loop(0, 2)
        def _(zz):
            rc[y, zz, x] = rc[y, zz, x] + cy[zz]
            rc[y, 2 + zz, x] = rc[y, 2 + zz, x] + cx[zz]

        self.start("depth")

    def total(self):
        x, y, z, core = self.where
        self.arrive("depth")
        summed = self.rc[y, z, x].astype(F32)
        for k in range(NZ - 1):
            summed = summed + self.bz[k].astype(F32)
        self.fin[y * 2 + core] = summed.astype(BF16)
        self.start("spread")

    def relay(self):
        self.copies("spread")[0].wait_recv()
        self.start("relay")

    def done(self):
        self.copies("spread")[1].wait_recv()
        self.arrive("relay")

    def drain(self):
        for stage in ("core", "plane", "turn", "depth", "spread", "relay"):
            for c in self.copies(stage):
                c.wait_send()


def attend_back_step(query, keys, values, powers, inverse, context_t, grad):
    q2 = query[...] * jnp.asarray(SCALE, BF16)
    k2, v2 = keys[...], values[...]
    grad_t = grad[...].astype(F32).T
    product = grad_t * context_t[...].astype(F32)
    k_t = k2.T
    inv = [inverse[h : h + 1] for h in range(2)]
    scaled_t = jnp.concatenate([grad_t[:HEAD_DIM] * inv[0], grad_t[HEAD_DIM:] * inv[1]], 0).astype(
        BF16
    )
    scaled = scaled_t.T
    dq, dk, dv = [], 0.0, 0.0
    for h in range(2):
        rows = slice(h * HEAD_DIM, (h + 1) * HEAD_DIM)
        inner = jnp.sum(product[rows], 0, keepdims=True) * inv[h]
        power = powers[h]
        grad_probs = dot(keep_half(h, v2), scaled_t)
        grad_scores = (power.astype(F32) * (grad_probs - inner)).astype(BF16)
        dv = dv + dot(power, keep_half(h, scaled))
        dk = dk + dot(grad_scores, keep_half(h, q2))
        dq.append(dot(k_t[rows], grad_scores))
    return (jnp.concatenate(dq, 0) * SCALE).astype(BF16).T, dk.astype(BF16), dv.astype(BF16)


def backward_kernel(
    part_d, err_two_h, pull_h, wd_h, wu_h, resid_two_h, normal_one_h, inverse_one, first_t_h,
    query_h, keys_h, values_h, powers_h, inverse, context_t_h, tokens_t_h, w4_h, vec, sums_in,
    o4, ou, od, ov, input_grad,
    part_u, own_d, err_one, grad_context, grad_in, tokens_t, context_t, sums, sums_up,
    pv, va, vb, *rest,
):
    count = 7 * (len(GRAD_DOWN) + len(GRAD_UP) + 4)
    scratch, (send, recv, load) = list(rest[:count]), rest[count:]
    where = x, y, z, core = place()
    shard, member = z * NX + x, y * 2 + core
    total, width = grad_in.shape
    length = total // 2
    columns = sums_up.shape[1]
    loops = columns // CHUNK
    wire = Wire(send, recv)

    def lanes_of(part, first, wide):
        return part.at[:, :, :, :, pl.ds(first, wide)]

    def own_part(part):
        return lambda yy, core, zz, xx: part[yy * 2 + core, zz, xx]

    def take():
        mine = scratch[:7]
        del scratch[:7]
        return mine

    d, u = [], []
    for i, part in enumerate(GRAD_DOWN):
        own = lanes_of(own_d, *part)
        d.append(
            Chunk(
                D0 + i, wire, where, lanes_of(part_d, *part),
                lambda yy, core, zz, xx, own=own: own[yy, zz, xx], take(),
            )
        )
    for i, part in enumerate(GRAD_UP):
        rows_u = lanes_of(part_u, *part)
        u.append(Chunk(U0 + i, wire, where, rows_u, own_part(rows_u), take()))
    chunks = {c.name: c for c in d + u}

    def rows_of(s):
        return pl.ds(pl.multiple_of(s * length, length), length)

    def block(j):
        return pl.ds(pl.multiple_of(j * CHUNK, CHUNK), CHUNK)

    own_loads = [
        pltpu.make_async_copy(part_d.at[yy * 2 + core], own_d.at[yy], load.at[0, yy])
        for yy in range(2)
    ]
    gain_one = vec[3:4].astype(F32)
    sums[...] = sums_in[...]
    sums_up[...] = jnp.zeros_like(sums_up)

    def feed_back(wd, wu, pull, err_two, normal_one, first_t, wo):
        first_loads = [
            pltpu.make_async_copy(err_two_h, err_two, load.at[1, 0]),
            pltpu.make_async_copy(resid_two_h, grad_in, load.at[1, 1]),
            pltpu.make_async_copy(normal_one_h, normal_one, load.at[1, 2]),
            pltpu.make_async_copy(w4_h.at[3], wo, load.at[1, 3]),
        ]
        late_loads = [
            pltpu.make_async_copy(first_t_h, first_t, load.at[2, 0]),
            pltpu.make_async_copy(context_t_h, context_t, load.at[2, 2]),
            pltpu.make_async_copy(tokens_t_h, tokens_t, load.at[2, 1]),
        ]

        def loads(j):
            return [
                pltpu.make_async_copy(wd_h.at[block(j)], wd.at[block(j)], load.at[3, j]),
                pltpu.make_async_copy(pull_h.at[:, block(j)], pull.at[:, block(j)], load.at[4, j]),
                pltpu.make_async_copy(wu_h.at[:, block(j)], wu.at[:, block(j)], load.at[5, j]),
            ]

        first_loads[0].start()
        for c in loads(0)[:2]:
            c.start()
        hello(all_peers())
        for j in range(1, loops):
            for c in loads(j)[:2]:
                c.start()
        for c in own_loads + first_loads[1:]:
            c.start()
        for j in range(loops):
            loads(j)[2].start()
        for c in late_loads:
            c.start()
        first_loads[0].wait()

        @pl.loop(0, 2 * loops)
        def _(t):
            j = t % loops
            rows = rows_of(t // loops)

            @pl.when(t < loops)
            def _():
                for c in loads(j)[:2]:
                    c.wait()

            grads = dot_t(err_two[rows, :], wd[block(j), :])
            low = (grads * pull[rows, block(j)].astype(F32)).astype(BF16)
            pull[rows, block(j)] = low
            sums_up[:, block(j)] += jnp.sum(low.astype(F32), 0, keepdims=True)

            @pl.when(t == 0)
            def _():
                all_here(all_peers())
                for c in d:
                    c.start("core")

            @pl.when(t == OWN_LOADED)
            def _():
                for c in own_loads:
                    c.wait()

            run_at(chunks, BACKWARD_PLAN, HIDDEN, t, 2 * loops)

        for c in late_loads[:1]:
            c.wait()

        for i, (first, wide) in enumerate(GRAD_UP):

            @pl.loop(0, 4)
            def _(m):
                cols = pl.ds(pl.multiple_of(m * width + first, 128), wide)
                part_u[m, :, :, :, first : first + wide] = (
                    dot(first_t[...], pull[:, cols]).astype(BF16).reshape(NZ, NX, ROWS, wide)
                )

                @pl.when(m == 3)
                def _():
                    u[i].start("core")

                run_at(chunks, BACKWARD_PLAN, GRAD_UP_STEPS[i], m, 4)

        for c in first_loads[1:] + late_loads[1:]:
            c.wait()
        for j in range(loops):
            loads(j)[2].wait()

        @pl.loop(0, 2)
        def _(s):
            rows = rows_of(s)
            grad_first = grad_in[rows, :] + dot_t(pull[rows, :], wu[...])
            run_at(chunks, BACKWARD_PLAN, FIRST, s, 2)
            normal = normal_one[rows, :]
            note(sums, 3, grad_first * normal)
            note(sums, 4, grad_first)
            resid = pull_back(grad_first * gain_one, normal, inverse_one[rows, :])
            grad_in[rows, :] = resid
            low = resid.astype(BF16)
            err_one[rows, :] = low
            note(sums, 2, low.astype(F32))
            grad_context[rows, :] = dot_t(low, wo[...]).astype(BF16)
            run_at(chunks, BACKWARD_PLAN, NORM, s, 2)

    pl.run_scoped(
        feed_back,
        pltpu.VMEM((columns, width), BF16),
        pltpu.VMEM((width, columns), BF16),
        pltpu.VMEM((total, columns), BF16),
        pltpu.VMEM((total, width), BF16),
        pltpu.VMEM((total, width), F32),
        pltpu.VMEM((width, total), BF16),
        pltpu.VMEM((width, width), BF16),
    )

    def attend_and_inputs(qkv, powers, grads, weights, part_q):
        halves = [part_q.at[0], part_q.at[1]] + [
            part_q.at[2, :, :, :, :, pl.ds(i * PAIR, PAIR)] for i in range(2)
        ]
        q = [
            Chunk(Q0 + i, wire, where, p, own_part(p), take())
            for i, p in enumerate(halves)
        ]
        chunks.update({c.name: c for c in q})

        def loads(t):
            pair, s = t // 2, t % 2
            rows, cols = rows_of(s), pl.ds(pl.multiple_of(pair * PAIR, PAIR), PAIR)
            return [
                pltpu.make_async_copy(a.at[rows, cols], qkv.at[s, i], load.at[6 + i, s])
                for i, a in enumerate((query_h, keys_h, values_h))
            ] + [
                pltpu.make_async_copy(
                    powers_h.at[s, pl.ds(pair * 2, 2)], powers.at[s], load.at[9, s]
                )
            ]

        weight_loads = [
            pltpu.make_async_copy(
                w4_h.at[i, :, pl.ds(g * GROUP, GROUP)],
                weights.at[g, :, pl.ds(i * GROUP, GROUP)],
                load.at[10 + g, i],
            )
            for g in range(3)
            for i in range(3)
        ]
        for c in loads(0) + weight_loads:
            c.start()

        @pl.loop(0, 3)
        def _(g):
            @pl.loop(0, 4)
            def _(k):
                t = g * 4 + k
                pair, s = t // 2, t % 2

                @pl.when(t < 11)
                def _():
                    for c in loads(t + 1):
                        c.start()

                for c in loads(t):
                    c.wait()
                rows, cols = rows_of(s), pl.ds(pl.multiple_of(pair * PAIR, PAIR), PAIR)
                values = attend_back_step(
                    qkv.at[s, 0], qkv.at[s, 1], qkv.at[s, 2], powers.at[s],
                    inverse.at[s, pair], context_t.at[cols, rows], grad_context.at[rows, cols],
                )
                for i, value in enumerate(values):
                    lane = pl.multiple_of(i * GROUP + (pair % 2) * PAIR, PAIR)
                    grads[g, rows, pl.ds(lane, PAIR)] = value
                run_at(chunks, BACKWARD_PLAN, ATTEND, t, 12)

            cols = pl.ds(pl.multiple_of(g * GROUP, GROUP), GROUP)
            for i in range(3):
                lanes = slice(i * GROUP, (i + 1) * GROUP)
                part_q[g, i] = (
                    dot(tokens_t[...], grads[g, :, lanes])
                    .astype(BF16)
                    .reshape(NZ, NX, ROWS, GROUP)
                )
            part_q[g, 3] = (
                dot(context_t[...], err_one[:, cols]).astype(BF16).reshape(NZ, NX, ROWS, GROUP)
            )
            for i in range(2):

                @pl.when(g == i)
                def _():
                    q[i].start("core")

            @pl.when(g == 2)
            def _():
                q[2].start("core")
                q[3].start("core")

            sums[0:1, cols] = jnp.sum(grads[g, :, :GROUP].astype(F32), 0, keepdims=True)
            sums[1:2, cols] = jnp.sum(grads[g, :, 2 * GROUP :].astype(F32), 0, keepdims=True)
            run_at(chunks, BACKWARD_PLAN, WEIGHTS, g, 3)

        pv[...] = jnp.zeros_like(pv)
        lanes = lax.broadcasted_iota(jnp.int32, (width, NX * NZ * 128), 1)
        rows = lax.broadcasted_iota(jnp.int32, (width, NX * NZ * 128), 0)
        pick = (rows == (lanes // 128) * ROWS + lanes % 128) & (lanes % 128 < ROWS)
        spread8 = lax.dot_general(
            sums[...], pick.astype(F32), (((1,), (0,)), ((), ())),
            precision=lax.Precision.HIGHEST, preferred_element_type=F32,
        )
        per = columns // (NX * NZ)
        for f in range(NX * NZ):
            pv[f, 0:8, :] = spread8[:, f * 128 : (f + 1) * 128]
            for i in range(3):
                first = f * per + i * 128
                pv[f, 8 + i : 9 + i, :] = sums_up[:, first : first + 128]

        def to_owner(k):
            to = (shard + k) % (NX * NZ)
            return wire.copy(("v", k), pv.at[to], va.at[k - 1], {"dp": member, "fsdp": to})

        for k in range(1, NX * NZ):
            to_owner(k).start()
        for c in weight_loads:
            c.wait()
        out = []
        for i in range(3):
            lanes = slice(i * GROUP, (i + 1) * GROUP)
            summed = grad_in[:, lanes]
            for g in range(3):
                summed = summed + dot_t(grads[g], weights[g, lanes, :])
            grad_in[:, lanes] = summed
            c = pltpu.make_async_copy(
                grad_in.at[:, lanes], input_grad.at[:, lanes], load.at[13, i]
            )
            c.start()
            out.append(c)
            run_events(chunks, BACKWARD_PLAN.get((INPUTS, i), ()))

        for k in range(1, NX * NZ):
            to_owner(k).wait_recv()
        partial = pv[shard]
        for k in range(NX * NZ - 1):
            partial = partial + va[k]
        vb[member] = partial

        def to_member(i):
            dy, dc = ((0, 1), (1, 0), (1, 1))[i]
            peer = at(x, (y + dy) % 2, z, (core + dc) % 2)
            return wire.copy(("w", i), vb.at[member], vb.at[member], peer)

        for i in range(3):
            to_member(i).start()
        run_events(chunks, BACKWARD_PLAN[DRAIN])
        for i in range(3):
            to_member(i).wait_recv()
        ov[...] = (vb[0] + vb[1]) + (vb[2] + vb[3])
        for out_ref, group, parts in ((od, d, GRAD_DOWN), (ou, u, GRAD_UP)):
            for c, (first, wide) in zip(group, parts):
                c.done()
                out_ref[:, :, first : first + wide] = c.fin[...]
        first = 0
        for c in q:
            c.done()
            last = first + c.fin.shape[2]
            o4[:, :, first:last] = c.fin[...]
            first = last
        for c in out:
            c.wait()
        for c in d + u + q:
            c.drain()
        for k in range(1, NX * NZ):
            to_owner(k).wait_send()
        for i in range(3):
            to_member(i).wait_send()

    pl.run_scoped(
        attend_and_inputs,
        pltpu.VMEM((2, 3, length, PAIR), BF16),
        pltpu.VMEM((2, 2, length, length), BF16),
        pltpu.VMEM((3, total, width), BF16),
        pltpu.VMEM((3, width, width), BF16),
        pltpu.VMEM((3, 4, NZ, NX, ROWS, GROUP), BF16),
    )


def backward(
    part_d, err_two, pull, wd, wu, resid_two, normal_one, inverse_one, first_t,
    query, keys, values, powers, inverse, context_t, tokens_t, w4, vec, sums_in,
):
    total, width = query.shape
    columns = wu.shape[1]
    per = columns // (NX * NZ)
    hbm, vmem = pl.BlockSpec(memory_space=pl.ANY), pl.BlockSpec(memory_space=pltpu.VMEM)
    d_block, copies = part_d.shape[3:], 7 + 3 + (len(GRAD_DOWN) + len(GRAD_UP) + 4) * 12
    scratch = [
        pltpu.VMEM((4, NZ, NX, ROWS, width), BF16),
        pltpu.VMEM((2, NZ, NX) + d_block, BF16),
        pltpu.VMEM((total, width), BF16),
        pltpu.VMEM((total, width), BF16),
        pltpu.VMEM((total, width), F32),
        pltpu.VMEM((width, total), BF16),
        pltpu.VMEM((width, total), BF16),
        pltpu.VMEM((8, width), F32),
        pltpu.VMEM((1, columns), F32),
        pltpu.VMEM((NX * NZ, 16, 128), F32),
        pltpu.VMEM((NX * NZ - 1, 16, 128), F32),
        pltpu.VMEM((4, 16, 128), F32),
    ]
    for _, wide in GRAD_DOWN:
        scratch += Chunk.scratch(d_block[0], wide)
    for _, wide in GRAD_UP:
        scratch += Chunk.scratch(ROWS, wide)
    scratch += Chunk.scratch(ROWS, GROUP) * 2 + Chunk.scratch(ROWS, PAIR) * 2
    scratch += [pltpu.SemaphoreType.DMA((copies,))] * 2 + [pltpu.SemaphoreType.DMA((14, 4))]
    return pl.pallas_call(
        backward_kernel,
        name="backward",
        in_specs=[hbm] * 7 + [vmem] + [hbm] * 5 + [vmem] + [hbm] * 3 + [vmem] * 2,
        out_specs=[vmem] * 4 + [hbm],
        out_shape=[
            Shape((4, ROWS, width), BF16),
            Shape((4, ROWS, width), BF16),
            Shape((4,) + part_d.shape[3:], BF16),
            Shape((16, 128), F32),
            Shape((total, width), F32),
        ],
        scratch_shapes=scratch,
        compiler_params=params(collective_id=1, has_side_effects=True),
    )(
        part_d, err_two, pull, wd, wu, resid_two, normal_one, inverse_one, first_t,
        query, keys, values, powers, inverse, context_t, tokens_t, w4, vec, sums_in,
    )


def finish_kernel(layer_in, grad_in, o4, ou, od, ov, layer_out, input_grad, *rest):
    outs, stage, (layer_v, grad_v, sem) = rest[:15], rest[15:30], rest[30:]
    part = grad_v.shape[0] // 4
    takes, gives = [], []
    for source, middle, target, first in (
        (layer_in, layer_v, layer_out, 6), (grad_in, grad_v, input_grad, 14),
    ):
        for i in range(4):
            span = slice(i * part, (i + 1) * part)
            takes.append(
                pltpu.make_async_copy(source.at[span], middle.at[span], sem.at[first + i])
            )
            gives.append(
                pltpu.make_async_copy(middle.at[span], target.at[span], sem.at[first + 4 + i])
            )
    for c in takes:
        c.start()
    sends = [pltpu.make_async_copy(stage[i], outs[i], sem.at[22 + i]) for i in range(15)]
    width, rows = o4.shape[2], od.shape[1]
    for i in range(8):
        stage[7 + i][...] = ov[i : i + 1, :ROWS]
    stage[6][...] = jnp.concatenate([ov[8 + i : 9 + i, :] for i in range(3)], 1).reshape(4 * ROWS)
    for i in range(6, 15):
        sends[i].start()

    def hand_on(first, last):
        for i in range(first, last):
            takes[i].wait()
            gives[i].start()

    for i in range(4):
        stage[i][...] = o4[i].astype(F32)
        sends[i].start()
    hand_on(0, 4)
    for i in range(4):
        stage[4][:, i * width : (i + 1) * width] = ou[i].astype(F32)
    sends[4].start()
    hand_on(4, 6)
    for i in range(4):
        stage[5][:, i * rows : (i + 1) * rows] = od[i].astype(F32).T
    sends[5].start()
    hand_on(6, 8)
    for c in sends + gives:
        c.wait()


def finish(layer_out, input_grad, o4, ou, od, ov):
    width = o4.shape[2]
    hbm, vmem = pl.BlockSpec(memory_space=pl.ANY), pl.BlockSpec(memory_space=pltpu.VMEM)
    small = [(4 * ROWS,)] + [(1, ROWS)] * 8
    large = [(ROWS, width)] * 4 + [(ROWS, 4 * width), (od.shape[2], 4 * od.shape[1])]
    return pl.pallas_call(
        finish_kernel,
        name="finish",
        in_specs=[hbm] * 2 + [vmem] * 4,
        out_specs=[hbm] * 17,
        out_shape=[Shape(layer_out.shape, BF16), Shape(input_grad.shape, F32)]
        + [Shape(shape, F32) for shape in large + small],
        scratch_shapes=[pltpu.VMEM(shape, F32) for shape in large + small]
        + [
            pltpu.VMEM(layer_out.shape, BF16),
            pltpu.VMEM(input_grad.shape, F32),
            pltpu.SemaphoreType.DMA((37,)),
        ],
        compiler_params=params(),
    )(layer_out, input_grad, o4, ou, od, ov)


def fused_layer(
    tokens, counts, cotangent, query_weight, key_weight, value_weight, out_weight, query_bias,
    value_bias, out_bias, attention_gain, attention_shift, up_weight, up_bias, down_weight,
    down_bias, feed_gain, feed_shift,
):
    width = tokens.shape[2]
    shards = NX * NZ
    columns = up_weight.shape[1]
    rows = tokens.reshape(-1, width)
    vectors = (
        query_bias, value_bias, out_bias, attention_gain, attention_shift, down_bias, feed_gain,
        feed_shift, up_bias,
    )
    (
        w4, wu, wd, layer_out, query, keys, values, powers, context_t, first_t, err_two, resid_two,
        normal_one, pull, part_d, tokens_t, vec8, inverse, inverse_one, sums,
    ) = forward(
        counts, rows, vectors, cotangent.reshape(-1, width), query_weight, key_weight, value_weight,
        out_weight, up_weight, down_weight,
    )
    o4, ou, od, ov, input_grad = backward(
        part_d, err_two, pull, wd.reshape(columns, width), wu.reshape(width, columns), resid_two,
        normal_one, inverse_one, first_t, query, keys, values, powers, inverse, context_t, tokens_t,
        w4.reshape(4, width, width), vec8, sums,
    )
    layer_out, input_grad, gq, gk, gv, go, gu, gd, gub, *v = finish(
        layer_out, input_grad, o4, ou, od, ov
    )
    v = [i.reshape(-1) for i in v]
    return (
        layer_out.reshape(tokens.shape),
        input_grad.reshape(tokens.shape),
        gq, gk, gv, go, v[0], v[1], v[2], v[3], v[4], gu, gub, gd, v[5], v[6], v[7],
    )


def exact_gelu(value):
    return jax.nn.gelu(value, approximate=False)


def norm_forward(resid, gain, shift):
    average = jnp.mean(resid, axis=-1, keepdims=True)
    centred = resid - average
    spread = jnp.mean(centred * centred, axis=-1, keepdims=True)
    inverse = lax.rsqrt(spread + epsilon)
    normal = centred * inverse
    return (normal * gain + shift, normal, inverse)


def norm_backward(grad_out, normal, inverse, gain):
    scaled = grad_out * gain
    first_mean = jnp.mean(scaled, axis=-1, keepdims=True)
    second_mean = jnp.mean(scaled * normal, axis=-1, keepdims=True)
    grad_resid = inverse * (scaled - first_mean - normal * second_mean)
    return (grad_resid, jnp.sum(grad_out * normal, 0), jnp.sum(grad_out, 0))


def linear(rows, weight):
    return jnp.dot(rows, weight, preferred_element_type=jnp.float32)


def linear_back(grads, weight):
    return lax.dot_general(
        grads, weight, (((1,), (1,)), ((), ())), preferred_element_type=jnp.float32
    )


def outer_sum(rows, grads):
    return lax.dot_general(
        rows, grads, (((0,), (0,)), ((), ())), preferred_element_type=jnp.float32
    )


def column_sum(grads):
    return jnp.sum(grads.astype(jnp.float32), 0)


def on_device(
    tokens,
    counts,
    cotangent,
    query_weight,
    key_weight,
    value_weight,
    out_weight,
    query_bias,
    value_bias,
    out_bias,
    attention_gain,
    attention_shift,
    up_weight,
    up_bias,
    down_weight,
    down_bias,
    feed_gain,
    feed_shift,
):
    slots, length, width = tokens.shape
    heads = width // HEAD_DIM
    factor = HEAD_DIM ** (-0.5)
    positions = jnp.arange(length, dtype=jnp.int32)

    def split_heads(value):
        return value.reshape(slots, length, heads, HEAD_DIM)

    def masked_scores(query, keys, count):
        raw = jnp.einsum("qhd,khd->hqk", query, keys, preferred_element_type=jnp.float32)
        live = positions < count
        return jnp.where(live[None, None, :], raw * factor, -1000000000.0)

    def attend_forward(block):
        query, keys, values, count = block
        scores = masked_scores(query, keys, count)
        highest = jnp.max(scores, axis=-1, keepdims=True)
        powers = jnp.exp(scores - highest)
        totals = jnp.sum(powers, axis=-1, keepdims=True)
        probs = (powers / totals).astype(jnp.bfloat16)
        context = jnp.einsum("hqk,khd->qhd", probs, values, preferred_element_type=jnp.float32)
        return (context.reshape(length, width), highest + jnp.log(totals))

    def attend_backward(block):
        query, keys, values, count, logsum, grad_context = block
        scores = masked_scores(query, keys, count)
        probs = jnp.exp(scores - logsum)
        probs_low = probs.astype(jnp.bfloat16)
        grad_probs = jnp.einsum(
            "qhd,khd->hqk", grad_context, values, preferred_element_type=jnp.float32
        )
        inner = jnp.sum(probs * grad_probs, axis=-1, keepdims=True)
        grad_scores = (probs * (grad_probs - inner) * factor).astype(jnp.bfloat16)
        grad_query = jnp.einsum(
            "hqk,khd->qhd", grad_scores, keys, preferred_element_type=jnp.float32
        )
        grad_keys = jnp.einsum(
            "hqk,qhd->khd", grad_scores, query, preferred_element_type=jnp.float32
        )
        grad_values = jnp.einsum(
            "hqk,qhd->khd", probs_low, grad_context, preferred_element_type=jnp.float32
        )
        return (
            grad_query.reshape(length, width).astype(jnp.bfloat16),
            grad_keys.reshape(length, width).astype(jnp.bfloat16),
            grad_values.reshape(length, width).astype(jnp.bfloat16),
        )

    attention_set = (
        lax.all_gather(query_weight, "fsdp", axis=0, tiled=True),
        lax.all_gather(key_weight, "fsdp", axis=0, tiled=True),
        lax.all_gather(value_weight, "fsdp", axis=0, tiled=True),
        lax.all_gather(out_weight, "fsdp", axis=0, tiled=True),
        lax.all_gather(query_bias, "fsdp", axis=0, tiled=True),
        lax.all_gather(value_bias, "fsdp", axis=0, tiled=True),
        lax.all_gather(out_bias, "fsdp", axis=0, tiled=True),
        lax.all_gather(attention_gain, "fsdp", axis=0, tiled=True),
        lax.all_gather(attention_shift, "fsdp", axis=0, tiled=True),
    )
    feed_set = (
        lax.all_gather(up_weight, "fsdp", axis=0, tiled=True),
        lax.all_gather(up_bias, "fsdp", axis=0, tiled=True),
        lax.all_gather(down_weight, "fsdp", axis=0, tiled=True),
        lax.all_gather(down_bias, "fsdp", axis=0, tiled=True),
        lax.all_gather(feed_gain, "fsdp", axis=0, tiled=True),
        lax.all_gather(feed_shift, "fsdp", axis=0, tiled=True),
    )
    whole_query, whole_key, whole_value, whole_out = (
        attention_set[0],
        attention_set[1],
        attention_set[2],
        attention_set[3],
    )
    whole_up, whole_down = (feed_set[0], feed_set[2])
    rows = tokens.reshape(-1, width)
    query = (linear(rows, whole_query) + attention_set[4].astype(jnp.float32)).astype(jnp.bfloat16)
    keys = linear(rows, whole_key).astype(jnp.bfloat16)
    values = (linear(rows, whole_value) + attention_set[5].astype(jnp.float32)).astype(jnp.bfloat16)
    context_rows, logsum = lax.map(
        attend_forward, (split_heads(query), split_heads(keys), split_heads(values), counts)
    )
    context = context_rows.reshape(-1, width).astype(jnp.bfloat16)
    branch = linear(context, whole_out) + attention_set[6].astype(jnp.float32)
    gain_one = attention_set[7].astype(jnp.float32)
    first, normal_one, inverse_one = norm_forward(
        rows.astype(jnp.float32) + branch, gain_one, attention_set[8].astype(jnp.float32)
    )
    first_low = first.astype(jnp.bfloat16)
    hidden = linear(first_low, whole_up) + feed_set[1].astype(jnp.float32)
    activated, gelu_pull = jax.vjp(exact_gelu, hidden)
    act_low = activated.astype(jnp.bfloat16)
    second = linear(act_low, whole_down) + feed_set[3].astype(jnp.float32)
    gain_two = feed_set[4].astype(jnp.float32)
    output, normal_two, inverse_two = norm_forward(
        first + second, gain_two, feed_set[5].astype(jnp.float32)
    )
    live = (positions[None, :] < counts[:, None]).reshape(-1, 1)
    layer_out = jnp.where(live, output, 0.0).astype(jnp.bfloat16).reshape(tokens.shape)
    back_feed = (
        lax.all_gather(up_weight, "fsdp", axis=0, tiled=True),
        lax.all_gather(down_weight, "fsdp", axis=0, tiled=True),
    )
    back_up, back_down = (back_feed[0], back_feed[1])
    grad_y = jnp.where(live, cotangent.reshape(-1, width).astype(jnp.float32), 0.0)
    resid_two, grad_feed_gain, grad_feed_shift = norm_backward(
        grad_y, normal_two, inverse_two, gain_two
    )
    err_two = resid_two.astype(jnp.bfloat16)
    grad_down_weight = outer_sum(act_low, err_two)
    grad_down_bias = column_sum(err_two)
    grad_act = linear_back(err_two, back_down)
    grad_hidden = gelu_pull(grad_act)[0].astype(jnp.bfloat16)
    grad_up_weight = outer_sum(first_low, grad_hidden)
    grad_up_bias = column_sum(grad_hidden)
    grad_first = resid_two + linear_back(grad_hidden, back_up)
    feed_shards = (
        lax.psum_scatter(
            grad_up_weight.astype(jnp.bfloat16), "fsdp", scatter_dimension=0, tiled=True
        ).astype(jnp.float32),
        lax.psum_scatter(
            grad_up_bias.astype(jnp.bfloat16), "fsdp", scatter_dimension=0, tiled=True
        ).astype(jnp.float32),
        lax.psum_scatter(
            grad_down_weight.astype(jnp.bfloat16), "fsdp", scatter_dimension=0, tiled=True
        ).astype(jnp.float32),
        lax.psum_scatter(
            grad_down_bias.astype(jnp.bfloat16), "fsdp", scatter_dimension=0, tiled=True
        ).astype(jnp.float32),
        lax.psum_scatter(
            grad_feed_gain.astype(jnp.bfloat16), "fsdp", scatter_dimension=0, tiled=True
        ).astype(jnp.float32),
        lax.psum_scatter(
            grad_feed_shift.astype(jnp.bfloat16), "fsdp", scatter_dimension=0, tiled=True
        ).astype(jnp.float32),
    )
    back_attention = (
        lax.all_gather(query_weight, "fsdp", axis=0, tiled=True),
        lax.all_gather(key_weight, "fsdp", axis=0, tiled=True),
        lax.all_gather(value_weight, "fsdp", axis=0, tiled=True),
        lax.all_gather(out_weight, "fsdp", axis=0, tiled=True),
    )
    back_query, back_key, back_value, back_out = (
        back_attention[0],
        back_attention[1],
        back_attention[2],
        back_attention[3],
    )
    resid_one, grad_attention_gain, grad_attention_shift = norm_backward(
        grad_first, normal_one, inverse_one, gain_one
    )
    err_one = resid_one.astype(jnp.bfloat16)
    grad_out_weight = outer_sum(context, err_one)
    grad_out_bias = column_sum(err_one)
    grad_context = linear_back(err_one, back_out).astype(jnp.bfloat16)
    grad_query, grad_keys, grad_values = lax.map(
        attend_backward,
        (
            split_heads(query),
            split_heads(keys),
            split_heads(values),
            counts,
            logsum,
            split_heads(grad_context),
        ),
    )
    grad_query = grad_query.reshape(-1, width)
    grad_keys = grad_keys.reshape(-1, width)
    grad_values = grad_values.reshape(-1, width)
    grad_query_weight = outer_sum(rows, grad_query)
    grad_key_weight = outer_sum(rows, grad_keys)
    grad_value_weight = outer_sum(rows, grad_values)
    grad_query_bias = column_sum(grad_query)
    grad_value_bias = column_sum(grad_values)
    input_grad = (
        resid_one
        + linear_back(grad_query, back_query)
        + linear_back(grad_keys, back_key)
        + linear_back(grad_values, back_value)
    )
    attention_shards = (
        lax.psum_scatter(
            grad_query_weight.astype(jnp.bfloat16), "fsdp", scatter_dimension=0, tiled=True
        ).astype(jnp.float32),
        lax.psum_scatter(
            grad_key_weight.astype(jnp.bfloat16), "fsdp", scatter_dimension=0, tiled=True
        ).astype(jnp.float32),
        lax.psum_scatter(
            grad_value_weight.astype(jnp.bfloat16), "fsdp", scatter_dimension=0, tiled=True
        ).astype(jnp.float32),
        lax.psum_scatter(
            grad_out_weight.astype(jnp.bfloat16), "fsdp", scatter_dimension=0, tiled=True
        ).astype(jnp.float32),
        lax.psum_scatter(
            grad_query_bias.astype(jnp.bfloat16), "fsdp", scatter_dimension=0, tiled=True
        ).astype(jnp.float32),
        lax.psum_scatter(
            grad_value_bias.astype(jnp.bfloat16), "fsdp", scatter_dimension=0, tiled=True
        ).astype(jnp.float32),
        lax.psum_scatter(
            grad_out_bias.astype(jnp.bfloat16), "fsdp", scatter_dimension=0, tiled=True
        ).astype(jnp.float32),
        lax.psum_scatter(
            grad_attention_gain.astype(jnp.bfloat16), "fsdp", scatter_dimension=0, tiled=True
        ).astype(jnp.float32),
        lax.psum_scatter(
            grad_attention_shift.astype(jnp.bfloat16), "fsdp", scatter_dimension=0, tiled=True
        ).astype(jnp.float32),
    )
    summed = lax.psum(
        (
            attention_shards[0],
            attention_shards[1],
            attention_shards[2],
            attention_shards[3],
            attention_shards[4],
            attention_shards[5],
            attention_shards[6],
            attention_shards[7],
            attention_shards[8],
            feed_shards[0],
            feed_shards[1],
            feed_shards[2],
            feed_shards[3],
            feed_shards[4],
            feed_shards[5],
        ),
        "dp",
    )
    return (
        layer_out,
        input_grad.reshape(tokens.shape),
        summed[0],
        summed[1],
        summed[2],
        summed[3],
        summed[4],
        summed[5],
        summed[6],
        summed[7],
        summed[8],
        summed[9],
        summed[10],
        summed[11],
        summed[12],
        summed[13],
        summed[14],
    )


def solution(mesh):
    small = mesh.shape["dp"] == 4 and mesh.shape["fsdp"] == NX * NZ
    return jax.shard_map(
        fused_layer if small else on_device,
        mesh=mesh,
        in_specs=(
            P(("dp", "fsdp"), None, None),
            P(("dp", "fsdp")),
            P(("dp", "fsdp"), None, None),
            P("fsdp", None),
            P("fsdp", None),
            P("fsdp", None),
            P("fsdp", None),
            P("fsdp"),
            P("fsdp"),
            P("fsdp"),
            P("fsdp"),
            P("fsdp"),
            P("fsdp", None),
            P("fsdp"),
            P("fsdp", None),
            P("fsdp"),
            P("fsdp"),
            P("fsdp"),
        ),
        out_specs=(
            P(("dp", "fsdp"), None, None),
            P(("dp", "fsdp"), None, None),
            P("fsdp", None),
            P("fsdp", None),
            P("fsdp", None),
            P("fsdp", None),
            P("fsdp"),
            P("fsdp"),
            P("fsdp"),
            P("fsdp"),
            P("fsdp"),
            P("fsdp", None),
            P("fsdp"),
            P("fsdp", None),
            P("fsdp"),
            P("fsdp"),
            P("fsdp"),
        ),
        check_vma=False,
    )
```
